32 devices in a mesh: grp: 4 (over x, core), ep: 8 (over z, y).
Axes of the slice: x: 2, y: 2, z: 4, core: 2. Of those that a mesh axis runs over, the one named last changes fastest.
Arguments:
- tokens: bfloat16 [32768, 512], P(('grp', 'ep')), may hold values from -6 to 6
- segments: int32 [128, 256], P(('grp', 'ep')), may hold values from 0 to 7, never falling along the last dimension, each value on 1 to 128 neighbouring positions
- patch_mask: int32 [128, 256], P(('grp', 'ep')), may hold values 0 or 1
- choices: int32 [32768, 2], P(('grp', 'ep')), may hold values from 0 to 7, all different within a row
- priority: int32 [32, 1024], P(('grp', 'ep')), may hold values from 0 to 1023, each once within a row
- first_gain: bfloat16 [512], P(('grp', 'ep')), may hold values from 0.5 to 1.5
- joint_weight: bfloat16 [512, 1536], P(('grp', 'ep')), may hold values from -0.25 to 0.25
- output_weight: bfloat16 [512, 512], P(('grp', 'ep')), may hold values from -1 to 1
- second_gain: bfloat16 [512], P(('grp', 'ep')), may hold values from 0.5 to 1.5
- router_weight: bfloat16 [512, 8], P(('grp', 'ep')), may hold values from -0.19921875 to 0.19921875
- expert_up: bfloat16 [8, 512, 2048], P('ep'), may hold values from -0.25 to 0.25
- expert_down: bfloat16 [8, 2048, 512], P('ep'), may hold values from -0.75 to 0.75
- out_grad: bfloat16 [32768, 512], P(('grp', 'ep')), may hold values from -6 to 6
Outputs:
- output: bfloat16 [32768, 512], P(('grp', 'ep'))
- tokens_grad: float32 [32768, 512], P(('grp', 'ep'))
- first_gain_grad: float32 [512], P(('grp', 'ep'))
- joint_weight_grad: float32 [512, 1536], P(('grp', 'ep'))
- output_weight_grad: float32 [512, 512], P(('grp', 'ep'))
- second_gain_grad: float32 [512], P(('grp', 'ep'))
- router_weight_grad: float32 [512, 8], P(('grp', 'ep'))
- expert_up_grad: float32 [8, 512, 2048], P('ep')
- expert_down_grad: float32 [8, 2048, 512], P('ep')
The draws below stay inside these ranges and needn't reach their ends.
Inputs may be any that keep to these rules, and one draw needn't show every extreme that they name: `segments`: within a sequence the ids never fall. `choices`: a token's two experts differ. `priority`: each row holds every number below 1024 once.
All inputs are finite; a program needn't handle non-finite values. No bound on the sum of `patch_mask` on one device may be relied on, other than what follows from the above.
Results may differ from the reference program's by a relative error of at most 0.013.
Values may be sent and summed in bfloat16 or wider, within the bound.
A program may use at most 192 MiB of HBM per device.

```python
import math
import jax
import jax.numpy as jnp
import numpy as np
from jax import lax

D = 512
HEADS = 8
HEAD = 64
FF = 2048
TOP = 2
LEN = 256
EXPERTS = 8
TOK_DEV = 1024
TOKENS = 32768
SEQS = 128
BLOCKS = 32
CAP = 269


def set_ends(array, rng, smallest, high):
    spot = [jax.random.randint(jax.random.fold_in(rng, axis), (), 0, length) for axis, length in enumerate(array.shape)]
    longest = array.shape.index(max(array.shape))
    next_to = spot[:longest] + [(spot[longest] + 1) % array.shape[longest]] + spot[longest + 1:]
    return array.at[tuple(spot)].set(smallest).at[tuple(next_to)].set(high)


def block_scale(own_key, extent, cuts, low, largest):
    def one(dim, shards_of):
        steps = jax.random.uniform(jax.random.fold_in(jax.random.fold_in(own_key, 6), dim), (shards_of,), jnp.float32, low / len(cuts), largest / len(cuts))
        return jnp.repeat(jnp.exp(steps), extent[dim] // shards_of).reshape((-1,) + (1,) * (len(extent) - dim - 1))

    level = one(*cuts[0])
    for cut in cuts[1:]:
        level = level * one(*cut)
    return level


def choose_distinct(rng, rows, amount, top, lift):
    ranking = jax.random.permutation(jax.random.fold_in(rng, 1), amount)
    favour = ranking
    for power in range(3):
        favour = favour * favour // amount
    favour = favour * lift // amount
    chance = jax.random.randint(jax.random.fold_in(rng, 2), (rows, amount), 0, 4096) + favour
    sure = jax.random.permutation(jax.random.fold_in(rng, 3), rows)[jnp.arange(amount) % rows]
    chance = jnp.where(jnp.arange(rows)[:, None] == sure[None, :], 1 << 14, chance)
    merit = chance * amount + jnp.arange(amount)
    return lax.top_k(merit.astype(jnp.int32), top)[1].astype(jnp.int32)


def profile(number_of, total, most, lean):
    weights = [(1 << 20) // math.isqrt(standing ** lean) + 1 for standing in range(2, number_of + 1)]
    surplus, given = total - most - (number_of - 1), [1] * (number_of - 1)
    while surplus > 0:
        free = [i for i in range(number_of - 1) if given[i] < most]
        pool, budget = sum([weights[i] for i in free]), surplus
        for i in free:
            more = min(most - given[i], max(1, budget * weights[i] // pool), surplus)
            given[i] = given[i] + more
            surplus = surplus - more
    return np.array([most] + given)


def uneven_parts(key, count, total, limit, skew):
    if count == 2:
        one = jax.random.randint(key, (), max(1, total - limit), min(limit, total - 1) + 1)
        return jnp.stack([one, total - one])
    lengths = jnp.asarray(profile(count, total, limit, skew), jnp.int32)
    couples = (count - 1) // 2
    source_of, sink = lengths[1:1 + 2 * couples:2], lengths[2:2 + 2 * couples:2]
    room = jnp.minimum(source_of - 1, limit - sink)
    passed = jax.random.randint(jax.random.fold_in(key, 1), (couples,), 0, 1 << 20) % (room + 1)
    lengths = lengths.at[1:1 + 2 * couples:2].set(source_of - passed).at[2:2 + 2 * couples:2].set(sink + passed)
    return lengths[jax.random.permutation(jax.random.fold_in(key, 2), count)]


def noise(stream_key, extent, deviation, limit, cuts=(), held_as=jnp.bfloat16):
    loudness = block_scale(stream_key, extent, cuts, -0.22, 0.18) if cuts else 1.0
    values = jax.random.normal(stream_key, extent, jnp.float32) * deviation * loudness
    return jnp.minimum(jnp.maximum(values, -limit), limit).astype(held_as)


def setup_inputs(seed: int = 0) -> dict:
    streams_of = jax.random.split(jax.random.key(seed), 14)
    tokens = noise(streams_of[0], (TOKENS, D), 1.0, 6.0, ((0, 32),))
    segments = jax.vmap(lambda own: jnp.searchsorted(jnp.cumsum(uneven_parts(own, 8, LEN, LEN // 2, 0)), jnp.arange(LEN), side="right"))(jax.random.split(streams_of[1], SEQS)).reshape((SEQS, LEN)).astype(jnp.int32)
    patch_mask = set_ends((jax.random.randint(streams_of[2], (SEQS, LEN), 0, 8) < 7).astype(jnp.int32), jax.random.fold_in(streams_of[2], 1), 0, 1)
    choices = choose_distinct(streams_of[3], TOKENS, EXPERTS, TOP, 2048)
    priority = jax.vmap(lambda own: jax.random.permutation(own, TOK_DEV))(jax.random.split(streams_of[4], BLOCKS)).reshape((BLOCKS, TOK_DEV)).astype(jnp.int32)
    first_gain = jnp.clip(1.0 + 0.1 * jax.random.normal(streams_of[5], (D,), jnp.float32), 0.5, 1.5).astype(jnp.bfloat16)
    joint_weight = noise(streams_of[6], (D, 3 * D), D ** -0.5, 0.25, ((0, 32),))
    output_weight = noise(streams_of[7], (D, D), (D // 16) ** -0.5, 1.0, ((0, 32),))
    second_gain = jnp.clip(1.0 + 0.1 * jax.random.normal(streams_of[8], (D,), jnp.float32), 0.5, 1.5).astype(jnp.bfloat16)
    router_weight = noise(streams_of[9], (D, EXPERTS), 0.035, 0.19921875, ((0, 32),))
    expert_up = noise(streams_of[10], (EXPERTS, D, FF), D ** -0.5, 0.25, ((0, 8),))
    expert_down = noise(streams_of[11], (EXPERTS, FF, D), (4096 // (EXPERTS * EXPERTS)) ** -0.5, 0.75, ((0, 8),))
    out_grad = noise(streams_of[12], (TOKENS, D), 1.0, 6.0, ((0, 32),))
    return dict(tokens=tokens, segments=segments, patch_mask=patch_mask, choices=choices, priority=priority, first_gain=first_gain, joint_weight=joint_weight, output_weight=output_weight, second_gain=second_gain, router_weight=router_weight, expert_up=expert_up, expert_down=expert_down, out_grad=out_grad)


@jax.custom_vjp
def low(v):
    return lax.optimization_barrier(v.astype(jnp.bfloat16)).astype(jnp.float32)

@jax.custom_vjp
def low_back(v):
    return v

def low_keep(v):
    return (low(v), None)

def low_pass(kept, grad):
    return (grad,)

def back_keep(v):
    return (v, None)

def back_low(kept, grad):
    return (low(grad),)
low.defvjp(low_keep, low_pass)
low_back.defvjp(back_keep, back_low)

def layer_norm(values, gain):
    mean = lax.optimization_barrier(jnp.mean(values, axis=-1, keepdims=True))
    centred = values - mean
    spread = lax.optimization_barrier(jnp.mean(centred * centred, axis=-1, keepdims=True))
    return centred * lax.rsqrt(spread + 1e-06) * gain

def matmul(left, right):
    return jnp.dot(left, right, precision=lax.Precision.HIGHEST)

def route(picks, live, ranks):
    row_count = picks.shape[0]
    labels = lax.broadcasted_iota(jnp.int32, (row_count, EXPERTS), 1)
    first = (picks[:, 0:1] == labels).astype(jnp.int32)
    second = (picks[:, 1:2] == labels).astype(jnp.int32)
    earlier = (ranks[None, :] < ranks[:, None]).astype(jnp.int32)
    live_row = live[None, :]
    same_one = (picks[None, :, 0] == picks[:, 0:1]).astype(jnp.int32) * live_row
    same_two = (picks[None, :, 1] == picks[:, 1:2]).astype(jnp.int32) * live_row
    cross = (picks[None, :, 0] == picks[:, 1:2]).astype(jnp.int32) * live_row
    place_one = lax.optimization_barrier(jnp.sum(earlier * same_one, axis=1)).astype(jnp.int32)
    place_two = (lax.optimization_barrier(jnp.sum(earlier * same_two, axis=1)) + lax.optimization_barrier(jnp.sum(cross, axis=1))).astype(jnp.int32)
    keep_one = (live > 0) & (place_one < CAP)
    keep_two = (live > 0) & (place_two < CAP)
    dummy = EXPERTS * CAP
    slot_one = jnp.where(keep_one, picks[:, 0] * CAP + place_one, dummy).astype(jnp.int32)
    slot_two = jnp.where(keep_two, picks[:, 1] * CAP + place_two, dummy).astype(jnp.int32)
    pick_one = (first * keep_one[:, None].astype(jnp.int32)).astype(jnp.float32)
    pick_two = (second * keep_two[:, None].astype(jnp.int32)).astype(jnp.float32)
    return (slot_one, slot_two, pick_one, pick_two)

def attend_packed(item):
    block, group, live = item
    query, key, value = (block[:, 0], block[:, 1], block[:, 2])
    rows = group.shape[0]
    index = lax.broadcasted_iota(jnp.int32, (rows, rows), 0)
    other = lax.broadcasted_iota(jnp.int32, (rows, rows), 1)
    allowed = (group[:, None] == group[None, :]) & ((live[None, :] > 0) | (index == other))
    scores = jnp.einsum('qhd,khd->hqk', query, key, precision=lax.Precision.HIGHEST) * HEAD ** (-0.5)
    scores = low_back(scores)
    masked = jnp.where(allowed[None], scores, -1e+30)
    top = lax.optimization_barrier(jnp.max(masked, axis=-1, keepdims=True))
    weights = jnp.exp(masked - top)
    probs = low(weights / lax.optimization_barrier(jnp.sum(weights, axis=-1, keepdims=True)))
    return jnp.einsum('hqk,khd->qhd', probs, value, precision=lax.Precision.HIGHEST)

def forward(inputs, first_gain, joint_weight, output_weight, second_gain, router_weight, expert_up, expert_down, group, live, routing):
    slot_one, slot_two, pick_one, pick_two = routing
    row_count = inputs.shape[0]
    block_rows = min(row_count, 512)
    normed = low(layer_norm(inputs, first_gain))
    joint = low_back(low(matmul(normed, joint_weight)))
    joint = joint.reshape(row_count // block_rows, block_rows, 3, HEADS, HEAD)
    groups = group.reshape(row_count // block_rows, block_rows)
    lives = live.reshape(row_count // block_rows, block_rows)
    mixed = lax.map(jax.checkpoint(attend_packed), (joint, groups, lives))
    mixed = low_back(low(mixed.reshape(row_count, D)))
    branch = low_back(matmul(mixed, output_weight))
    state = inputs + branch
    normed_two = low(layer_norm(state, second_gain))
    logits = low_back(matmul(normed_two, router_weight))
    gate = jax.nn.softmax(logits, axis=-1)
    buffer = jnp.zeros((EXPERTS * CAP + 1, D), jnp.float32)
    buffer = buffer.at[slot_one].add(normed_two).at[slot_two].add(normed_two)
    buffer = low_back(buffer[:EXPERTS * CAP].reshape(EXPERTS, CAP, D))
    pre = low_back(jnp.einsum('ecd,edf->ecf', buffer, expert_up, precision=lax.Precision.HIGHEST))
    act = low(jax.nn.gelu(pre, approximate=False))
    returned = low_back(low(jnp.einsum('ecf,efd->ecd', act, expert_down, precision=lax.Precision.HIGHEST)))
    padded = jnp.concatenate([returned.reshape(EXPERTS * CAP, D), jnp.zeros((1, D), jnp.float32)], axis=0)
    gate_one = lax.optimization_barrier(jnp.sum(gate * pick_one, axis=1))
    gate_two = lax.optimization_barrier(jnp.sum(gate * pick_two, axis=1))
    mixture = gate_one[:, None] * padded[slot_one] + gate_two[:, None] * padded[slot_two]
    return state + mixture

def reference(tokens, segments, patch_mask, choices, priority, first_gain, joint_weight, output_weight, second_gain, router_weight, expert_up, expert_down, out_grad):
    weights = (first_gain.astype(jnp.float32), joint_weight.astype(jnp.float32), output_weight.astype(jnp.float32), second_gain.astype(jnp.float32), router_weight.astype(jnp.float32), expert_up.astype(jnp.float32), expert_down.astype(jnp.float32))
    inputs_all = tokens.astype(jnp.float32).reshape(BLOCKS, TOK_DEV, D)
    grads_all = out_grad.astype(jnp.float32).reshape(BLOCKS, TOK_DEV, D)
    seg_all = segments.reshape(BLOCKS, TOK_DEV)
    live_all = patch_mask.reshape(BLOCKS, TOK_DEV)
    picks_all = choices.reshape(BLOCKS, TOK_DEV, TOP)
    position = jnp.arange(TOK_DEV, dtype=jnp.int32)

    def step(totals, item):
        inputs, seg, live, picks, ranks, grad = item
        routing = route(picks, live, ranks)
        group = position // LEN * LEN + seg

        def run(values, gain_a, joint_w, out_w, gain_b, router_w, up_w, down_w):
            return forward(values, gain_a, joint_w, out_w, gain_b, router_w, up_w, down_w, group, live, routing)
        result, pull = jax.vjp(run, inputs, *weights)
        grads = pull(grad)
        totals = tuple((total + part for total, part in zip(totals, grads[1:])))
        return (totals, (result.astype(jnp.bfloat16), grads[0]))
    start = tuple((jnp.zeros_like(weight) for weight in weights))
    totals, (results, input_grads) = lax.scan(step, start, (inputs_all, seg_all, live_all, picks_all, priority, grads_all))
    return (results.reshape(TOKENS, D), input_grads.reshape(TOKENS, D), totals[0], totals[1], totals[2], totals[3], totals[4], totals[5], totals[6])
```

```python
import functools

import jax
import jax.numpy as jnp
from jax import lax
from jax.experimental import pallas as pl
from jax.experimental.pallas import tpu as pltpu
from jax.sharding import PartitionSpec as P

MESH = pl.DeviceIdType.MESH
MIB = 1 << 20

HEADS = 8


EPSILON = 1e-06
NEGATIVE = -1e30


def normalize(values, gain):
    mean = jnp.mean(values, axis=-1, keepdims=True)
    centred = values - mean
    inverse = lax.rsqrt(jnp.mean(centred * centred, axis=-1, keepdims=True) + EPSILON)
    unit = centred * inverse
    return (unit * gain, unit, inverse)


def normalize_back(incoming, gain, unit, inverse):
    scaled = incoming * gain
    inner = (
        scaled
        - jnp.mean(scaled, axis=-1, keepdims=True)
        - unit * jnp.mean(scaled * unit, axis=-1, keepdims=True)
    )
    return (inverse * inner, jnp.sum(incoming * unit, axis=0))


def outer(left, right):
    return lax.dot_general(
        left, right, (((0,), (0,)), ((), ())), preferred_element_type=jnp.float32
    )


def times_t(left, right):
    return lax.dot_general(
        left, right, (((1,), (1,)), ((), ())), preferred_element_type=jnp.float32
    )


def route(picks, live, ranks, expert_count, capacity):
    row_count = picks.shape[0]
    labels = lax.broadcasted_iota(jnp.int32, (row_count, expert_count), 1)
    first = (picks[:, 0:1] == labels).astype(jnp.int32)
    second = (picks[:, 1:2] == labels).astype(jnp.int32)
    live_col = live[:, None]
    earlier = (ranks[None, :] < ranks[:, None]).astype(jnp.int32)
    first_live = first * live_col
    second_live = second * live_col
    place_one = jnp.sum(
        jnp.dot(earlier, first_live, preferred_element_type=jnp.int32) * first, axis=1
    )
    ahead = (
        jnp.dot(earlier, second_live, preferred_element_type=jnp.int32)
        + jnp.sum(first_live, axis=0)[None, :]
    )
    place_two = jnp.sum(ahead * second, axis=1)
    keep_one = (live > 0) & (place_one < capacity)
    keep_two = (live > 0) & (place_two < capacity)
    stride = -(-capacity // 16) * 16
    dummy = expert_count * stride
    slot_one = jnp.where(keep_one, picks[:, 0] * stride + place_one, dummy)
    slot_two = jnp.where(keep_two, picks[:, 1] * stride + place_two, dummy)
    return (slot_one, slot_two)


def visible(group, live):
    rows = group.shape[0]
    index = lax.broadcasted_iota(jnp.int32, (rows, rows), 0)
    other = lax.broadcasted_iota(jnp.int32, (rows, rows), 1)
    return (group[:, None] == group[None, :]) & ((live[None, :] > 0) | (index == other))


def attend_forward(query, key, value, allowed, factor):
    scores = jnp.einsum("qhd,khd->hqk", query, key, preferred_element_type=jnp.float32) * factor
    masked = jnp.where(allowed[None], scores, NEGATIVE)
    top = jnp.max(masked, axis=-1, keepdims=True)
    weights = jnp.exp(masked - top)
    total = jnp.sum(weights, axis=-1, keepdims=True)
    probs = (weights / total).astype(jnp.bfloat16)
    mixed = jnp.einsum("hqk,khd->qhd", probs, value, preferred_element_type=jnp.float32)
    return (mixed, top + jnp.log(total))


def attend_backward(query, key, value, allowed, log_total, grad_mixed, factor):
    scores = jnp.einsum("qhd,khd->hqk", query, key, preferred_element_type=jnp.float32) * factor
    masked = jnp.where(allowed[None], scores, NEGATIVE)
    probs = jnp.exp(masked - log_total)
    grad_value = jnp.einsum(
        "hqk,qhd->khd", probs.astype(jnp.bfloat16), grad_mixed, preferred_element_type=jnp.float32
    )
    grad_probs = jnp.einsum("qhd,khd->hqk", grad_mixed, value, preferred_element_type=jnp.float32)
    delta = jnp.sum(probs * grad_probs, axis=-1, keepdims=True)
    grad_scores = (probs * (grad_probs - delta)).astype(jnp.bfloat16)
    grad_query = (
        jnp.einsum("hqk,khd->qhd", grad_scores, key, preferred_element_type=jnp.float32) * factor
    )
    grad_key = (
        jnp.einsum("hqk,qhd->khd", grad_scores, query, preferred_element_type=jnp.float32) * factor
    )
    return jnp.stack([grad_query, grad_key, grad_value], axis=1)


def partner(me, step, count):
    other, bit = 0, 1
    while bit < count:
        other = other + bit * lax.rem(lax.div(me, bit) + lax.div(step, bit), 2)
        bit *= 2
    return other


def expert_kernel(
    count,
    experts,
    sent_rows,
    sent_grads,
    up_ref,
    down_ref,
    router_ref,
    back_ref,
    ret_ref,
    grad_up_ref,
    grad_down_ref,
    grad_router_ref,
    rows,
    grads,
    gated,
    act,
    grad_pre,
    logit_grads,
    out_grads,
    out_ret,
    turned,
    sems,
    local_sem,
):
    me = lax.axis_index("ep")
    block, width = rows.shape[1:]
    hidden = up_ref.shape[1]
    chunk = 512
    barrier = pltpu.get_barrier_semaphore()

    def greet(step, carry):
        pl.semaphore_signal(
            barrier, inc=1, device_id={"ep": partner(me, step, count)}, device_id_type=MESH
        )
        return carry

    lax.fori_loop(1, count, greet, 0)
    pl.semaphore_wait(barrier, count - 1)

    def remote(kind, source, target, step):
        return pltpu.make_async_remote_copy(
            src_ref=source,
            dst_ref=target,
            send_sem=sems.at[2 * kind, step],
            recv_sem=sems.at[2 * kind + 1, step],
            device_id={"ep": partner(me, step, count)},
            device_id_type=MESH,
        )

    def send_rows(step):
        return remote(0, sent_rows.at[partner(me, step, count)], rows.at[step], step)

    def send_grads(step):
        return remote(1, sent_grads.at[partner(me, step, count)], grads.at[step], step)

    def send_back(step):
        return remote(2, out_grads.at[step], back_ref.at[me], step)

    def send_ret(step):
        return remote(3, out_ret.at[step], ret_ref.at[me], step)

    own = [
        pltpu.make_async_copy(sent_rows.at[me], rows.at[0], local_sem.at[0]),
        pltpu.make_async_copy(sent_grads.at[me], grads.at[0], local_sem.at[1]),
        pltpu.make_async_copy(out_grads.at[0], back_ref.at[me], local_sem.at[2]),
        pltpu.make_async_copy(out_ret.at[0], ret_ref.at[me], local_sem.at[3]),
    ]
    own[0].start()
    own[1].start()

    def start(step, carry):
        send_rows(step).start()
        send_grads(step).start()
        return carry

    lax.fori_loop(1, count, start, 0)
    own[0].wait()
    own[1].wait()
    lanes = lax.broadcasted_iota(jnp.int32, (block, router_ref.shape[1]), 1)

    def one_block(step, carry):
        @pl.when(step > 0)
        def _():
            send_rows(step).wait_recv()
            send_grads(step).wait_recv()

        mine = rows[step]
        cotangent = grads[step].astype(jnp.float32)
        place = pl.ds(pl.multiple_of(step * block, 16), block)
        logits = jnp.dot(mine, router_ref[...], preferred_element_type=jnp.float32)
        logits = jnp.where(lanes < experts, logits, NEGATIVE)
        weights = jnp.exp(logits - jnp.max(logits, axis=1, keepdims=True))
        gate_all = weights / jnp.sum(weights, axis=1, keepdims=True)
        here = (lanes == me).astype(jnp.float32)
        gate = jnp.sum(gate_all * here, axis=1, keepdims=True)
        pair = (gate * cotangent).astype(jnp.bfloat16)
        gated[place, :] = pair
        ret = jnp.zeros((block, width), jnp.float32)
        back = jnp.zeros((block, width), jnp.float32)
        for first in range(0, hidden, chunk):
            span = slice(first, first + chunk)
            pre = jnp.dot(mine, up_ref[:, span], preferred_element_type=jnp.float32)
            cdf = 0.5 * (1.0 + lax.erf(pre * 0.7071067811865476))
            density = jnp.exp(-0.5 * pre * pre) * 0.3989422804014327
            low = (pre * cdf).astype(jnp.bfloat16)
            act[place, span] = low
            ret = ret + jnp.dot(low, down_ref[span, :], preferred_element_type=jnp.float32)
            grad_act = times_t(pair, down_ref[span, :])
            slope = (grad_act * (cdf + pre * density)).astype(jnp.bfloat16)
            grad_pre[place, span] = slope
            back = back + times_t(slope, up_ref[:, span])
        ret = ret.astype(jnp.bfloat16).astype(jnp.float32)
        out_ret[step] = (gate * ret).astype(jnp.bfloat16)
        gate_grad = jnp.sum(cotangent * ret, axis=1, keepdims=True)
        low_logits = (gate * gate_grad * (here - gate_all)).astype(jnp.bfloat16)
        logit_grads[place, :] = low_logits
        back = back + times_t(low_logits, router_ref[...])
        out_grads[step] = back.astype(jnp.bfloat16)

        @pl.when(step > 0)
        def _():
            send_back(step).start()

        @pl.when(step == 0)
        def _():
            own[2].start()

        return carry

    lax.fori_loop(0, count, one_block, 0)
    own[3].start()

    def start_ret(step, carry):
        send_ret(step).start()
        return carry

    lax.fori_loop(1, count, start_ret, 0)
    turned[...] = jnp.transpose(rows[...].reshape(count * block, width))
    grad_router_ref[...] = jnp.dot(
        turned[...], logit_grads[...], preferred_element_type=jnp.float32
    )

    def up_chunk(index, carry):
        span = pl.ds(pl.multiple_of(index * chunk, chunk), chunk)
        grad_up_ref[:, span] = jnp.dot(
            turned[...], grad_pre[:, span], preferred_element_type=jnp.float32
        ).astype(jnp.bfloat16)
        return carry

    lax.fori_loop(0, hidden // chunk, up_chunk, 0)
    turned[...] = jnp.transpose(gated[...])

    def down_chunk(index, carry):
        span = pl.ds(pl.multiple_of(index * chunk, chunk), chunk)
        part = jnp.dot(turned[...], act[:, span], preferred_element_type=jnp.float32)
        grad_down_ref[span, :] = jnp.transpose(part).astype(jnp.bfloat16)
        return carry

    lax.fori_loop(0, hidden // chunk, down_chunk, 0)

    def finish(step, carry):
        send_rows(step).wait_send()
        send_grads(step).wait_send()
        send_back(step).wait()
        send_ret(step).wait()
        return carry

    lax.fori_loop(1, count, finish, 0)
    own[2].wait()
    own[3].wait()


def experts_both_ways(sent_rows, sent_grads, up, down, router):
    count, block, width = sent_rows.shape
    experts = router.shape[1]
    hidden = up.shape[1]
    router = jnp.pad(router, ((0, 0), (0, 128 - experts)))
    any_space = pl.BlockSpec(memory_space=pl.ANY)
    vmem = pl.BlockSpec(memory_space=pltpu.VMEM)
    low = jnp.bfloat16
    slots = count * block
    return pl.pallas_call(
        functools.partial(expert_kernel, count, experts),
        out_shape=(
            jax.ShapeDtypeStruct((count, block, width), low),
            jax.ShapeDtypeStruct((count, block, width), low),
            jax.ShapeDtypeStruct((width, hidden), low),
            jax.ShapeDtypeStruct((hidden, width), low),
            jax.ShapeDtypeStruct((width, 128), jnp.float32),
        ),
        in_specs=[any_space, any_space, vmem, vmem, vmem],
        out_specs=(any_space, any_space, vmem, vmem, vmem),
        scratch_shapes=[
            pltpu.VMEM((count, block, width), low),
            pltpu.VMEM((count, block, width), low),
            pltpu.VMEM((slots, width), low),
            pltpu.VMEM((slots, hidden), low),
            pltpu.VMEM((slots, hidden), low),
            pltpu.VMEM((slots, 128), low),
            pltpu.VMEM((count, block, width), low),
            pltpu.VMEM((count, block, width), low),
            pltpu.VMEM((width, slots), low),
            pltpu.SemaphoreType.DMA((8, count)),
            pltpu.SemaphoreType.DMA((4,)),
        ],
        compiler_params=pltpu.CompilerParams(
            collective_id=1, has_side_effects=True, vmem_limit_bytes=58 * MIB
        ),
        cost_estimate=pl.CostEstimate(
            flops=12 * slots * width * hidden, bytes_accessed=16 * MIB, transcendentals=0
        ),
    )(sent_rows, sent_grads, up, down, router)


def per_device(
    tokens,
    segments,
    patch_mask,
    choices,
    priority,
    first_gain,
    joint_weight,
    output_weight,
    second_gain,
    router_weight,
    expert_up,
    expert_down,
    out_grad,
):
    row_count, width = tokens.shape
    head_size = width // HEADS
    factor = head_size ** (-0.5)
    expert_count = router_weight.shape[1]
    length = segments.shape[1]
    capacity = (21 * choices.shape[1] * row_count + 20 * expert_count - 1) // (20 * expert_count)
    block_rows = min(row_count, 512)
    gain_one, joint_full, output_full, gain_two, router_full = (
        lax.all_gather(first_gain, ("grp", "ep"), axis=0, tiled=True),
        lax.all_gather(joint_weight, ("grp", "ep"), axis=0, tiled=True),
        lax.all_gather(output_weight, ("grp", "ep"), axis=0, tiled=True),
        lax.all_gather(second_gain, ("grp", "ep"), axis=0, tiled=True),
        lax.all_gather(router_weight, ("grp", "ep"), axis=0, tiled=True),
    )
    inputs = tokens.astype(jnp.float32)
    gain_one = gain_one.astype(jnp.float32)
    gain_two = gain_two.astype(jnp.float32)
    normed_f, unit_one, inverse_one = normalize(inputs, gain_one)
    normed = normed_f.astype(jnp.bfloat16)
    joint = jnp.dot(normed, joint_full, preferred_element_type=jnp.float32).astype(jnp.bfloat16)
    joint = joint.reshape(row_count, 3, HEADS, head_size)
    live = patch_mask.reshape(row_count)
    position = lax.broadcasted_iota(jnp.int32, (row_count,), 0)
    group = position // length * length + segments.reshape(row_count)
    masks = []
    mixed_parts = []
    log_parts = []
    for start in range(0, row_count, block_rows):
        allowed = visible(group[start : start + block_rows], live[start : start + block_rows])
        block = joint[start : start + block_rows]
        mixed_block, log_total = attend_forward(
            block[:, 0], block[:, 1], block[:, 2], allowed, factor
        )
        masks.append(allowed)
        mixed_parts.append(mixed_block)
        log_parts.append(log_total)
    mixed = jnp.concatenate(mixed_parts, axis=0).reshape(row_count, width).astype(jnp.bfloat16)
    state = inputs + jnp.dot(mixed, output_full, preferred_element_type=jnp.float32)
    normed_two_f, unit_two, inverse_two = normalize(state, gain_two)
    normed_two = normed_two_f.astype(jnp.bfloat16)
    slot_one, slot_two = route(
        choices, live, priority.reshape(row_count), expert_count, capacity
    )
    block = -(-capacity // 16) * 16
    slots = expert_count * block
    index = lax.broadcasted_iota(jnp.int32, (slots, row_count), 0)
    chosen = ((index == slot_one[None, :]) | (index == slot_two[None, :])).astype(jnp.bfloat16)
    spread = lambda values: (
        jnp.dot(chosen, values, preferred_element_type=jnp.float32)
        .astype(jnp.bfloat16)
        .reshape(expert_count, block, width)
    )
    collect = lambda values: outer(chosen, values.reshape(slots, width))
    grad = out_grad.astype(jnp.float32)
    back, returned, grad_up, grad_down, grad_router = experts_both_ways(
        spread(normed_two), spread(out_grad), expert_up[0], expert_down[0], router_full
    )
    output = (state + collect(returned)).astype(jnp.bfloat16)
    grad_router = grad_router[:, :expert_count]
    grad_normed_two = collect(back)
    grad_state_in, grad_gain_two = normalize_back(grad_normed_two, gain_two, unit_two, inverse_two)
    grad_state = grad + grad_state_in
    grad_branch = grad_state.astype(jnp.bfloat16)
    grad_output_w = outer(mixed, grad_branch)
    grad_mixed = (
        times_t(grad_branch, output_full).astype(jnp.bfloat16).reshape(row_count, HEADS, head_size)
    )
    grad_parts = []
    for number, start in enumerate(range(0, row_count, block_rows)):
        block = joint[start : start + block_rows]
        grad_parts.append(
            attend_backward(
                block[:, 0],
                block[:, 1],
                block[:, 2],
                masks[number],
                log_parts[number],
                grad_mixed[start : start + block_rows],
                factor,
            )
        )
    grad_joint = (
        jnp.concatenate(grad_parts, axis=0).reshape(row_count, 3 * width).astype(jnp.bfloat16)
    )
    grad_joint_w = outer(normed, grad_joint)
    grad_normed = times_t(grad_joint, joint_full)
    grad_inputs_in, grad_gain_one = normalize_back(grad_normed, gain_one, unit_one, inverse_one)
    tokens_grad = grad_state + grad_inputs_in
    shares = (
        lax.psum_scatter(grad_gain_one, ("grp", "ep"), scatter_dimension=0, tiled=True),
        lax.psum_scatter(grad_joint_w, ("grp", "ep"), scatter_dimension=0, tiled=True),
        lax.psum_scatter(grad_output_w, ("grp", "ep"), scatter_dimension=0, tiled=True),
        lax.psum_scatter(grad_gain_two, ("grp", "ep"), scatter_dimension=0, tiled=True),
        lax.psum_scatter(grad_router, ("grp", "ep"), scatter_dimension=0, tiled=True),
    )
    grad_up, grad_down = (
        lax.psum(grad_up, "grp").astype(jnp.float32)[None],
        lax.psum(grad_down, "grp").astype(jnp.float32)[None],
    )
    return (
        output,
        tokens_grad,
        shares[0],
        shares[1],
        shares[2],
        shares[3],
        shares[4],
        grad_up,
        grad_down,
    )


def solution(mesh):
    in_specs = (
        P(("grp", "ep"), None),
        P(("grp", "ep"), None),
        P(("grp", "ep"), None),
        P(("grp", "ep"), None),
        P(("grp", "ep"), None),
        P(("grp", "ep")),
        P(("grp", "ep"), None),
        P(("grp", "ep"), None),
        P(("grp", "ep")),
        P(("grp", "ep"), None),
        P("ep", None, None),
        P("ep", None, None),
        P(("grp", "ep"), None),
    )
    out_specs = (
        P(("grp", "ep"), None),
        P(("grp", "ep"), None),
        P(("grp", "ep")),
        P(("grp", "ep"), None),
        P(("grp", "ep"), None),
        P(("grp", "ep")),
        P(("grp", "ep"), None),
        P("ep", None, None),
        P("ep", None, None),
    )
    return jax.shard_map(
        per_device, mesh=mesh, in_specs=in_specs, out_specs=out_specs, check_vma=False
    )
```

```python
import functools

import jax
import jax.numpy as jnp
from jax import lax
from jax.experimental import pallas as pl
from jax.experimental.pallas import tpu as pltpu
from jax.sharding import PartitionSpec as P

MESH = pl.DeviceIdType.MESH
MIB = 1 << 20

HEADS = 8


EPSILON = 1e-06
NEGATIVE = -1e30


def normalize(values, gain):
    mean = jnp.mean(values, axis=-1, keepdims=True)
    centred = values - mean
    inverse = lax.rsqrt(jnp.mean(centred * centred, axis=-1, keepdims=True) + EPSILON)
    unit = centred * inverse
    return (unit * gain, unit, inverse)


def normalize_back(incoming, gain, unit, inverse):
    scaled = incoming * gain
    inner = (
        scaled
        - jnp.mean(scaled, axis=-1, keepdims=True)
        - unit * jnp.mean(scaled * unit, axis=-1, keepdims=True)
    )
    return (inverse * inner, jnp.sum(incoming * unit, axis=0))


def outer(left, right):
    return lax.dot_general(
        left, right, (((0,), (0,)), ((), ())), preferred_element_type=jnp.float32
    )


def times_t(left, right):
    return lax.dot_general(
        left, right, (((1,), (1,)), ((), ())), preferred_element_type=jnp.float32
    )


def route(picks, live, ranks, expert_count, capacity):
    row_count = picks.shape[0]
    labels = lax.broadcasted_iota(jnp.int32, (row_count, expert_count), 1)
    first = (picks[:, 0:1] == labels).astype(jnp.int32)
    second = (picks[:, 1:2] == labels).astype(jnp.int32)
    live_col = live[:, None]
    earlier = (ranks[None, :] < ranks[:, None]).astype(jnp.int32)
    first_live = first * live_col
    second_live = second * live_col
    place_one = jnp.sum(
        jnp.dot(earlier, first_live, preferred_element_type=jnp.int32) * first, axis=1
    )
    ahead = (
        jnp.dot(earlier, second_live, preferred_element_type=jnp.int32)
        + jnp.sum(first_live, axis=0)[None, :]
    )
    place_two = jnp.sum(ahead * second, axis=1)
    keep_one = (live > 0) & (place_one < capacity)
    keep_two = (live > 0) & (place_two < capacity)
    stride = -(-capacity // 16) * 16
    dummy = expert_count * stride
    slot_one = jnp.where(keep_one, picks[:, 0] * stride + place_one, dummy)
    slot_two = jnp.where(keep_two, picks[:, 1] * stride + place_two, dummy)
    return (slot_one, slot_two)


def visible(group, live):
    rows = group.shape[0]
    index = lax.broadcasted_iota(jnp.int32, (rows, rows), 0)
    other = lax.broadcasted_iota(jnp.int32, (rows, rows), 1)
    return (group[:, None] == group[None, :]) & ((live[None, :] > 0) | (index == other))


def attend_forward(query, key, value, allowed, factor):
    scores = jnp.einsum("qhd,khd->hqk", query, key, preferred_element_type=jnp.float32) * factor
    masked = jnp.where(allowed[None], scores, NEGATIVE)
    top = jnp.max(masked, axis=-1, keepdims=True)
    weights = jnp.exp(masked - top)
    total = jnp.sum(weights, axis=-1, keepdims=True)
    probs = (weights / total).astype(jnp.bfloat16)
    mixed = jnp.einsum("hqk,khd->qhd", probs, value, preferred_element_type=jnp.float32)
    return (mixed, top + jnp.log(total))


def attend_backward(query, key, value, allowed, log_total, grad_mixed, factor):
    scores = jnp.einsum("qhd,khd->hqk", query, key, preferred_element_type=jnp.float32) * factor
    masked = jnp.where(allowed[None], scores, NEGATIVE)
    probs = jnp.exp(masked - log_total)
    grad_value = jnp.einsum(
        "hqk,qhd->khd", probs.astype(jnp.bfloat16), grad_mixed, preferred_element_type=jnp.float32
    )
    grad_probs = jnp.einsum("qhd,khd->hqk", grad_mixed, value, preferred_element_type=jnp.float32)
    delta = jnp.sum(probs * grad_probs, axis=-1, keepdims=True)
    grad_scores = (probs * (grad_probs - delta)).astype(jnp.bfloat16)
    grad_query = (
        jnp.einsum("hqk,khd->qhd", grad_scores, key, preferred_element_type=jnp.float32) * factor
    )
    grad_key = (
        jnp.einsum("hqk,qhd->khd", grad_scores, query, preferred_element_type=jnp.float32) * factor
    )
    return jnp.stack([grad_query, grad_key, grad_value], axis=1)


def partner(me, step, count):
    other, bit = 0, 1
    while bit < count:
        other = other + bit * lax.rem(lax.div(me, bit) + lax.div(step, bit), 2)
        bit *= 2
    return other


def expert_kernel(
    count,
    experts,
    sent_rows,
    sent_grads,
    up_ref,
    down_ref,
    router_ref,
    back_ref,
    ret_ref,
    grad_up_ref,
    grad_down_ref,
    grad_router_ref,
    rows,
    grads,
    gated,
    act,
    grad_pre,
    logit_grads,
    out_grads,
    out_ret,
    turned,
    sems,
    local_sem,
):
    me = lax.axis_index("ep")
    block, width = rows.shape[1:]
    hidden = up_ref.shape[1]
    chunk = 512
    barrier = pltpu.get_barrier_semaphore()

    def greet(step, carry):
        pl.semaphore_signal(
            barrier, inc=1, device_id={"ep": partner(me, step, count)}, device_id_type=MESH
        )
        return carry

    lax.fori_loop(1, count, greet, 0)
    pl.semaphore_wait(barrier, count - 1)

    def remote(kind, source, target, step):
        return pltpu.make_async_remote_copy(
            src_ref=source,
            dst_ref=target,
            send_sem=sems.at[2 * kind, step],
            recv_sem=sems.at[2 * kind + 1, step],
            device_id={"ep": partner(me, step, count)},
            device_id_type=MESH,
        )

    def send_rows(step):
        return remote(0, sent_rows.at[partner(me, step, count)], rows.at[step], step)

    def send_grads(step):
        return remote(1, sent_grads.at[partner(me, step, count)], grads.at[step], step)

    def send_back(step):
        return remote(2, out_grads.at[step], back_ref.at[me], step)

    def send_ret(step):
        return remote(3, out_ret.at[step], ret_ref.at[me], step)

    own = [
        pltpu.make_async_copy(sent_rows.at[me], rows.at[0], local_sem.at[0]),
        pltpu.make_async_copy(sent_grads.at[me], grads.at[0], local_sem.at[1]),
        pltpu.make_async_copy(out_grads.at[0], back_ref.at[me], local_sem.at[2]),
        pltpu.make_async_copy(out_ret.at[0], ret_ref.at[me], local_sem.at[3]),
    ]
    own[0].start()
    own[1].start()

    def start(step, carry):
        send_rows(step).start()
        send_grads(step).start()
        return carry

    lax.fori_loop(1, count, start, 0)
    own[0].wait()
    own[1].wait()
    lanes = lax.broadcasted_iota(jnp.int32, (block, router_ref.shape[1]), 1)

    def one_block(step, carry):
        @pl.when(step > 0)
        def _():
            send_rows(step).wait_recv()
            send_grads(step).wait_recv()

        mine = rows[step]
        cotangent = grads[step].astype(jnp.float32)
        place = pl.ds(pl.multiple_of(step * block, 16), block)
        logits = jnp.dot(mine, router_ref[...], preferred_element_type=jnp.float32)
        logits = jnp.where(lanes < experts, logits, NEGATIVE)
        weights = jnp.exp(logits - jnp.max(logits, axis=1, keepdims=True))
        gate_all = weights / jnp.sum(weights, axis=1, keepdims=True)
        here = (lanes == me).astype(jnp.float32)
        gate = jnp.sum(gate_all * here, axis=1, keepdims=True)
        pair = (gate * cotangent).astype(jnp.bfloat16)
        gated[place, :] = pair
        ret = jnp.zeros((block, width), jnp.float32)
        back = jnp.zeros((block, width), jnp.float32)
        for first in range(0, hidden, chunk):
            span = slice(first, first + chunk)
            pre = jnp.dot(mine, up_ref[:, span], preferred_element_type=jnp.float32)
            cdf = 0.5 * (1.0 + lax.erf(pre * 0.7071067811865476))
            density = jnp.exp(-0.5 * pre * pre) * 0.3989422804014327
            low = (pre * cdf).astype(jnp.bfloat16)
            act[place, span] = low
            ret = ret + jnp.dot(low, down_ref[span, :], preferred_element_type=jnp.float32)
            grad_act = times_t(pair, down_ref[span, :])
            slope = (grad_act * (cdf + pre * density)).astype(jnp.bfloat16)
            grad_pre[place, span] = slope
            back = back + times_t(slope, up_ref[:, span])
        ret = ret.astype(jnp.bfloat16).astype(jnp.float32)
        out_ret[step] = (gate * ret).astype(jnp.bfloat16)
        gate_grad = jnp.sum(cotangent * ret, axis=1, keepdims=True)
        low_logits = (gate * gate_grad * (here - gate_all)).astype(jnp.bfloat16)
        logit_grads[place, :] = low_logits
        back = back + times_t(low_logits, router_ref[...])
        out_grads[step] = back.astype(jnp.bfloat16)

        @pl.when(step > 0)
        def _():
            send_back(step).start()

        @pl.when(step == 0)
        def _():
            own[2].start()

        return carry

    lax.fori_loop(0, count, one_block, 0)
    own[3].start()

    def start_ret(step, carry):
        send_ret(step).start()
        return carry

    lax.fori_loop(1, count, start_ret, 0)
    turned[...] = jnp.transpose(rows[...].reshape(count * block, width))
    grad_router_ref[...] = jnp.dot(
        turned[...], logit_grads[...], preferred_element_type=jnp.float32
    )

    def up_chunk(index, carry):
        span = pl.ds(pl.multiple_of(index * chunk, chunk), chunk)
        grad_up_ref[:, span] = jnp.dot(
            turned[...], grad_pre[:, span], preferred_element_type=jnp.float32
        ).astype(jnp.bfloat16)
        return carry

    lax.fori_loop(0, hidden // chunk, up_chunk, 0)
    turned[...] = jnp.transpose(gated[...])

    def down_chunk(index, carry):
        span = pl.ds(pl.multiple_of(index * chunk, chunk), chunk)
        part = jnp.dot(turned[...], act[:, span], preferred_element_type=jnp.float32)
        grad_down_ref[span, :] = jnp.transpose(part).astype(jnp.bfloat16)
        return carry

    lax.fori_loop(0, hidden // chunk, down_chunk, 0)

    def finish(step, carry):
        send_rows(step).wait_send()
        send_grads(step).wait_send()
        send_back(step).wait()
        send_ret(step).wait()
        return carry

    lax.fori_loop(1, count, finish, 0)
    own[2].wait()
    own[3].wait()


def column(values, lane):
    lanes = lax.broadcasted_iota(jnp.int32, values.shape, 1)
    return jnp.sum(jnp.where(lanes == lane, values, 0), axis=1, keepdims=True)


def core_peer(grp):
    return grp + 1 - 2 * lax.rem(grp, 2)


def x_peer(grp):
    return lax.rem(grp + 2, 4)


def flags(condition):
    return jnp.where(condition, 1.0, 0.0).astype(jnp.bfloat16)


def remote_copy(source, target, send_sem, recv_sem, device):
    return pltpu.make_async_remote_copy(
        src_ref=source,
        dst_ref=target,
        send_sem=send_sem,
        recv_sem=recv_sem,
        device_id=device,
        device_id_type=MESH,
    )


def greet_all(count, me, grp):
    barrier = pltpu.get_barrier_semaphore()

    def greet(step, carry):
        pl.semaphore_signal(
            barrier, inc=1, device_id={"ep": partner(me, step, count)}, device_id_type=MESH
        )
        return carry

    lax.fori_loop(1, count, greet, 0)
    for peer in (core_peer(grp), x_peer(grp)):
        pl.semaphore_signal(barrier, inc=1, device_id={"grp": peer}, device_id_type=MESH)
    pl.semaphore_wait(barrier, count + 1)


def seen(segment_row, live_row, segment_col):
    length = segment_row.shape[1]
    index = lax.broadcasted_iota(jnp.int32, (length, length), 0)
    other = lax.broadcasted_iota(jnp.int32, (length, length), 1)
    return (segment_col == segment_row) & ((live_row > 0) | (index == other))


def forward_kernel(
    count,
    capacity,
    tokens,
    segments,
    live,
    picks,
    ranks,
    out_grad,
    joint_shard,
    output_shard,
    pack_shard,
    weights,
    joint,
    mixed,
    state,
    sent_rows,
    logs,
    slots,
    grads,
    own_grads,
    normed_two,
    int_columns,
    ep_sems,
    x_sems,
    core_sems,
    grad_sems,
    local_sems,
):
    me, grp = lax.axis_index("ep"), lax.axis_index("grp")
    row_count, width = tokens.shape
    sequences, length = segments.shape
    block = sent_rows.shape[1]
    joint_width = joint.shape[1]
    head_size = width // HEADS
    factor = head_size ** (-0.5)
    mate, across = core_peer(grp), x_peer(grp)
    greet_all(count, me, grp)

    def shard(owner_grp, owner):
        return weights.at[owner_grp * count + owner]

    def to_ep(step):
        place = shard(grp, me)
        other = partner(me, step, count)
        return remote_copy(place, place, ep_sems.at[0, step], ep_sems.at[1, step], {"ep": other})

    def to_x(step):
        place = shard(grp, partner(me, step, count))
        return remote_copy(place, place, x_sems.at[0, step], x_sems.at[1, step], {"grp": across})

    def to_core(owner_grp, part, step):
        place = shard(owner_grp, partner(me, step, count))
        sems = core_sems.at[0, part, step], core_sems.at[1, part, step]
        return remote_copy(place, place, *sems, {"grp": mate})

    def send_grads(step):
        return remote_copy(
            own_grads.at[step],
            grads.at[step],
            grad_sems.at[0, step],
            grad_sems.at[1, step],
            {"ep": partner(me, step, count)},
        )

    mine = grp * count + me
    fill = [
        pltpu.make_async_copy(
            joint_shard, weights.at[mine, :, pl.ds(0, joint_width)], local_sems.at[0]
        ),
        pltpu.make_async_copy(
            output_shard, weights.at[mine, :, pl.ds(joint_width, width)], local_sems.at[1]
        ),
        pltpu.make_async_copy(
            pack_shard, weights.at[mine, :, pl.ds(joint_width + width, 128)], local_sems.at[2]
        ),
    ]
    for copy in fill:
        copy.start()
    for copy in fill:
        copy.wait()

    def first_hop(step, carry):
        to_ep(step).start()
        return carry

    lax.fori_loop(1, count, first_hop, 0)
    to_x(0).start()
    to_core(grp, 0, 0).start()

    ints = jnp.concatenate([segments[...], live[...]], axis=0).astype(jnp.float32)
    turned = jnp.transpose(ints)
    int_columns[...] = turned.astype(jnp.int32)
    live_col = jnp.concatenate(
        [turned[:, sequences + i : sequences + i + 1] for i in range(sequences)], axis=0
    )
    rank_row = ranks[...].astype(jnp.float32)
    rank_col = jnp.transpose(jnp.broadcast_to(rank_row, (8, row_count)))[:, 0:1]
    earlier = flags(rank_row < rank_col)
    first, second = picks[:, 0:1], picks[:, 1:2]
    lanes = lax.broadcasted_iota(jnp.int32, (row_count, 128), 1)
    one = jnp.where(lanes == first, 1.0, 0.0)
    two = jnp.where(lanes == second + count, 1.0, 0.0)
    counts = jnp.dot(
        earlier, ((one + two) * live_col).astype(jnp.bfloat16), preferred_element_type=jnp.float32
    )
    ahead = jnp.sum(jnp.where(lanes == first + count, live_col, 0.0), axis=0, keepdims=True)
    place_one = jnp.sum(counts * one, axis=1, keepdims=True)
    place_two = jnp.sum((counts + ahead) * two, axis=1, keepdims=True)
    nowhere = 1.0 * count * block
    slot_one = jnp.where(
        (live_col > 0) & (place_one < capacity),
        first.astype(jnp.float32) * block + place_one,
        nowhere,
    )
    slot_two = jnp.where(
        (live_col > 0) & (place_two < capacity),
        second.astype(jnp.float32) * block + place_two,
        nowhere,
    )
    both = jnp.where(lanes == 0, slot_one, jnp.where(lanes == 1, slot_two, nowhere))
    slots[...] = both.astype(jnp.int32)
    slot_rows = jnp.transpose(both)[0:8].astype(jnp.int32)
    row_one, row_two = slot_rows[0:1], slot_rows[1:2]

    def rows_of(expert, values):
        index = lax.broadcasted_iota(jnp.int32, (block, row_count), 0) + expert * block
        chosen = flags((index == row_one) | (index == row_two))
        return jnp.dot(chosen, values[...], preferred_element_type=jnp.float32).astype(jnp.bfloat16)

    def spread_grads(step, carry):
        own_grads[step] = rows_of(partner(me, step, count), out_grad)

        @pl.when(step > 0)
        def _():
            send_grads(step).start()

        return carry

    lax.fori_loop(0, count, spread_grads, 0)
    keep = pltpu.make_async_copy(own_grads.at[0], grads.at[0], local_sems.at[3])
    keep.start()

    def pass_on(step, carry):
        to_ep(step).wait_recv()
        to_x(step).start()
        to_core(grp, 0, step).start()
        return carry

    lax.fori_loop(1, count, pass_on, 0)

    def pass_further(step, carry):
        to_x(step).wait_recv()
        to_core(across, 1, step).start()
        return carry

    lax.fori_loop(0, count, pass_further, 0)

    def arrive(step, carry):
        to_core(mate, 0, step).wait_recv()
        to_core(x_peer(mate), 1, step).wait_recv()
        return carry

    lax.fori_loop(0, count, arrive, 0)

    devices = weights.shape[0]
    total = devices * weights.shape[1]
    pack = weights[:, :, joint_width + width :].reshape(total, 128)
    gains = jnp.transpose(pack.astype(jnp.float32))
    gain_one = gains[count : count + 1]
    gain_two = gains[count + 1 : count + 2]
    half = lax.broadcasted_iota(jnp.int32, (length, 128), 1) < head_size
    halves = (flags(half), flags(jnp.logical_not(half)))

    def attend(number, carry):
        rows = pl.ds(pl.multiple_of(number * length, length), length)
        values = tokens[rows, :].astype(jnp.float32)
        normed = normalize(values, gain_one)[0].astype(jnp.bfloat16)
        joint[rows, :] = jnp.dot(
            normed,
            weights[:, :, :joint_width].reshape(total, joint_width),
            preferred_element_type=jnp.float32,
        ).astype(jnp.bfloat16)
        allowed = seen(
            segments[pl.ds(number, 1), :], live[pl.ds(number, 1), :], column(int_columns[...], number)
        )
        log_all = jnp.zeros((length, 128), jnp.float32)
        log_lanes = lax.broadcasted_iota(jnp.int32, (length, 128), 1)
        for pair in range(HEADS // 2):
            at = pair * 128
            query = joint[rows, at : at + 128]
            key = joint[rows, width + at : width + at + 128]
            value = joint[rows, 2 * width + at : 2 * width + at + 128]
            results = []
            for side in range(2):
                scores = times_t(query * halves[side], key) * factor
                masked = jnp.where(allowed, scores, NEGATIVE)
                top = jnp.max(masked, axis=-1, keepdims=True)
                powers = jnp.exp(masked - top)
                added = jnp.sum(powers, axis=-1, keepdims=True)
                probs = (powers * (1.0 / added)).astype(jnp.bfloat16)
                results.append(jnp.dot(probs, value, preferred_element_type=jnp.float32))
                log_all = jnp.where(log_lanes == 2 * pair + side, top + jnp.log(added), log_all)
            mixed[rows, at : at + 128] = jnp.where(half, results[0], results[1]).astype(jnp.bfloat16)
        logs[rows, :] = log_all
        after = values + jnp.dot(
            mixed[rows, :],
            weights[:, :, joint_width : joint_width + width].reshape(total, width),
            preferred_element_type=jnp.float32,
        )
        state[rows, :] = after
        normed_two[rows, :] = normalize(after, gain_two)[0].astype(jnp.bfloat16)
        return carry

    lax.fori_loop(0, sequences, attend, 0)

    def spread_rows(expert, carry):
        sent_rows[expert] = rows_of(expert, normed_two)
        return carry

    lax.fori_loop(0, count, spread_rows, 0)
    keep.wait()
    to_x(0).wait_send()
    to_core(grp, 0, 0).wait_send()
    to_core(across, 1, 0).wait_send()

    def finish(step, carry):
        to_ep(step).wait_send()
        to_x(step).wait_send()
        to_core(grp, 0, step).wait_send()
        to_core(across, 1, step).wait_send()
        send_grads(step).wait()
        return carry

    lax.fori_loop(1, count, finish, 0)


def forward(
    count, capacity, block, tokens, segments, live, picks, ranks, out_grad, joint, output, pack
):
    row_count, width = tokens.shape
    devices = width // joint.shape[0]
    all_width = joint.shape[1] + width + 128
    any_space = pl.BlockSpec(memory_space=pl.ANY)
    vmem = pl.BlockSpec(memory_space=pltpu.VMEM)
    low = jnp.bfloat16
    return pl.pallas_call(
        functools.partial(forward_kernel, count, capacity),
        out_shape=(
            jax.ShapeDtypeStruct((devices, joint.shape[0], all_width), low),
            jax.ShapeDtypeStruct((row_count, joint.shape[1]), low),
            jax.ShapeDtypeStruct((row_count, width), low),
            jax.ShapeDtypeStruct((row_count, width), jnp.float32),
            jax.ShapeDtypeStruct((count, block, width), low),
            jax.ShapeDtypeStruct((row_count, 128), jnp.float32),
            jax.ShapeDtypeStruct((row_count, 128), jnp.int32),
            jax.ShapeDtypeStruct((count, block, width), low),
        ),
        in_specs=[vmem] * 6 + [any_space] * 3,
        out_specs=(vmem,) * 7 + (any_space,),
        scratch_shapes=[
            pltpu.VMEM((count, block, width), low),
            pltpu.VMEM((row_count, width), low),
            pltpu.VMEM((segments.shape[1], 2 * segments.shape[0]), jnp.int32),
            pltpu.SemaphoreType.DMA((2, count)),
            pltpu.SemaphoreType.DMA((2, count)),
            pltpu.SemaphoreType.DMA((2, 2, count)),
            pltpu.SemaphoreType.DMA((2, count)),
            pltpu.SemaphoreType.DMA((4,)),
        ],
        compiler_params=pltpu.CompilerParams(
            collective_id=2, has_side_effects=True, vmem_limit_bytes=48 * MIB
        ),
    )(tokens, segments, live, picks, ranks, out_grad, joint, output, pack)


def middle_kernel(
    count,
    sent_rows,
    grads,
    up_ref,
    down_ref,
    router_ref,
    back_ref,
    out_ret,
    grad_up_ref,
    grad_down_ref,
    grad_router_ref,
    rows,
    gated,
    act,
    grad_pre,
    logit_grads,
    out_grads,
    turned,
    part_up,
    part_down,
    mate_up,
    mate_down,
    half_up,
    half_down,
    far_up,
    far_down,
    sems,
    sum_sems,
    local_sem,
):
    me, grp = lax.axis_index("ep"), lax.axis_index("grp")
    mate, across = core_peer(grp), x_peer(grp)
    core = lax.rem(grp, 2)
    block, width = rows.shape[1:]
    hidden = up_ref.shape[1]
    chunk = 512
    greet_all(count, me, grp)

    def send_rows(step):
        other = partner(me, step, count)
        return remote_copy(
            sent_rows.at[other], rows.at[step], sems.at[0, step], sems.at[1, step], {"ep": other}
        )

    def send_back(step):
        other = partner(me, step, count)
        return remote_copy(
            out_grads.at[step], back_ref.at[me], sems.at[2, step], sems.at[3, step], {"ep": other}
        )

    own = [
        pltpu.make_async_copy(sent_rows.at[me], rows.at[0], local_sem.at[0]),
        pltpu.make_async_copy(out_grads.at[0], back_ref.at[me], local_sem.at[1]),
    ]
    own[0].start()

    def start(step, carry):
        send_rows(step).start()
        return carry

    lax.fori_loop(1, count, start, 0)
    own[0].wait()
    lanes = lax.broadcasted_iota(jnp.int32, (block, router_ref.shape[1]), 1)

    def one_block(step, carry):
        @pl.when(step > 0)
        def _():
            send_rows(step).wait_recv()

        mine = rows[step]
        cotangent = grads[step].astype(jnp.float32)
        place = pl.ds(pl.multiple_of(step * block, 16), block)
        logits = jnp.dot(mine, router_ref[...], preferred_element_type=jnp.float32)
        logits = jnp.where(lanes < count, logits, NEGATIVE)
        weights = jnp.exp(logits - jnp.max(logits, axis=1, keepdims=True))
        gate_all = weights / jnp.sum(weights, axis=1, keepdims=True)
        here = (lanes == me).astype(jnp.float32)
        gate = jnp.sum(gate_all * here, axis=1, keepdims=True)
        pair = (gate * cotangent).astype(jnp.bfloat16)
        gated[place, :] = pair
        ret = jnp.zeros((block, width), jnp.float32)
        back = jnp.zeros((block, width), jnp.float32)
        for first in range(0, hidden, chunk):
            span = slice(first, first + chunk)
            pre = jnp.dot(mine, up_ref[:, span], preferred_element_type=jnp.float32)
            cdf = 0.5 * (1.0 + lax.erf(pre * 0.7071067811865476))
            density = jnp.exp(-0.5 * pre * pre) * 0.3989422804014327
            low = (pre * cdf).astype(jnp.bfloat16)
            act[place, span] = low
            ret = ret + jnp.dot(low, down_ref[span, :], preferred_element_type=jnp.float32)
            grad_act = times_t(pair, down_ref[span, :])
            slope = (grad_act * (cdf + pre * density)).astype(jnp.bfloat16)
            grad_pre[place, span] = slope
            back = back + times_t(slope, up_ref[:, span])
        ret = ret.astype(jnp.bfloat16).astype(jnp.float32)
        out_ret[step] = (gate * ret).astype(jnp.bfloat16)
        gate_grad = jnp.sum(cotangent * ret, axis=1, keepdims=True)
        low_logits = (gate * gate_grad * (here - gate_all)).astype(jnp.bfloat16)
        logit_grads[place, :] = low_logits
        back = back + times_t(low_logits, router_ref[...])
        out_grads[step] = back.astype(jnp.bfloat16)

        @pl.when(step > 0)
        def _():
            send_back(step).start()

        @pl.when(step == 0)
        def _():
            own[1].start()

        return carry

    lax.fori_loop(0, count, one_block, 0)
    turned[...] = jnp.transpose(rows[...].reshape(count * block, width))
    grad_router_ref[...] = jnp.dot(
        turned[...], logit_grads[...], preferred_element_type=jnp.float32
    )

    up_rows, down_rows = half_up.shape[0], half_down.shape[0]
    groups = (
        (part_up, mate_up, half_up, far_up, grad_up_ref, up_rows),
        (part_down, mate_down, half_down, far_down, grad_down_ref, down_rows),
    )

    def half_of(which, size):
        return pl.ds(pl.multiple_of(which * size, size), size)

    def to_mate(layer):
        part, landing, _, _, _, size = groups[layer]
        sem = sum_sems.at[0, layer], sum_sems.at[1, layer]
        return remote_copy(part.at[half_of(1 - core, size)], landing, *sem, {"grp": mate})

    def to_across(layer):
        _, _, half, far, _, _ = groups[layer]
        sem = sum_sems.at[2, layer], sum_sems.at[3, layer]
        return remote_copy(half, far, *sem, {"grp": across})

    def to_mate_again(layer):
        result, size = groups[layer][4:]
        sem = sum_sems.at[4, layer], sum_sems.at[5, layer]
        place = result.at[half_of(core, size)]
        return remote_copy(place, place, *sem, {"grp": mate})

    def add_mate(layer):
        part, landing, half, _, _, size = groups[layer]
        to_mate(layer).wait_recv()
        kept = part[half_of(core, size), :].astype(jnp.float32)
        half[...] = (kept + landing[...].astype(jnp.float32)).astype(jnp.bfloat16)
        to_across(layer).start()

    def add_across(layer):
        _, _, half, far, result, size = groups[layer]
        to_across(layer).wait_recv()
        result[half_of(core, size), :] = (
            half[...].astype(jnp.float32) + far[...].astype(jnp.float32)
        ).astype(jnp.bfloat16)
        to_mate_again(layer).start()

    def up_chunk(index, carry):
        span = pl.ds(pl.multiple_of(index * chunk, chunk), chunk)
        part_up[:, span] = jnp.dot(
            turned[...], grad_pre[:, span], preferred_element_type=jnp.float32
        ).astype(jnp.bfloat16)
        return carry

    lax.fori_loop(0, hidden // chunk, up_chunk, 0)
    to_mate(0).start()
    turned[...] = jnp.transpose(gated[...])

    def down_chunk(index, carry):
        span = pl.ds(pl.multiple_of(index * chunk, chunk), chunk)
        part = jnp.dot(turned[...], act[:, span], preferred_element_type=jnp.float32)
        part_down[span, :] = jnp.transpose(part).astype(jnp.bfloat16)
        return carry

    lax.fori_loop(0, hidden // chunk, down_chunk, 0)
    to_mate(1).start()
    add_mate(0)
    add_mate(1)
    add_across(0)
    add_across(1)
    for layer in range(2):
        to_mate(layer).wait_send()
        to_across(layer).wait_send()
        to_mate_again(layer).wait()

    def finish(step, carry):
        send_rows(step).wait_send()
        send_back(step).wait()
        return carry

    lax.fori_loop(1, count, finish, 0)
    own[1].wait()


def middle(sent_rows, grads, up, down, router):
    count, block, width = sent_rows.shape
    hidden = up.shape[1]
    any_space = pl.BlockSpec(memory_space=pl.ANY)
    vmem = pl.BlockSpec(memory_space=pltpu.VMEM)
    low = jnp.bfloat16
    slots = count * block
    return pl.pallas_call(
        functools.partial(middle_kernel, count),
        out_shape=(
            jax.ShapeDtypeStruct((count, block, width), low),
            jax.ShapeDtypeStruct((count, block, width), low),
            jax.ShapeDtypeStruct((width, hidden), low),
            jax.ShapeDtypeStruct((hidden, width), low),
            jax.ShapeDtypeStruct((width, 128), jnp.float32),
        ),
        in_specs=[any_space, vmem, vmem, vmem, vmem],
        out_specs=(any_space, vmem, vmem, vmem, vmem),
        scratch_shapes=[
            pltpu.VMEM((count, block, width), low),
            pltpu.VMEM((slots, width), low),
            pltpu.VMEM((slots, hidden), low),
            pltpu.VMEM((slots, hidden), low),
            pltpu.VMEM((slots, 128), low),
            pltpu.VMEM((count, block, width), low),
            pltpu.VMEM((width, slots), low),
            pltpu.VMEM((width, hidden), low),
            pltpu.VMEM((hidden, width), low),
            pltpu.VMEM((width // 2, hidden), low),
            pltpu.VMEM((hidden // 2, width), low),
            pltpu.VMEM((width // 2, hidden), low),
            pltpu.VMEM((hidden // 2, width), low),
            pltpu.VMEM((width // 2, hidden), low),
            pltpu.VMEM((hidden // 2, width), low),
            pltpu.SemaphoreType.DMA((4, count)),
            pltpu.SemaphoreType.DMA((6, 2)),
            pltpu.SemaphoreType.DMA((2,)),
        ],
        compiler_params=pltpu.CompilerParams(
            collective_id=3, has_side_effects=True, vmem_limit_bytes=60 * MIB
        ),
        cost_estimate=pl.CostEstimate(
            flops=12 * slots * width * hidden, bytes_accessed=16 * MIB, transcendentals=0
        ),
    )(sent_rows, grads, up, down, router)


def backward_kernel(
    count,
    tokens,
    segments,
    live,
    out_grad,
    weights,
    joint,
    mixed,
    state,
    logs,
    slots,
    back,
    out_ret,
    grad_router,
    output,
    tokens_grad,
    shares,
    returned,
    grad_joint,
    normed_all,
    branch_all,
    part,
    mate_part,
    pair_part,
    far_part,
    x_part,
    ep_part,
    turned,
    ret_sems,
    mate_sems,
    x_sems,
    ep_sems,
    local_sems,
):
    me, grp = lax.axis_index("ep"), lax.axis_index("grp")
    row_count, width = tokens.shape
    sequences, length = segments.shape
    block = back.shape[1]
    slot_count = count * block
    joint_width = joint.shape[1]
    head_size = width // HEADS
    factor = head_size ** (-0.5)
    mate, across = core_peer(grp), x_peer(grp)
    core, side_x = lax.rem(grp, 2), lax.div(grp, 2)
    devices = weights.shape[0]
    total = devices * weights.shape[1]
    greet_all(count, me, grp)

    def send_ret(step):
        return remote_copy(
            out_ret.at[step],
            returned.at[me],
            ret_sems.at[0, step],
            ret_sems.at[1, step],
            {"ep": partner(me, step, count)},
        )

    keep = pltpu.make_async_copy(out_ret.at[0], returned.at[me], local_sems.at[0])
    keep.start()

    def start(step, carry):
        send_ret(step).start()
        return carry

    lax.fori_loop(1, count, start, 0)
    pack = weights[:, :, joint_width + width :].reshape(total, 128)
    gains = jnp.transpose(pack.astype(jnp.float32))
    gain_one = gains[count : count + 1]
    gain_two = gains[count + 1 : count + 2]
    half = lax.broadcasted_iota(jnp.int32, (length, 128), 1) < head_size
    halves = (flags(half), flags(jnp.logical_not(half)))
    ints = jnp.transpose(segments[...].astype(jnp.float32)).astype(jnp.int32)

    def chosen_of(rows):
        index = lax.broadcasted_iota(jnp.int32, (length, slot_count), 1)
        pair = slots[rows, :]
        return flags((index == pair[:, 0:1]) | (index == pair[:, 1:2]))

    def one_sequence(number, carry):
        grad_one, grad_two = carry
        rows = pl.ds(pl.multiple_of(number * length, length), length)
        grad_normed_two = jnp.dot(
            chosen_of(rows),
            back[...].reshape(slot_count, width),
            preferred_element_type=jnp.float32,
        )
        _, unit, inverse = normalize(state[rows, :], gain_two)
        inner, share = normalize_back(grad_normed_two, gain_two, unit, inverse)
        grad_two = grad_two + share[None, :]
        grad_state = out_grad[rows, :].astype(jnp.float32) + inner
        branch = grad_state.astype(jnp.bfloat16)
        branch_all[rows, :] = branch
        grad_mixed = times_t(
            branch, weights[:, :, joint_width : joint_width + width].reshape(total, width)
        ).astype(jnp.bfloat16)
        allowed = seen(segments[pl.ds(number, 1), :], live[pl.ds(number, 1), :], column(ints, number))
        log_all = logs[rows, :]
        for pair in range(HEADS // 2):
            at = pair * 128
            query = joint[rows, at : at + 128]
            key = joint[rows, width + at : width + at + 128]
            value = joint[rows, 2 * width + at : 2 * width + at + 128]
            grad_out = grad_mixed[:, at : at + 128]
            results = []
            for side in range(2):
                scores = times_t(query * halves[side], key) * factor
                head = 2 * pair + side
                masked = jnp.where(allowed, scores, NEGATIVE)
                probs = jnp.exp(masked - log_all[:, head : head + 1])
                grad_value = outer(probs.astype(jnp.bfloat16), grad_out)
                grad_probs = times_t(grad_out * halves[side], value)
                delta = jnp.sum(probs * grad_probs, axis=-1, keepdims=True)
                grad_scores = (probs * (grad_probs - delta)).astype(jnp.bfloat16)
                grad_query = jnp.dot(grad_scores, key, preferred_element_type=jnp.float32) * factor
                grad_key = outer(grad_scores, query) * factor
                results.append((grad_query, grad_key, grad_value))
            for third in range(3):
                grad_joint[rows, third * width + at : third * width + at + 128] = jnp.where(
                    half, results[0][third], results[1][third]
                ).astype(jnp.bfloat16)
        grad_normed = times_t(
            grad_joint[rows, :], weights[:, :, :joint_width].reshape(total, joint_width)
        )
        normed, unit, inverse = normalize(tokens[rows, :].astype(jnp.float32), gain_one)
        normed_all[rows, :] = normed.astype(jnp.bfloat16)
        inner, share = normalize_back(grad_normed, gain_one, unit, inverse)
        grad_one = grad_one + share[None, :]
        tokens_grad[rows, :] = grad_state + inner
        return grad_one, grad_two

    nothing = jnp.zeros((1, width), jnp.float32)
    grad_one, grad_two = lax.fori_loop(0, sequences, one_sequence, (nothing, nothing))

    shape = (devices, total // devices)
    turned[...] = jnp.transpose(mixed[...])
    part[:, :, joint_width : joint_width + width] = (
        jnp.dot(turned[...], branch_all[...], preferred_element_type=jnp.float32)
        .astype(jnp.bfloat16)
        .reshape(*shape, width)
    )
    lines = lax.broadcasted_iota(jnp.int32, (128, width), 0)
    gain_lines = jnp.where(
        lines == count, grad_one, jnp.where(lines == count + 1, grad_two, 0.0)
    )
    part[:, :, joint_width + width :] = (
        (grad_router[...] + jnp.transpose(gain_lines)).astype(jnp.bfloat16).reshape(*shape, 128)
    )
    turned[...] = jnp.transpose(normed_all[...])
    for third in range(3):
        span = slice(third * width, (third + 1) * width)
        part[:, :, span] = (
            jnp.dot(turned[...], grad_joint[:, span], preferred_element_type=jnp.float32)
            .astype(jnp.bfloat16)
            .reshape(*shape, width)
        )

    def to_mate(which):
        owner = 2 * which + 1 - core
        return remote_copy(
            part.at[pl.ds(owner * count, count)],
            mate_part.at[which],
            mate_sems.at[0, which],
            mate_sems.at[1, which],
            {"grp": mate},
        )

    to_x = remote_copy(pair_part, x_part, x_sems.at[0], x_sems.at[1], {"grp": across})

    def to_ep(step):
        other = partner(me, step, count)
        return remote_copy(
            far_part.at[other], ep_part.at[step], ep_sems.at[0, step], ep_sems.at[1, step], {"ep": other}
        )

    def summed(which, landing):
        owner = 2 * which + core
        return part[pl.ds(owner * count, count)].astype(jnp.float32) + landing.astype(jnp.float32)

    to_mate(1 - side_x).start()
    to_mate(side_x).start()
    to_mate(1 - side_x).wait_recv()
    pair_part[...] = summed(1 - side_x, mate_part[1 - side_x]).astype(jnp.bfloat16)
    to_x.start()
    to_mate(side_x).wait_recv()
    to_x.wait_recv()
    far_part[...] = (summed(side_x, mate_part[side_x]) + x_part[...].astype(jnp.float32)).astype(
        jnp.bfloat16
    )

    def to_all(step, carry):
        to_ep(step).start()
        return carry

    lax.fori_loop(1, count, to_all, 0)
    keep.wait()

    def from_all(step, carry):
        send_ret(step).wait()
        return carry

    lax.fori_loop(1, count, from_all, 0)

    def combine(number, carry):
        rows = pl.ds(pl.multiple_of(number * length, length), length)
        gathered = jnp.dot(
            chosen_of(rows),
            returned[...].reshape(slot_count, width),
            preferred_element_type=jnp.float32,
        )
        output[rows, :] = (state[rows, :] + gathered).astype(jnp.bfloat16)
        return carry

    lax.fori_loop(0, sequences, combine, 0)

    def add_share(step, added):
        to_ep(step).wait_recv()
        return added + ep_part[step].astype(jnp.float32)

    shares[...] = lax.fori_loop(1, count, add_share, far_part[me].astype(jnp.float32))
    to_mate(0).wait_send()
    to_mate(1).wait_send()
    to_x.wait_send()

    def finish(step, carry):
        to_ep(step).wait_send()
        return carry

    lax.fori_loop(1, count, finish, 0)


def backward(
    tokens, segments, live, out_grad, weights, joint, mixed, state, logs, slots, back, ret, router
):
    row_count, width = tokens.shape
    count = back.shape[0]
    devices, shard_rows, all_width = weights.shape
    any_space = pl.BlockSpec(memory_space=pl.ANY)
    vmem = pl.BlockSpec(memory_space=pltpu.VMEM)
    low = jnp.bfloat16
    quarter = (count, shard_rows, all_width)
    return pl.pallas_call(
        functools.partial(backward_kernel, count),
        out_shape=(
            jax.ShapeDtypeStruct((row_count, width), low),
            jax.ShapeDtypeStruct((row_count, width), jnp.float32),
            jax.ShapeDtypeStruct((shard_rows, all_width), jnp.float32),
        ),
        in_specs=[vmem] * 11 + [any_space, vmem],
        out_specs=(vmem,) * 3,
        scratch_shapes=[
            pltpu.VMEM(back.shape, low),
            pltpu.VMEM(joint.shape, low),
            pltpu.VMEM((row_count, width), low),
            pltpu.VMEM((row_count, width), low),
            pltpu.VMEM(weights.shape, low),
            pltpu.VMEM((2,) + quarter, low),
            pltpu.VMEM(quarter, low),
            pltpu.VMEM(quarter, low),
            pltpu.VMEM(quarter, low),
            pltpu.VMEM(quarter, low),
            pltpu.VMEM((width, row_count), low),
            pltpu.SemaphoreType.DMA((2, count)),
            pltpu.SemaphoreType.DMA((2, 2)),
            pltpu.SemaphoreType.DMA((2,)),
            pltpu.SemaphoreType.DMA((2, count)),
            pltpu.SemaphoreType.DMA((1,)),
        ],
        compiler_params=pltpu.CompilerParams(
            collective_id=4, has_side_effects=True, vmem_limit_bytes=56 * MIB
        ),
    )(tokens, segments, live, out_grad, weights, joint, mixed, state, logs, slots, back, ret, router)


def per_device_fused(
    tokens,
    segments,
    patch_mask,
    choices,
    priority,
    first_gain,
    joint_weight,
    output_weight,
    second_gain,
    router_weight,
    expert_up,
    expert_down,
    out_grad,
):
    row_count, width = tokens.shape
    experts = router_weight.shape[1]
    capacity = (21 * choices.shape[1] * row_count + 20 * experts - 1) // (20 * experts)
    block = -(-capacity // 16) * 16
    shard_rows = first_gain.shape[0]
    pack = jnp.concatenate(
        [
            router_weight,
            first_gain[:, None],
            second_gain[:, None],
            jnp.zeros((shard_rows, 128 - experts - 2), jnp.bfloat16),
        ],
        axis=1,
    )
    weights, joint, mixed, state, sent_rows, logs, slots, grads = forward(
        experts,
        capacity,
        block,
        tokens,
        segments,
        patch_mask,
        choices,
        priority,
        out_grad,
        joint_weight,
        output_weight,
        pack,
    )
    router = weights[:, :, joint.shape[1] + width :].reshape(width, 128)
    back, ret, grad_up, grad_down, grad_router = middle(
        sent_rows, grads, expert_up[0], expert_down[0], router
    )
    output, tokens_grad, shares = backward(
        tokens,
        segments,
        patch_mask,
        out_grad,
        weights,
        joint,
        mixed,
        state,
        logs,
        slots,
        back,
        ret,
        grad_router,
    )
    start = joint.shape[1] + width
    return (
        output,
        tokens_grad,
        shares[:, start + experts],
        shares[:, : joint.shape[1]],
        shares[:, joint.shape[1] : start],
        shares[:, start + experts + 1],
        shares[:, start : start + experts],
        grad_up.astype(jnp.float32)[None],
        grad_down.astype(jnp.float32)[None],
    )


def experts_both_ways(sent_rows, sent_grads, up, down, router):
    count, block, width = sent_rows.shape
    experts = router.shape[1]
    hidden = up.shape[1]
    router = jnp.pad(router, ((0, 0), (0, 128 - experts)))
    any_space = pl.BlockSpec(memory_space=pl.ANY)
    vmem = pl.BlockSpec(memory_space=pltpu.VMEM)
    low = jnp.bfloat16
    slots = count * block
    return pl.pallas_call(
        functools.partial(expert_kernel, count, experts),
        out_shape=(
            jax.ShapeDtypeStruct((count, block, width), low),
            jax.ShapeDtypeStruct((count, block, width), low),
            jax.ShapeDtypeStruct((width, hidden), low),
            jax.ShapeDtypeStruct((hidden, width), low),
            jax.ShapeDtypeStruct((width, 128), jnp.float32),
        ),
        in_specs=[any_space, any_space, vmem, vmem, vmem],
        out_specs=(any_space, any_space, vmem, vmem, vmem),
        scratch_shapes=[
            pltpu.VMEM((count, block, width), low),
            pltpu.VMEM((count, block, width), low),
            pltpu.VMEM((slots, width), low),
            pltpu.VMEM((slots, hidden), low),
            pltpu.VMEM((slots, hidden), low),
            pltpu.VMEM((slots, 128), low),
            pltpu.VMEM((count, block, width), low),
            pltpu.VMEM((count, block, width), low),
            pltpu.VMEM((width, slots), low),
            pltpu.SemaphoreType.DMA((8, count)),
            pltpu.SemaphoreType.DMA((4,)),
        ],
        compiler_params=pltpu.CompilerParams(
            collective_id=1, has_side_effects=True, vmem_limit_bytes=58 * MIB
        ),
        cost_estimate=pl.CostEstimate(
            flops=12 * slots * width * hidden, bytes_accessed=16 * MIB, transcendentals=0
        ),
    )(sent_rows, sent_grads, up, down, router)


def per_device(
    tokens,
    segments,
    patch_mask,
    choices,
    priority,
    first_gain,
    joint_weight,
    output_weight,
    second_gain,
    router_weight,
    expert_up,
    expert_down,
    out_grad,
):
    row_count, width = tokens.shape
    head_size = width // HEADS
    factor = head_size ** (-0.5)
    expert_count = router_weight.shape[1]
    length = segments.shape[1]
    capacity = (21 * choices.shape[1] * row_count + 20 * expert_count - 1) // (20 * expert_count)
    block_rows = min(row_count, 512)
    gain_one, joint_full, output_full, gain_two, router_full = (
        lax.all_gather(first_gain, ("grp", "ep"), axis=0, tiled=True),
        lax.all_gather(joint_weight, ("grp", "ep"), axis=0, tiled=True),
        lax.all_gather(output_weight, ("grp", "ep"), axis=0, tiled=True),
        lax.all_gather(second_gain, ("grp", "ep"), axis=0, tiled=True),
        lax.all_gather(router_weight, ("grp", "ep"), axis=0, tiled=True),
    )
    inputs = tokens.astype(jnp.float32)
    gain_one = gain_one.astype(jnp.float32)
    gain_two = gain_two.astype(jnp.float32)
    normed_f, unit_one, inverse_one = normalize(inputs, gain_one)
    normed = normed_f.astype(jnp.bfloat16)
    joint = jnp.dot(normed, joint_full, preferred_element_type=jnp.float32).astype(jnp.bfloat16)
    joint = joint.reshape(row_count, 3, HEADS, head_size)
    live = patch_mask.reshape(row_count)
    position = lax.broadcasted_iota(jnp.int32, (row_count,), 0)
    group = position // length * length + segments.reshape(row_count)
    masks = []
    mixed_parts = []
    log_parts = []
    for start in range(0, row_count, block_rows):
        allowed = visible(group[start : start + block_rows], live[start : start + block_rows])
        block = joint[start : start + block_rows]
        mixed_block, log_total = attend_forward(
            block[:, 0], block[:, 1], block[:, 2], allowed, factor
        )
        masks.append(allowed)
        mixed_parts.append(mixed_block)
        log_parts.append(log_total)
    mixed = jnp.concatenate(mixed_parts, axis=0).reshape(row_count, width).astype(jnp.bfloat16)
    state = inputs + jnp.dot(mixed, output_full, preferred_element_type=jnp.float32)
    normed_two_f, unit_two, inverse_two = normalize(state, gain_two)
    normed_two = normed_two_f.astype(jnp.bfloat16)
    slot_one, slot_two = route(
        choices, live, priority.reshape(row_count), expert_count, capacity
    )
    block = -(-capacity // 16) * 16
    slots = expert_count * block
    index = lax.broadcasted_iota(jnp.int32, (slots, row_count), 0)
    chosen = ((index == slot_one[None, :]) | (index == slot_two[None, :])).astype(jnp.bfloat16)
    spread = lambda values: (
        jnp.dot(chosen, values, preferred_element_type=jnp.float32)
        .astype(jnp.bfloat16)
        .reshape(expert_count, block, width)
    )
    collect = lambda values: outer(chosen, values.reshape(slots, width))
    grad = out_grad.astype(jnp.float32)
    back, returned, grad_up, grad_down, grad_router = experts_both_ways(
        spread(normed_two), spread(out_grad), expert_up[0], expert_down[0], router_full
    )
    output = (state + collect(returned)).astype(jnp.bfloat16)
    grad_router = grad_router[:, :expert_count]
    grad_normed_two = collect(back)
    grad_state_in, grad_gain_two = normalize_back(grad_normed_two, gain_two, unit_two, inverse_two)
    grad_state = grad + grad_state_in
    grad_branch = grad_state.astype(jnp.bfloat16)
    grad_output_w = outer(mixed, grad_branch)
    grad_mixed = (
        times_t(grad_branch, output_full).astype(jnp.bfloat16).reshape(row_count, HEADS, head_size)
    )
    grad_parts = []
    for number, start in enumerate(range(0, row_count, block_rows)):
        block = joint[start : start + block_rows]
        grad_parts.append(
            attend_backward(
                block[:, 0],
                block[:, 1],
                block[:, 2],
                masks[number],
                log_parts[number],
                grad_mixed[start : start + block_rows],
                factor,
            )
        )
    grad_joint = (
        jnp.concatenate(grad_parts, axis=0).reshape(row_count, 3 * width).astype(jnp.bfloat16)
    )
    grad_joint_w = outer(normed, grad_joint)
    grad_normed = times_t(grad_joint, joint_full)
    grad_inputs_in, grad_gain_one = normalize_back(grad_normed, gain_one, unit_one, inverse_one)
    tokens_grad = grad_state + grad_inputs_in
    shares = (
        lax.psum_scatter(grad_gain_one, ("grp", "ep"), scatter_dimension=0, tiled=True),
        lax.psum_scatter(grad_joint_w, ("grp", "ep"), scatter_dimension=0, tiled=True),
        lax.psum_scatter(grad_output_w, ("grp", "ep"), scatter_dimension=0, tiled=True),
        lax.psum_scatter(grad_gain_two, ("grp", "ep"), scatter_dimension=0, tiled=True),
        lax.psum_scatter(grad_router, ("grp", "ep"), scatter_dimension=0, tiled=True),
    )
    grad_up, grad_down = (
        lax.psum(grad_up, "grp").astype(jnp.float32)[None],
        lax.psum(grad_down, "grp").astype(jnp.float32)[None],
    )
    return (
        output,
        tokens_grad,
        shares[0],
        shares[1],
        shares[2],
        shares[3],
        shares[4],
        grad_up,
        grad_down,
    )


def solution(mesh):
    in_specs = (
        P(("grp", "ep"), None),
        P(("grp", "ep"), None),
        P(("grp", "ep"), None),
        P(("grp", "ep"), None),
        P(("grp", "ep"), None),
        P(("grp", "ep")),
        P(("grp", "ep"), None),
        P(("grp", "ep"), None),
        P(("grp", "ep")),
        P(("grp", "ep"), None),
        P("ep", None, None),
        P("ep", None, None),
        P(("grp", "ep"), None),
    )
    out_specs = (
        P(("grp", "ep"), None),
        P(("grp", "ep"), None),
        P(("grp", "ep")),
        P(("grp", "ep"), None),
        P(("grp", "ep"), None),
        P(("grp", "ep")),
        P(("grp", "ep"), None),
        P("ep", None, None),
        P("ep", None, None),
    )
    fused = mesh.shape["grp"] == 4 and mesh.shape["ep"] == 8
    return jax.shard_map(
        per_device_fused if fused else per_device, mesh=mesh, in_specs=in_specs, out_specs=out_specs, check_vma=False
    )
```

```python
import functools

import jax
import jax.numpy as jnp
from jax import lax
from jax.experimental import pallas as pl
from jax.experimental.pallas import tpu as pltpu
from jax.sharding import PartitionSpec as P

MESH = pl.DeviceIdType.MESH
MIB = 1 << 20
PIECES = 4
CHUNKS = 2 * PIECES
EARLY = ((0, 0), (0, 1), (1, 0), (1, 1))
LATE = ((0, 2), (0, 3), (1, 2), (1, 3))

HEADS = 8


EPSILON = 1e-06
NEGATIVE = -1e30


def normalize(values, gain):
    mean = jnp.mean(values, axis=-1, keepdims=True)
    centred = values - mean
    inverse = lax.rsqrt(jnp.mean(centred * centred, axis=-1, keepdims=True) + EPSILON)
    unit = centred * inverse
    return (unit * gain, unit, inverse)


def normalize_back(incoming, gain, unit, inverse):
    scaled = incoming * gain
    inner = (
        scaled
        - jnp.mean(scaled, axis=-1, keepdims=True)
        - unit * jnp.mean(scaled * unit, axis=-1, keepdims=True)
    )
    return (inverse * inner, jnp.sum(incoming * unit, axis=0))


def outer(left, right):
    return lax.dot_general(
        left, right, (((0,), (0,)), ((), ())), preferred_element_type=jnp.float32
    )


def times_t(left, right):
    return lax.dot_general(
        left, right, (((1,), (1,)), ((), ())), preferred_element_type=jnp.float32
    )


def route(picks, live, ranks, expert_count, capacity):
    row_count = picks.shape[0]
    labels = lax.broadcasted_iota(jnp.int32, (row_count, expert_count), 1)
    first = (picks[:, 0:1] == labels).astype(jnp.int32)
    second = (picks[:, 1:2] == labels).astype(jnp.int32)
    live_col = live[:, None]
    earlier = (ranks[None, :] < ranks[:, None]).astype(jnp.int32)
    first_live = first * live_col
    second_live = second * live_col
    place_one = jnp.sum(
        jnp.dot(earlier, first_live, preferred_element_type=jnp.int32) * first, axis=1
    )
    ahead = (
        jnp.dot(earlier, second_live, preferred_element_type=jnp.int32)
        + jnp.sum(first_live, axis=0)[None, :]
    )
    place_two = jnp.sum(ahead * second, axis=1)
    keep_one = (live > 0) & (place_one < capacity)
    keep_two = (live > 0) & (place_two < capacity)
    stride = -(-capacity // 16) * 16
    dummy = expert_count * stride
    slot_one = jnp.where(keep_one, picks[:, 0] * stride + place_one, dummy)
    slot_two = jnp.where(keep_two, picks[:, 1] * stride + place_two, dummy)
    return (slot_one, slot_two)


def visible(group, live):
    rows = group.shape[0]
    index = lax.broadcasted_iota(jnp.int32, (rows, rows), 0)
    other = lax.broadcasted_iota(jnp.int32, (rows, rows), 1)
    return (group[:, None] == group[None, :]) & ((live[None, :] > 0) | (index == other))


def attend_forward(query, key, value, allowed, factor):
    scores = jnp.einsum("qhd,khd->hqk", query, key, preferred_element_type=jnp.float32) * factor
    masked = jnp.where(allowed[None], scores, NEGATIVE)
    top = jnp.max(masked, axis=-1, keepdims=True)
    weights = jnp.exp(masked - top)
    total = jnp.sum(weights, axis=-1, keepdims=True)
    probs = (weights / total).astype(jnp.bfloat16)
    mixed = jnp.einsum("hqk,khd->qhd", probs, value, preferred_element_type=jnp.float32)
    return (mixed, top + jnp.log(total))


def attend_backward(query, key, value, allowed, log_total, grad_mixed, factor):
    scores = jnp.einsum("qhd,khd->hqk", query, key, preferred_element_type=jnp.float32) * factor
    masked = jnp.where(allowed[None], scores, NEGATIVE)
    probs = jnp.exp(masked - log_total)
    grad_value = jnp.einsum(
        "hqk,qhd->khd", probs.astype(jnp.bfloat16), grad_mixed, preferred_element_type=jnp.float32
    )
    grad_probs = jnp.einsum("qhd,khd->hqk", grad_mixed, value, preferred_element_type=jnp.float32)
    delta = jnp.sum(probs * grad_probs, axis=-1, keepdims=True)
    grad_scores = (probs * (grad_probs - delta)).astype(jnp.bfloat16)
    grad_query = (
        jnp.einsum("hqk,khd->qhd", grad_scores, key, preferred_element_type=jnp.float32) * factor
    )
    grad_key = (
        jnp.einsum("hqk,qhd->khd", grad_scores, query, preferred_element_type=jnp.float32) * factor
    )
    return jnp.stack([grad_query, grad_key, grad_value], axis=1)


def partner(me, step, count):
    other, bit = 0, 1
    while bit < count:
        other = other + bit * lax.rem(lax.div(me, bit) + lax.div(step, bit), 2)
        bit *= 2
    return other


def expert_kernel(
    count,
    experts,
    sent_rows,
    sent_grads,
    up_ref,
    down_ref,
    router_ref,
    back_ref,
    ret_ref,
    grad_up_ref,
    grad_down_ref,
    grad_router_ref,
    rows,
    grads,
    gated,
    act,
    grad_pre,
    logit_grads,
    out_grads,
    out_ret,
    turned,
    sems,
    local_sem,
):
    me = lax.axis_index("ep")
    block, width = rows.shape[1:]
    hidden = up_ref.shape[1]
    chunk = 512
    barrier = pltpu.get_barrier_semaphore()

    def greet(step, carry):
        pl.semaphore_signal(
            barrier, inc=1, device_id={"ep": partner(me, step, count)}, device_id_type=MESH
        )
        return carry

    lax.fori_loop(1, count, greet, 0)
    pl.semaphore_wait(barrier, count - 1)

    def remote(kind, source, target, step):
        return pltpu.make_async_remote_copy(
            src_ref=source,
            dst_ref=target,
            send_sem=sems.at[2 * kind, step],
            recv_sem=sems.at[2 * kind + 1, step],
            device_id={"ep": partner(me, step, count)},
            device_id_type=MESH,
        )

    def send_rows(step):
        return remote(0, sent_rows.at[partner(me, step, count)], rows.at[step], step)

    def send_grads(step):
        return remote(1, sent_grads.at[partner(me, step, count)], grads.at[step], step)

    def send_back(step):
        return remote(2, out_grads.at[step], back_ref.at[me], step)

    def send_ret(step):
        return remote(3, out_ret.at[step], ret_ref.at[me], step)

    own = [
        pltpu.make_async_copy(sent_rows.at[me], rows.at[0], local_sem.at[0]),
        pltpu.make_async_copy(sent_grads.at[me], grads.at[0], local_sem.at[1]),
        pltpu.make_async_copy(out_grads.at[0], back_ref.at[me], local_sem.at[2]),
        pltpu.make_async_copy(out_ret.at[0], ret_ref.at[me], local_sem.at[3]),
    ]
    own[0].start()
    own[1].start()

    def start(step, carry):
        send_rows(step).start()
        send_grads(step).start()
        return carry

    lax.fori_loop(1, count, start, 0)
    own[0].wait()
    own[1].wait()
    lanes = lax.broadcasted_iota(jnp.int32, (block, router_ref.shape[1]), 1)

    def one_block(step, carry):
        @pl.when(step > 0)
        def _():
            send_rows(step).wait_recv()
            send_grads(step).wait_recv()

        mine = rows[step]
        cotangent = grads[step].astype(jnp.float32)
        place = pl.ds(pl.multiple_of(step * block, 16), block)
        logits = jnp.dot(mine, router_ref[...], preferred_element_type=jnp.float32)
        logits = jnp.where(lanes < experts, logits, NEGATIVE)
        weights = jnp.exp(logits - jnp.max(logits, axis=1, keepdims=True))
        gate_all = weights / jnp.sum(weights, axis=1, keepdims=True)
        here = (lanes == me).astype(jnp.float32)
        gate = jnp.sum(gate_all * here, axis=1, keepdims=True)
        pair = (gate * cotangent).astype(jnp.bfloat16)
        gated[place, :] = pair
        ret = jnp.zeros((block, width), jnp.float32)
        back = jnp.zeros((block, width), jnp.float32)
        for first in range(0, hidden, chunk):
            span = slice(first, first + chunk)
            pre = jnp.dot(mine, up_ref[:, span], preferred_element_type=jnp.float32)
            cdf = 0.5 * (1.0 + lax.erf(pre * 0.7071067811865476))
            density = jnp.exp(-0.5 * pre * pre) * 0.3989422804014327
            low = (pre * cdf).astype(jnp.bfloat16)
            act[place, span] = low
            ret = ret + jnp.dot(low, down_ref[span, :], preferred_element_type=jnp.float32)
            grad_act = times_t(pair, down_ref[span, :])
            slope = (grad_act * (cdf + pre * density)).astype(jnp.bfloat16)
            grad_pre[place, span] = slope
            back = back + times_t(slope, up_ref[:, span])
        ret = ret.astype(jnp.bfloat16).astype(jnp.float32)
        out_ret[step] = (gate * ret).astype(jnp.bfloat16)
        gate_grad = jnp.sum(cotangent * ret, axis=1, keepdims=True)
        low_logits = (gate * gate_grad * (here - gate_all)).astype(jnp.bfloat16)
        logit_grads[place, :] = low_logits
        back = back + times_t(low_logits, router_ref[...])
        out_grads[step] = back.astype(jnp.bfloat16)

        @pl.when(step > 0)
        def _():
            send_back(step).start()

        @pl.when(step == 0)
        def _():
            own[2].start()

        return carry

    lax.fori_loop(0, count, one_block, 0)
    own[3].start()

    def start_ret(step, carry):
        send_ret(step).start()
        return carry

    lax.fori_loop(1, count, start_ret, 0)
    turned[...] = jnp.transpose(rows[...].reshape(count * block, width))
    grad_router_ref[...] = jnp.dot(
        turned[...], logit_grads[...], preferred_element_type=jnp.float32
    )

    def up_chunk(index, carry):
        span = pl.ds(pl.multiple_of(index * chunk, chunk), chunk)
        grad_up_ref[:, span] = jnp.dot(
            turned[...], grad_pre[:, span], preferred_element_type=jnp.float32
        ).astype(jnp.bfloat16)
        return carry

    lax.fori_loop(0, hidden // chunk, up_chunk, 0)
    turned[...] = jnp.transpose(gated[...])

    def down_chunk(index, carry):
        span = pl.ds(pl.multiple_of(index * chunk, chunk), chunk)
        part = jnp.dot(turned[...], act[:, span], preferred_element_type=jnp.float32)
        grad_down_ref[span, :] = jnp.transpose(part).astype(jnp.bfloat16)
        return carry

    lax.fori_loop(0, hidden // chunk, down_chunk, 0)

    def finish(step, carry):
        send_rows(step).wait_send()
        send_grads(step).wait_send()
        send_back(step).wait()
        send_ret(step).wait()
        return carry

    lax.fori_loop(1, count, finish, 0)
    own[2].wait()
    own[3].wait()


def column(values, lane):
    lanes = lax.broadcasted_iota(jnp.int32, values.shape, 1)
    return jnp.sum(jnp.where(lanes == lane, values, 0), axis=1, keepdims=True)


def core_peer(grp):
    return grp + 1 - 2 * lax.rem(grp, 2)


def x_peer(grp):
    return lax.rem(grp + 2, 4)


def flags(condition):
    return jnp.where(condition, 1.0, 0.0).astype(jnp.bfloat16)


def remote_copy(source, target, send_sem, recv_sem, device):
    return pltpu.make_async_remote_copy(
        src_ref=source,
        dst_ref=target,
        send_sem=send_sem,
        recv_sem=recv_sem,
        device_id=device,
        device_id_type=MESH,
    )


def expert_of(me, grp, count):
    half = count // 2
    other = lax.rem(lax.div(me, half) + lax.rem(grp, 2), 2)
    return lax.rem(me, half) + half * other


def seat(me, grp, step, count):
    half = count // 2
    core = lax.rem(lax.rem(grp, 2) + lax.div(step, half), 2)
    return {
        "grp": 2 * lax.div(grp, 2) + core,
        "ep": partner(me, lax.rem(step, half), count),
    }


def visit(index, count):
    return lax.div(index, 2) + (count // 2) * lax.rem(index, 2)


def greet_all(count, me, grp):
    barrier = pltpu.get_barrier_semaphore()
    half = count // 2

    def greet(step, carry):
        device = {"grp": grp, "ep": partner(me, step, count)}
        pl.semaphore_signal(barrier, inc=1, device_id=device, device_id_type=MESH)
        return carry

    lax.fori_loop(1, count, greet, 0)

    def greet_mate(step, carry):
        device = {"grp": core_peer(grp), "ep": partner(me, step, count)}
        pl.semaphore_signal(barrier, inc=1, device_id=device, device_id_type=MESH)
        return carry

    lax.fori_loop(0, half + 1, greet_mate, 0)
    pl.semaphore_signal(barrier, inc=1, device_id={"grp": x_peer(grp)}, device_id_type=MESH)
    pl.semaphore_wait(barrier, count + half + 1)


def pieces_of(layer_rows):
    def rows(chunk, side):
        size = layer_rows[chunk // PIECES] // (2 * PIECES)
        first = side * PIECES * size + (chunk % PIECES) * size
        return pl.ds(pl.multiple_of(first, size), size)

    return rows


def up_piece(piece, side, side_rows, columns):
    rows = pl.ds(pl.multiple_of(side * side_rows, side_rows), side_rows)
    return rows, pl.ds(piece * columns, columns)


def down_piece(piece, side, size):
    return pl.ds(pl.multiple_of(piece * 2 * size + side * size, size), size)


def seen(segment_row, live_row, segment_col):
    length = segment_row.shape[1]
    index = lax.broadcasted_iota(jnp.int32, (length, length), 0)
    other = lax.broadcasted_iota(jnp.int32, (length, length), 1)
    return (segment_col == segment_row) & ((live_row > 0) | (index == other))


def forward_kernel(
    count,
    capacity,
    tokens,
    segments,
    live,
    picks,
    ranks,
    out_grad,
    joint_shard,
    output_shard,
    pack_shard,
    own_up,
    own_down,
    weights,
    joint,
    mixed,
    state,
    sent_rows,
    logs,
    slots,
    grads,
    used_up,
    used_down,
    own_grads,
    normed_two,
    int_columns,
    ep_sems,
    x_sems,
    core_sems,
    grad_sems,
    fetch_sems,
    local_sems,
):
    me, grp = lax.axis_index("ep"), lax.axis_index("grp")
    expert = expert_of(me, grp, count)
    core, side_x = lax.rem(grp, 2), lax.div(grp, 2)
    half_ep = count // 2
    row_count, width = tokens.shape
    sequences, length = segments.shape
    block = sent_rows.shape[1]
    joint_width = joint.shape[1]
    head_size = width // HEADS
    factor = head_size ** (-0.5)
    mate, across = core_peer(grp), x_peer(grp)
    greet_all(count, me, grp)

    def shard(owner_grp, owner):
        return weights.at[owner_grp * count + owner]

    def to_ep(step):
        place = shard(grp, me)
        other = partner(me, step, count)
        return remote_copy(place, place, ep_sems.at[0, step], ep_sems.at[1, step], {"ep": other})

    def relay(step):
        place = shard(grp, partner(me, half_ep, count))
        sems = ep_sems.at[0, half_ep + step], ep_sems.at[1, half_ep + step]
        return remote_copy(place, place, *sems, {"ep": partner(me, step, count)})

    def to_x(step):
        place = shard(grp, partner(me, step, count))
        return remote_copy(place, place, x_sems.at[0, step], x_sems.at[1, step], {"grp": across})

    def to_core(owner_grp, part, step):
        place = shard(owner_grp, partner(me, step, count))
        sems = core_sems.at[0, part, step], core_sems.at[1, part, step]
        return remote_copy(place, place, *sems, {"grp": mate})

    def send_grads(step):
        return remote_copy(
            own_grads.at[step],
            grads.at[step],
            grad_sems.at[0, step],
            grad_sems.at[1, step],
            seat(me, grp, step, count),
        )

    layers = ((own_up, used_up), (own_down, used_down))
    rows_at = pieces_of((own_up.shape[0], own_down.shape[0]))

    def fetch(chunk):
        source, target = layers[chunk // PIECES]
        place = rows_at(chunk, side_x)
        sems = fetch_sems.at[0, chunk], fetch_sems.at[1, chunk]
        device = {"grp": mate, "ep": partner(me, half_ep, count)}
        return remote_copy(source.at[place], target.at[place], *sems, device)

    def share_fetch(chunk):
        place = layers[chunk // PIECES][1].at[rows_at(chunk, side_x)]
        sems = fetch_sems.at[2, chunk], fetch_sems.at[3, chunk]
        return remote_copy(place, place, *sems, {"grp": across})

    far_steps = [step for step in range(count) if step % half_ep >= half_ep // 2]

    def advance_grads(index):
        send_grads(far_steps[index]).wait_send()
        if index + 1 < len(far_steps):
            send_grads(far_steps[index + 1]).start()

    def advance(chunk):
        @pl.when(core == 0)
        def _():
            fetch(chunk).wait_send()
            if chunk + 2 < CHUNKS:
                fetch(chunk + 2).start()

        @pl.when(core == 1)
        def _():
            fetch(chunk).wait_recv()
            share_fetch(chunk).start()

    mine = grp * count + me
    fill = [
        pltpu.make_async_copy(
            joint_shard, weights.at[mine, :, pl.ds(0, joint_width)], local_sems.at[0]
        ),
        pltpu.make_async_copy(
            output_shard, weights.at[mine, :, pl.ds(joint_width, width)], local_sems.at[1]
        ),
        pltpu.make_async_copy(
            pack_shard, weights.at[mine, :, pl.ds(joint_width + width, 128)], local_sems.at[2]
        ),
    ]
    for copy in fill:
        copy.start()
    for copy in fill:
        copy.wait()

    def first_hop(step, carry):
        to_ep(step).start()
        return carry

    lax.fori_loop(1, half_ep + 1, first_hop, 0)
    to_x(0).start()
    to_core(grp, 0, 0).start()

    @pl.when(core == 0)
    def _():
        fetch(0).start()
        fetch(1).start()

    ints = jnp.concatenate([segments[...], live[...]], axis=0).astype(jnp.float32)
    turned = jnp.transpose(ints)
    int_columns[...] = turned.astype(jnp.int32)
    live_col = jnp.concatenate(
        [turned[:, sequences + i : sequences + i + 1] for i in range(sequences)], axis=0
    )
    rank_row = ranks[...].astype(jnp.float32)
    rank_col = jnp.transpose(jnp.broadcast_to(rank_row, (8, row_count)))[:, 0:1]
    earlier = flags(rank_row < rank_col)
    first, second = picks[:, 0:1], picks[:, 1:2]
    lanes = lax.broadcasted_iota(jnp.int32, (row_count, 128), 1)
    one = jnp.where(lanes == first, 1.0, 0.0)
    two = jnp.where(lanes == second + count, 1.0, 0.0)
    counts = jnp.dot(
        earlier, ((one + two) * live_col).astype(jnp.bfloat16), preferred_element_type=jnp.float32
    )
    ahead = jnp.sum(jnp.where(lanes == first + count, live_col, 0.0), axis=0, keepdims=True)
    place_one = jnp.sum(counts * one, axis=1, keepdims=True)
    place_two = jnp.sum((counts + ahead) * two, axis=1, keepdims=True)
    nowhere = 1.0 * count * block
    slot_one = jnp.where(
        (live_col > 0) & (place_one < capacity),
        first.astype(jnp.float32) * block + place_one,
        nowhere,
    )
    slot_two = jnp.where(
        (live_col > 0) & (place_two < capacity),
        second.astype(jnp.float32) * block + place_two,
        nowhere,
    )
    both = jnp.where(lanes == 0, slot_one, jnp.where(lanes == 1, slot_two, nowhere))
    slots[...] = both.astype(jnp.int32)
    slot_rows = jnp.transpose(both)[0:8].astype(jnp.int32)
    row_one, row_two = slot_rows[0:1], slot_rows[1:2]

    def rows_of(number, values):
        index = lax.broadcasted_iota(jnp.int32, (block, row_count), 0) + number * block
        chosen = flags((index == row_one) | (index == row_two))
        return jnp.dot(chosen, values[...], preferred_element_type=jnp.float32).astype(jnp.bfloat16)

    def spread_grads(index, carry):
        step = visit(index, count)
        own_grads[step] = rows_of(partner(expert, step, count), out_grad)

        @pl.when((step > 0) & (lax.rem(step, half_ep) < half_ep // 2))
        def _():
            send_grads(step).start()

        return carry

    lax.fori_loop(0, count, spread_grads, 0)
    send_grads(far_steps[0]).start()
    keep = pltpu.make_async_copy(own_grads.at[0], grads.at[0], local_sems.at[3])
    keep.start()

    to_ep(half_ep).wait_recv()

    def pass_far(step, carry):
        relay(step).start()
        return carry

    lax.fori_loop(1, half_ep, pass_far, 0)
    to_x(half_ep).start()
    to_core(grp, 0, half_ep).start()

    def pass_on(step, carry):
        @pl.when(step != half_ep)
        def _():
            to_ep(step).wait_recv()
            to_x(step).start()
            to_core(grp, 0, step).start()

        return carry

    lax.fori_loop(1, count, pass_on, 0)

    def pass_further(step, carry):
        to_x(step).wait_recv()
        to_core(across, 1, step).start()
        return carry

    lax.fori_loop(0, count, pass_further, 0)

    def arrive(step, carry):
        to_core(mate, 0, step).wait_recv()
        to_core(x_peer(mate), 1, step).wait_recv()
        return carry

    lax.fori_loop(0, count, arrive, 0)
    advance(0)
    advance_grads(0)

    devices = weights.shape[0]
    total = devices * weights.shape[1]
    pack = weights[:, :, joint_width + width :].reshape(total, 128)
    gains = jnp.transpose(pack.astype(jnp.float32))
    gain_one = gains[count : count + 1]
    gain_two = gains[count + 1 : count + 2]
    half = lax.broadcasted_iota(jnp.int32, (length, 128), 1) < head_size
    halves = (flags(half), flags(jnp.logical_not(half)))

    def attend(number, carry):
        rows = pl.ds(pl.multiple_of(number * length, length), length)
        values = tokens[rows, :].astype(jnp.float32)
        normed = normalize(values, gain_one)[0].astype(jnp.bfloat16)
        joint[rows, :] = jnp.dot(
            normed,
            weights[:, :, :joint_width].reshape(total, joint_width),
            preferred_element_type=jnp.float32,
        ).astype(jnp.bfloat16)
        allowed = seen(
            segments[pl.ds(number, 1), :], live[pl.ds(number, 1), :], column(int_columns[...], number)
        )
        log_all = jnp.zeros((length, 128), jnp.float32)
        log_lanes = lax.broadcasted_iota(jnp.int32, (length, 128), 1)
        for pair in range(HEADS // 2):
            at = pair * 128
            query = joint[rows, at : at + 128]
            key = joint[rows, width + at : width + at + 128]
            value = joint[rows, 2 * width + at : 2 * width + at + 128]
            results = []
            for side in range(2):
                scores = times_t(query * halves[side], key) * factor
                masked = jnp.where(allowed, scores, NEGATIVE)
                top = jnp.max(masked, axis=-1, keepdims=True)
                powers = jnp.exp(masked - top)
                added = jnp.sum(powers, axis=-1, keepdims=True)
                probs = (powers * (1.0 / added)).astype(jnp.bfloat16)
                results.append(jnp.dot(probs, value, preferred_element_type=jnp.float32))
                log_all = jnp.where(log_lanes == 2 * pair + side, top + jnp.log(added), log_all)
            mixed[rows, at : at + 128] = jnp.where(half, results[0], results[1]).astype(jnp.bfloat16)
        logs[rows, :] = log_all
        after = values + jnp.dot(
            mixed[rows, :],
            weights[:, :, joint_width : joint_width + width].reshape(total, width),
            preferred_element_type=jnp.float32,
        )
        state[rows, :] = after
        normed_two[rows, :] = normalize(after, gain_two)[0].astype(jnp.bfloat16)
        for place in range(sequences):

            @pl.when(number == place)
            def _(place=place):
                advance(place + 1)
                if place % 2 == 1:
                    advance_grads((place + 1) // 2)

        return carry

    lax.fori_loop(0, sequences, attend, 0)

    def spread_rows(number, carry):
        sent_rows[number] = rows_of(number, normed_two)
        return carry

    lax.fori_loop(0, count, spread_rows, 0)

    for chunk in range(sequences + 1, CHUNKS):
        advance(chunk)
    advance_grads(3)

    @pl.when(core == 1)
    def _():
        for chunk in range(CHUNKS):
            share_fetch(chunk).wait()

    keep.wait()
    to_x(0).wait_send()
    to_core(grp, 0, 0).wait_send()
    to_core(across, 1, 0).wait_send()

    def finish(step, carry):
        to_ep(step).wait_send()
        to_x(step).wait_send()
        to_core(grp, 0, step).wait_send()
        to_core(across, 1, step).wait_send()
        send_grads(step).wait_recv()

        @pl.when(lax.rem(step, half_ep) < half_ep // 2)
        def _():
            send_grads(step).wait_send()

        return carry

    lax.fori_loop(1, count, finish, 0)


def forward(
    count,
    capacity,
    block,
    tokens,
    segments,
    live,
    picks,
    ranks,
    out_grad,
    joint,
    output,
    pack,
    up,
    down,
):
    row_count, width = tokens.shape
    devices = width // joint.shape[0]
    all_width = joint.shape[1] + width + 128
    any_space = pl.BlockSpec(memory_space=pl.ANY)
    hbm = pl.BlockSpec(memory_space=pltpu.HBM)
    vmem = pl.BlockSpec(memory_space=pltpu.VMEM)
    low = jnp.bfloat16
    return pl.pallas_call(
        functools.partial(forward_kernel, count, capacity),
        out_shape=(
            jax.ShapeDtypeStruct((devices, joint.shape[0], all_width), low),
            jax.ShapeDtypeStruct((row_count, joint.shape[1]), low),
            jax.ShapeDtypeStruct((row_count, width), low),
            jax.ShapeDtypeStruct((row_count, width), jnp.float32),
            jax.ShapeDtypeStruct((count, block, width), low),
            jax.ShapeDtypeStruct((row_count, 128), jnp.float32),
            jax.ShapeDtypeStruct((row_count, 128), jnp.int32),
            jax.ShapeDtypeStruct((count, block, width), low),
            jax.ShapeDtypeStruct(up.shape, low),
            jax.ShapeDtypeStruct(down.shape, low),
        ),
        in_specs=[vmem] * 6 + [any_space] * 3 + [hbm] * 2,
        out_specs=(vmem,) * 7 + (hbm,) * 3,
        scratch_shapes=[
            pltpu.VMEM((count, block, width), low),
            pltpu.VMEM((row_count, width), low),
            pltpu.VMEM((segments.shape[1], 2 * segments.shape[0]), jnp.int32),
            pltpu.SemaphoreType.DMA((2, count)),
            pltpu.SemaphoreType.DMA((2, count)),
            pltpu.SemaphoreType.DMA((2, 2, count)),
            pltpu.SemaphoreType.DMA((2, count)),
            pltpu.SemaphoreType.DMA((4, CHUNKS)),
            pltpu.SemaphoreType.DMA((4,)),
        ],
        compiler_params=pltpu.CompilerParams(
            collective_id=2, has_side_effects=True, vmem_limit_bytes=48 * MIB
        ),
    )(tokens, segments, live, picks, ranks, out_grad, joint, output, pack, up, down)


def middle_kernel(
    count,
    sent_rows,
    grads,
    own_up,
    own_down,
    used_up,
    used_down,
    router_ref,
    back_ref,
    out_ret,
    part_up,
    part_down,
    early_up,
    early_down,
    grad_router_ref,
    rows,
    gated,
    act,
    grad_pre,
    logit_grads,
    out_grads,
    turned,
    turned_gated,
    up_ref,
    down_ref,
    ret_sums,
    back_sums,
    x_up,
    x_down,
    sems,
    x_sems,
    local_sem,
):
    me, grp = lax.axis_index("ep"), lax.axis_index("grp")
    expert = expert_of(me, grp, count)
    block, width = rows.shape[1:]
    hidden = up_ref.shape[1]
    chunk = 512

    def load(up, down):
        return (
            pltpu.make_async_copy(up, up_ref, local_sem.at[2]),
            pltpu.make_async_copy(down, down_ref, local_sem.at[3]),
        )

    @pl.when(lax.rem(grp, 2) == 0)
    def _():
        for copy in load(own_up, own_down):
            copy.start()

    @pl.when(lax.rem(grp, 2) == 1)
    def _():
        for copy in load(used_up, used_down):
            copy.start()

    greet_all(count, me, grp)

    def send_rows(step):
        other = partner(expert, step, count)
        there = seat(me, grp, step, count)
        return remote_copy(
            sent_rows.at[other], rows.at[step], sems.at[0, step], sems.at[1, step], there
        )

    def send_back(step):
        there = seat(me, grp, step, count)
        return remote_copy(
            out_grads.at[step], back_ref.at[expert], sems.at[2, step], sems.at[3, step], there
        )

    own = [
        pltpu.make_async_copy(sent_rows.at[expert], rows.at[0], local_sem.at[0]),
        pltpu.make_async_copy(out_grads.at[0], back_ref.at[expert], local_sem.at[1]),
    ]
    own[0].start()

    def start(index, carry):
        send_rows(visit(index, count)).start()
        return carry

    lax.fori_loop(1, count, start, 0)
    own[0].wait()
    for copy in load(used_up, used_down):
        copy.wait()
    lanes = lax.broadcasted_iota(jnp.int32, (block, router_ref.shape[1]), 1)

    across, side_x = x_peer(grp), lax.div(grp, 2)
    part_hidden = hidden // 2
    early = len(EARLY)

    def over_x(index):
        layer, piece = EARLY[index]
        sems = x_sems.at[0, index], x_sems.at[1, index]
        if layer == 0:
            source = part_up.at[up_piece(piece, 1 - side_x, width // 2, chunk)]
            target = x_up.at[:, pl.ds(piece * chunk, chunk)]
        else:
            source = part_down.at[down_piece(piece, 1 - side_x, chunk // 2)]
            target = x_down.at[pl.ds(piece * chunk // 2, chunk // 2)]
        return remote_copy(source, target, *sems, {"grp": across})

    def gates_of(values):
        logits = jnp.dot(values, router_ref[...], preferred_element_type=jnp.float32)
        logits = jnp.where(lanes < count, logits, NEGATIVE)
        weights = jnp.exp(logits - jnp.max(logits, axis=1, keepdims=True))
        return weights / jnp.sum(weights, axis=1, keepdims=True)

    here = (lanes == expert).astype(jnp.float32)

    def through(step, mine, pair, base):
        place = pl.ds(pl.multiple_of(step * block, 16), block)
        ret = jnp.zeros((block, width), jnp.float32)
        back = jnp.zeros((block, width), jnp.float32)
        for first in range(0, part_hidden, chunk):
            span = slice(base + first, base + first + chunk)
            kept = slice(first, first + chunk)
            pre = jnp.dot(mine, up_ref[:, span], preferred_element_type=jnp.float32)
            cdf = 0.5 * (1.0 + lax.erf(pre * 0.7071067811865476))
            density = jnp.exp(-0.5 * pre * pre) * 0.3989422804014327
            low = (pre * cdf).astype(jnp.bfloat16)
            act[place, kept] = low
            ret = ret + jnp.dot(low, down_ref[span, :], preferred_element_type=jnp.float32)
            grad_act = times_t(pair, down_ref[span, :])
            slope = (grad_act * (cdf + pre * density)).astype(jnp.bfloat16)
            grad_pre[place, kept] = slope
            back = back + times_t(slope, up_ref[:, span])
        return ret, back

    def first_half(index, carry):
        step = visit(index, count)

        @pl.when(step > 0)
        def _():
            send_rows(step).wait_recv()

        mine = rows[step]
        gate = jnp.sum(gates_of(mine) * here, axis=1, keepdims=True)
        pair = (gate * grads[step].astype(jnp.float32)).astype(jnp.bfloat16)
        gated[pl.ds(pl.multiple_of(step * block, 16), block), :] = pair
        ret_sums[step], back_sums[step] = through(step, mine, pair, 0)
        return carry

    def second_half(index, carry):
        step = visit(index, count)
        mine = rows[step]
        cotangent = grads[step].astype(jnp.float32)
        place = pl.ds(pl.multiple_of(step * block, 16), block)
        gate_all = gates_of(mine)
        gate = jnp.sum(gate_all * here, axis=1, keepdims=True)
        ret, back = through(step, mine, gated[place, :], part_hidden)
        ret = (ret + ret_sums[step]).astype(jnp.bfloat16).astype(jnp.float32)
        out_ret[step] = (gate * ret).astype(jnp.bfloat16)
        gate_grad = jnp.sum(cotangent * ret, axis=1, keepdims=True)
        low_logits = (gate * gate_grad * (here - gate_all)).astype(jnp.bfloat16)
        logit_grads[place, :] = low_logits
        back = back + back_sums[step] + times_t(low_logits, router_ref[...])
        out_grads[step] = back.astype(jnp.bfloat16)

        @pl.when(step > 0)
        def _():
            send_back(step).start()

        @pl.when(step == 0)
        def _():
            own[1].start()

        return carry

    def layer_sums(base):
        def up_chunk(index, carry):
            span = pl.ds(pl.multiple_of(index * chunk, chunk), chunk)
            part_up[:, pl.ds(pl.multiple_of(base + index * chunk, chunk), chunk)] = jnp.dot(
                turned[...], grad_pre[:, span], preferred_element_type=jnp.float32
            ).astype(jnp.bfloat16)
            return carry

        def down_chunk(index, carry):
            span = pl.ds(pl.multiple_of(index * chunk, chunk), chunk)
            part = jnp.dot(turned_gated[...], act[:, span], preferred_element_type=jnp.float32)
            part_down[pl.ds(pl.multiple_of(base + index * chunk, chunk), chunk), :] = jnp.transpose(
                part
            ).astype(jnp.bfloat16)
            return carry

        lax.fori_loop(0, part_hidden // chunk, up_chunk, 0)
        lax.fori_loop(0, part_hidden // chunk, down_chunk, 0)

    lax.fori_loop(0, count, first_half, 0)
    turned[...] = jnp.transpose(rows[...].reshape(count * block, width))
    turned_gated[...] = jnp.transpose(gated[...])
    layer_sums(0)
    for index in range(early):
        over_x(index).start()
    lax.fori_loop(0, count, second_half, 0)
    layer_sums(part_hidden)
    grad_router_ref[...] = jnp.dot(
        turned[...], logit_grads[...], preferred_element_type=jnp.float32
    )
    for index in range(early):
        layer, piece = EARLY[index]
        over_x(index).wait_recv()
        if layer == 0:
            kept = part_up[up_piece(piece, side_x, width // 2, chunk)]
            span = slice(piece * chunk, (piece + 1) * chunk)
            added = kept.astype(jnp.float32) + x_up[:, span].astype(jnp.float32)
            early_up[:, span] = added.astype(jnp.bfloat16)
        else:
            kept = part_down[down_piece(piece, side_x, chunk // 2), :]
            span = slice(piece * chunk // 2, (piece + 1) * chunk // 2)
            added = kept.astype(jnp.float32) + x_down[span, :].astype(jnp.float32)
            early_down[span, :] = added.astype(jnp.bfloat16)
    for index in range(early):
        over_x(index).wait_send()

    def finish(step, carry):
        send_rows(step).wait_send()
        send_back(step).wait()
        return carry

    lax.fori_loop(1, count, finish, 0)
    own[1].wait()


def middle(sent_rows, grads, up, down, used_up, used_down, router):
    count, block, width = sent_rows.shape
    hidden = up.shape[1]
    any_space = pl.BlockSpec(memory_space=pl.ANY)
    hbm = pl.BlockSpec(memory_space=pltpu.HBM)
    vmem = pl.BlockSpec(memory_space=pltpu.VMEM)
    low = jnp.bfloat16
    slots = count * block
    return pl.pallas_call(
        functools.partial(middle_kernel, count),
        out_shape=(
            jax.ShapeDtypeStruct((count, block, width), low),
            jax.ShapeDtypeStruct((count, block, width), low),
            jax.ShapeDtypeStruct((width, hidden), low),
            jax.ShapeDtypeStruct((hidden, width), low),
            jax.ShapeDtypeStruct((width // 2, hidden // 2), low),
            jax.ShapeDtypeStruct((hidden // 4, width), low),
            jax.ShapeDtypeStruct((width, 128), jnp.float32),
        ),
        in_specs=[any_space, vmem, hbm, hbm, hbm, hbm, vmem],
        out_specs=(any_space,) + (vmem,) * 6,
        scratch_shapes=[
            pltpu.VMEM((count, block, width), low),
            pltpu.VMEM((slots, width), low),
            pltpu.VMEM((slots, hidden // 2), low),
            pltpu.VMEM((slots, hidden // 2), low),
            pltpu.VMEM((slots, 128), low),
            pltpu.VMEM((count, block, width), low),
            pltpu.VMEM((width, slots), low),
            pltpu.VMEM((width, slots), low),
            pltpu.VMEM(up.shape, low),
            pltpu.VMEM(down.shape, low),
            pltpu.VMEM((count, block, width), jnp.float32),
            pltpu.VMEM((count, block, width), jnp.float32),
            pltpu.VMEM((width // 2, hidden // 2), low),
            pltpu.VMEM((hidden // 4, width), low),
            pltpu.SemaphoreType.DMA((4, count)),
            pltpu.SemaphoreType.DMA((2, len(EARLY))),
            pltpu.SemaphoreType.DMA((4,)),
        ],
        compiler_params=pltpu.CompilerParams(
            collective_id=3, has_side_effects=True, vmem_limit_bytes=60 * MIB
        ),
        cost_estimate=pl.CostEstimate(
            flops=12 * slots * width * hidden, bytes_accessed=16 * MIB, transcendentals=0
        ),
    )(sent_rows, grads, up, down, used_up, used_down, router)


def backward_kernel(
    count,
    tokens,
    segments,
    live,
    out_grad,
    weights,
    joint,
    mixed,
    state,
    logs,
    slots,
    back,
    out_ret,
    grad_router,
    part_up,
    part_down,
    early_up,
    early_down,
    output,
    tokens_grad,
    joint_share,
    output_share,
    pack_share,
    sum_up,
    sum_down,
    returned,
    grad_joint,
    normed_all,
    branch_all,
    mixed_grads,
    hidden_pairs,
    part,
    mate_part,
    pair_part,
    x_part,
    far_part,
    ep_part,
    turned,
    x_up,
    x_down,
    half_up,
    half_down,
    far_up,
    far_down,
    ret_sems,
    mate_sems,
    x_sems,
    ep_sems,
    sum_sems,
    local_sems,
):
    me, grp = lax.axis_index("ep"), lax.axis_index("grp")
    row_count, width = tokens.shape
    sequences, length = segments.shape
    block = back.shape[1]
    slot_count = count * block
    joint_width = joint.shape[1]
    head_size = width // HEADS
    factor = head_size ** (-0.5)
    mate, across = core_peer(grp), x_peer(grp)
    core, side_x = lax.rem(grp, 2), lax.div(grp, 2)
    devices = weights.shape[0]
    total = devices * weights.shape[1]
    expert = expert_of(me, grp, count)
    greet_all(count, me, grp)

    parts = EARLY + LATE
    early = len(EARLY)
    rows_up, size_up = part_up.shape[0] // 2, part_up.shape[1] // PIECES
    size_down = part_down.shape[0] // (2 * PIECES)

    def whole(index, arrays, side):
        layer, piece = parts[index]
        if layer == 0:
            return arrays[0].at[up_piece(piece, side, rows_up, size_up)]
        return arrays[1].at[down_piece(piece, side, size_down)]

    def narrow(index, arrays):
        layer, piece = parts[index]
        if layer == 0:
            return arrays[0].at[:, pl.ds((piece % 2) * size_up, size_up)]
        return arrays[1].at[pl.ds((piece % 2) * size_down, size_down)]

    def summed_x(index):
        return narrow(index, (early_up, early_down) if index < early else (half_up, half_down))

    def from_foreign(index):
        return narrow(index, (far_up.at[index // early], far_down.at[index // early]))

    def over_x(index):
        sems = sum_sems.at[0, index], sum_sems.at[1, index]
        source = whole(index, (part_up, part_down), 1 - side_x)
        return remote_copy(source, narrow(index, (x_up, x_down)), *sems, {"grp": across})

    def go_home(index):
        sems = sum_sems.at[2, index], sum_sems.at[3, index]
        device = {"grp": mate, "ep": partner(me, count // 2, count)}
        return remote_copy(summed_x(index), from_foreign(index), *sems, device)

    def spread_x(index):
        place = whole(index, (sum_up, sum_down), side_x)
        sems = sum_sems.at[4, index], sum_sems.at[5, index]
        return remote_copy(place, place, *sems, {"grp": across})

    def spread_core(index, side, first):
        place = whole(index, (sum_up, sum_down), side)
        sems = sum_sems.at[first, index], sum_sems.at[first + 1, index]
        return remote_copy(place, place, *sems, {"grp": mate})

    def own_half(index):
        return spread_core(index, side_x, 6)

    def other_half(index):
        return spread_core(index, 1 - side_x, 8)

    def leave(index):
        @pl.when(core == 1)
        def _():
            go_home(index).start()

    def add_x(index):
        over_x(index).wait_recv()
        kept = whole(index, (part_up, part_down), side_x)[...].astype(jnp.float32)
        landed = narrow(index, (x_up, x_down))[...].astype(jnp.float32)
        summed_x(index)[...] = (kept + landed).astype(jnp.bfloat16)
        if index + 2 < len(parts):
            over_x(index + 2).start()
        leave(index)

    def add_home(index):
        @pl.when(core == 0)
        def _():
            go_home(index).wait_recv()
            near = summed_x(index)[...].astype(jnp.float32)
            foreign = from_foreign(index)[...].astype(jnp.float32)
            whole(index, (sum_up, sum_down), side_x)[...] = (near + foreign).astype(jnp.bfloat16)
            spread_x(index).start()
            own_half(index).start()

    def pass_half(index):
        @pl.when(core == 0)
        def _():
            spread_x(index).wait_recv()
            other_half(index).start()

    for index in range(early):
        leave(index)
    over_x(early).start()
    over_x(early + 1).start()

    def send_ret(step):
        return remote_copy(
            out_ret.at[step],
            returned.at[expert],
            ret_sems.at[0, step],
            ret_sems.at[1, step],
            seat(me, grp, step, count),
        )

    keep = pltpu.make_async_copy(out_ret.at[0], returned.at[expert], local_sems.at[0])
    keep.start()

    def start(step, carry):
        send_ret(step).start()
        return carry

    lax.fori_loop(1, count, start, 0)
    pairs = HEADS // 2
    columns = [(pair * 384, 384) for pair in range(pairs)]
    columns += [(joint_width, width), (joint_width + width, 128)]
    pack = weights[:, :, joint_width + width :].reshape(total, 128)
    gains = jnp.transpose(pack.astype(jnp.float32))
    gain_one = gains[count : count + 1]
    gain_two = gains[count + 1 : count + 2]
    half = lax.broadcasted_iota(jnp.int32, (length, 128), 1) < head_size
    halves = (flags(half), flags(jnp.logical_not(half)))
    ints = jnp.transpose(segments[...].astype(jnp.float32)).astype(jnp.int32)

    def chosen_of(rows):
        index = lax.broadcasted_iota(jnp.int32, (length, slot_count), 1)
        pair = slots[rows, :]
        return flags((index == pair[:, 0:1]) | (index == pair[:, 1:2]))

    def to_mate(chunk, which):
        first, size = columns[chunk]
        span = pl.ds(first, size)
        return remote_copy(
            part.at[pl.ds((2 * which + 1 - core) * count, count), :, span],
            mate_part.at[which, :, :, span],
            mate_sems.at[0, chunk, which],
            mate_sems.at[1, chunk, which],
            {"grp": mate},
        )

    def to_x(chunk):
        first, size = columns[chunk]
        span = pl.ds(first, size)
        sems = x_sems.at[0, chunk], x_sems.at[1, chunk]
        source = pair_part.at[1 - side_x, :, :, span]
        return remote_copy(source, x_part.at[:, :, span], *sems, {"grp": across})

    def to_ep(chunk, step):
        first, size = columns[chunk]
        span = pl.ds(first, size)
        other = partner(me, step, count)
        return remote_copy(
            far_part.at[other, :, span],
            ep_part.at[step, :, span],
            ep_sems.at[0, chunk, step],
            ep_sems.at[1, chunk, step],
            {"ep": other},
        )

    def sum_core(chunk):
        first, size = columns[chunk]
        span = slice(first, first + size)
        for which in range(2):
            to_mate(chunk, which).wait_recv()
            owner = 2 * which + core
            pair_part[which, :, :, span] = (
                part[pl.ds(owner * count, count), :, span].astype(jnp.float32)
                + mate_part[which, :, :, span].astype(jnp.float32)
            ).astype(jnp.bfloat16)
        to_x(chunk).start()

    def sum_x(chunk):
        first, size = columns[chunk]
        span = slice(first, first + size)
        to_x(chunk).wait_recv()
        far_part[:, :, span] = (
            pair_part[side_x, :, :, span].astype(jnp.float32) + x_part[:, :, span].astype(jnp.float32)
        ).astype(jnp.bfloat16)

        def start(step, carry):
            to_ep(chunk, step).start()
            return carry

        lax.fori_loop(1, count, start, 0)

    def sum_ep(chunk):
        first, size = columns[chunk]
        span = slice(first, first + size)

        def add(step, added):
            to_ep(chunk, step).wait_recv()
            return added + ep_part[step, :, span].astype(jnp.float32)

        share = lax.fori_loop(1, count, add, far_part[me, :, span].astype(jnp.float32))
        if chunk < pairs:
            for third in range(3):
                at = third * width + chunk * 128
                joint_share[:, at : at + 128] = share[:, third * 128 : third * 128 + 128]
        elif chunk == pairs:
            output_share[...] = share
        else:
            pack_share[...] = share

    shape = (devices, total // devices)

    def lower_part(number, carry):
        rows = pl.ds(pl.multiple_of(number * length, length), length)
        grad_normed_two = jnp.dot(
            chosen_of(rows),
            back[...].reshape(slot_count, width),
            preferred_element_type=jnp.float32,
        )
        _, unit, inverse = normalize(state[rows, :], gain_two)
        inner, share = normalize_back(grad_normed_two, gain_two, unit, inverse)
        grad_state = out_grad[rows, :].astype(jnp.float32) + inner
        tokens_grad[rows, :] = grad_state
        branch = grad_state.astype(jnp.bfloat16)
        branch_all[rows, :] = branch
        mixed_grads[rows, :] = times_t(
            branch, weights[:, :, joint_width : joint_width + width].reshape(total, width)
        ).astype(jnp.bfloat16)
        allowed = seen(segments[pl.ds(number, 1), :], live[pl.ds(number, 1), :], column(ints, number))
        hidden_pairs[rows, :] = jnp.where(allowed, 0.0, NEGATIVE)
        normed = normalize(tokens[rows, :].astype(jnp.float32), gain_one)[0]
        normed_all[rows, :] = normed.astype(jnp.bfloat16)
        return carry + share[None, :]

    nothing = jnp.zeros((1, width), jnp.float32)
    grad_two = lax.fori_loop(0, sequences, lower_part, nothing)
    turned[...] = jnp.transpose(mixed[...])
    first, size = columns[pairs]
    part[:, :, first : first + size] = (
        jnp.dot(turned[...], branch_all[...], preferred_element_type=jnp.float32)
        .astype(jnp.bfloat16)
        .reshape(*shape, size)
    )
    to_mate(pairs, 0).start()
    to_mate(pairs, 1).start()
    turned[...] = jnp.transpose(normed_all[...])

    for pair in range(pairs):
        at = pair * 128

        def attend(number, carry, pair=pair, at=at):
            rows = pl.ds(pl.multiple_of(number * length, length), length)
            query = joint[rows, at : at + 128]
            key = joint[rows, width + at : width + at + 128]
            value = joint[rows, 2 * width + at : 2 * width + at + 128]
            grad_out = mixed_grads[rows, at : at + 128]
            unseen = hidden_pairs[rows, :]
            results = []
            for side in range(2):
                scores = times_t(query * halves[side], key) * factor
                log_all = logs[rows, 2 * pair + side : 2 * pair + side + 1]
                probs = jnp.exp(scores + unseen - log_all)
                grad_value = outer(probs.astype(jnp.bfloat16), grad_out)
                grad_probs = times_t(grad_out * halves[side], value)
                delta = jnp.sum(probs * grad_probs, axis=-1, keepdims=True)
                grad_scores = (probs * (grad_probs - delta)).astype(jnp.bfloat16)
                grad_query = jnp.dot(grad_scores, key, preferred_element_type=jnp.float32) * factor
                grad_key = outer(grad_scores, query) * factor
                results.append((grad_query, grad_key, grad_value))
            for third in range(3):
                grad_joint[rows, third * width + at : third * width + at + 128] = jnp.where(
                    half, results[0][third], results[1][third]
                ).astype(jnp.bfloat16)
            return carry

        lax.fori_loop(0, sequences, attend, 0, unroll=4)
        first, size = columns[pair]
        mine = jnp.concatenate(
            [grad_joint[:, third * width + at : third * width + at + 128] for third in range(3)], axis=1
        )
        part[:, :, first : first + size] = (
            jnp.dot(turned[...], mine, preferred_element_type=jnp.float32)
            .astype(jnp.bfloat16)
            .reshape(*shape, size)
        )
        to_mate(pair, 0).start()
        to_mate(pair, 1).start()
        sum_core(pairs if pair == 0 else pair - 1)
        if pair == 0:
            add_x(early)
            add_x(early + 1)
        elif pair == 1:
            sum_x(pairs)
        else:
            sum_x(pair - 2)
        if pair == 2:
            for index in range(early):
                add_home(index)
            add_x(early + 2)
            add_x(early + 3)
            sum_ep(pairs)

    def upper_part(number, carry):
        rows = pl.ds(pl.multiple_of(number * length, length), length)
        grad_normed = times_t(
            grad_joint[rows, :], weights[:, :, :joint_width].reshape(total, joint_width)
        )
        _, unit, inverse = normalize(tokens[rows, :].astype(jnp.float32), gain_one)
        inner, share = normalize_back(grad_normed, gain_one, unit, inverse)
        tokens_grad[rows, :] = tokens_grad[rows, :] + inner
        return carry + share[None, :]

    grad_one = lax.fori_loop(0, sequences, upper_part, nothing)
    lines = lax.broadcasted_iota(jnp.int32, (128, width), 0)
    gain_lines = jnp.where(
        lines == count, grad_one, jnp.where(lines == count + 1, grad_two, 0.0)
    )
    first, size = columns[pairs + 1]
    part[:, :, first : first + size] = (
        (grad_router[...] + jnp.transpose(gain_lines)).astype(jnp.bfloat16).reshape(*shape, 128)
    )
    to_mate(pairs + 1, 0).start()
    to_mate(pairs + 1, 1).start()
    sum_core(pairs - 1)
    sum_core(pairs + 1)
    sum_x(pairs - 2)
    keep.wait()

    def from_all(step, carry):
        send_ret(step).wait()
        return carry

    lax.fori_loop(1, count, from_all, 0)

    def combine(number, carry):
        rows = pl.ds(pl.multiple_of(number * length, length), length)
        gathered = jnp.dot(
            chosen_of(rows),
            returned[...].reshape(slot_count, width),
            preferred_element_type=jnp.float32,
        )
        output[rows, :] = (state[rows, :] + gathered).astype(jnp.bfloat16)
        return carry

    lax.fori_loop(0, sequences, combine, 0)
    sum_x(pairs - 1)
    sum_x(pairs + 1)
    for index in range(early):
        pass_half(index)
    add_home(early)
    add_home(early + 1)
    for chunk in range(pairs):
        sum_ep(chunk)
    sum_ep(pairs + 1)
    add_home(early + 2)
    pass_half(early)
    pass_half(early + 1)
    add_home(early + 3)
    pass_half(early + 2)
    pass_half(early + 3)

    @pl.when(core == 0)
    def _():
        for chunk in range(CHUNKS):
            spread_x(chunk).wait_send()
            own_half(chunk).wait_send()
            other_half(chunk).wait_send()

    @pl.when(core == 1)
    def _():
        for chunk in range(CHUNKS):
            go_home(chunk).wait_send()
            own_half(chunk).wait_recv()
            other_half(chunk).wait_recv()

    for index in range(early, len(parts)):
        over_x(index).wait_send()
    for chunk in range(len(columns)):
        to_mate(chunk, 0).wait_send()
        to_mate(chunk, 1).wait_send()
        to_x(chunk).wait_send()

        def finish(step, carry, chunk=chunk):
            to_ep(chunk, step).wait_send()
            return carry

        lax.fori_loop(1, count, finish, 0)


def backward(
    tokens,
    segments,
    live,
    out_grad,
    weights,
    joint,
    mixed,
    state,
    logs,
    slots,
    back,
    ret,
    router,
    part_up,
    part_down,
    early_up,
    early_down,
):
    row_count, width = tokens.shape
    count = back.shape[0]
    devices, shard_rows, all_width = weights.shape
    any_space = pl.BlockSpec(memory_space=pl.ANY)
    vmem = pl.BlockSpec(memory_space=pltpu.VMEM)
    low = jnp.bfloat16
    quarter = (count, shard_rows, all_width)
    return pl.pallas_call(
        functools.partial(backward_kernel, count),
        out_shape=(
            jax.ShapeDtypeStruct((row_count, width), low),
            jax.ShapeDtypeStruct((row_count, width), jnp.float32),
            jax.ShapeDtypeStruct((shard_rows, joint.shape[1]), jnp.float32),
            jax.ShapeDtypeStruct((shard_rows, width), jnp.float32),
            jax.ShapeDtypeStruct((shard_rows, 128), jnp.float32),
            jax.ShapeDtypeStruct(part_up.shape, low),
            jax.ShapeDtypeStruct(part_down.shape, low),
        ),
        in_specs=[vmem] * 11 + [any_space] + [vmem] * 5,
        out_specs=(vmem,) * 7,
        scratch_shapes=[
            pltpu.VMEM(back.shape, low),
            pltpu.VMEM(joint.shape, low),
            pltpu.VMEM((row_count, width), low),
            pltpu.VMEM((row_count, width), low),
            pltpu.VMEM((row_count, width), low),
            pltpu.VMEM((row_count, segments.shape[1]), jnp.float32),
            pltpu.VMEM(weights.shape, low),
            pltpu.VMEM((2,) + quarter, low),
            pltpu.VMEM((2,) + quarter, low),
            pltpu.VMEM(quarter, low),
            pltpu.VMEM(quarter, low),
            pltpu.VMEM(quarter, low),
            pltpu.VMEM((width, row_count), low),
            pltpu.VMEM(early_up.shape, low),
            pltpu.VMEM(early_down.shape, low),
            pltpu.VMEM(early_up.shape, low),
            pltpu.VMEM(early_down.shape, low),
            pltpu.VMEM((2,) + early_up.shape, low),
            pltpu.VMEM((2,) + early_down.shape, low),
            pltpu.SemaphoreType.DMA((2, count)),
            pltpu.SemaphoreType.DMA((2, HEADS // 2 + 2, 2)),
            pltpu.SemaphoreType.DMA((2, HEADS // 2 + 2)),
            pltpu.SemaphoreType.DMA((2, HEADS // 2 + 2, count)),
            pltpu.SemaphoreType.DMA((10, CHUNKS)),
            pltpu.SemaphoreType.DMA((1,)),
        ],
        compiler_params=pltpu.CompilerParams(
            collective_id=4, has_side_effects=True, vmem_limit_bytes=60 * MIB
        ),
    )(
        tokens,
        segments,
        live,
        out_grad,
        weights,
        joint,
        mixed,
        state,
        logs,
        slots,
        back,
        ret,
        router,
        part_up,
        part_down,
        early_up,
        early_down,
    )


def per_device_fused(
    tokens,
    segments,
    patch_mask,
    choices,
    priority,
    first_gain,
    joint_weight,
    output_weight,
    second_gain,
    router_weight,
    expert_up,
    expert_down,
    out_grad,
):
    row_count, width = tokens.shape
    experts = router_weight.shape[1]
    capacity = (21 * choices.shape[1] * row_count + 20 * experts - 1) // (20 * experts)
    block = -(-capacity // 16) * 16
    shard_rows = first_gain.shape[0]
    pack = jnp.concatenate(
        [
            router_weight,
            first_gain[:, None],
            second_gain[:, None],
            jnp.zeros((shard_rows, 128 - experts - 2), jnp.bfloat16),
        ],
        axis=1,
    )
    weights, joint, mixed, state, sent_rows, logs, slots, grads, used_up, used_down = forward(
        experts,
        capacity,
        block,
        tokens,
        segments,
        patch_mask,
        choices,
        priority,
        out_grad,
        joint_weight,
        output_weight,
        pack,
        expert_up[0],
        expert_down[0],
    )
    router = weights[:, :, joint.shape[1] + width :].reshape(width, 128)
    back, ret, part_up, part_down, early_up, early_down, grad_router = middle(
        sent_rows, grads, expert_up[0], expert_down[0], used_up, used_down, router
    )
    output, tokens_grad, grad_joint, grad_output, grad_pack, grad_up, grad_down = backward(
        tokens,
        segments,
        patch_mask,
        out_grad,
        weights,
        joint,
        mixed,
        state,
        logs,
        slots,
        back,
        ret,
        grad_router,
        part_up,
        part_down,
        early_up,
        early_down,
    )
    return (
        output,
        tokens_grad,
        grad_pack[:, experts],
        grad_joint,
        grad_output,
        grad_pack[:, experts + 1],
        grad_pack[:, :experts],
        grad_up.astype(jnp.float32)[None],
        grad_down.astype(jnp.float32)[None],
    )


def experts_both_ways(sent_rows, sent_grads, up, down, router):
    count, block, width = sent_rows.shape
    experts = router.shape[1]
    hidden = up.shape[1]
    router = jnp.pad(router, ((0, 0), (0, 128 - experts)))
    any_space = pl.BlockSpec(memory_space=pl.ANY)
    vmem = pl.BlockSpec(memory_space=pltpu.VMEM)
    low = jnp.bfloat16
    slots = count * block
    return pl.pallas_call(
        functools.partial(expert_kernel, count, experts),
        out_shape=(
            jax.ShapeDtypeStruct((count, block, width), low),
            jax.ShapeDtypeStruct((count, block, width), low),
            jax.ShapeDtypeStruct((width, hidden), low),
            jax.ShapeDtypeStruct((hidden, width), low),
            jax.ShapeDtypeStruct((width, 128), jnp.float32),
        ),
        in_specs=[any_space, any_space, vmem, vmem, vmem],
        out_specs=(any_space, any_space, vmem, vmem, vmem),
        scratch_shapes=[
            pltpu.VMEM((count, block, width), low),
            pltpu.VMEM((count, block, width), low),
            pltpu.VMEM((slots, width), low),
            pltpu.VMEM((slots, hidden), low),
            pltpu.VMEM((slots, hidden), low),
            pltpu.VMEM((slots, 128), low),
            pltpu.VMEM((count, block, width), low),
            pltpu.VMEM((count, block, width), low),
            pltpu.VMEM((width, slots), low),
            pltpu.SemaphoreType.DMA((8, count)),
            pltpu.SemaphoreType.DMA((4,)),
        ],
        compiler_params=pltpu.CompilerParams(
            collective_id=1, has_side_effects=True, vmem_limit_bytes=58 * MIB
        ),
        cost_estimate=pl.CostEstimate(
            flops=12 * slots * width * hidden, bytes_accessed=16 * MIB, transcendentals=0
        ),
    )(sent_rows, sent_grads, up, down, router)


def per_device(
    tokens,
    segments,
    patch_mask,
    choices,
    priority,
    first_gain,
    joint_weight,
    output_weight,
    second_gain,
    router_weight,
    expert_up,
    expert_down,
    out_grad,
):
    row_count, width = tokens.shape
    head_size = width // HEADS
    factor = head_size ** (-0.5)
    expert_count = router_weight.shape[1]
    length = segments.shape[1]
    capacity = (21 * choices.shape[1] * row_count + 20 * expert_count - 1) // (20 * expert_count)
    block_rows = min(row_count, 512)
    gain_one, joint_full, output_full, gain_two, router_full = (
        lax.all_gather(first_gain, ("grp", "ep"), axis=0, tiled=True),
        lax.all_gather(joint_weight, ("grp", "ep"), axis=0, tiled=True),
        lax.all_gather(output_weight, ("grp", "ep"), axis=0, tiled=True),
        lax.all_gather(second_gain, ("grp", "ep"), axis=0, tiled=True),
        lax.all_gather(router_weight, ("grp", "ep"), axis=0, tiled=True),
    )
    inputs = tokens.astype(jnp.float32)
    gain_one = gain_one.astype(jnp.float32)
    gain_two = gain_two.astype(jnp.float32)
    normed_f, unit_one, inverse_one = normalize(inputs, gain_one)
    normed = normed_f.astype(jnp.bfloat16)
    joint = jnp.dot(normed, joint_full, preferred_element_type=jnp.float32).astype(jnp.bfloat16)
    joint = joint.reshape(row_count, 3, HEADS, head_size)
    live = patch_mask.reshape(row_count)
    position = lax.broadcasted_iota(jnp.int32, (row_count,), 0)
    group = position // length * length + segments.reshape(row_count)
    masks = []
    mixed_parts = []
    log_parts = []
    for start in range(0, row_count, block_rows):
        allowed = visible(group[start : start + block_rows], live[start : start + block_rows])
        block = joint[start : start + block_rows]
        mixed_block, log_total = attend_forward(
            block[:, 0], block[:, 1], block[:, 2], allowed, factor
        )
        masks.append(allowed)
        mixed_parts.append(mixed_block)
        log_parts.append(log_total)
    mixed = jnp.concatenate(mixed_parts, axis=0).reshape(row_count, width).astype(jnp.bfloat16)
    state = inputs + jnp.dot(mixed, output_full, preferred_element_type=jnp.float32)
    normed_two_f, unit_two, inverse_two = normalize(state, gain_two)
    normed_two = normed_two_f.astype(jnp.bfloat16)
    slot_one, slot_two = route(
        choices, live, priority.reshape(row_count), expert_count, capacity
    )
    block = -(-capacity // 16) * 16
    slots = expert_count * block
    index = lax.broadcasted_iota(jnp.int32, (slots, row_count), 0)
    chosen = ((index == slot_one[None, :]) | (index == slot_two[None, :])).astype(jnp.bfloat16)
    spread = lambda values: (
        jnp.dot(chosen, values, preferred_element_type=jnp.float32)
        .astype(jnp.bfloat16)
        .reshape(expert_count, block, width)
    )
    collect = lambda values: outer(chosen, values.reshape(slots, width))
    grad = out_grad.astype(jnp.float32)
    back, returned, grad_up, grad_down, grad_router = experts_both_ways(
        spread(normed_two), spread(out_grad), expert_up[0], expert_down[0], router_full
    )
    output = (state + collect(returned)).astype(jnp.bfloat16)
    grad_router = grad_router[:, :expert_count]
    grad_normed_two = collect(back)
    grad_state_in, grad_gain_two = normalize_back(grad_normed_two, gain_two, unit_two, inverse_two)
    grad_state = grad + grad_state_in
    grad_branch = grad_state.astype(jnp.bfloat16)
    grad_output_w = outer(mixed, grad_branch)
    grad_mixed = (
        times_t(grad_branch, output_full).astype(jnp.bfloat16).reshape(row_count, HEADS, head_size)
    )
    grad_parts = []
    for number, start in enumerate(range(0, row_count, block_rows)):
        block = joint[start : start + block_rows]
        grad_parts.append(
            attend_backward(
                block[:, 0],
                block[:, 1],
                block[:, 2],
                masks[number],
                log_parts[number],
                grad_mixed[start : start + block_rows],
                factor,
            )
        )
    grad_joint = (
        jnp.concatenate(grad_parts, axis=0).reshape(row_count, 3 * width).astype(jnp.bfloat16)
    )
    grad_joint_w = outer(normed, grad_joint)
    grad_normed = times_t(grad_joint, joint_full)
    grad_inputs_in, grad_gain_one = normalize_back(grad_normed, gain_one, unit_one, inverse_one)
    tokens_grad = grad_state + grad_inputs_in
    shares = (
        lax.psum_scatter(grad_gain_one, ("grp", "ep"), scatter_dimension=0, tiled=True),
        lax.psum_scatter(grad_joint_w, ("grp", "ep"), scatter_dimension=0, tiled=True),
        lax.psum_scatter(grad_output_w, ("grp", "ep"), scatter_dimension=0, tiled=True),
        lax.psum_scatter(grad_gain_two, ("grp", "ep"), scatter_dimension=0, tiled=True),
        lax.psum_scatter(grad_router, ("grp", "ep"), scatter_dimension=0, tiled=True),
    )
    grad_up, grad_down = (
        lax.psum(grad_up, "grp").astype(jnp.float32)[None],
        lax.psum(grad_down, "grp").astype(jnp.float32)[None],
    )
    return (
        output,
        tokens_grad,
        shares[0],
        shares[1],
        shares[2],
        shares[3],
        shares[4],
        grad_up,
        grad_down,
    )


def solution(mesh):
    in_specs = (
        P(("grp", "ep"), None),
        P(("grp", "ep"), None),
        P(("grp", "ep"), None),
        P(("grp", "ep"), None),
        P(("grp", "ep"), None),
        P(("grp", "ep")),
        P(("grp", "ep"), None),
        P(("grp", "ep"), None),
        P(("grp", "ep")),
        P(("grp", "ep"), None),
        P("ep", None, None),
        P("ep", None, None),
        P(("grp", "ep"), None),
    )
    out_specs = (
        P(("grp", "ep"), None),
        P(("grp", "ep"), None),
        P(("grp", "ep")),
        P(("grp", "ep"), None),
        P(("grp", "ep"), None),
        P(("grp", "ep")),
        P(("grp", "ep"), None),
        P("ep", None, None),
        P("ep", None, None),
    )
    fused = mesh.shape["grp"] == 4 and mesh.shape["ep"] == 8
    return jax.shard_map(
        per_device_fused if fused else per_device, mesh=mesh, in_specs=in_specs, out_specs=out_specs, check_vma=False
    )
```

```python
import functools

import jax
import jax.numpy as jnp
from jax import lax
from jax.experimental import pallas as pl
from jax.experimental.pallas import tpu as pltpu
from jax.sharding import PartitionSpec as P

MESH = pl.DeviceIdType.MESH
MIB = 1 << 20
PIECES = 4
CHUNKS = 2 * PIECES
EARLY = ((0, 0), (0, 1), (1, 0), (1, 1))
LATE = ((0, 2), (0, 3), (1, 2), (1, 3))

HEADS = 8


EPSILON = 1e-06
NEGATIVE = -1e30


def normalize(values, gain):
    mean = jnp.mean(values, axis=-1, keepdims=True)
    centred = values - mean
    inverse = lax.rsqrt(jnp.mean(centred * centred, axis=-1, keepdims=True) + EPSILON)
    unit = centred * inverse
    return (unit * gain, unit, inverse)


def normalize_back(incoming, gain, unit, inverse):
    scaled = incoming * gain
    inner = (
        scaled
        - jnp.mean(scaled, axis=-1, keepdims=True)
        - unit * jnp.mean(scaled * unit, axis=-1, keepdims=True)
    )
    return (inverse * inner, jnp.sum(incoming * unit, axis=0))


def outer(left, right):
    return lax.dot_general(
        left, right, (((0,), (0,)), ((), ())), preferred_element_type=jnp.float32
    )


def times_t(left, right):
    return lax.dot_general(
        left, right, (((1,), (1,)), ((), ())), preferred_element_type=jnp.float32
    )


def route(picks, live, ranks, expert_count, capacity):
    row_count = picks.shape[0]
    labels = lax.broadcasted_iota(jnp.int32, (row_count, expert_count), 1)
    first = (picks[:, 0:1] == labels).astype(jnp.int32)
    second = (picks[:, 1:2] == labels).astype(jnp.int32)
    live_col = live[:, None]
    earlier = (ranks[None, :] < ranks[:, None]).astype(jnp.int32)
    first_live = first * live_col
    second_live = second * live_col
    place_one = jnp.sum(
        jnp.dot(earlier, first_live, preferred_element_type=jnp.int32) * first, axis=1
    )
    ahead = (
        jnp.dot(earlier, second_live, preferred_element_type=jnp.int32)
        + jnp.sum(first_live, axis=0)[None, :]
    )
    place_two = jnp.sum(ahead * second, axis=1)
    keep_one = (live > 0) & (place_one < capacity)
    keep_two = (live > 0) & (place_two < capacity)
    stride = -(-capacity // 16) * 16
    dummy = expert_count * stride
    slot_one = jnp.where(keep_one, picks[:, 0] * stride + place_one, dummy)
    slot_two = jnp.where(keep_two, picks[:, 1] * stride + place_two, dummy)
    return (slot_one, slot_two)


def visible(group, live):
    rows = group.shape[0]
    index = lax.broadcasted_iota(jnp.int32, (rows, rows), 0)
    other = lax.broadcasted_iota(jnp.int32, (rows, rows), 1)
    return (group[:, None] == group[None, :]) & ((live[None, :] > 0) | (index == other))


def attend_forward(query, key, value, allowed, factor):
    scores = jnp.einsum("qhd,khd->hqk", query, key, preferred_element_type=jnp.float32) * factor
    masked = jnp.where(allowed[None], scores, NEGATIVE)
    top = jnp.max(masked, axis=-1, keepdims=True)
    weights = jnp.exp(masked - top)
    total = jnp.sum(weights, axis=-1, keepdims=True)
    probs = (weights / total).astype(jnp.bfloat16)
    mixed = jnp.einsum("hqk,khd->qhd", probs, value, preferred_element_type=jnp.float32)
    return (mixed, top + jnp.log(total))


def attend_backward(query, key, value, allowed, log_total, grad_mixed, factor):
    scores = jnp.einsum("qhd,khd->hqk", query, key, preferred_element_type=jnp.float32) * factor
    masked = jnp.where(allowed[None], scores, NEGATIVE)
    probs = jnp.exp(masked - log_total)
    grad_value = jnp.einsum(
        "hqk,qhd->khd", probs.astype(jnp.bfloat16), grad_mixed, preferred_element_type=jnp.float32
    )
    grad_probs = jnp.einsum("qhd,khd->hqk", grad_mixed, value, preferred_element_type=jnp.float32)
    delta = jnp.sum(probs * grad_probs, axis=-1, keepdims=True)
    grad_scores = (probs * (grad_probs - delta)).astype(jnp.bfloat16)
    grad_query = (
        jnp.einsum("hqk,khd->qhd", grad_scores, key, preferred_element_type=jnp.float32) * factor
    )
    grad_key = (
        jnp.einsum("hqk,qhd->khd", grad_scores, query, preferred_element_type=jnp.float32) * factor
    )
    return jnp.stack([grad_query, grad_key, grad_value], axis=1)


def partner(me, step, count):
    other, bit = 0, 1
    while bit < count:
        other = other + bit * lax.rem(lax.div(me, bit) + lax.div(step, bit), 2)
        bit *= 2
    return other


def expert_kernel(
    count,
    experts,
    sent_rows,
    sent_grads,
    up_ref,
    down_ref,
    router_ref,
    back_ref,
    ret_ref,
    grad_up_ref,
    grad_down_ref,
    grad_router_ref,
    rows,
    grads,
    gated,
    act,
    grad_pre,
    logit_grads,
    out_grads,
    out_ret,
    turned,
    sems,
    local_sem,
):
    me = lax.axis_index("ep")
    block, width = rows.shape[1:]
    hidden = up_ref.shape[1]
    chunk = 512
    barrier = pltpu.get_barrier_semaphore()

    def greet(step, carry):
        pl.semaphore_signal(
            barrier, inc=1, device_id={"ep": partner(me, step, count)}, device_id_type=MESH
        )
        return carry

    lax.fori_loop(1, count, greet, 0)
    pl.semaphore_wait(barrier, count - 1)

    def remote(kind, source, target, step):
        return pltpu.make_async_remote_copy(
            src_ref=source,
            dst_ref=target,
            send_sem=sems.at[2 * kind, step],
            recv_sem=sems.at[2 * kind + 1, step],
            device_id={"ep": partner(me, step, count)},
            device_id_type=MESH,
        )

    def send_rows(step):
        return remote(0, sent_rows.at[partner(me, step, count)], rows.at[step], step)

    def send_grads(step):
        return remote(1, sent_grads.at[partner(me, step, count)], grads.at[step], step)

    def send_back(step):
        return remote(2, out_grads.at[step], back_ref.at[me], step)

    def send_ret(step):
        return remote(3, out_ret.at[step], ret_ref.at[me], step)

    own = [
        pltpu.make_async_copy(sent_rows.at[me], rows.at[0], local_sem.at[0]),
        pltpu.make_async_copy(sent_grads.at[me], grads.at[0], local_sem.at[1]),
        pltpu.make_async_copy(out_grads.at[0], back_ref.at[me], local_sem.at[2]),
        pltpu.make_async_copy(out_ret.at[0], ret_ref.at[me], local_sem.at[3]),
    ]
    own[0].start()
    own[1].start()

    def start(step, carry):
        send_rows(step).start()
        send_grads(step).start()
        return carry

    lax.fori_loop(1, count, start, 0)
    own[0].wait()
    own[1].wait()
    lanes = lax.broadcasted_iota(jnp.int32, (block, router_ref.shape[1]), 1)

    def one_block(step, carry):
        @pl.when(step > 0)
        def _():
            send_rows(step).wait_recv()
            send_grads(step).wait_recv()

        mine = rows[step]
        cotangent = grads[step].astype(jnp.float32)
        place = pl.ds(pl.multiple_of(step * block, 16), block)
        logits = jnp.dot(mine, router_ref[...], preferred_element_type=jnp.float32)
        logits = jnp.where(lanes < experts, logits, NEGATIVE)
        weights = jnp.exp(logits - jnp.max(logits, axis=1, keepdims=True))
        gate_all = weights / jnp.sum(weights, axis=1, keepdims=True)
        here = (lanes == me).astype(jnp.float32)
        gate = jnp.sum(gate_all * here, axis=1, keepdims=True)
        pair = (gate * cotangent).astype(jnp.bfloat16)
        gated[place, :] = pair
        ret = jnp.zeros((block, width), jnp.float32)
        back = jnp.zeros((block, width), jnp.float32)
        for first in range(0, hidden, chunk):
            span = slice(first, first + chunk)
            pre = jnp.dot(mine, up_ref[:, span], preferred_element_type=jnp.float32)
            cdf = 0.5 * (1.0 + lax.erf(pre * 0.7071067811865476))
            density = jnp.exp(-0.5 * pre * pre) * 0.3989422804014327
            low = (pre * cdf).astype(jnp.bfloat16)
            act[place, span] = low
            ret = ret + jnp.dot(low, down_ref[span, :], preferred_element_type=jnp.float32)
            grad_act = times_t(pair, down_ref[span, :])
            slope = (grad_act * (cdf + pre * density)).astype(jnp.bfloat16)
            grad_pre[place, span] = slope
            back = back + times_t(slope, up_ref[:, span])
        ret = ret.astype(jnp.bfloat16).astype(jnp.float32)
        out_ret[step] = (gate * ret).astype(jnp.bfloat16)
        gate_grad = jnp.sum(cotangent * ret, axis=1, keepdims=True)
        low_logits = (gate * gate_grad * (here - gate_all)).astype(jnp.bfloat16)
        logit_grads[place, :] = low_logits
        back = back + times_t(low_logits, router_ref[...])
        out_grads[step] = back.astype(jnp.bfloat16)

        @pl.when(step > 0)
        def _():
            send_back(step).start()

        @pl.when(step == 0)
        def _():
            own[2].start()

        return carry

    lax.fori_loop(0, count, one_block, 0)
    own[3].start()

    def start_ret(step, carry):
        send_ret(step).start()
        return carry

    lax.fori_loop(1, count, start_ret, 0)
    turned[...] = jnp.transpose(rows[...].reshape(count * block, width))
    grad_router_ref[...] = jnp.dot(
        turned[...], logit_grads[...], preferred_element_type=jnp.float32
    )

    def up_chunk(index, carry):
        span = pl.ds(pl.multiple_of(index * chunk, chunk), chunk)
        grad_up_ref[:, span] = jnp.dot(
            turned[...], grad_pre[:, span], preferred_element_type=jnp.float32
        ).astype(jnp.bfloat16)
        return carry

    lax.fori_loop(0, hidden // chunk, up_chunk, 0)
    turned[...] = jnp.transpose(gated[...])

    def down_chunk(index, carry):
        span = pl.ds(pl.multiple_of(index * chunk, chunk), chunk)
        part = jnp.dot(turned[...], act[:, span], preferred_element_type=jnp.float32)
        grad_down_ref[span, :] = jnp.transpose(part).astype(jnp.bfloat16)
        return carry

    lax.fori_loop(0, hidden // chunk, down_chunk, 0)

    def finish(step, carry):
        send_rows(step).wait_send()
        send_grads(step).wait_send()
        send_back(step).wait()
        send_ret(step).wait()
        return carry

    lax.fori_loop(1, count, finish, 0)
    own[2].wait()
    own[3].wait()


def column(values, lane):
    lanes = lax.broadcasted_iota(jnp.int32, values.shape, 1)
    return jnp.sum(jnp.where(lanes == lane, values, 0), axis=1, keepdims=True)


def core_peer(grp):
    return grp + 1 - 2 * lax.rem(grp, 2)


def x_peer(grp):
    return lax.rem(grp + 2, 4)


def flags(condition):
    return jnp.where(condition, 1.0, 0.0).astype(jnp.bfloat16)


def remote_copy(source, target, send_sem, recv_sem, device):
    return pltpu.make_async_remote_copy(
        src_ref=source,
        dst_ref=target,
        send_sem=send_sem,
        recv_sem=recv_sem,
        device_id=device,
        device_id_type=MESH,
    )


def expert_of(me, grp, count):
    half = count // 2
    other = lax.rem(lax.div(me, half) + lax.rem(grp, 2), 2)
    return lax.rem(me, half) + half * other


def seat(me, grp, step, count):
    half = count // 2
    core = lax.rem(lax.rem(grp, 2) + lax.div(step, half), 2)
    return {
        "grp": 2 * lax.div(grp, 2) + core,
        "ep": partner(me, lax.rem(step, half), count),
    }


def visit(index, count):
    return lax.div(index, 2) + (count // 2) * lax.rem(index, 2)


def greet_all(count, me, grp):
    barrier = pltpu.get_barrier_semaphore()
    half = count // 2

    def greet(step, carry):
        device = {"grp": grp, "ep": partner(me, step, count)}
        pl.semaphore_signal(barrier, inc=1, device_id=device, device_id_type=MESH)
        return carry

    lax.fori_loop(1, count, greet, 0)

    def greet_mate(step, carry):
        device = {"grp": core_peer(grp), "ep": partner(me, step, count)}
        pl.semaphore_signal(barrier, inc=1, device_id=device, device_id_type=MESH)
        return carry

    lax.fori_loop(0, half + 1, greet_mate, 0)
    pl.semaphore_signal(barrier, inc=1, device_id={"grp": x_peer(grp)}, device_id_type=MESH)
    pl.semaphore_wait(barrier, count + half + 1)


def pieces_of(layer_rows):
    def rows(chunk, side):
        size = layer_rows[chunk // PIECES] // (2 * PIECES)
        first = side * PIECES * size + (chunk % PIECES) * size
        return pl.ds(pl.multiple_of(first, size), size)

    return rows


def up_piece(piece, side, side_rows, columns):
    rows = pl.ds(pl.multiple_of(side * side_rows, side_rows), side_rows)
    return rows, pl.ds(piece * columns, columns)


def down_piece(piece, side, size):
    return pl.ds(pl.multiple_of(piece * 2 * size + side * size, size), size)


def seen(segment_row, live_row, segment_col):
    length = segment_row.shape[1]
    index = lax.broadcasted_iota(jnp.int32, (length, length), 0)
    other = lax.broadcasted_iota(jnp.int32, (length, length), 1)
    return (segment_col == segment_row) & ((live_row > 0) | (index == other))


def forward_kernel(
    count,
    capacity,
    tokens_in,
    segments,
    live,
    picks,
    ranks,
    out_grad_in,
    joint_shard,
    output_shard,
    gains_shard,
    router_shard,
    own_up,
    own_down,
    weights_out,
    joint_out,
    mixed_out,
    state_out,
    rows_out,
    logs_out,
    slots_out,
    router_out,
    grads,
    used_up,
    used_down,
    tokens,
    out_grad,
    weights,
    joint,
    mixed,
    state,
    sent_rows,
    logs,
    slots,
    own_grads,
    normed_two,
    int_columns,
    ep_sems,
    x_sems,
    core_sems,
    grad_sems,
    fetch_sems,
    local_sems,
    move_sems,
):
    me, grp = lax.axis_index("ep"), lax.axis_index("grp")
    expert = expert_of(me, grp, count)
    core, side_x = lax.rem(grp, 2), lax.div(grp, 2)
    half_ep = count // 2
    row_count, width = tokens.shape
    sequences, length = segments.shape
    block = sent_rows.shape[1]
    moves = {
        name: pltpu.make_async_copy(source, target, move_sems.at[place])
        for place, (name, source, target) in enumerate(
            (
                ("out_grad", out_grad_in, out_grad),
                ("tokens", tokens_in, tokens),
                ("slots", slots, slots_out),
                ("weights", weights, weights_out),
                ("joint", joint, joint_out),
                ("mixed", mixed, mixed_out),
                ("state", state, state_out),
                ("logs", logs, logs_out),
                ("rows", sent_rows, rows_out),
            )
        )
    }
    moves["out_grad"].start()
    moves["tokens"].start()
    joint_width = joint.shape[1]
    head_size = width // HEADS
    factor = head_size ** (-0.5)
    mate, across = core_peer(grp), x_peer(grp)
    greet_all(count, me, grp)

    def shard(owner_grp, owner):
        return weights.at[owner_grp * count + owner]

    def to_ep(step):
        place = shard(grp, me)
        other = partner(me, step, count)
        return remote_copy(place, place, ep_sems.at[0, step], ep_sems.at[1, step], {"ep": other})

    def relay(step):
        place = shard(grp, partner(me, half_ep, count))
        sems = ep_sems.at[0, half_ep + step], ep_sems.at[1, half_ep + step]
        return remote_copy(place, place, *sems, {"ep": partner(me, step, count)})

    def to_x(step):
        place = shard(grp, partner(me, step, count))
        return remote_copy(place, place, x_sems.at[0, step], x_sems.at[1, step], {"grp": across})

    def to_core(owner_grp, part, step):
        place = shard(owner_grp, partner(me, step, count))
        sems = core_sems.at[0, part, step], core_sems.at[1, part, step]
        return remote_copy(place, place, *sems, {"grp": mate})

    def send_grads(step):
        return remote_copy(
            own_grads.at[step],
            grads.at[step],
            grad_sems.at[0, step],
            grad_sems.at[1, step],
            seat(me, grp, step, count),
        )

    layers = ((own_up, used_up), (own_down, used_down))
    rows_at = pieces_of((own_up.shape[0], own_down.shape[0]))

    def fetch(chunk):
        source, target = layers[chunk // PIECES]
        place = rows_at(chunk, side_x)
        sems = fetch_sems.at[0, chunk], fetch_sems.at[1, chunk]
        device = {"grp": mate, "ep": partner(me, half_ep, count)}
        return remote_copy(source.at[place], target.at[place], *sems, device)

    def share_fetch(chunk):
        place = layers[chunk // PIECES][1].at[rows_at(chunk, side_x)]
        sems = fetch_sems.at[2, chunk], fetch_sems.at[3, chunk]
        return remote_copy(place, place, *sems, {"grp": across})

    far_steps = [step for step in range(count) if step % half_ep >= half_ep // 2]

    def advance_grads(index):
        send_grads(far_steps[index]).wait_send()
        if index + 1 < len(far_steps):
            send_grads(far_steps[index + 1]).start()

    def advance(chunk):
        @pl.when(core == 0)
        def _():
            fetch(chunk).wait_send()
            if chunk + 2 < CHUNKS:
                fetch(chunk + 2).start()

        @pl.when(core == 1)
        def _():
            fetch(chunk).wait_recv()
            share_fetch(chunk).start()

    mine = grp * count + me
    fill = [
        pltpu.make_async_copy(
            joint_shard, weights.at[mine, :, pl.ds(0, joint_width)], local_sems.at[0]
        ),
        pltpu.make_async_copy(
            output_shard, weights.at[mine, :, pl.ds(joint_width, width)], local_sems.at[1]
        ),
    ]
    for copy in fill:
        copy.start()
    shard_rows = weights.shape[1]
    stacked = jnp.concatenate(
        [
            router_shard[...].astype(jnp.float32),
            gains_shard[...].astype(jnp.float32),
            jnp.zeros((16 - count - 2, shard_rows), jnp.float32),
        ],
        axis=0,
    ).astype(jnp.bfloat16)
    tile = (16, 128)
    diagonal = flags(
        lax.broadcasted_iota(jnp.int32, tile, 0) == lax.broadcasted_iota(jnp.int32, tile, 1)
    )
    weights[mine, :, joint_width + width :] = outer(stacked, diagonal).astype(jnp.bfloat16)
    for copy in fill:
        copy.wait()

    def first_hop(step, carry):
        to_ep(step).start()
        return carry

    lax.fori_loop(1, half_ep + 1, first_hop, 0)
    to_x(0).start()
    to_core(grp, 0, 0).start()

    @pl.when(core == 0)
    def _():
        fetch(0).start()
        fetch(1).start()

    ints = jnp.concatenate([segments[...], live[...]], axis=0).astype(jnp.float32)
    turned = jnp.transpose(ints)
    int_columns[...] = turned.astype(jnp.int32)
    live_col = jnp.concatenate(
        [turned[:, sequences + i : sequences + i + 1] for i in range(sequences)], axis=0
    )
    rank_row = ranks[...].astype(jnp.float32)
    lines = jnp.concatenate(
        [rank_row, picks[...].astype(jnp.float32), jnp.zeros((5, row_count), jnp.float32)], axis=0
    )
    token_columns = jnp.transpose(lines)
    rank_col = token_columns[:, 0:1]
    earlier = flags(rank_row < rank_col)
    first = token_columns[:, 1:2].astype(jnp.int32)
    second = token_columns[:, 2:3].astype(jnp.int32)
    lanes = lax.broadcasted_iota(jnp.int32, (row_count, 128), 1)
    one = jnp.where(lanes == first, 1.0, 0.0)
    two = jnp.where(lanes == second + count, 1.0, 0.0)
    counts = jnp.dot(
        earlier, ((one + two) * live_col).astype(jnp.bfloat16), preferred_element_type=jnp.float32
    )
    ahead = jnp.sum(jnp.where(lanes == first + count, live_col, 0.0), axis=0, keepdims=True)
    place_one = jnp.sum(counts * one, axis=1, keepdims=True)
    place_two = jnp.sum((counts + ahead) * two, axis=1, keepdims=True)
    nowhere = 1.0 * count * block
    slot_one = jnp.where(
        (live_col > 0) & (place_one < capacity),
        first.astype(jnp.float32) * block + place_one,
        nowhere,
    )
    slot_two = jnp.where(
        (live_col > 0) & (place_two < capacity),
        second.astype(jnp.float32) * block + place_two,
        nowhere,
    )
    both = jnp.where(lanes == 0, slot_one, jnp.where(lanes == 1, slot_two, nowhere))
    slots[...] = both.astype(jnp.int32)
    moves["slots"].start()
    moves["out_grad"].wait()
    slot_rows = jnp.transpose(both)[0:8].astype(jnp.int32)
    row_one, row_two = slot_rows[0:1], slot_rows[1:2]

    def rows_of(number, values):
        index = lax.broadcasted_iota(jnp.int32, (block, row_count), 0) + number * block
        chosen = flags((index == row_one) | (index == row_two))
        return jnp.dot(chosen, values[...], preferred_element_type=jnp.float32).astype(jnp.bfloat16)

    def spread_grads(index, carry):
        step = visit(index, count)
        own_grads[step] = rows_of(partner(expert, step, count), out_grad)

        @pl.when((step > 0) & (lax.rem(step, half_ep) < half_ep // 2))
        def _():
            send_grads(step).start()

        return carry

    lax.fori_loop(0, count, spread_grads, 0)
    send_grads(far_steps[0]).start()
    keep = pltpu.make_async_copy(own_grads.at[0], grads.at[0], local_sems.at[3])
    keep.start()

    to_ep(half_ep).wait_recv()

    def pass_far(step, carry):
        relay(step).start()
        return carry

    lax.fori_loop(1, half_ep, pass_far, 0)
    to_x(half_ep).start()
    to_core(grp, 0, half_ep).start()

    def pass_on(step, carry):
        @pl.when(step != half_ep)
        def _():
            to_ep(step).wait_recv()
            to_x(step).start()
            to_core(grp, 0, step).start()

        return carry

    lax.fori_loop(1, count, pass_on, 0)

    def pass_further(step, carry):
        to_x(step).wait_recv()
        to_core(across, 1, step).start()
        return carry

    lax.fori_loop(0, count, pass_further, 0)

    def arrive(step, carry):
        to_core(mate, 0, step).wait_recv()
        to_core(x_peer(mate), 1, step).wait_recv()
        return carry

    lax.fori_loop(0, count, arrive, 0)
    advance(0)
    advance_grads(0)

    moves["weights"].start()
    moves["tokens"].wait()
    devices = weights.shape[0]
    total = devices * weights.shape[1]
    pack = weights[:, :, joint_width + width :].reshape(total, 128)
    router_out[...] = pack
    gains = jnp.transpose(pack.astype(jnp.float32))
    gain_one = gains[count : count + 1]
    gain_two = gains[count + 1 : count + 2]
    half = lax.broadcasted_iota(jnp.int32, (length, 128), 1) < head_size
    halves = (flags(half), flags(jnp.logical_not(half)))

    def attend(number, carry):
        rows = pl.ds(pl.multiple_of(number * length, length), length)
        values = tokens[rows, :].astype(jnp.float32)
        normed = normalize(values, gain_one)[0].astype(jnp.bfloat16)
        joint[rows, :] = jnp.dot(
            normed,
            weights[:, :, :joint_width].reshape(total, joint_width),
            preferred_element_type=jnp.float32,
        ).astype(jnp.bfloat16)
        allowed = seen(
            segments[pl.ds(number, 1), :], live[pl.ds(number, 1), :], column(int_columns[...], number)
        )
        log_all = jnp.zeros((length, 128), jnp.float32)
        log_lanes = lax.broadcasted_iota(jnp.int32, (length, 128), 1)
        for pair in range(HEADS // 2):
            at = pair * 128
            query = joint[rows, at : at + 128]
            key = joint[rows, width + at : width + at + 128]
            value = joint[rows, 2 * width + at : 2 * width + at + 128]
            results = []
            for side in range(2):
                scores = times_t(query * halves[side], key) * factor
                masked = jnp.where(allowed, scores, NEGATIVE)
                top = jnp.max(masked, axis=-1, keepdims=True)
                powers = jnp.exp(masked - top)
                added = jnp.sum(powers, axis=-1, keepdims=True)
                probs = (powers * (1.0 / added)).astype(jnp.bfloat16)
                results.append(jnp.dot(probs, value, preferred_element_type=jnp.float32))
                log_all = jnp.where(log_lanes == 2 * pair + side, top + jnp.log(added), log_all)
            mixed[rows, at : at + 128] = jnp.where(half, results[0], results[1]).astype(jnp.bfloat16)
        logs[rows, :] = log_all
        after = values + jnp.dot(
            mixed[rows, :],
            weights[:, :, joint_width : joint_width + width].reshape(total, width),
            preferred_element_type=jnp.float32,
        )
        state[rows, :] = after
        normed_two[rows, :] = normalize(after, gain_two)[0].astype(jnp.bfloat16)
        for place in range(sequences):

            @pl.when(number == place)
            def _(place=place):
                advance(place + 1)
                if place % 2 == 1:
                    advance_grads((place + 1) // 2)

        return carry

    lax.fori_loop(0, sequences, attend, 0)
    for name in ("joint", "mixed", "state", "logs"):
        moves[name].start()

    def spread_rows(number, carry):
        sent_rows[number] = rows_of(number, normed_two)
        return carry

    lax.fori_loop(0, count, spread_rows, 0)
    moves["rows"].start()

    for chunk in range(sequences + 1, CHUNKS):
        advance(chunk)
    advance_grads(3)

    @pl.when(core == 1)
    def _():
        for chunk in range(CHUNKS):
            share_fetch(chunk).wait()

    for name in ("slots", "weights", "joint", "mixed", "state", "logs", "rows"):
        moves[name].wait()
    keep.wait()
    to_x(0).wait_send()
    to_core(grp, 0, 0).wait_send()
    to_core(across, 1, 0).wait_send()

    def finish(step, carry):
        to_ep(step).wait_send()
        to_x(step).wait_send()
        to_core(grp, 0, step).wait_send()
        to_core(across, 1, step).wait_send()
        send_grads(step).wait_recv()

        @pl.when(lax.rem(step, half_ep) < half_ep // 2)
        def _():
            send_grads(step).wait_send()

        return carry

    lax.fori_loop(1, count, finish, 0)


def forward(
    count,
    capacity,
    block,
    tokens,
    segments,
    live,
    picks,
    ranks,
    out_grad,
    joint,
    output,
    gains,
    router,
    up,
    down,
):
    row_count, width = tokens.shape
    devices = width // joint.shape[0]
    all_width = joint.shape[1] + width + 128
    hbm = pl.BlockSpec(memory_space=pltpu.HBM)
    vmem = pl.BlockSpec(memory_space=pltpu.VMEM)
    low = jnp.bfloat16
    return pl.pallas_call(
        functools.partial(forward_kernel, count, capacity),
        out_shape=(
            jax.ShapeDtypeStruct((devices, joint.shape[0], all_width), low),
            jax.ShapeDtypeStruct((row_count, joint.shape[1]), low),
            jax.ShapeDtypeStruct((row_count, width), low),
            jax.ShapeDtypeStruct((row_count, width), jnp.float32),
            jax.ShapeDtypeStruct((count, block, width), low),
            jax.ShapeDtypeStruct((row_count, 128), jnp.float32),
            jax.ShapeDtypeStruct((row_count, 128), jnp.int32),
            jax.ShapeDtypeStruct((width, 128), low),
            jax.ShapeDtypeStruct((count, block, width), low),
            jax.ShapeDtypeStruct(up.shape, low),
            jax.ShapeDtypeStruct(down.shape, low),
        ),
        in_specs=[hbm] + [vmem] * 4 + [hbm] * 3 + [vmem] * 2 + [hbm] * 2,
        out_specs=(hbm,) * 7 + (vmem,) + (hbm,) * 3,
        scratch_shapes=[
            pltpu.VMEM(tokens.shape, low),
            pltpu.VMEM(out_grad.shape, low),
            pltpu.VMEM((devices, joint.shape[0], all_width), low),
            pltpu.VMEM((row_count, joint.shape[1]), low),
            pltpu.VMEM((row_count, width), low),
            pltpu.VMEM((row_count, width), jnp.float32),
            pltpu.VMEM((count, block, width), low),
            pltpu.VMEM((row_count, 128), jnp.float32),
            pltpu.VMEM((row_count, 128), jnp.int32),
            pltpu.VMEM((count, block, width), low),
            pltpu.VMEM((row_count, width), low),
            pltpu.VMEM((segments.shape[1], 2 * segments.shape[0]), jnp.int32),
            pltpu.SemaphoreType.DMA((2, count)),
            pltpu.SemaphoreType.DMA((2, count)),
            pltpu.SemaphoreType.DMA((2, 2, count)),
            pltpu.SemaphoreType.DMA((2, count)),
            pltpu.SemaphoreType.DMA((4, CHUNKS)),
            pltpu.SemaphoreType.DMA((4,)),
            pltpu.SemaphoreType.DMA((9,)),
        ],
        compiler_params=pltpu.CompilerParams(
            collective_id=2, has_side_effects=True, vmem_limit_bytes=63 * MIB
        ),
    )(
        tokens,
        segments,
        live,
        picks,
        ranks,
        out_grad,
        joint,
        output,
        gains,
        router,
        up,
        down,
    )


def middle_kernel(
    count,
    sent_rows,
    grads_in,
    own_up,
    own_down,
    used_up,
    used_down,
    router_ref,
    back_ref,
    out_ret,
    part_up,
    part_down,
    early_up,
    early_down,
    grad_router_ref,
    grads,
    rows,
    gated,
    act,
    grad_pre,
    logit_grads,
    out_grads,
    turned,
    turned_gated,
    up_ref,
    down_ref,
    ret_sums,
    back_sums,
    x_up,
    x_down,
    sems,
    x_sems,
    local_sem,
):
    me, grp = lax.axis_index("ep"), lax.axis_index("grp")
    expert = expert_of(me, grp, count)
    block, width = rows.shape[1:]
    hidden = up_ref.shape[1]
    chunk = 512

    bring = pltpu.make_async_copy(grads_in, grads, local_sem.at[4])
    bring.start()

    def load(up, down):
        return (
            pltpu.make_async_copy(up, up_ref, local_sem.at[2]),
            pltpu.make_async_copy(down, down_ref, local_sem.at[3]),
        )

    @pl.when(lax.rem(grp, 2) == 0)
    def _():
        for copy in load(own_up, own_down):
            copy.start()

    @pl.when(lax.rem(grp, 2) == 1)
    def _():
        for copy in load(used_up, used_down):
            copy.start()

    greet_all(count, me, grp)

    def send_rows(step):
        other = partner(expert, step, count)
        there = seat(me, grp, step, count)
        return remote_copy(
            sent_rows.at[other], rows.at[step], sems.at[0, step], sems.at[1, step], there
        )

    def send_back(step):
        there = seat(me, grp, step, count)
        return remote_copy(
            out_grads.at[step], back_ref.at[expert], sems.at[2, step], sems.at[3, step], there
        )

    own = [
        pltpu.make_async_copy(sent_rows.at[expert], rows.at[0], local_sem.at[0]),
        pltpu.make_async_copy(out_grads.at[0], back_ref.at[expert], local_sem.at[1]),
    ]
    own[0].start()

    def start(index, carry):
        send_rows(visit(index, count)).start()
        return carry

    lax.fori_loop(1, count, start, 0)
    own[0].wait()
    for copy in load(used_up, used_down):
        copy.wait()
    bring.wait()
    lanes = lax.broadcasted_iota(jnp.int32, (block, router_ref.shape[1]), 1)

    across, side_x = x_peer(grp), lax.div(grp, 2)
    part_hidden = hidden // 2
    early = len(EARLY)

    def over_x(index):
        layer, piece = EARLY[index]
        sems = x_sems.at[0, index], x_sems.at[1, index]
        if layer == 0:
            source = part_up.at[up_piece(piece, 1 - side_x, width // 2, chunk)]
            target = x_up.at[:, pl.ds(piece * chunk, chunk)]
        else:
            source = part_down.at[down_piece(piece, 1 - side_x, chunk // 2)]
            target = x_down.at[pl.ds(piece * chunk // 2, chunk // 2)]
        return remote_copy(source, target, *sems, {"grp": across})

    def gates_of(values):
        logits = jnp.dot(values, router_ref[...], preferred_element_type=jnp.float32)
        logits = jnp.where(lanes < count, logits, NEGATIVE)
        weights = jnp.exp(logits - jnp.max(logits, axis=1, keepdims=True))
        return weights / jnp.sum(weights, axis=1, keepdims=True)

    here = (lanes == expert).astype(jnp.float32)

    def through(step, mine, pair, base):
        place = pl.ds(pl.multiple_of(step * block, 16), block)
        ret = jnp.zeros((block, width), jnp.float32)
        back = jnp.zeros((block, width), jnp.float32)
        for first in range(0, part_hidden, chunk):
            span = slice(base + first, base + first + chunk)
            kept = slice(first, first + chunk)
            pre = jnp.dot(mine, up_ref[:, span], preferred_element_type=jnp.float32)
            cdf = 0.5 * (1.0 + lax.erf(pre * 0.7071067811865476))
            density = jnp.exp(-0.5 * pre * pre) * 0.3989422804014327
            low = (pre * cdf).astype(jnp.bfloat16)
            act[place, kept] = low
            ret = ret + jnp.dot(low, down_ref[span, :], preferred_element_type=jnp.float32)
            grad_act = times_t(pair, down_ref[span, :])
            slope = (grad_act * (cdf + pre * density)).astype(jnp.bfloat16)
            grad_pre[place, kept] = slope
            back = back + times_t(slope, up_ref[:, span])
        return ret, back

    def first_half(index, carry):
        step = visit(index, count)

        @pl.when(step > 0)
        def _():
            send_rows(step).wait_recv()

        mine = rows[step]
        gate = jnp.sum(gates_of(mine) * here, axis=1, keepdims=True)
        pair = (gate * grads[step].astype(jnp.float32)).astype(jnp.bfloat16)
        gated[pl.ds(pl.multiple_of(step * block, 16), block), :] = pair
        ret_sums[step], back_sums[step] = through(step, mine, pair, 0)
        return carry

    def second_half(index, carry):
        step = visit(index, count)
        mine = rows[step]
        cotangent = grads[step].astype(jnp.float32)
        place = pl.ds(pl.multiple_of(step * block, 16), block)
        gate_all = gates_of(mine)
        gate = jnp.sum(gate_all * here, axis=1, keepdims=True)
        ret, back = through(step, mine, gated[place, :], part_hidden)
        ret = (ret + ret_sums[step]).astype(jnp.bfloat16).astype(jnp.float32)
        out_ret[step] = (gate * ret).astype(jnp.bfloat16)
        gate_grad = jnp.sum(cotangent * ret, axis=1, keepdims=True)
        low_logits = (gate * gate_grad * (here - gate_all)).astype(jnp.bfloat16)
        logit_grads[place, :] = low_logits
        back = back + back_sums[step] + times_t(low_logits, router_ref[...])
        out_grads[step] = back.astype(jnp.bfloat16)

        @pl.when(step > 0)
        def _():
            send_back(step).start()

        @pl.when(step == 0)
        def _():
            own[1].start()

        return carry

    def layer_sums(base):
        def up_chunk(index, carry):
            span = pl.ds(pl.multiple_of(index * chunk, chunk), chunk)
            part_up[:, pl.ds(pl.multiple_of(base + index * chunk, chunk), chunk)] = jnp.dot(
                turned[...], grad_pre[:, span], preferred_element_type=jnp.float32
            ).astype(jnp.bfloat16)
            return carry

        def down_chunk(index, carry):
            span = pl.ds(pl.multiple_of(index * chunk, chunk), chunk)
            part = jnp.dot(turned_gated[...], act[:, span], preferred_element_type=jnp.float32)
            part_down[pl.ds(pl.multiple_of(base + index * chunk, chunk), chunk), :] = jnp.transpose(
                part
            ).astype(jnp.bfloat16)
            return carry

        lax.fori_loop(0, part_hidden // chunk, up_chunk, 0)
        lax.fori_loop(0, part_hidden // chunk, down_chunk, 0)

    lax.fori_loop(0, count, first_half, 0)
    turned[...] = jnp.transpose(rows[...].reshape(count * block, width))
    turned_gated[...] = jnp.transpose(gated[...])
    layer_sums(0)
    for index in range(early):
        over_x(index).start()
    lax.fori_loop(0, count, second_half, 0)
    layer_sums(part_hidden)
    grad_router_ref[...] = jnp.dot(
        turned[...], logit_grads[...], preferred_element_type=jnp.float32
    )
    for index in range(early):
        layer, piece = EARLY[index]
        over_x(index).wait_recv()
        if layer == 0:
            kept = part_up[up_piece(piece, side_x, width // 2, chunk)]
            span = slice(piece * chunk, (piece + 1) * chunk)
            added = kept.astype(jnp.float32) + x_up[:, span].astype(jnp.float32)
            early_up[:, span] = added.astype(jnp.bfloat16)
        else:
            kept = part_down[down_piece(piece, side_x, chunk // 2), :]
            span = slice(piece * chunk // 2, (piece + 1) * chunk // 2)
            added = kept.astype(jnp.float32) + x_down[span, :].astype(jnp.float32)
            early_down[span, :] = added.astype(jnp.bfloat16)
    for index in range(early):
        over_x(index).wait_send()

    def finish(step, carry):
        send_rows(step).wait_send()
        send_back(step).wait()
        return carry

    lax.fori_loop(1, count, finish, 0)
    own[1].wait()


def middle(sent_rows, grads, up, down, used_up, used_down, router):
    count, block, width = sent_rows.shape
    hidden = up.shape[1]
    any_space = pl.BlockSpec(memory_space=pl.ANY)
    hbm = pl.BlockSpec(memory_space=pltpu.HBM)
    vmem = pl.BlockSpec(memory_space=pltpu.VMEM)
    low = jnp.bfloat16
    slots = count * block
    return pl.pallas_call(
        functools.partial(middle_kernel, count),
        out_shape=(
            jax.ShapeDtypeStruct((count, block, width), low),
            jax.ShapeDtypeStruct((count, block, width), low),
            jax.ShapeDtypeStruct((width, hidden), low),
            jax.ShapeDtypeStruct((hidden, width), low),
            jax.ShapeDtypeStruct((width // 2, hidden // 2), low),
            jax.ShapeDtypeStruct((hidden // 4, width), low),
            jax.ShapeDtypeStruct((width, 128), jnp.float32),
        ),
        in_specs=[hbm] * 6 + [vmem],
        out_specs=(any_space,) + (vmem,) * 6,
        scratch_shapes=[
            pltpu.VMEM((count, block, width), low),
            pltpu.VMEM((count, block, width), low),
            pltpu.VMEM((slots, width), low),
            pltpu.VMEM((slots, hidden // 2), low),
            pltpu.VMEM((slots, hidden // 2), low),
            pltpu.VMEM((slots, 128), low),
            pltpu.VMEM((count, block, width), low),
            pltpu.VMEM((width, slots), low),
            pltpu.VMEM((width, slots), low),
            pltpu.VMEM(up.shape, low),
            pltpu.VMEM(down.shape, low),
            pltpu.VMEM((count, block, width), jnp.float32),
            pltpu.VMEM((count, block, width), jnp.float32),
            pltpu.VMEM((width // 2, hidden // 2), low),
            pltpu.VMEM((hidden // 4, width), low),
            pltpu.SemaphoreType.DMA((4, count)),
            pltpu.SemaphoreType.DMA((2, len(EARLY))),
            pltpu.SemaphoreType.DMA((5,)),
        ],
        compiler_params=pltpu.CompilerParams(
            collective_id=3, has_side_effects=True, vmem_limit_bytes=63 * MIB
        ),
        cost_estimate=pl.CostEstimate(
            flops=12 * slots * width * hidden, bytes_accessed=16 * MIB, transcendentals=0
        ),
    )(sent_rows, grads, up, down, used_up, used_down, router)


def backward_kernel(
    count,
    tokens_in,
    segments,
    live,
    out_grad_in,
    weights_in,
    joint_in,
    mixed_in,
    state_in,
    logs_in,
    slots_in,
    back_in,
    out_ret,
    grad_router,
    part_up_in,
    part_down_in,
    early_up_in,
    early_down_in,
    output,
    tokens_grad,
    joint_share,
    output_share,
    pack_share,
    sum_up,
    sum_down,
    tokens,
    out_grad,
    weights,
    joint,
    mixed,
    state,
    logs,
    slots,
    back,
    part_up,
    part_down,
    early_up,
    early_down,
    returned,
    grad_joint,
    normed_all,
    branch_all,
    mixed_grads,
    hidden_pairs,
    part,
    mate_part,
    pair_part,
    x_part,
    far_part,
    ep_part,
    turned,
    x_up,
    x_down,
    half_up,
    half_down,
    far_up,
    far_down,
    ret_sems,
    mate_sems,
    x_sems,
    ep_sems,
    sum_sems,
    local_sems,
    bring_sems,
):
    bring = [
        pltpu.make_async_copy(source, target, bring_sems.at[place])
        for place, (source, target) in enumerate(
            (
                (weights_in, weights),
                (slots_in, slots),
                (back_in, back),
                (state_in, state),
                (out_grad_in, out_grad),
                (tokens_in, tokens),
                (mixed_in, mixed),
                (joint_in, joint),
                (logs_in, logs),
                (part_up_in, part_up),
                (part_down_in, part_down),
                (early_up_in, early_up),
                (early_down_in, early_down),
            )
        )
    ]
    for copy in bring:
        copy.start()
    me, grp = lax.axis_index("ep"), lax.axis_index("grp")
    row_count, width = tokens.shape
    sequences, length = segments.shape
    block = back.shape[1]
    slot_count = count * block
    joint_width = joint.shape[1]
    head_size = width // HEADS
    factor = head_size ** (-0.5)
    mate, across = core_peer(grp), x_peer(grp)
    core, side_x = lax.rem(grp, 2), lax.div(grp, 2)
    devices = weights.shape[0]
    total = devices * weights.shape[1]
    expert = expert_of(me, grp, count)
    greet_all(count, me, grp)

    parts = EARLY + LATE
    early = len(EARLY)
    rows_up, size_up = part_up.shape[0] // 2, part_up.shape[1] // PIECES
    size_down = part_down.shape[0] // (2 * PIECES)

    def whole(index, arrays, side):
        layer, piece = parts[index]
        if layer == 0:
            return arrays[0].at[up_piece(piece, side, rows_up, size_up)]
        return arrays[1].at[down_piece(piece, side, size_down)]

    def narrow(index, arrays):
        layer, piece = parts[index]
        if layer == 0:
            return arrays[0].at[:, pl.ds((piece % 2) * size_up, size_up)]
        return arrays[1].at[pl.ds((piece % 2) * size_down, size_down)]

    def summed_x(index):
        return narrow(index, (early_up, early_down) if index < early else (half_up, half_down))

    def from_foreign(index):
        return narrow(index, (far_up.at[index // early], far_down.at[index // early]))

    def over_x(index):
        sems = sum_sems.at[0, index], sum_sems.at[1, index]
        source = whole(index, (part_up_in, part_down_in), 1 - side_x)
        return remote_copy(source, narrow(index, (x_up, x_down)), *sems, {"grp": across})

    def go_home(index):
        sems = sum_sems.at[2, index], sum_sems.at[3, index]
        device = {"grp": mate, "ep": partner(me, count // 2, count)}
        source = narrow(index, (early_up_in, early_down_in)) if index < early else summed_x(index)
        return remote_copy(source, from_foreign(index), *sems, device)

    def spread_x(index):
        place = whole(index, (sum_up, sum_down), side_x)
        sems = sum_sems.at[4, index], sum_sems.at[5, index]
        return remote_copy(place, place, *sems, {"grp": across})

    def spread_core(index, side, first):
        place = whole(index, (sum_up, sum_down), side)
        sems = sum_sems.at[first, index], sum_sems.at[first + 1, index]
        return remote_copy(place, place, *sems, {"grp": mate})

    def own_half(index):
        return spread_core(index, side_x, 6)

    def other_half(index):
        return spread_core(index, 1 - side_x, 8)

    def leave(index):
        @pl.when(core == 1)
        def _():
            go_home(index).start()

    def add_x(index):
        over_x(index).wait_recv()
        kept = whole(index, (part_up, part_down), side_x)[...].astype(jnp.float32)
        landed = narrow(index, (x_up, x_down))[...].astype(jnp.float32)
        summed_x(index)[...] = (kept + landed).astype(jnp.bfloat16)
        if index + 2 < len(parts):
            over_x(index + 2).start()
        leave(index)

    def add_home(index):
        @pl.when(core == 0)
        def _():
            go_home(index).wait_recv()
            near = summed_x(index)[...].astype(jnp.float32)
            foreign = from_foreign(index)[...].astype(jnp.float32)
            whole(index, (sum_up, sum_down), side_x)[...] = (near + foreign).astype(jnp.bfloat16)
            spread_x(index).start()
            own_half(index).start()

    def pass_half(index):
        @pl.when(core == 0)
        def _():
            spread_x(index).wait_recv()
            other_half(index).start()

    for index in range(early):
        leave(index)
    over_x(early).start()
    over_x(early + 1).start()

    def send_ret(step):
        return remote_copy(
            out_ret.at[step],
            returned.at[expert],
            ret_sems.at[0, step],
            ret_sems.at[1, step],
            seat(me, grp, step, count),
        )

    keep = pltpu.make_async_copy(out_ret.at[0], returned.at[expert], local_sems.at[0])
    keep.start()

    def start(step, carry):
        send_ret(step).start()
        return carry

    lax.fori_loop(1, count, start, 0)
    pairs = HEADS // 2
    columns = [(pair * 384, 384) for pair in range(pairs)]
    columns += [(joint_width, width), (joint_width + width, 128)]
    for copy in bring[:6]:
        copy.wait()
    pack = weights[:, :, joint_width + width :].reshape(total, 128)
    gains = jnp.transpose(pack.astype(jnp.float32))
    gain_one = gains[count : count + 1]
    gain_two = gains[count + 1 : count + 2]
    half = lax.broadcasted_iota(jnp.int32, (length, 128), 1) < head_size
    halves = (flags(half), flags(jnp.logical_not(half)))
    ints = jnp.transpose(segments[...].astype(jnp.float32)).astype(jnp.int32)

    def chosen_of(rows):
        index = lax.broadcasted_iota(jnp.int32, (length, slot_count), 1)
        pair = slots[rows, :]
        return flags((index == pair[:, 0:1]) | (index == pair[:, 1:2]))

    def to_mate(chunk, which):
        first, size = columns[chunk]
        span = pl.ds(first, size)
        return remote_copy(
            part.at[pl.ds((2 * which + 1 - core) * count, count), :, span],
            mate_part.at[which, :, :, span],
            mate_sems.at[0, chunk, which],
            mate_sems.at[1, chunk, which],
            {"grp": mate},
        )

    def to_x(chunk):
        first, size = columns[chunk]
        span = pl.ds(first, size)
        sems = x_sems.at[0, chunk], x_sems.at[1, chunk]
        source = pair_part.at[1 - side_x, :, :, span]
        return remote_copy(source, x_part.at[:, :, span], *sems, {"grp": across})

    def to_ep(chunk, step):
        first, size = columns[chunk]
        span = pl.ds(first, size)
        other = partner(me, step, count)
        return remote_copy(
            far_part.at[other, :, span],
            ep_part.at[step, :, span],
            ep_sems.at[0, chunk, step],
            ep_sems.at[1, chunk, step],
            {"ep": other},
        )

    def sum_core(chunk):
        first, size = columns[chunk]
        span = slice(first, first + size)
        for which in range(2):
            to_mate(chunk, which).wait_recv()
            owner = 2 * which + core
            pair_part[which, :, :, span] = (
                part[pl.ds(owner * count, count), :, span].astype(jnp.float32)
                + mate_part[which, :, :, span].astype(jnp.float32)
            ).astype(jnp.bfloat16)
        to_x(chunk).start()

    def sum_x(chunk):
        first, size = columns[chunk]
        span = slice(first, first + size)
        to_x(chunk).wait_recv()
        far_part[:, :, span] = (
            pair_part[side_x, :, :, span].astype(jnp.float32) + x_part[:, :, span].astype(jnp.float32)
        ).astype(jnp.bfloat16)

        def start(step, carry):
            to_ep(chunk, step).start()
            return carry

        lax.fori_loop(1, count, start, 0)

    def sum_ep(chunk):
        first, size = columns[chunk]
        span = slice(first, first + size)

        def add(step, added):
            to_ep(chunk, step).wait_recv()
            return added + ep_part[step, :, span].astype(jnp.float32)

        share = lax.fori_loop(1, count, add, far_part[me, :, span].astype(jnp.float32))
        if chunk < pairs:
            for third in range(3):
                at = third * width + chunk * 128
                joint_share[:, at : at + 128] = share[:, third * 128 : third * 128 + 128]
        elif chunk == pairs:
            output_share[...] = share
        else:
            pack_share[...] = share

    shape = (devices, total // devices)

    def lower_part(number, carry):
        rows = pl.ds(pl.multiple_of(number * length, length), length)
        grad_normed_two = jnp.dot(
            chosen_of(rows),
            back[...].reshape(slot_count, width),
            preferred_element_type=jnp.float32,
        )
        _, unit, inverse = normalize(state[rows, :], gain_two)
        inner, share = normalize_back(grad_normed_two, gain_two, unit, inverse)
        grad_state = out_grad[rows, :].astype(jnp.float32) + inner
        tokens_grad[rows, :] = grad_state
        branch = grad_state.astype(jnp.bfloat16)
        branch_all[rows, :] = branch
        mixed_grads[rows, :] = times_t(
            branch, weights[:, :, joint_width : joint_width + width].reshape(total, width)
        ).astype(jnp.bfloat16)
        allowed = seen(segments[pl.ds(number, 1), :], live[pl.ds(number, 1), :], column(ints, number))
        hidden_pairs[rows, :] = jnp.where(allowed, 0.0, NEGATIVE)
        normed = normalize(tokens[rows, :].astype(jnp.float32), gain_one)[0]
        normed_all[rows, :] = normed.astype(jnp.bfloat16)
        return carry + share[None, :]

    nothing = jnp.zeros((1, width), jnp.float32)
    grad_two = lax.fori_loop(0, sequences, lower_part, nothing)
    for copy in bring[6:]:
        copy.wait()
    turned[...] = jnp.transpose(mixed[...])
    first, size = columns[pairs]
    part[:, :, first : first + size] = (
        jnp.dot(turned[...], branch_all[...], preferred_element_type=jnp.float32)
        .astype(jnp.bfloat16)
        .reshape(*shape, size)
    )
    to_mate(pairs, 0).start()
    to_mate(pairs, 1).start()
    turned[...] = jnp.transpose(normed_all[...])

    for pair in range(pairs):
        at = pair * 128

        def attend(number, carry, pair=pair, at=at):
            rows = pl.ds(pl.multiple_of(number * length, length), length)
            query = joint[rows, at : at + 128]
            key = joint[rows, width + at : width + at + 128]
            value = joint[rows, 2 * width + at : 2 * width + at + 128]
            grad_out = mixed_grads[rows, at : at + 128]
            unseen = hidden_pairs[rows, :]
            results = []
            for side in range(2):
                scores = times_t(query * halves[side], key) * factor
                log_all = logs[rows, 2 * pair + side : 2 * pair + side + 1]
                probs = jnp.exp(scores + unseen - log_all)
                grad_value = outer(probs.astype(jnp.bfloat16), grad_out)
                grad_probs = times_t(grad_out * halves[side], value)
                delta = jnp.sum(probs * grad_probs, axis=-1, keepdims=True)
                grad_scores = (probs * (grad_probs - delta)).astype(jnp.bfloat16)
                grad_query = jnp.dot(grad_scores, key, preferred_element_type=jnp.float32) * factor
                grad_key = outer(grad_scores, query) * factor
                results.append((grad_query, grad_key, grad_value))
            for third in range(3):
                grad_joint[rows, third * width + at : third * width + at + 128] = jnp.where(
                    half, results[0][third], results[1][third]
                ).astype(jnp.bfloat16)
            return carry

        lax.fori_loop(0, sequences, attend, 0, unroll=4)
        first, size = columns[pair]
        mine = jnp.concatenate(
            [grad_joint[:, third * width + at : third * width + at + 128] for third in range(3)], axis=1
        )
        part[:, :, first : first + size] = (
            jnp.dot(turned[...], mine, preferred_element_type=jnp.float32)
            .astype(jnp.bfloat16)
            .reshape(*shape, size)
        )
        to_mate(pair, 0).start()
        to_mate(pair, 1).start()
        sum_core(pairs if pair == 0 else pair - 1)
        if pair == 0:
            add_x(early)
            add_x(early + 1)
        elif pair == 1:
            sum_x(pairs)
        else:
            sum_x(pair - 2)
        if pair == 2:
            for index in range(early):
                add_home(index)
            add_x(early + 2)
            add_x(early + 3)
            sum_ep(pairs)

    def upper_part(number, carry):
        rows = pl.ds(pl.multiple_of(number * length, length), length)
        grad_normed = times_t(
            grad_joint[rows, :], weights[:, :, :joint_width].reshape(total, joint_width)
        )
        _, unit, inverse = normalize(tokens[rows, :].astype(jnp.float32), gain_one)
        inner, share = normalize_back(grad_normed, gain_one, unit, inverse)
        tokens_grad[rows, :] = tokens_grad[rows, :] + inner
        return carry + share[None, :]

    grad_one = lax.fori_loop(0, sequences, upper_part, nothing)
    lines = lax.broadcasted_iota(jnp.int32, (128, width), 0)
    gain_lines = jnp.where(
        lines == count, grad_one, jnp.where(lines == count + 1, grad_two, 0.0)
    )
    first, size = columns[pairs + 1]
    part[:, :, first : first + size] = (
        (grad_router[...] + jnp.transpose(gain_lines)).astype(jnp.bfloat16).reshape(*shape, 128)
    )
    to_mate(pairs + 1, 0).start()
    to_mate(pairs + 1, 1).start()
    sum_core(pairs - 1)
    sum_core(pairs + 1)
    sum_x(pairs - 2)
    keep.wait()

    def from_all(step, carry):
        send_ret(step).wait()
        return carry

    lax.fori_loop(1, count, from_all, 0)

    def combine(number, carry):
        rows = pl.ds(pl.multiple_of(number * length, length), length)
        gathered = jnp.dot(
            chosen_of(rows),
            returned[...].reshape(slot_count, width),
            preferred_element_type=jnp.float32,
        )
        output[rows, :] = (state[rows, :] + gathered).astype(jnp.bfloat16)
        return carry

    lax.fori_loop(0, sequences, combine, 0)
    sum_x(pairs - 1)
    sum_x(pairs + 1)
    for index in range(early):
        pass_half(index)
    add_home(early)
    add_home(early + 1)
    for chunk in range(pairs):
        sum_ep(chunk)
    sum_ep(pairs + 1)
    add_home(early + 2)
    pass_half(early)
    pass_half(early + 1)
    add_home(early + 3)
    pass_half(early + 2)
    pass_half(early + 3)

    @pl.when(core == 0)
    def _():
        for chunk in range(CHUNKS):
            spread_x(chunk).wait_send()
            own_half(chunk).wait_send()
            other_half(chunk).wait_send()

    @pl.when(core == 1)
    def _():
        for chunk in range(CHUNKS):
            go_home(chunk).wait_send()
            own_half(chunk).wait_recv()
            other_half(chunk).wait_recv()

    for index in range(early, len(parts)):
        over_x(index).wait_send()
    for chunk in range(len(columns)):
        to_mate(chunk, 0).wait_send()
        to_mate(chunk, 1).wait_send()
        to_x(chunk).wait_send()

        def finish(step, carry, chunk=chunk):
            to_ep(chunk, step).wait_send()
            return carry

        lax.fori_loop(1, count, finish, 0)


def backward(
    tokens,
    segments,
    live,
    out_grad,
    weights,
    joint,
    mixed,
    state,
    logs,
    slots,
    back,
    ret,
    router,
    part_up,
    part_down,
    early_up,
    early_down,
):
    row_count, width = tokens.shape
    count = back.shape[0]
    devices, shard_rows, all_width = weights.shape
    hbm = pl.BlockSpec(memory_space=pltpu.HBM)
    vmem = pl.BlockSpec(memory_space=pltpu.VMEM)
    low = jnp.bfloat16
    quarter = (count, shard_rows, all_width)
    return pl.pallas_call(
        functools.partial(backward_kernel, count),
        out_shape=(
            jax.ShapeDtypeStruct((row_count, width), low),
            jax.ShapeDtypeStruct((row_count, width), jnp.float32),
            jax.ShapeDtypeStruct((shard_rows, joint.shape[1]), jnp.float32),
            jax.ShapeDtypeStruct((shard_rows, width), jnp.float32),
            jax.ShapeDtypeStruct((shard_rows, 128), jnp.float32),
            jax.ShapeDtypeStruct(part_up.shape, low),
            jax.ShapeDtypeStruct(part_down.shape, low),
        ),
        in_specs=[hbm, vmem, vmem] + [hbm] * 9 + [vmem] + [hbm] * 4,
        out_specs=(vmem,) * 7,
        scratch_shapes=[
            pltpu.VMEM(array.shape, array.dtype)
            for array in (
                tokens,
                out_grad,
                weights,
                joint,
                mixed,
                state,
                logs,
                slots,
                back,
                part_up,
                part_down,
                early_up,
                early_down,
            )
        ]
        + [
            pltpu.VMEM(back.shape, low),
            pltpu.VMEM(joint.shape, low),
            pltpu.VMEM((row_count, width), low),
            pltpu.VMEM((row_count, width), low),
            pltpu.VMEM((row_count, width), low),
            pltpu.VMEM((row_count, segments.shape[1]), jnp.float32),
            pltpu.VMEM(weights.shape, low),
            pltpu.VMEM((2,) + quarter, low),
            pltpu.VMEM((2,) + quarter, low),
            pltpu.VMEM(quarter, low),
            pltpu.VMEM(quarter, low),
            pltpu.VMEM(quarter, low),
            pltpu.VMEM((width, row_count), low),
            pltpu.VMEM(early_up.shape, low),
            pltpu.VMEM(early_down.shape, low),
            pltpu.VMEM(early_up.shape, low),
            pltpu.VMEM(early_down.shape, low),
            pltpu.VMEM((2,) + early_up.shape, low),
            pltpu.VMEM((2,) + early_down.shape, low),
            pltpu.SemaphoreType.DMA((2, count)),
            pltpu.SemaphoreType.DMA((2, HEADS // 2 + 2, 2)),
            pltpu.SemaphoreType.DMA((2, HEADS // 2 + 2)),
            pltpu.SemaphoreType.DMA((2, HEADS // 2 + 2, count)),
            pltpu.SemaphoreType.DMA((10, CHUNKS)),
            pltpu.SemaphoreType.DMA((1,)),
            pltpu.SemaphoreType.DMA((13,)),
        ],
        compiler_params=pltpu.CompilerParams(
            collective_id=4, has_side_effects=True, vmem_limit_bytes=63 * MIB
        ),
    )(
        tokens,
        segments,
        live,
        out_grad,
        weights,
        joint,
        mixed,
        state,
        logs,
        slots,
        back,
        ret,
        router,
        part_up,
        part_down,
        early_up,
        early_down,
    )


def per_device_fused(
    tokens,
    segments,
    patch_mask,
    choices,
    priority,
    first_gain,
    joint_weight,
    output_weight,
    second_gain,
    router_weight,
    expert_up,
    expert_down,
    out_grad,
):
    row_count, width = tokens.shape
    experts = router_weight.shape[1]
    capacity = (21 * choices.shape[1] * row_count + 20 * experts - 1) // (20 * experts)
    block = -(-capacity // 16) * 16
    weights, joint, mixed, state, sent_rows, logs, slots, router, grads, used_up, used_down = forward(
        experts,
        capacity,
        block,
        tokens,
        segments,
        patch_mask,
        choices.T,
        priority,
        out_grad,
        joint_weight,
        output_weight,
        jnp.stack([first_gain, second_gain]),
        router_weight.T,
        expert_up[0],
        expert_down[0],
    )
    back, ret, part_up, part_down, early_up, early_down, grad_router = middle(
        sent_rows, grads, expert_up[0], expert_down[0], used_up, used_down, router
    )
    output, tokens_grad, grad_joint, grad_output, grad_pack, grad_up, grad_down = backward(
        tokens,
        segments,
        patch_mask,
        out_grad,
        weights,
        joint,
        mixed,
        state,
        logs,
        slots,
        back,
        ret,
        grad_router,
        part_up,
        part_down,
        early_up,
        early_down,
    )
    return (
        output,
        tokens_grad,
        grad_pack[:, experts],
        grad_joint,
        grad_output,
        grad_pack[:, experts + 1],
        grad_pack[:, :experts],
        grad_up.astype(jnp.float32)[None],
        grad_down.astype(jnp.float32)[None],
    )


def experts_both_ways(sent_rows, sent_grads, up, down, router):
    count, block, width = sent_rows.shape
    experts = router.shape[1]
    hidden = up.shape[1]
    router = jnp.pad(router, ((0, 0), (0, 128 - experts)))
    any_space = pl.BlockSpec(memory_space=pl.ANY)
    vmem = pl.BlockSpec(memory_space=pltpu.VMEM)
    low = jnp.bfloat16
    slots = count * block
    return pl.pallas_call(
        functools.partial(expert_kernel, count, experts),
        out_shape=(
            jax.ShapeDtypeStruct((count, block, width), low),
            jax.ShapeDtypeStruct((count, block, width), low),
            jax.ShapeDtypeStruct((width, hidden), low),
            jax.ShapeDtypeStruct((hidden, width), low),
            jax.ShapeDtypeStruct((width, 128), jnp.float32),
        ),
        in_specs=[any_space, any_space, vmem, vmem, vmem],
        out_specs=(any_space, any_space, vmem, vmem, vmem),
        scratch_shapes=[
            pltpu.VMEM((count, block, width), low),
            pltpu.VMEM((count, block, width), low),
            pltpu.VMEM((slots, width), low),
            pltpu.VMEM((slots, hidden), low),
            pltpu.VMEM((slots, hidden), low),
            pltpu.VMEM((slots, 128), low),
            pltpu.VMEM((count, block, width), low),
            pltpu.VMEM((count, block, width), low),
            pltpu.VMEM((width, slots), low),
            pltpu.SemaphoreType.DMA((8, count)),
            pltpu.SemaphoreType.DMA((4,)),
        ],
        compiler_params=pltpu.CompilerParams(
            collective_id=1, has_side_effects=True, vmem_limit_bytes=58 * MIB
        ),
        cost_estimate=pl.CostEstimate(
            flops=12 * slots * width * hidden, bytes_accessed=16 * MIB, transcendentals=0
        ),
    )(sent_rows, sent_grads, up, down, router)


def per_device(
    tokens,
    segments,
    patch_mask,
    choices,
    priority,
    first_gain,
    joint_weight,
    output_weight,
    second_gain,
    router_weight,
    expert_up,
    expert_down,
    out_grad,
):
    row_count, width = tokens.shape
    head_size = width // HEADS
    factor = head_size ** (-0.5)
    expert_count = router_weight.shape[1]
    length = segments.shape[1]
    capacity = (21 * choices.shape[1] * row_count + 20 * expert_count - 1) // (20 * expert_count)
    block_rows = min(row_count, 512)
    gain_one, joint_full, output_full, gain_two, router_full = (
        lax.all_gather(first_gain, ("grp", "ep"), axis=0, tiled=True),
        lax.all_gather(joint_weight, ("grp", "ep"), axis=0, tiled=True),
        lax.all_gather(output_weight, ("grp", "ep"), axis=0, tiled=True),
        lax.all_gather(second_gain, ("grp", "ep"), axis=0, tiled=True),
        lax.all_gather(router_weight, ("grp", "ep"), axis=0, tiled=True),
    )
    inputs = tokens.astype(jnp.float32)
    gain_one = gain_one.astype(jnp.float32)
    gain_two = gain_two.astype(jnp.float32)
    normed_f, unit_one, inverse_one = normalize(inputs, gain_one)
    normed = normed_f.astype(jnp.bfloat16)
    joint = jnp.dot(normed, joint_full, preferred_element_type=jnp.float32).astype(jnp.bfloat16)
    joint = joint.reshape(row_count, 3, HEADS, head_size)
    live = patch_mask.reshape(row_count)
    position = lax.broadcasted_iota(jnp.int32, (row_count,), 0)
    group = position // length * length + segments.reshape(row_count)
    masks = []
    mixed_parts = []
    log_parts = []
    for start in range(0, row_count, block_rows):
        allowed = visible(group[start : start + block_rows], live[start : start + block_rows])
        block = joint[start : start + block_rows]
        mixed_block, log_total = attend_forward(
            block[:, 0], block[:, 1], block[:, 2], allowed, factor
        )
        masks.append(allowed)
        mixed_parts.append(mixed_block)
        log_parts.append(log_total)
    mixed = jnp.concatenate(mixed_parts, axis=0).reshape(row_count, width).astype(jnp.bfloat16)
    state = inputs + jnp.dot(mixed, output_full, preferred_element_type=jnp.float32)
    normed_two_f, unit_two, inverse_two = normalize(state, gain_two)
    normed_two = normed_two_f.astype(jnp.bfloat16)
    slot_one, slot_two = route(
        choices, live, priority.reshape(row_count), expert_count, capacity
    )
    block = -(-capacity // 16) * 16
    slots = expert_count * block
    index = lax.broadcasted_iota(jnp.int32, (slots, row_count), 0)
    chosen = ((index == slot_one[None, :]) | (index == slot_two[None, :])).astype(jnp.bfloat16)
    spread = lambda values: (
        jnp.dot(chosen, values, preferred_element_type=jnp.float32)
        .astype(jnp.bfloat16)
        .reshape(expert_count, block, width)
    )
    collect = lambda values: outer(chosen, values.reshape(slots, width))
    grad = out_grad.astype(jnp.float32)
    back, returned, grad_up, grad_down, grad_router = experts_both_ways(
        spread(normed_two), spread(out_grad), expert_up[0], expert_down[0], router_full
    )
    output = (state + collect(returned)).astype(jnp.bfloat16)
    grad_router = grad_router[:, :expert_count]
    grad_normed_two = collect(back)
    grad_state_in, grad_gain_two = normalize_back(grad_normed_two, gain_two, unit_two, inverse_two)
    grad_state = grad + grad_state_in
    grad_branch = grad_state.astype(jnp.bfloat16)
    grad_output_w = outer(mixed, grad_branch)
    grad_mixed = (
        times_t(grad_branch, output_full).astype(jnp.bfloat16).reshape(row_count, HEADS, head_size)
    )
    grad_parts = []
    for number, start in enumerate(range(0, row_count, block_rows)):
        block = joint[start : start + block_rows]
        grad_parts.append(
            attend_backward(
                block[:, 0],
                block[:, 1],
                block[:, 2],
                masks[number],
                log_parts[number],
                grad_mixed[start : start + block_rows],
                factor,
            )
        )
    grad_joint = (
        jnp.concatenate(grad_parts, axis=0).reshape(row_count, 3 * width).astype(jnp.bfloat16)
    )
    grad_joint_w = outer(normed, grad_joint)
    grad_normed = times_t(grad_joint, joint_full)
    grad_inputs_in, grad_gain_one = normalize_back(grad_normed, gain_one, unit_one, inverse_one)
    tokens_grad = grad_state + grad_inputs_in
    shares = (
        lax.psum_scatter(grad_gain_one, ("grp", "ep"), scatter_dimension=0, tiled=True),
        lax.psum_scatter(grad_joint_w, ("grp", "ep"), scatter_dimension=0, tiled=True),
        lax.psum_scatter(grad_output_w, ("grp", "ep"), scatter_dimension=0, tiled=True),
        lax.psum_scatter(grad_gain_two, ("grp", "ep"), scatter_dimension=0, tiled=True),
        lax.psum_scatter(grad_router, ("grp", "ep"), scatter_dimension=0, tiled=True),
    )
    grad_up, grad_down = (
        lax.psum(grad_up, "grp").astype(jnp.float32)[None],
        lax.psum(grad_down, "grp").astype(jnp.float32)[None],
    )
    return (
        output,
        tokens_grad,
        shares[0],
        shares[1],
        shares[2],
        shares[3],
        shares[4],
        grad_up,
        grad_down,
    )


def solution(mesh):
    in_specs = (
        P(("grp", "ep"), None),
        P(("grp", "ep"), None),
        P(("grp", "ep"), None),
        P(("grp", "ep"), None),
        P(("grp", "ep"), None),
        P(("grp", "ep")),
        P(("grp", "ep"), None),
        P(("grp", "ep"), None),
        P(("grp", "ep")),
        P(("grp", "ep"), None),
        P("ep", None, None),
        P("ep", None, None),
        P(("grp", "ep"), None),
    )
    out_specs = (
        P(("grp", "ep"), None),
        P(("grp", "ep"), None),
        P(("grp", "ep")),
        P(("grp", "ep"), None),
        P(("grp", "ep"), None),
        P(("grp", "ep")),
        P(("grp", "ep"), None),
        P("ep", None, None),
        P("ep", None, None),
    )
    fused = mesh.shape["grp"] == 4 and mesh.shape["ep"] == 8
    return jax.shard_map(
        per_device_fused if fused else per_device, mesh=mesh, in_specs=in_specs, out_specs=out_specs, check_vma=False
    )
```

```python
import functools

import jax
import jax.numpy as jnp
from jax import lax
from jax.experimental import pallas as pl
from jax.experimental.pallas import tpu as pltpu
from jax.sharding import PartitionSpec as P

MESH = pl.DeviceIdType.MESH
MIB = 1 << 20
PIECES = 4
CHUNKS = 2 * PIECES
EARLY = ((0, 0), (0, 1), (1, 0), (1, 1))
SETTLED = 2
LATE = ((0, 2), (0, 3), (1, 2), (1, 3))

HEADS = 8


EPSILON = 1e-06
NEGATIVE = -1e30


def normalize(values, gain):
    mean = jnp.mean(values, axis=-1, keepdims=True)
    centred = values - mean
    inverse = lax.rsqrt(jnp.mean(centred * centred, axis=-1, keepdims=True) + EPSILON)
    unit = centred * inverse
    return (unit * gain, unit, inverse)


def normalize_back(incoming, gain, unit, inverse):
    scaled = incoming * gain
    inner = (
        scaled
        - jnp.mean(scaled, axis=-1, keepdims=True)
        - unit * jnp.mean(scaled * unit, axis=-1, keepdims=True)
    )
    return (inverse * inner, jnp.sum(incoming * unit, axis=0))


def outer(left, right):
    return lax.dot_general(
        left, right, (((0,), (0,)), ((), ())), preferred_element_type=jnp.float32
    )


def times_t(left, right):
    return lax.dot_general(
        left, right, (((1,), (1,)), ((), ())), preferred_element_type=jnp.float32
    )


def route(picks, live, ranks, expert_count, capacity):
    row_count = picks.shape[0]
    labels = lax.broadcasted_iota(jnp.int32, (row_count, expert_count), 1)
    first = (picks[:, 0:1] == labels).astype(jnp.int32)
    second = (picks[:, 1:2] == labels).astype(jnp.int32)
    live_col = live[:, None]
    earlier = (ranks[None, :] < ranks[:, None]).astype(jnp.int32)
    first_live = first * live_col
    second_live = second * live_col
    place_one = jnp.sum(
        jnp.dot(earlier, first_live, preferred_element_type=jnp.int32) * first, axis=1
    )
    ahead = (
        jnp.dot(earlier, second_live, preferred_element_type=jnp.int32)
        + jnp.sum(first_live, axis=0)[None, :]
    )
    place_two = jnp.sum(ahead * second, axis=1)
    keep_one = (live > 0) & (place_one < capacity)
    keep_two = (live > 0) & (place_two < capacity)
    stride = -(-capacity // 16) * 16
    dummy = expert_count * stride
    slot_one = jnp.where(keep_one, picks[:, 0] * stride + place_one, dummy)
    slot_two = jnp.where(keep_two, picks[:, 1] * stride + place_two, dummy)
    return (slot_one, slot_two)


def visible(group, live):
    rows = group.shape[0]
    index = lax.broadcasted_iota(jnp.int32, (rows, rows), 0)
    other = lax.broadcasted_iota(jnp.int32, (rows, rows), 1)
    return (group[:, None] == group[None, :]) & ((live[None, :] > 0) | (index == other))


def attend_forward(query, key, value, allowed, factor):
    scores = jnp.einsum("qhd,khd->hqk", query, key, preferred_element_type=jnp.float32) * factor
    masked = jnp.where(allowed[None], scores, NEGATIVE)
    top = jnp.max(masked, axis=-1, keepdims=True)
    weights = jnp.exp(masked - top)
    total = jnp.sum(weights, axis=-1, keepdims=True)
    probs = (weights / total).astype(jnp.bfloat16)
    mixed = jnp.einsum("hqk,khd->qhd", probs, value, preferred_element_type=jnp.float32)
    return (mixed, top + jnp.log(total))


def attend_backward(query, key, value, allowed, log_total, grad_mixed, factor):
    scores = jnp.einsum("qhd,khd->hqk", query, key, preferred_element_type=jnp.float32) * factor
    masked = jnp.where(allowed[None], scores, NEGATIVE)
    probs = jnp.exp(masked - log_total)
    grad_value = jnp.einsum(
        "hqk,qhd->khd", probs.astype(jnp.bfloat16), grad_mixed, preferred_element_type=jnp.float32
    )
    grad_probs = jnp.einsum("qhd,khd->hqk", grad_mixed, value, preferred_element_type=jnp.float32)
    delta = jnp.sum(probs * grad_probs, axis=-1, keepdims=True)
    grad_scores = (probs * (grad_probs - delta)).astype(jnp.bfloat16)
    grad_query = (
        jnp.einsum("hqk,khd->qhd", grad_scores, key, preferred_element_type=jnp.float32) * factor
    )
    grad_key = (
        jnp.einsum("hqk,qhd->khd", grad_scores, query, preferred_element_type=jnp.float32) * factor
    )
    return jnp.stack([grad_query, grad_key, grad_value], axis=1)


def partner(me, step, count):
    other, bit = 0, 1
    while bit < count:
        other = other + bit * lax.rem(lax.div(me, bit) + lax.div(step, bit), 2)
        bit *= 2
    return other


def expert_kernel(
    count,
    experts,
    sent_rows,
    sent_grads,
    up_ref,
    down_ref,
    router_ref,
    back_ref,
    ret_ref,
    grad_up_ref,
    grad_down_ref,
    grad_router_ref,
    rows,
    grads,
    gated,
    act,
    grad_pre,
    logit_grads,
    out_grads,
    out_ret,
    turned,
    sems,
    local_sem,
):
    me = lax.axis_index("ep")
    block, width = rows.shape[1:]
    hidden = up_ref.shape[1]
    chunk = 512
    barrier = pltpu.get_barrier_semaphore()

    def greet(step, carry):
        pl.semaphore_signal(
            barrier, inc=1, device_id={"ep": partner(me, step, count)}, device_id_type=MESH
        )
        return carry

    lax.fori_loop(1, count, greet, 0)
    pl.semaphore_wait(barrier, count - 1)

    def remote(kind, source, target, step):
        return pltpu.make_async_remote_copy(
            src_ref=source,
            dst_ref=target,
            send_sem=sems.at[2 * kind, step],
            recv_sem=sems.at[2 * kind + 1, step],
            device_id={"ep": partner(me, step, count)},
            device_id_type=MESH,
        )

    def send_rows(step):
        return remote(0, sent_rows.at[partner(me, step, count)], rows.at[step], step)

    def send_grads(step):
        return remote(1, sent_grads.at[partner(me, step, count)], grads.at[step], step)

    def send_back(step):
        return remote(2, out_grads.at[step], back_ref.at[me], step)

    def send_ret(step):
        return remote(3, out_ret.at[step], ret_ref.at[me], step)

    own = [
        pltpu.make_async_copy(sent_rows.at[me], rows.at[0], local_sem.at[0]),
        pltpu.make_async_copy(sent_grads.at[me], grads.at[0], local_sem.at[1]),
        pltpu.make_async_copy(out_grads.at[0], back_ref.at[me], local_sem.at[2]),
        pltpu.make_async_copy(out_ret.at[0], ret_ref.at[me], local_sem.at[3]),
    ]
    own[0].start()
    own[1].start()

    def start(step, carry):
        send_rows(step).start()
        send_grads(step).start()
        return carry

    lax.fori_loop(1, count, start, 0)
    own[0].wait()
    own[1].wait()
    lanes = lax.broadcasted_iota(jnp.int32, (block, router_ref.shape[1]), 1)

    def one_block(step, carry):
        @pl.when(step > 0)
        def _():
            send_rows(step).wait_recv()
            send_grads(step).wait_recv()

        mine = rows[step]
        cotangent = grads[step].astype(jnp.float32)
        place = pl.ds(pl.multiple_of(step * block, 16), block)
        logits = jnp.dot(mine, router_ref[...], preferred_element_type=jnp.float32)
        logits = jnp.where(lanes < experts, logits, NEGATIVE)
        weights = jnp.exp(logits - jnp.max(logits, axis=1, keepdims=True))
        gate_all = weights / jnp.sum(weights, axis=1, keepdims=True)
        here = (lanes == me).astype(jnp.float32)
        gate = jnp.sum(gate_all * here, axis=1, keepdims=True)
        pair = (gate * cotangent).astype(jnp.bfloat16)
        gated[place, :] = pair
        ret = jnp.zeros((block, width), jnp.float32)
        back = jnp.zeros((block, width), jnp.float32)
        for first in range(0, hidden, chunk):
            span = slice(first, first + chunk)
            pre = jnp.dot(mine, up_ref[:, span], preferred_element_type=jnp.float32)
            cdf = 0.5 * (1.0 + lax.erf(pre * 0.7071067811865476))
            density = jnp.exp(-0.5 * pre * pre) * 0.3989422804014327
            low = (pre * cdf).astype(jnp.bfloat16)
            act[place, span] = low
            ret = ret + jnp.dot(low, down_ref[span, :], preferred_element_type=jnp.float32)
            grad_act = times_t(pair, down_ref[span, :])
            slope = (grad_act * (cdf + pre * density)).astype(jnp.bfloat16)
            grad_pre[place, span] = slope
            back = back + times_t(slope, up_ref[:, span])
        ret = ret.astype(jnp.bfloat16).astype(jnp.float32)
        out_ret[step] = (gate * ret).astype(jnp.bfloat16)
        gate_grad = jnp.sum(cotangent * ret, axis=1, keepdims=True)
        low_logits = (gate * gate_grad * (here - gate_all)).astype(jnp.bfloat16)
        logit_grads[place, :] = low_logits
        back = back + times_t(low_logits, router_ref[...])
        out_grads[step] = back.astype(jnp.bfloat16)

        @pl.when(step > 0)
        def _():
            send_back(step).start()

        @pl.when(step == 0)
        def _():
            own[2].start()

        return carry

    lax.fori_loop(0, count, one_block, 0)
    own[3].start()

    def start_ret(step, carry):
        send_ret(step).start()
        return carry

    lax.fori_loop(1, count, start_ret, 0)
    turned[...] = jnp.transpose(rows[...].reshape(count * block, width))
    grad_router_ref[...] = jnp.dot(
        turned[...], logit_grads[...], preferred_element_type=jnp.float32
    )

    def up_chunk(index, carry):
        span = pl.ds(pl.multiple_of(index * chunk, chunk), chunk)
        grad_up_ref[:, span] = jnp.dot(
            turned[...], grad_pre[:, span], preferred_element_type=jnp.float32
        ).astype(jnp.bfloat16)
        return carry

    lax.fori_loop(0, hidden // chunk, up_chunk, 0)
    turned[...] = jnp.transpose(gated[...])

    def down_chunk(index, carry):
        span = pl.ds(pl.multiple_of(index * chunk, chunk), chunk)
        part = jnp.dot(turned[...], act[:, span], preferred_element_type=jnp.float32)
        grad_down_ref[span, :] = jnp.transpose(part).astype(jnp.bfloat16)
        return carry

    lax.fori_loop(0, hidden // chunk, down_chunk, 0)

    def finish(step, carry):
        send_rows(step).wait_send()
        send_grads(step).wait_send()
        send_back(step).wait()
        send_ret(step).wait()
        return carry

    lax.fori_loop(1, count, finish, 0)
    own[2].wait()
    own[3].wait()


def column(values, lane):
    lanes = lax.broadcasted_iota(jnp.int32, values.shape, 1)
    return jnp.sum(jnp.where(lanes == lane, values, 0), axis=1, keepdims=True)


def core_peer(grp):
    return grp + 1 - 2 * lax.rem(grp, 2)


def x_peer(grp):
    return lax.rem(grp + 2, 4)


def flags(condition):
    return jnp.where(condition, 1.0, 0.0).astype(jnp.bfloat16)


def remote_copy(source, target, send_sem, recv_sem, device):
    return pltpu.make_async_remote_copy(
        src_ref=source,
        dst_ref=target,
        send_sem=send_sem,
        recv_sem=recv_sem,
        device_id=device,
        device_id_type=MESH,
    )


def expert_of(me, grp, count):
    half = count // 2
    other = lax.rem(lax.div(me, half) + lax.rem(grp, 2), 2)
    return lax.rem(me, half) + half * other


def seat(me, grp, step, count):
    half = count // 2
    core = lax.rem(lax.rem(grp, 2) + lax.div(step, half), 2)
    return {
        "grp": 2 * lax.div(grp, 2) + core,
        "ep": partner(me, lax.rem(step, half), count),
    }


def visit(index, count):
    return lax.div(index, 2) + (count // 2) * lax.rem(index, 2)


def greet_all(count, me, grp):
    barrier = pltpu.get_barrier_semaphore()
    half = count // 2

    def greet(step, carry):
        device = {"grp": grp, "ep": partner(me, step, count)}
        pl.semaphore_signal(barrier, inc=1, device_id=device, device_id_type=MESH)
        return carry

    lax.fori_loop(1, count, greet, 0)

    def greet_mate(step, carry):
        device = {"grp": core_peer(grp), "ep": partner(me, step, count)}
        pl.semaphore_signal(barrier, inc=1, device_id=device, device_id_type=MESH)
        return carry

    lax.fori_loop(0, half + 1, greet_mate, 0)
    pl.semaphore_signal(barrier, inc=1, device_id={"grp": x_peer(grp)}, device_id_type=MESH)
    pl.semaphore_wait(barrier, count + half + 1)


def pieces_of(layer_rows):
    def rows(chunk, side):
        size = layer_rows[chunk // PIECES] // (2 * PIECES)
        first = side * PIECES * size + (chunk % PIECES) * size
        return pl.ds(pl.multiple_of(first, size), size)

    return rows


def up_piece(piece, side, side_rows, columns):
    rows = pl.ds(pl.multiple_of(side * side_rows, side_rows), side_rows)
    return rows, pl.ds(piece * columns, columns)


def down_piece(piece, side, size):
    return pl.ds(pl.multiple_of(piece * 2 * size + side * size, size), size)


def seen(segment_row, live_row, segment_col):
    length = segment_row.shape[1]
    index = lax.broadcasted_iota(jnp.int32, (length, length), 0)
    other = lax.broadcasted_iota(jnp.int32, (length, length), 1)
    return (segment_col == segment_row) & ((live_row > 0) | (index == other))


def forward_kernel(
    count,
    capacity,
    tokens_in,
    segments,
    live,
    picks,
    ranks,
    out_grad_in,
    joint_shard,
    output_shard,
    gains_shard,
    router_shard,
    own_up,
    own_down,
    weights_out,
    joint_out,
    mixed_out,
    state_out,
    rows_out,
    logs_out,
    slots_out,
    router_out,
    grads,
    used_up,
    used_down,
    tokens,
    out_grad,
    weights,
    joint,
    mixed,
    state,
    sent_rows,
    logs,
    slots,
    own_grads,
    normed_two,
    int_columns,
    ep_sems,
    x_sems,
    core_sems,
    grad_sems,
    fetch_sems,
    local_sems,
    move_sems,
):
    me, grp = lax.axis_index("ep"), lax.axis_index("grp")
    expert = expert_of(me, grp, count)
    core, side_x = lax.rem(grp, 2), lax.div(grp, 2)
    half_ep = count // 2
    row_count, width = tokens.shape
    sequences, length = segments.shape
    block = sent_rows.shape[1]
    moves = {
        name: pltpu.make_async_copy(source, target, move_sems.at[place])
        for place, (name, source, target) in enumerate(
            (
                ("out_grad", out_grad_in, out_grad),
                ("tokens", tokens_in, tokens),
                ("slots", slots, slots_out),
                ("weights", weights, weights_out),
                ("joint", joint, joint_out),
                ("mixed", mixed, mixed_out),
                ("state", state, state_out),
                ("logs", logs, logs_out),
                ("rows", sent_rows, rows_out),
            )
        )
    }
    moves["out_grad"].start()
    moves["tokens"].start()
    joint_width = joint.shape[1]
    head_size = width // HEADS
    factor = head_size ** (-0.5)
    mate, across = core_peer(grp), x_peer(grp)
    greet_all(count, me, grp)

    def shard(owner_grp, owner):
        return weights.at[owner_grp * count + owner]

    def to_ep(step):
        place = shard(grp, me)
        other = partner(me, step, count)
        return remote_copy(place, place, ep_sems.at[0, step], ep_sems.at[1, step], {"ep": other})

    def relay(step):
        place = shard(grp, partner(me, half_ep, count))
        sems = ep_sems.at[0, half_ep + step], ep_sems.at[1, half_ep + step]
        return remote_copy(place, place, *sems, {"ep": partner(me, step, count)})

    def to_x(step):
        place = shard(grp, partner(me, step, count))
        return remote_copy(place, place, x_sems.at[0, step], x_sems.at[1, step], {"grp": across})

    def to_core(owner_grp, part, step):
        place = shard(owner_grp, partner(me, step, count))
        sems = core_sems.at[0, part, step], core_sems.at[1, part, step]
        return remote_copy(place, place, *sems, {"grp": mate})

    def send_grads(step):
        return remote_copy(
            own_grads.at[step],
            grads.at[step],
            grad_sems.at[0, step],
            grad_sems.at[1, step],
            seat(me, grp, step, count),
        )

    layers = ((own_up, used_up), (own_down, used_down))
    rows_at = pieces_of((own_up.shape[0], own_down.shape[0]))

    def fetch(chunk):
        source, target = layers[chunk // PIECES]
        place = rows_at(chunk, side_x)
        sems = fetch_sems.at[0, chunk], fetch_sems.at[1, chunk]
        device = {"grp": mate, "ep": partner(me, half_ep, count)}
        return remote_copy(source.at[place], target.at[place], *sems, device)

    def share_fetch(chunk):
        place = layers[chunk // PIECES][1].at[rows_at(chunk, side_x)]
        sems = fetch_sems.at[2, chunk], fetch_sems.at[3, chunk]
        return remote_copy(place, place, *sems, {"grp": across})

    far_steps = [step for step in range(count) if step % half_ep >= half_ep // 2]

    def advance_grads(index):
        send_grads(far_steps[index]).wait_send()
        if index + 1 < len(far_steps):
            send_grads(far_steps[index + 1]).start()

    def advance(chunk):
        @pl.when(core == 0)
        def _():
            fetch(chunk).wait_send()
            if chunk + 2 < CHUNKS:
                fetch(chunk + 2).start()

        @pl.when(core == 1)
        def _():
            fetch(chunk).wait_recv()
            share_fetch(chunk).start()

    mine = grp * count + me
    fill = [
        pltpu.make_async_copy(
            joint_shard, weights.at[mine, :, pl.ds(0, joint_width)], local_sems.at[0]
        ),
        pltpu.make_async_copy(
            output_shard, weights.at[mine, :, pl.ds(joint_width, width)], local_sems.at[1]
        ),
    ]
    for copy in fill:
        copy.start()
    shard_rows = weights.shape[1]
    stacked = jnp.concatenate(
        [
            router_shard[...].astype(jnp.float32),
            gains_shard[...].astype(jnp.float32),
            jnp.zeros((16 - count - 2, shard_rows), jnp.float32),
        ],
        axis=0,
    ).astype(jnp.bfloat16)
    tile = (16, 128)
    diagonal = flags(
        lax.broadcasted_iota(jnp.int32, tile, 0) == lax.broadcasted_iota(jnp.int32, tile, 1)
    )
    weights[mine, :, joint_width + width :] = outer(stacked, diagonal).astype(jnp.bfloat16)
    for copy in fill:
        copy.wait()

    def first_hop(step, carry):
        to_ep(step).start()
        return carry

    lax.fori_loop(1, half_ep + 1, first_hop, 0)
    to_x(0).start()
    to_core(grp, 0, 0).start()

    @pl.when(core == 0)
    def _():
        fetch(0).start()
        fetch(1).start()

    ints = jnp.concatenate([segments[...], live[...]], axis=0).astype(jnp.float32)
    turned = jnp.transpose(ints)
    int_columns[...] = turned.astype(jnp.int32)
    live_col = jnp.concatenate(
        [turned[:, sequences + i : sequences + i + 1] for i in range(sequences)], axis=0
    )
    rank_row = ranks[...].astype(jnp.float32)
    lines = jnp.concatenate(
        [rank_row, picks[...].astype(jnp.float32), jnp.zeros((5, row_count), jnp.float32)], axis=0
    )
    token_columns = jnp.transpose(lines)
    rank_col = token_columns[:, 0:1]
    earlier = flags(rank_row < rank_col)
    first = token_columns[:, 1:2].astype(jnp.int32)
    second = token_columns[:, 2:3].astype(jnp.int32)
    lanes = lax.broadcasted_iota(jnp.int32, (row_count, 128), 1)
    one = jnp.where(lanes == first, 1.0, 0.0)
    two = jnp.where(lanes == second + count, 1.0, 0.0)
    counts = jnp.dot(
        earlier, ((one + two) * live_col).astype(jnp.bfloat16), preferred_element_type=jnp.float32
    )
    ahead = jnp.sum(jnp.where(lanes == first + count, live_col, 0.0), axis=0, keepdims=True)
    place_one = jnp.sum(counts * one, axis=1, keepdims=True)
    place_two = jnp.sum((counts + ahead) * two, axis=1, keepdims=True)
    nowhere = 1.0 * count * block
    slot_one = jnp.where(
        (live_col > 0) & (place_one < capacity),
        first.astype(jnp.float32) * block + place_one,
        nowhere,
    )
    slot_two = jnp.where(
        (live_col > 0) & (place_two < capacity),
        second.astype(jnp.float32) * block + place_two,
        nowhere,
    )
    both = jnp.where(lanes == 0, slot_one, jnp.where(lanes == 1, slot_two, nowhere))
    slots[...] = both.astype(jnp.int32)
    moves["slots"].start()
    moves["out_grad"].wait()
    slot_rows = jnp.transpose(both)[0:8].astype(jnp.int32)
    row_one, row_two = slot_rows[0:1], slot_rows[1:2]

    def rows_of(number, values):
        index = lax.broadcasted_iota(jnp.int32, (block, row_count), 0) + number * block
        chosen = flags((index == row_one) | (index == row_two))
        return jnp.dot(chosen, values[...], preferred_element_type=jnp.float32).astype(jnp.bfloat16)

    def spread_grads(index, carry):
        step = visit(index, count)
        own_grads[step] = rows_of(partner(expert, step, count), out_grad)

        @pl.when((step > 0) & (lax.rem(step, half_ep) < half_ep // 2))
        def _():
            send_grads(step).start()

        return carry

    lax.fori_loop(0, count, spread_grads, 0)
    send_grads(far_steps[0]).start()
    keep = pltpu.make_async_copy(own_grads.at[0], grads.at[0], local_sems.at[3])
    keep.start()

    to_ep(half_ep).wait_recv()

    def pass_far(step, carry):
        relay(step).start()
        return carry

    lax.fori_loop(1, half_ep, pass_far, 0)
    to_x(half_ep).start()
    to_core(grp, 0, half_ep).start()

    def pass_on(step, carry):
        @pl.when(step != half_ep)
        def _():
            to_ep(step).wait_recv()
            to_x(step).start()
            to_core(grp, 0, step).start()

        return carry

    lax.fori_loop(1, count, pass_on, 0)

    def pass_further(step, carry):
        to_x(step).wait_recv()
        to_core(across, 1, step).start()
        return carry

    lax.fori_loop(0, count, pass_further, 0)

    def arrive(step, carry):
        to_core(mate, 0, step).wait_recv()
        to_core(x_peer(mate), 1, step).wait_recv()
        return carry

    lax.fori_loop(0, count, arrive, 0)
    advance(0)
    advance_grads(0)

    moves["weights"].start()
    moves["tokens"].wait()
    devices = weights.shape[0]
    total = devices * weights.shape[1]
    pack = weights[:, :, joint_width + width :].reshape(total, 128)
    router_out[...] = pack
    gains = jnp.transpose(pack.astype(jnp.float32))
    gain_one = gains[count : count + 1]
    gain_two = gains[count + 1 : count + 2]
    half = lax.broadcasted_iota(jnp.int32, (length, 128), 1) < head_size
    halves = (flags(half), flags(jnp.logical_not(half)))

    def attend(number, carry):
        rows = pl.ds(pl.multiple_of(number * length, length), length)
        values = tokens[rows, :].astype(jnp.float32)
        normed = normalize(values, gain_one)[0].astype(jnp.bfloat16)
        joint[rows, :] = jnp.dot(
            normed,
            weights[:, :, :joint_width].reshape(total, joint_width),
            preferred_element_type=jnp.float32,
        ).astype(jnp.bfloat16)
        allowed = seen(
            segments[pl.ds(number, 1), :], live[pl.ds(number, 1), :], column(int_columns[...], number)
        )
        log_all = jnp.zeros((length, 128), jnp.float32)
        log_lanes = lax.broadcasted_iota(jnp.int32, (length, 128), 1)
        for pair in range(HEADS // 2):
            at = pair * 128
            query = joint[rows, at : at + 128]
            key = joint[rows, width + at : width + at + 128]
            value = joint[rows, 2 * width + at : 2 * width + at + 128]
            results = []
            for side in range(2):
                scores = times_t(query * halves[side], key) * factor
                masked = jnp.where(allowed, scores, NEGATIVE)
                top = jnp.max(masked, axis=-1, keepdims=True)
                powers = jnp.exp(masked - top)
                added = jnp.sum(powers, axis=-1, keepdims=True)
                probs = (powers * (1.0 / added)).astype(jnp.bfloat16)
                results.append(jnp.dot(probs, value, preferred_element_type=jnp.float32))
                log_all = jnp.where(log_lanes == 2 * pair + side, top + jnp.log(added), log_all)
            mixed[rows, at : at + 128] = jnp.where(half, results[0], results[1]).astype(jnp.bfloat16)
        logs[rows, :] = log_all
        after = values + jnp.dot(
            mixed[rows, :],
            weights[:, :, joint_width : joint_width + width].reshape(total, width),
            preferred_element_type=jnp.float32,
        )
        state[rows, :] = after
        normed_two[rows, :] = normalize(after, gain_two)[0].astype(jnp.bfloat16)
        for place in range(sequences):

            @pl.when(number == place)
            def _(place=place):
                advance(place + 1)
                if place % 2 == 1:
                    advance_grads((place + 1) // 2)

        return carry

    lax.fori_loop(0, sequences, attend, 0)
    for name in ("joint", "mixed", "state", "logs"):
        moves[name].start()

    def spread_rows(number, carry):
        sent_rows[number] = rows_of(number, normed_two)
        return carry

    lax.fori_loop(0, count, spread_rows, 0)
    moves["rows"].start()

    for chunk in range(sequences + 1, CHUNKS):
        advance(chunk)
    advance_grads(3)

    @pl.when(core == 1)
    def _():
        for chunk in range(CHUNKS):
            share_fetch(chunk).wait()

    for name in ("slots", "weights", "joint", "mixed", "state", "logs", "rows"):
        moves[name].wait()
    keep.wait()
    to_x(0).wait_send()
    to_core(grp, 0, 0).wait_send()
    to_core(across, 1, 0).wait_send()

    def finish(step, carry):
        to_ep(step).wait_send()
        to_x(step).wait_send()
        to_core(grp, 0, step).wait_send()
        to_core(across, 1, step).wait_send()
        send_grads(step).wait_recv()

        @pl.when(lax.rem(step, half_ep) < half_ep // 2)
        def _():
            send_grads(step).wait_send()

        return carry

    lax.fori_loop(1, count, finish, 0)


def forward(
    count,
    capacity,
    block,
    tokens,
    segments,
    live,
    picks,
    ranks,
    out_grad,
    joint,
    output,
    gains,
    router,
    up,
    down,
):
    row_count, width = tokens.shape
    devices = width // joint.shape[0]
    all_width = joint.shape[1] + width + 128
    hbm = pl.BlockSpec(memory_space=pltpu.HBM)
    vmem = pl.BlockSpec(memory_space=pltpu.VMEM)
    low = jnp.bfloat16
    return pl.pallas_call(
        functools.partial(forward_kernel, count, capacity),
        out_shape=(
            jax.ShapeDtypeStruct((devices, joint.shape[0], all_width), low),
            jax.ShapeDtypeStruct((row_count, joint.shape[1]), low),
            jax.ShapeDtypeStruct((row_count, width), low),
            jax.ShapeDtypeStruct((row_count, width), jnp.float32),
            jax.ShapeDtypeStruct((count, block, width), low),
            jax.ShapeDtypeStruct((row_count, 128), jnp.float32),
            jax.ShapeDtypeStruct((row_count, 128), jnp.int32),
            jax.ShapeDtypeStruct((width, 128), low),
            jax.ShapeDtypeStruct((count, block, width), low),
            jax.ShapeDtypeStruct(up.shape, low),
            jax.ShapeDtypeStruct(down.shape, low),
        ),
        in_specs=[hbm] + [vmem] * 4 + [hbm] * 3 + [vmem] * 2 + [hbm] * 2,
        out_specs=(hbm,) * 7 + (vmem,) + (hbm,) * 3,
        scratch_shapes=[
            pltpu.VMEM(tokens.shape, low),
            pltpu.VMEM(out_grad.shape, low),
            pltpu.VMEM((devices, joint.shape[0], all_width), low),
            pltpu.VMEM((row_count, joint.shape[1]), low),
            pltpu.VMEM((row_count, width), low),
            pltpu.VMEM((row_count, width), jnp.float32),
            pltpu.VMEM((count, block, width), low),
            pltpu.VMEM((row_count, 128), jnp.float32),
            pltpu.VMEM((row_count, 128), jnp.int32),
            pltpu.VMEM((count, block, width), low),
            pltpu.VMEM((row_count, width), low),
            pltpu.VMEM((segments.shape[1], 2 * segments.shape[0]), jnp.int32),
            pltpu.SemaphoreType.DMA((2, count)),
            pltpu.SemaphoreType.DMA((2, count)),
            pltpu.SemaphoreType.DMA((2, 2, count)),
            pltpu.SemaphoreType.DMA((2, count)),
            pltpu.SemaphoreType.DMA((4, CHUNKS)),
            pltpu.SemaphoreType.DMA((4,)),
            pltpu.SemaphoreType.DMA((9,)),
        ],
        compiler_params=pltpu.CompilerParams(
            collective_id=2, has_side_effects=True, vmem_limit_bytes=63 * MIB
        ),
    )(
        tokens,
        segments,
        live,
        picks,
        ranks,
        out_grad,
        joint,
        output,
        gains,
        router,
        up,
        down,
    )


def middle_kernel(
    count,
    sent_rows,
    grads_in,
    own_up,
    own_down,
    used_up,
    used_down,
    router_ref,
    back_ref,
    out_ret,
    part_up,
    part_down,
    early_up,
    early_down,
    grad_router_ref,
    grads,
    rows,
    gated,
    act,
    grad_pre,
    logit_grads,
    out_grads,
    turned,
    turned_gated,
    up_ref,
    down_ref,
    ret_sums,
    back_sums,
    x_up,
    x_down,
    half_up,
    far_up,
    sems,
    x_sems,
    local_sem,
):
    me, grp = lax.axis_index("ep"), lax.axis_index("grp")
    expert = expert_of(me, grp, count)
    block, width = rows.shape[1:]
    hidden = up_ref.shape[1]
    chunk = 512

    bring = pltpu.make_async_copy(grads_in, grads, local_sem.at[4])
    bring.start()

    def load(up, down):
        return (
            pltpu.make_async_copy(up, up_ref, local_sem.at[2]),
            pltpu.make_async_copy(down, down_ref, local_sem.at[3]),
        )

    @pl.when(lax.rem(grp, 2) == 0)
    def _():
        for copy in load(own_up, own_down):
            copy.start()

    @pl.when(lax.rem(grp, 2) == 1)
    def _():
        for copy in load(used_up, used_down):
            copy.start()

    greet_all(count, me, grp)

    def send_rows(step):
        other = partner(expert, step, count)
        there = seat(me, grp, step, count)
        return remote_copy(
            sent_rows.at[other], rows.at[step], sems.at[0, step], sems.at[1, step], there
        )

    def send_back(step):
        there = seat(me, grp, step, count)
        return remote_copy(
            out_grads.at[step], back_ref.at[expert], sems.at[2, step], sems.at[3, step], there
        )

    own = [
        pltpu.make_async_copy(sent_rows.at[expert], rows.at[0], local_sem.at[0]),
        pltpu.make_async_copy(out_grads.at[0], back_ref.at[expert], local_sem.at[1]),
    ]
    own[0].start()

    def start(index, carry):
        send_rows(visit(index, count)).start()
        return carry

    lax.fori_loop(1, count, start, 0)
    own[0].wait()
    for copy in load(used_up, used_down):
        copy.wait()
    bring.wait()
    lanes = lax.broadcasted_iota(jnp.int32, (block, router_ref.shape[1]), 1)

    across, side_x = x_peer(grp), lax.div(grp, 2)
    part_hidden = hidden // 2
    early = len(EARLY)

    def over_x(index):
        layer, piece = EARLY[index]
        sems = x_sems.at[0, index], x_sems.at[1, index]
        if layer == 0:
            source = part_up.at[up_piece(piece, 1 - side_x, width // 2, chunk)]
            target = x_up.at[:, pl.ds(piece * chunk, chunk)]
        else:
            source = part_down.at[down_piece(piece, 1 - side_x, chunk // 2)]
            target = x_down.at[pl.ds(piece * chunk // 2, chunk // 2)]
        return remote_copy(source, target, *sems, {"grp": across})

    def go_home(index):
        place = pl.ds(EARLY[index][1] * chunk, chunk)
        sems = x_sems.at[2, index], x_sems.at[3, index]
        device = {"grp": core_peer(grp), "ep": partner(me, count // 2, count)}
        return remote_copy(half_up.at[:, place], far_up.at[:, place], *sems, device)

    def add_x(index):
        layer, piece = EARLY[index]
        over_x(index).wait_recv()
        if layer == 0:
            kept = part_up[up_piece(piece, side_x, width // 2, chunk)]
            span = slice(piece * chunk, (piece + 1) * chunk)
            added = kept.astype(jnp.float32) + x_up[:, span].astype(jnp.float32)
            half_up[:, span] = added.astype(jnp.bfloat16)

            @pl.when(lax.rem(grp, 2) == 1)
            def _():
                go_home(index).start()

        else:
            kept = part_down[down_piece(piece, side_x, chunk // 2), :]
            span = slice(piece * chunk // 2, (piece + 1) * chunk // 2)
            added = kept.astype(jnp.float32) + x_down[span, :].astype(jnp.float32)
            early_down[span, :] = added.astype(jnp.bfloat16)

    def gates_of(values):
        logits = jnp.dot(values, router_ref[...], preferred_element_type=jnp.float32)
        logits = jnp.where(lanes < count, logits, NEGATIVE)
        weights = jnp.exp(logits - jnp.max(logits, axis=1, keepdims=True))
        return weights / jnp.sum(weights, axis=1, keepdims=True)

    here = (lanes == expert).astype(jnp.float32)

    def through(step, mine, pair, base):
        place = pl.ds(pl.multiple_of(step * block, 16), block)
        ret = jnp.zeros((block, width), jnp.float32)
        back = jnp.zeros((block, width), jnp.float32)
        for first in range(0, part_hidden, chunk):
            span = slice(base + first, base + first + chunk)
            kept = slice(first, first + chunk)
            pre = jnp.dot(mine, up_ref[:, span], preferred_element_type=jnp.float32)
            cdf = 0.5 * (1.0 + lax.erf(pre * 0.7071067811865476))
            density = jnp.exp(-0.5 * pre * pre) * 0.3989422804014327
            low = (pre * cdf).astype(jnp.bfloat16)
            act[place, kept] = low
            ret = ret + jnp.dot(low, down_ref[span, :], preferred_element_type=jnp.float32)
            grad_act = times_t(pair, down_ref[span, :])
            slope = (grad_act * (cdf + pre * density)).astype(jnp.bfloat16)
            grad_pre[place, kept] = slope
            back = back + times_t(slope, up_ref[:, span])
        return ret, back

    def first_half(index, carry):
        step = visit(index, count)

        @pl.when(step > 0)
        def _():
            send_rows(step).wait_recv()

        mine = rows[step]
        gate = jnp.sum(gates_of(mine) * here, axis=1, keepdims=True)
        pair = (gate * grads[step].astype(jnp.float32)).astype(jnp.bfloat16)
        gated[pl.ds(pl.multiple_of(step * block, 16), block), :] = pair
        ret_sums[step], back_sums[step] = through(step, mine, pair, 0)
        return carry

    def second_half(index, carry):
        step = visit(index, count)
        mine = rows[step]
        cotangent = grads[step].astype(jnp.float32)
        place = pl.ds(pl.multiple_of(step * block, 16), block)
        gate_all = gates_of(mine)
        gate = jnp.sum(gate_all * here, axis=1, keepdims=True)
        ret, back = through(step, mine, gated[place, :], part_hidden)
        ret = (ret + ret_sums[step]).astype(jnp.bfloat16).astype(jnp.float32)
        out_ret[step] = (gate * ret).astype(jnp.bfloat16)
        gate_grad = jnp.sum(cotangent * ret, axis=1, keepdims=True)
        low_logits = (gate * gate_grad * (here - gate_all)).astype(jnp.bfloat16)
        logit_grads[place, :] = low_logits
        back = back + back_sums[step] + times_t(low_logits, router_ref[...])
        out_grads[step] = back.astype(jnp.bfloat16)

        @pl.when(step > 0)
        def _():
            send_back(step).start()

        @pl.when(step == 0)
        def _():
            own[1].start()

        @pl.when(index == count // 2)
        def _():
            for part in range(SETTLED):
                add_x(part)
            for part in range(SETTLED, early):
                over_x(part).start()

        return carry

    def layer_sums(base):
        def up_chunk(index, carry):
            span = pl.ds(pl.multiple_of(index * chunk, chunk), chunk)
            part_up[:, pl.ds(pl.multiple_of(base + index * chunk, chunk), chunk)] = jnp.dot(
                turned[...], grad_pre[:, span], preferred_element_type=jnp.float32
            ).astype(jnp.bfloat16)
            return carry

        def down_chunk(index, carry):
            span = pl.ds(pl.multiple_of(index * chunk, chunk), chunk)
            part = jnp.dot(turned_gated[...], act[:, span], preferred_element_type=jnp.float32)
            part_down[pl.ds(pl.multiple_of(base + index * chunk, chunk), chunk), :] = jnp.transpose(
                part
            ).astype(jnp.bfloat16)
            return carry

        lax.fori_loop(0, part_hidden // chunk, up_chunk, 0)
        lax.fori_loop(0, part_hidden // chunk, down_chunk, 0)

    lax.fori_loop(0, count, first_half, 0)
    turned[...] = jnp.transpose(rows[...].reshape(count * block, width))
    turned_gated[...] = jnp.transpose(gated[...])
    layer_sums(0)
    for index in range(SETTLED):
        over_x(index).start()
    lax.fori_loop(0, count, second_half, 0)
    layer_sums(part_hidden)
    grad_router_ref[...] = jnp.dot(
        turned[...], logit_grads[...], preferred_element_type=jnp.float32
    )
    for index in range(SETTLED, early):
        add_x(index)

    @pl.when(lax.rem(grp, 2) == 0)
    def _():
        for index in range(SETTLED):
            go_home(index).wait_recv()
        early_up[...] = (half_up[...].astype(jnp.float32) + far_up[...].astype(jnp.float32)).astype(
            jnp.bfloat16
        )

    @pl.when(lax.rem(grp, 2) == 1)
    def _():
        for index in range(SETTLED):
            go_home(index).wait_send()

    for index in range(early):
        over_x(index).wait_send()

    def finish(step, carry):
        send_rows(step).wait_send()
        send_back(step).wait()
        return carry

    lax.fori_loop(1, count, finish, 0)
    own[1].wait()


def middle(sent_rows, grads, up, down, used_up, used_down, router):
    count, block, width = sent_rows.shape
    hidden = up.shape[1]
    any_space = pl.BlockSpec(memory_space=pl.ANY)
    hbm = pl.BlockSpec(memory_space=pltpu.HBM)
    vmem = pl.BlockSpec(memory_space=pltpu.VMEM)
    low = jnp.bfloat16
    slots = count * block
    return pl.pallas_call(
        functools.partial(middle_kernel, count),
        out_shape=(
            jax.ShapeDtypeStruct((count, block, width), low),
            jax.ShapeDtypeStruct((count, block, width), low),
            jax.ShapeDtypeStruct((width, hidden), low),
            jax.ShapeDtypeStruct((hidden, width), low),
            jax.ShapeDtypeStruct((width // 2, hidden // 2), low),
            jax.ShapeDtypeStruct((hidden // 4, width), low),
            jax.ShapeDtypeStruct((width, 128), jnp.float32),
        ),
        in_specs=[hbm] * 6 + [vmem],
        out_specs=(any_space,) + (vmem,) * 6,
        scratch_shapes=[
            pltpu.VMEM((count, block, width), low),
            pltpu.VMEM((count, block, width), low),
            pltpu.VMEM((slots, width), low),
            pltpu.VMEM((slots, hidden // 2), low),
            pltpu.VMEM((slots, hidden // 2), low),
            pltpu.VMEM((slots, 128), low),
            pltpu.VMEM((count, block, width), low),
            pltpu.VMEM((width, slots), low),
            pltpu.VMEM((width, slots), low),
            pltpu.VMEM(up.shape, low),
            pltpu.VMEM(down.shape, low),
            pltpu.VMEM((count, block, width), jnp.float32),
            pltpu.VMEM((count, block, width), jnp.float32),
            pltpu.VMEM((width // 2, hidden // 2), low),
            pltpu.VMEM((hidden // 4, width), low),
            pltpu.VMEM((width // 2, hidden // 2), low),
            pltpu.VMEM((width // 2, hidden // 2), low),
            pltpu.SemaphoreType.DMA((4, count)),
            pltpu.SemaphoreType.DMA((4, len(EARLY))),
            pltpu.SemaphoreType.DMA((5,)),
        ],
        compiler_params=pltpu.CompilerParams(
            collective_id=3, has_side_effects=True, vmem_limit_bytes=63 * MIB
        ),
        cost_estimate=pl.CostEstimate(
            flops=12 * slots * width * hidden, bytes_accessed=16 * MIB, transcendentals=0
        ),
    )(sent_rows, grads, up, down, used_up, used_down, router)


def backward_kernel(
    count,
    tokens_in,
    segments,
    live,
    out_grad_in,
    weights_in,
    joint_in,
    mixed_in,
    state_in,
    logs_in,
    slots_in,
    back_in,
    out_ret,
    grad_router,
    part_up_in,
    part_down_in,
    early_up_in,
    early_down_in,
    output_out,
    tokens_grad_out,
    joint_share,
    output_share,
    pack_share,
    sum_up,
    sum_down,
    tokens,
    out_grad,
    weights,
    joint,
    mixed,
    state,
    logs,
    slots,
    back,
    part_up,
    part_down,
    early_up,
    early_down,
    output,
    tokens_grad,
    returned,
    grad_joint,
    normed_all,
    branch_all,
    mixed_grads,
    hidden_pairs,
    part,
    mate_part,
    pair_part,
    x_part,
    far_part,
    ep_part,
    turned,
    x_up,
    x_down,
    half_up,
    half_down,
    far_up,
    far_down,
    ret_sems,
    mate_sems,
    x_sems,
    ep_sems,
    sum_sems,
    local_sems,
    bring_sems,
):
    bring = [
        pltpu.make_async_copy(source, target, bring_sems.at[place])
        for place, (source, target) in enumerate(
            (
                (weights_in, weights),
                (slots_in, slots),
                (back_in, back),
                (state_in, state),
                (out_grad_in, out_grad),
                (tokens_in, tokens),
                (mixed_in, mixed),
                (joint_in, joint),
                (logs_in, logs),
                (part_up_in, part_up),
                (part_down_in, part_down),
                (early_up_in, early_up),
                (early_down_in, early_down),
            )
        )
    ]
    for copy in bring:
        copy.start()
    me, grp = lax.axis_index("ep"), lax.axis_index("grp")
    row_count, width = tokens.shape
    sequences, length = segments.shape
    block = back.shape[1]
    slot_count = count * block
    joint_width = joint.shape[1]
    head_size = width // HEADS
    factor = head_size ** (-0.5)
    mate, across = core_peer(grp), x_peer(grp)
    core, side_x = lax.rem(grp, 2), lax.div(grp, 2)
    devices = weights.shape[0]
    total = devices * weights.shape[1]
    expert = expert_of(me, grp, count)
    greet_all(count, me, grp)

    parts = EARLY + LATE
    early = len(EARLY)
    rows_up, size_up = part_up.shape[0] // 2, part_up.shape[1] // PIECES
    size_down = part_down.shape[0] // (2 * PIECES)

    def whole(index, arrays, side):
        layer, piece = parts[index]
        if layer == 0:
            return arrays[0].at[up_piece(piece, side, rows_up, size_up)]
        return arrays[1].at[down_piece(piece, side, size_down)]

    def narrow(index, arrays):
        layer, piece = parts[index]
        if layer == 0:
            return arrays[0].at[:, pl.ds((piece % 2) * size_up, size_up)]
        return arrays[1].at[pl.ds((piece % 2) * size_down, size_down)]

    def summed_x(index):
        return narrow(index, (early_up, early_down) if index < early else (half_up, half_down))

    def from_foreign(index):
        return narrow(index, (far_up.at[index // early], far_down.at[index // early]))

    def over_x(index):
        sems = sum_sems.at[0, index], sum_sems.at[1, index]
        source = whole(index, (part_up_in, part_down_in), 1 - side_x)
        return remote_copy(source, narrow(index, (x_up, x_down)), *sems, {"grp": across})

    def go_home(index):
        sems = sum_sems.at[2, index], sum_sems.at[3, index]
        device = {"grp": mate, "ep": partner(me, count // 2, count)}
        source = narrow(index, (early_up_in, early_down_in)) if index < early else summed_x(index)
        return remote_copy(source, from_foreign(index), *sems, device)

    def spread_x(index):
        place = whole(index, (sum_up, sum_down), side_x)
        sems = sum_sems.at[4, index], sum_sems.at[5, index]
        return remote_copy(place, place, *sems, {"grp": across})

    def spread_core(index, side, first):
        place = whole(index, (sum_up, sum_down), side)
        sems = sum_sems.at[first, index], sum_sems.at[first + 1, index]
        return remote_copy(place, place, *sems, {"grp": mate})

    def own_half(index):
        return spread_core(index, side_x, 6)

    def other_half(index):
        return spread_core(index, 1 - side_x, 8)

    def leave(index):
        @pl.when(core == 1)
        def _():
            go_home(index).start()

    def add_x(index):
        over_x(index).wait_recv()
        kept = whole(index, (part_up, part_down), side_x)[...].astype(jnp.float32)
        landed = narrow(index, (x_up, x_down))[...].astype(jnp.float32)
        summed_x(index)[...] = (kept + landed).astype(jnp.bfloat16)
        if index + 2 < len(parts):
            over_x(index + 2).start()
        leave(index)

    def spread(index):
        spread_x(index).start()
        own_half(index).start()

    def add_home(index):
        @pl.when(core == 0)
        def _():
            go_home(index).wait_recv()
            near = summed_x(index)[...].astype(jnp.float32)
            foreign = from_foreign(index)[...].astype(jnp.float32)
            whole(index, (sum_up, sum_down), side_x)[...] = (near + foreign).astype(jnp.bfloat16)
            spread(index)

    def pass_half(index):
        @pl.when(core == 0)
        def _():
            spread_x(index).wait_recv()
            other_half(index).start()

    for index in range(SETTLED, early):
        leave(index)
    over_x(early).start()
    over_x(early + 1).start()

    def send_ret(step):
        return remote_copy(
            out_ret.at[step],
            returned.at[expert],
            ret_sems.at[0, step],
            ret_sems.at[1, step],
            seat(me, grp, step, count),
        )

    keep = pltpu.make_async_copy(out_ret.at[0], returned.at[expert], local_sems.at[0])
    keep.start()

    def start(step, carry):
        send_ret(step).start()
        return carry

    lax.fori_loop(1, count, start, 0)
    pairs = HEADS // 2
    columns = [(pair * 384, 384) for pair in range(pairs)]
    columns += [(joint_width, width), (joint_width + width, 128)]
    for copy in bring[:6]:
        copy.wait()
    pack = weights[:, :, joint_width + width :].reshape(total, 128)
    gains = jnp.transpose(pack.astype(jnp.float32))
    gain_one = gains[count : count + 1]
    gain_two = gains[count + 1 : count + 2]
    half = lax.broadcasted_iota(jnp.int32, (length, 128), 1) < head_size
    halves = (flags(half), flags(jnp.logical_not(half)))
    ints = jnp.transpose(segments[...].astype(jnp.float32)).astype(jnp.int32)

    def chosen_of(rows):
        index = lax.broadcasted_iota(jnp.int32, (length, slot_count), 1)
        pair = slots[rows, :]
        return flags((index == pair[:, 0:1]) | (index == pair[:, 1:2]))

    def to_mate(chunk, which):
        first, size = columns[chunk]
        span = pl.ds(first, size)
        return remote_copy(
            part.at[pl.ds((2 * which + 1 - core) * count, count), :, span],
            mate_part.at[which, :, :, span],
            mate_sems.at[0, chunk, which],
            mate_sems.at[1, chunk, which],
            {"grp": mate},
        )

    def to_x(chunk):
        first, size = columns[chunk]
        span = pl.ds(first, size)
        sems = x_sems.at[0, chunk], x_sems.at[1, chunk]
        source = pair_part.at[1 - side_x, :, :, span]
        return remote_copy(source, x_part.at[:, :, span], *sems, {"grp": across})

    def to_ep(chunk, step):
        first, size = columns[chunk]
        span = pl.ds(first, size)
        other = partner(me, step, count)
        return remote_copy(
            far_part.at[other, :, span],
            ep_part.at[step, :, span],
            ep_sems.at[0, chunk, step],
            ep_sems.at[1, chunk, step],
            {"ep": other},
        )

    def sum_core(chunk):
        first, size = columns[chunk]
        span = slice(first, first + size)
        for which in range(2):
            to_mate(chunk, which).wait_recv()
            owner = 2 * which + core
            pair_part[which, :, :, span] = (
                part[pl.ds(owner * count, count), :, span].astype(jnp.float32)
                + mate_part[which, :, :, span].astype(jnp.float32)
            ).astype(jnp.bfloat16)
        to_x(chunk).start()

    def sum_x(chunk):
        first, size = columns[chunk]
        span = slice(first, first + size)
        to_x(chunk).wait_recv()
        far_part[:, :, span] = (
            pair_part[side_x, :, :, span].astype(jnp.float32) + x_part[:, :, span].astype(jnp.float32)
        ).astype(jnp.bfloat16)

        def start(step, carry):
            to_ep(chunk, step).start()
            return carry

        lax.fori_loop(1, count, start, 0)

    def sum_ep(chunk):
        first, size = columns[chunk]
        span = slice(first, first + size)

        def add(step, added):
            to_ep(chunk, step).wait_recv()
            return added + ep_part[step, :, span].astype(jnp.float32)

        share = lax.fori_loop(1, count, add, far_part[me, :, span].astype(jnp.float32))
        if chunk < pairs:
            for third in range(3):
                at = third * width + chunk * 128
                joint_share[:, at : at + 128] = share[:, third * 128 : third * 128 + 128]
        elif chunk == pairs:
            output_share[...] = share
        else:
            pack_share[...] = share

    shape = (devices, total // devices)

    def lower_part(number, carry):
        rows = pl.ds(pl.multiple_of(number * length, length), length)
        grad_normed_two = jnp.dot(
            chosen_of(rows),
            back[...].reshape(slot_count, width),
            preferred_element_type=jnp.float32,
        )
        _, unit, inverse = normalize(state[rows, :], gain_two)
        inner, share = normalize_back(grad_normed_two, gain_two, unit, inverse)
        grad_state = out_grad[rows, :].astype(jnp.float32) + inner
        tokens_grad[rows, :] = grad_state
        branch = grad_state.astype(jnp.bfloat16)
        branch_all[rows, :] = branch
        mixed_grads[rows, :] = times_t(
            branch, weights[:, :, joint_width : joint_width + width].reshape(total, width)
        ).astype(jnp.bfloat16)
        allowed = seen(segments[pl.ds(number, 1), :], live[pl.ds(number, 1), :], column(ints, number))
        hidden_pairs[rows, :] = jnp.where(allowed, 0.0, NEGATIVE)
        normed = normalize(tokens[rows, :].astype(jnp.float32), gain_one)[0]
        normed_all[rows, :] = normed.astype(jnp.bfloat16)
        return carry + share[None, :]

    nothing = jnp.zeros((1, width), jnp.float32)
    grad_two = lax.fori_loop(0, sequences, lower_part, nothing)
    for copy in bring[6:]:
        copy.wait()

    @pl.when(core == 0)
    def _():
        for index in range(SETTLED):
            whole(index, (sum_up, sum_down), side_x)[...] = summed_x(index)[...]
            spread(index)

    turned[...] = jnp.transpose(mixed[...])
    first, size = columns[pairs]
    part[:, :, first : first + size] = (
        jnp.dot(turned[...], branch_all[...], preferred_element_type=jnp.float32)
        .astype(jnp.bfloat16)
        .reshape(*shape, size)
    )
    to_mate(pairs, 0).start()
    to_mate(pairs, 1).start()
    turned[...] = jnp.transpose(normed_all[...])

    for pair in range(pairs):
        at = pair * 128

        def attend(number, carry, pair=pair, at=at):
            rows = pl.ds(pl.multiple_of(number * length, length), length)
            query = joint[rows, at : at + 128]
            key = joint[rows, width + at : width + at + 128]
            value = joint[rows, 2 * width + at : 2 * width + at + 128]
            grad_out = mixed_grads[rows, at : at + 128]
            unseen = hidden_pairs[rows, :]
            results = []
            for side in range(2):
                scores = times_t(query * halves[side], key) * factor
                log_all = logs[rows, 2 * pair + side : 2 * pair + side + 1]
                probs = jnp.exp(scores + unseen - log_all)
                grad_value = outer(probs.astype(jnp.bfloat16), grad_out)
                grad_probs = times_t(grad_out * halves[side], value)
                delta = jnp.sum(probs * grad_probs, axis=-1, keepdims=True)
                grad_scores = (probs * (grad_probs - delta)).astype(jnp.bfloat16)
                grad_query = jnp.dot(grad_scores, key, preferred_element_type=jnp.float32) * factor
                grad_key = outer(grad_scores, query) * factor
                results.append((grad_query, grad_key, grad_value))
            for third in range(3):
                grad_joint[rows, third * width + at : third * width + at + 128] = jnp.where(
                    half, results[0][third], results[1][third]
                ).astype(jnp.bfloat16)
            return carry

        lax.fori_loop(0, sequences, attend, 0, unroll=4)
        first, size = columns[pair]
        mine = jnp.concatenate(
            [grad_joint[:, third * width + at : third * width + at + 128] for third in range(3)], axis=1
        )
        part[:, :, first : first + size] = (
            jnp.dot(turned[...], mine, preferred_element_type=jnp.float32)
            .astype(jnp.bfloat16)
            .reshape(*shape, size)
        )
        to_mate(pair, 0).start()
        to_mate(pair, 1).start()
        sum_core(pairs if pair == 0 else pair - 1)
        if pair == 0:
            add_x(early)
            add_x(early + 1)
        elif pair == 1:
            sum_x(pairs)
        else:
            sum_x(pair - 2)
        if pair == 2:
            for index in range(SETTLED, early):
                add_home(index)
            add_x(early + 2)
            add_x(early + 3)
            sum_ep(pairs)

    def upper_part(number, carry):
        rows = pl.ds(pl.multiple_of(number * length, length), length)
        grad_normed = times_t(
            grad_joint[rows, :], weights[:, :, :joint_width].reshape(total, joint_width)
        )
        _, unit, inverse = normalize(tokens[rows, :].astype(jnp.float32), gain_one)
        inner, share = normalize_back(grad_normed, gain_one, unit, inverse)
        tokens_grad[rows, :] = tokens_grad[rows, :] + inner
        return carry + share[None, :]

    grad_one = lax.fori_loop(0, sequences, upper_part, nothing)
    leaving = (
        pltpu.make_async_copy(tokens_grad, tokens_grad_out, bring_sems.at[len(bring)]),
        pltpu.make_async_copy(output, output_out, bring_sems.at[len(bring) + 1]),
    )
    leaving[0].start()
    lines = lax.broadcasted_iota(jnp.int32, (128, width), 0)
    gain_lines = jnp.where(
        lines == count, grad_one, jnp.where(lines == count + 1, grad_two, 0.0)
    )
    first, size = columns[pairs + 1]
    part[:, :, first : first + size] = (
        (grad_router[...] + jnp.transpose(gain_lines)).astype(jnp.bfloat16).reshape(*shape, 128)
    )
    to_mate(pairs + 1, 0).start()
    to_mate(pairs + 1, 1).start()
    for index in range(SETTLED):
        pass_half(index)
    sum_core(pairs - 1)
    sum_core(pairs + 1)
    sum_x(pairs - 2)
    add_home(early)
    add_home(early + 1)
    sum_x(pairs - 1)
    sum_x(pairs + 1)
    for index in range(SETTLED, early):
        pass_half(index)
    keep.wait()

    def from_all(step, carry):
        send_ret(step).wait()
        return carry

    lax.fori_loop(1, count, from_all, 0)

    def combine(number, carry):
        rows = pl.ds(pl.multiple_of(number * length, length), length)
        gathered = jnp.dot(
            chosen_of(rows),
            returned[...].reshape(slot_count, width),
            preferred_element_type=jnp.float32,
        )
        output[rows, :] = (state[rows, :] + gathered).astype(jnp.bfloat16)
        return carry

    lax.fori_loop(0, sequences, combine, 0)
    leaving[1].start()
    add_home(early + 2)
    pass_half(early)
    pass_half(early + 1)
    add_home(early + 3)
    for chunk in range(pairs):
        sum_ep(chunk)
    sum_ep(pairs + 1)
    pass_half(early + 2)
    pass_half(early + 3)

    @pl.when(core == 0)
    def _():
        for chunk in range(CHUNKS):
            spread_x(chunk).wait_send()
            own_half(chunk).wait_send()
            other_half(chunk).wait_send()

    @pl.when(core == 1)
    def _():
        for index in range(SETTLED, CHUNKS):
            go_home(index).wait_send()
        for chunk in range(CHUNKS):
            own_half(chunk).wait_recv()
            other_half(chunk).wait_recv()

    for copy in leaving:
        copy.wait()
    for index in range(early, len(parts)):
        over_x(index).wait_send()
    for chunk in range(len(columns)):
        to_mate(chunk, 0).wait_send()
        to_mate(chunk, 1).wait_send()
        to_x(chunk).wait_send()

        def finish(step, carry, chunk=chunk):
            to_ep(chunk, step).wait_send()
            return carry

        lax.fori_loop(1, count, finish, 0)


def backward(
    tokens,
    segments,
    live,
    out_grad,
    weights,
    joint,
    mixed,
    state,
    logs,
    slots,
    back,
    ret,
    router,
    part_up,
    part_down,
    early_up,
    early_down,
):
    row_count, width = tokens.shape
    count = back.shape[0]
    devices, shard_rows, all_width = weights.shape
    hbm = pl.BlockSpec(memory_space=pltpu.HBM)
    vmem = pl.BlockSpec(memory_space=pltpu.VMEM)
    low = jnp.bfloat16
    quarter = (count, shard_rows, all_width)
    return pl.pallas_call(
        functools.partial(backward_kernel, count),
        out_shape=(
            jax.ShapeDtypeStruct((row_count, width), low),
            jax.ShapeDtypeStruct((row_count, width), jnp.float32),
            jax.ShapeDtypeStruct((shard_rows, joint.shape[1]), jnp.float32),
            jax.ShapeDtypeStruct((shard_rows, width), jnp.float32),
            jax.ShapeDtypeStruct((shard_rows, 128), jnp.float32),
            jax.ShapeDtypeStruct(part_up.shape, low),
            jax.ShapeDtypeStruct(part_down.shape, low),
        ),
        in_specs=[hbm, vmem, vmem] + [hbm] * 9 + [vmem] + [hbm] * 4,
        out_specs=(hbm,) * 2 + (vmem,) * 5,
        scratch_shapes=[
            pltpu.VMEM(array.shape, array.dtype)
            for array in (
                tokens,
                out_grad,
                weights,
                joint,
                mixed,
                state,
                logs,
                slots,
                back,
                part_up,
                part_down,
                early_up,
                early_down,
            )
        ]
        + [
            pltpu.VMEM((row_count, width), low),
            pltpu.VMEM((row_count, width), jnp.float32),
            pltpu.VMEM(back.shape, low),
            pltpu.VMEM(joint.shape, low),
            pltpu.VMEM((row_count, width), low),
            pltpu.VMEM((row_count, width), low),
            pltpu.VMEM((row_count, width), low),
            pltpu.VMEM((row_count, segments.shape[1]), jnp.float32),
            pltpu.VMEM(weights.shape, low),
            pltpu.VMEM((2,) + quarter, low),
            pltpu.VMEM((2,) + quarter, low),
            pltpu.VMEM(quarter, low),
            pltpu.VMEM(quarter, low),
            pltpu.VMEM(quarter, low),
            pltpu.VMEM((width, row_count), low),
            pltpu.VMEM(early_up.shape, low),
            pltpu.VMEM(early_down.shape, low),
            pltpu.VMEM(early_up.shape, low),
            pltpu.VMEM(early_down.shape, low),
            pltpu.VMEM((2,) + early_up.shape, low),
            pltpu.VMEM((2,) + early_down.shape, low),
            pltpu.SemaphoreType.DMA((2, count)),
            pltpu.SemaphoreType.DMA((2, HEADS // 2 + 2, 2)),
            pltpu.SemaphoreType.DMA((2, HEADS // 2 + 2)),
            pltpu.SemaphoreType.DMA((2, HEADS // 2 + 2, count)),
            pltpu.SemaphoreType.DMA((10, CHUNKS)),
            pltpu.SemaphoreType.DMA((1,)),
            pltpu.SemaphoreType.DMA((15,)),
        ],
        compiler_params=pltpu.CompilerParams(
            collective_id=4, has_side_effects=True, vmem_limit_bytes=63 * MIB
        ),
    )(
        tokens,
        segments,
        live,
        out_grad,
        weights,
        joint,
        mixed,
        state,
        logs,
        slots,
        back,
        ret,
        router,
        part_up,
        part_down,
        early_up,
        early_down,
    )


def finish_kernel(
    copied_in,
    pack,
    summed_in,
    copied_out,
    pack_out,
    summed_out,
    copied,
    narrow,
    wide,
    in_sems,
    out_sems,
    piece_sems,
):
    arrive = [
        pltpu.make_async_copy(source, target, in_sems.at[place])
        for place, (source, target) in enumerate(zip(copied_in, copied))
    ]
    leave = [
        pltpu.make_async_copy(source, target, out_sems.at[place])
        for place, (source, target) in enumerate(zip(copied, copied_out))
    ]

    def piece(layer, number):
        size = narrow[layer].shape[0] // PIECES
        rows = pl.ds(number * size, size)
        return (
            pltpu.make_async_copy(
                summed_in[layer].at[rows], narrow[layer].at[rows], piece_sems.at[0, layer, number]
            ),
            pltpu.make_async_copy(
                wide[layer].at[rows], summed_out[layer].at[rows], piece_sems.at[1, layer, number]
            ),
            rows,
        )

    pieces = [piece(layer, number) for number in range(PIECES) for layer in range(2)]
    for number, part in enumerate(pieces):
        part[0].start()
        if number < len(arrive):
            arrive[number].start()
    shard_rows = pack.shape[0]
    tall = jnp.concatenate([pack[...], jnp.zeros((128 - shard_rows, 128), jnp.float32)], axis=0)
    pack_out[...] = jnp.transpose(tall)[:16, :shard_rows]
    for number, (load, store, rows) in enumerate(pieces):
        load.wait()
        wide[number % 2][rows, :] = narrow[number % 2][rows, :].astype(jnp.float32)
        store.start()
        if number < len(arrive):
            arrive[number].wait()
            leave[number].start()
    for copy in leave:
        copy.wait()
    for _, store, _ in pieces:
        store.wait()


def finish(copied, pack, summed):
    hbm = pl.BlockSpec(memory_space=pltpu.HBM)
    vmem = pl.BlockSpec(memory_space=pltpu.VMEM)
    wide = [jax.ShapeDtypeStruct(array.shape, jnp.float32) for array in summed]
    return pl.pallas_call(
        finish_kernel,
        out_shape=(
            [jax.ShapeDtypeStruct(array.shape, array.dtype) for array in copied],
            jax.ShapeDtypeStruct((16, pack.shape[0]), jnp.float32),
            wide,
        ),
        in_specs=[[hbm] * len(copied), vmem, [hbm] * 2],
        out_specs=([hbm] * len(copied), vmem, [hbm] * 2),
        scratch_shapes=[
            [pltpu.VMEM(array.shape, array.dtype) for array in copied],
            [pltpu.VMEM(array.shape, array.dtype) for array in summed],
            [pltpu.VMEM(array.shape, jnp.float32) for array in summed],
            pltpu.SemaphoreType.DMA((len(copied),)),
            pltpu.SemaphoreType.DMA((len(copied),)),
            pltpu.SemaphoreType.DMA((2, 2, PIECES)),
        ],
        compiler_params=pltpu.CompilerParams(vmem_limit_bytes=63 * MIB),
    )(copied, pack, summed)


def per_device_fused(
    tokens,
    segments,
    patch_mask,
    choices,
    priority,
    first_gain,
    joint_weight,
    output_weight,
    second_gain,
    router_weight,
    expert_up,
    expert_down,
    out_grad,
):
    row_count, width = tokens.shape
    experts = router_weight.shape[1]
    capacity = (21 * choices.shape[1] * row_count + 20 * experts - 1) // (20 * experts)
    block = -(-capacity // 16) * 16
    weights, joint, mixed, state, sent_rows, logs, slots, router, grads, used_up, used_down = forward(
        experts,
        capacity,
        block,
        tokens,
        segments,
        patch_mask,
        choices.T,
        priority,
        out_grad,
        joint_weight,
        output_weight,
        jnp.stack([first_gain, second_gain]),
        router_weight.T,
        expert_up[0],
        expert_down[0],
    )
    back, ret, part_up, part_down, early_up, early_down, grad_router = middle(
        sent_rows, grads, expert_up[0], expert_down[0], used_up, used_down, router
    )
    output, tokens_grad, grad_joint, grad_output, grad_pack, grad_up, grad_down = backward(
        tokens,
        segments,
        patch_mask,
        out_grad,
        weights,
        joint,
        mixed,
        state,
        logs,
        slots,
        back,
        ret,
        grad_router,
        part_up,
        part_down,
        early_up,
        early_down,
    )
    (output, tokens_grad, grad_joint, grad_output), lines, (grad_up, grad_down) = finish(
        [output, tokens_grad, grad_joint, grad_output], grad_pack, [grad_up, grad_down]
    )
    return (
        output,
        tokens_grad,
        lines[experts],
        grad_joint,
        grad_output,
        lines[experts + 1],
        lines[:experts].T,
        grad_up[None],
        grad_down[None],
    )


def experts_both_ways(sent_rows, sent_grads, up, down, router):
    count, block, width = sent_rows.shape
    experts = router.shape[1]
    hidden = up.shape[1]
    router = jnp.pad(router, ((0, 0), (0, 128 - experts)))
    any_space = pl.BlockSpec(memory_space=pl.ANY)
    vmem = pl.BlockSpec(memory_space=pltpu.VMEM)
    low = jnp.bfloat16
    slots = count * block
    return pl.pallas_call(
        functools.partial(expert_kernel, count, experts),
        out_shape=(
            jax.ShapeDtypeStruct((count, block, width), low),
            jax.ShapeDtypeStruct((count, block, width), low),
            jax.ShapeDtypeStruct((width, hidden), low),
            jax.ShapeDtypeStruct((hidden, width), low),
            jax.ShapeDtypeStruct((width, 128), jnp.float32),
        ),
        in_specs=[any_space, any_space, vmem, vmem, vmem],
        out_specs=(any_space, any_space, vmem, vmem, vmem),
        scratch_shapes=[
            pltpu.VMEM((count, block, width), low),
            pltpu.VMEM((count, block, width), low),
            pltpu.VMEM((slots, width), low),
            pltpu.VMEM((slots, hidden), low),
            pltpu.VMEM((slots, hidden), low),
            pltpu.VMEM((slots, 128), low),
            pltpu.VMEM((count, block, width), low),
            pltpu.VMEM((count, block, width), low),
            pltpu.VMEM((width, slots), low),
            pltpu.SemaphoreType.DMA((8, count)),
            pltpu.SemaphoreType.DMA((4,)),
        ],
        compiler_params=pltpu.CompilerParams(
            collective_id=1, has_side_effects=True, vmem_limit_bytes=58 * MIB
        ),
        cost_estimate=pl.CostEstimate(
            flops=12 * slots * width * hidden, bytes_accessed=16 * MIB, transcendentals=0
        ),
    )(sent_rows, sent_grads, up, down, router)


def per_device(
    tokens,
    segments,
    patch_mask,
    choices,
    priority,
    first_gain,
    joint_weight,
    output_weight,
    second_gain,
    router_weight,
    expert_up,
    expert_down,
    out_grad,
):
    row_count, width = tokens.shape
    head_size = width // HEADS
    factor = head_size ** (-0.5)
    expert_count = router_weight.shape[1]
    length = segments.shape[1]
    capacity = (21 * choices.shape[1] * row_count + 20 * expert_count - 1) // (20 * expert_count)
    block_rows = min(row_count, 512)
    gain_one, joint_full, output_full, gain_two, router_full = (
        lax.all_gather(first_gain, ("grp", "ep"), axis=0, tiled=True),
        lax.all_gather(joint_weight, ("grp", "ep"), axis=0, tiled=True),
        lax.all_gather(output_weight, ("grp", "ep"), axis=0, tiled=True),
        lax.all_gather(second_gain, ("grp", "ep"), axis=0, tiled=True),
        lax.all_gather(router_weight, ("grp", "ep"), axis=0, tiled=True),
    )
    inputs = tokens.astype(jnp.float32)
    gain_one = gain_one.astype(jnp.float32)
    gain_two = gain_two.astype(jnp.float32)
    normed_f, unit_one, inverse_one = normalize(inputs, gain_one)
    normed = normed_f.astype(jnp.bfloat16)
    joint = jnp.dot(normed, joint_full, preferred_element_type=jnp.float32).astype(jnp.bfloat16)
    joint = joint.reshape(row_count, 3, HEADS, head_size)
    live = patch_mask.reshape(row_count)
    position = lax.broadcasted_iota(jnp.int32, (row_count,), 0)
    group = position // length * length + segments.reshape(row_count)
    masks = []
    mixed_parts = []
    log_parts = []
    for start in range(0, row_count, block_rows):
        allowed = visible(group[start : start + block_rows], live[start : start + block_rows])
        block = joint[start : start + block_rows]
        mixed_block, log_total = attend_forward(
            block[:, 0], block[:, 1], block[:, 2], allowed, factor
        )
        masks.append(allowed)
        mixed_parts.append(mixed_block)
        log_parts.append(log_total)
    mixed = jnp.concatenate(mixed_parts, axis=0).reshape(row_count, width).astype(jnp.bfloat16)
    state = inputs + jnp.dot(mixed, output_full, preferred_element_type=jnp.float32)
    normed_two_f, unit_two, inverse_two = normalize(state, gain_two)
    normed_two = normed_two_f.astype(jnp.bfloat16)
    slot_one, slot_two = route(
        choices, live, priority.reshape(row_count), expert_count, capacity
    )
    block = -(-capacity // 16) * 16
    slots = expert_count * block
    index = lax.broadcasted_iota(jnp.int32, (slots, row_count), 0)
    chosen = ((index == slot_one[None, :]) | (index == slot_two[None, :])).astype(jnp.bfloat16)
    spread = lambda values: (
        jnp.dot(chosen, values, preferred_element_type=jnp.float32)
        .astype(jnp.bfloat16)
        .reshape(expert_count, block, width)
    )
    collect = lambda values: outer(chosen, values.reshape(slots, width))
    grad = out_grad.astype(jnp.float32)
    back, returned, grad_up, grad_down, grad_router = experts_both_ways(
        spread(normed_two), spread(out_grad), expert_up[0], expert_down[0], router_full
    )
    output = (state + collect(returned)).astype(jnp.bfloat16)
    grad_router = grad_router[:, :expert_count]
    grad_normed_two = collect(back)
    grad_state_in, grad_gain_two = normalize_back(grad_normed_two, gain_two, unit_two, inverse_two)
    grad_state = grad + grad_state_in
    grad_branch = grad_state.astype(jnp.bfloat16)
    grad_output_w = outer(mixed, grad_branch)
    grad_mixed = (
        times_t(grad_branch, output_full).astype(jnp.bfloat16).reshape(row_count, HEADS, head_size)
    )
    grad_parts = []
    for number, start in enumerate(range(0, row_count, block_rows)):
        block = joint[start : start + block_rows]
        grad_parts.append(
            attend_backward(
                block[:, 0],
                block[:, 1],
                block[:, 2],
                masks[number],
                log_parts[number],
                grad_mixed[start : start + block_rows],
                factor,
            )
        )
    grad_joint = (
        jnp.concatenate(grad_parts, axis=0).reshape(row_count, 3 * width).astype(jnp.bfloat16)
    )
    grad_joint_w = outer(normed, grad_joint)
    grad_normed = times_t(grad_joint, joint_full)
    grad_inputs_in, grad_gain_one = normalize_back(grad_normed, gain_one, unit_one, inverse_one)
    tokens_grad = grad_state + grad_inputs_in
    shares = (
        lax.psum_scatter(grad_gain_one, ("grp", "ep"), scatter_dimension=0, tiled=True),
        lax.psum_scatter(grad_joint_w, ("grp", "ep"), scatter_dimension=0, tiled=True),
        lax.psum_scatter(grad_output_w, ("grp", "ep"), scatter_dimension=0, tiled=True),
        lax.psum_scatter(grad_gain_two, ("grp", "ep"), scatter_dimension=0, tiled=True),
        lax.psum_scatter(grad_router, ("grp", "ep"), scatter_dimension=0, tiled=True),
    )
    grad_up, grad_down = (
        lax.psum(grad_up, "grp").astype(jnp.float32)[None],
        lax.psum(grad_down, "grp").astype(jnp.float32)[None],
    )
    return (
        output,
        tokens_grad,
        shares[0],
        shares[1],
        shares[2],
        shares[3],
        shares[4],
        grad_up,
        grad_down,
    )


def solution(mesh):
    in_specs = (
        P(("grp", "ep"), None),
        P(("grp", "ep"), None),
        P(("grp", "ep"), None),
        P(("grp", "ep"), None),
        P(("grp", "ep"), None),
        P(("grp", "ep")),
        P(("grp", "ep"), None),
        P(("grp", "ep"), None),
        P(("grp", "ep")),
        P(("grp", "ep"), None),
        P("ep", None, None),
        P("ep", None, None),
        P(("grp", "ep"), None),
    )
    out_specs = (
        P(("grp", "ep"), None),
        P(("grp", "ep"), None),
        P(("grp", "ep")),
        P(("grp", "ep"), None),
        P(("grp", "ep"), None),
        P(("grp", "ep")),
        P(("grp", "ep"), None),
        P("ep", None, None),
        P("ep", None, None),
    )
    fused = mesh.shape["grp"] == 4 and mesh.shape["ep"] == 8
    return jax.shard_map(
        per_device_fused if fused else per_device, mesh=mesh, in_specs=in_specs, out_specs=out_specs, check_vma=False
    )
```

```python
import functools

import jax
import jax.numpy as jnp
from jax import lax
from jax.experimental import pallas as pl
from jax.experimental.pallas import tpu as pltpu
from jax.sharding import PartitionSpec as P

MESH = pl.DeviceIdType.MESH
MIB = 1 << 20
PIECES = 4
CHUNKS = 2 * PIECES
EARLY = ((0, 0), (0, 1), (1, 0), (1, 1))
SETTLED = 2
LATE = ((0, 2), (0, 3), (1, 2), (1, 3))

HEADS = 8


EPSILON = 1e-06
NEGATIVE = -1e30


def normalize(values, gain):
    mean = jnp.mean(values, axis=-1, keepdims=True)
    centred = values - mean
    inverse = lax.rsqrt(jnp.mean(centred * centred, axis=-1, keepdims=True) + EPSILON)
    unit = centred * inverse
    return (unit * gain, unit, inverse)


def normalize_back(incoming, gain, unit, inverse):
    scaled = incoming * gain
    inner = (
        scaled
        - jnp.mean(scaled, axis=-1, keepdims=True)
        - unit * jnp.mean(scaled * unit, axis=-1, keepdims=True)
    )
    return (inverse * inner, jnp.sum(incoming * unit, axis=0))


def outer(left, right):
    return lax.dot_general(
        left, right, (((0,), (0,)), ((), ())), preferred_element_type=jnp.float32
    )


def times_t(left, right):
    return lax.dot_general(
        left, right, (((1,), (1,)), ((), ())), preferred_element_type=jnp.float32
    )


def route(picks, live, ranks, expert_count, capacity):
    row_count = picks.shape[0]
    labels = lax.broadcasted_iota(jnp.int32, (row_count, expert_count), 1)
    first = (picks[:, 0:1] == labels).astype(jnp.int32)
    second = (picks[:, 1:2] == labels).astype(jnp.int32)
    live_col = live[:, None]
    earlier = (ranks[None, :] < ranks[:, None]).astype(jnp.int32)
    first_live = first * live_col
    second_live = second * live_col
    place_one = jnp.sum(
        jnp.dot(earlier, first_live, preferred_element_type=jnp.int32) * first, axis=1
    )
    ahead = (
        jnp.dot(earlier, second_live, preferred_element_type=jnp.int32)
        + jnp.sum(first_live, axis=0)[None, :]
    )
    place_two = jnp.sum(ahead * second, axis=1)
    keep_one = (live > 0) & (place_one < capacity)
    keep_two = (live > 0) & (place_two < capacity)
    stride = -(-capacity // 16) * 16
    dummy = expert_count * stride
    slot_one = jnp.where(keep_one, picks[:, 0] * stride + place_one, dummy)
    slot_two = jnp.where(keep_two, picks[:, 1] * stride + place_two, dummy)
    return (slot_one, slot_two)


def visible(group, live):
    rows = group.shape[0]
    index = lax.broadcasted_iota(jnp.int32, (rows, rows), 0)
    other = lax.broadcasted_iota(jnp.int32, (rows, rows), 1)
    return (group[:, None] == group[None, :]) & ((live[None, :] > 0) | (index == other))


def attend_forward(query, key, value, allowed, factor):
    scores = jnp.einsum("qhd,khd->hqk", query, key, preferred_element_type=jnp.float32) * factor
    masked = jnp.where(allowed[None], scores, NEGATIVE)
    top = jnp.max(masked, axis=-1, keepdims=True)
    weights = jnp.exp(masked - top)
    total = jnp.sum(weights, axis=-1, keepdims=True)
    probs = (weights / total).astype(jnp.bfloat16)
    mixed = jnp.einsum("hqk,khd->qhd", probs, value, preferred_element_type=jnp.float32)
    return (mixed, top + jnp.log(total))


def attend_backward(query, key, value, allowed, log_total, grad_mixed, factor):
    scores = jnp.einsum("qhd,khd->hqk", query, key, preferred_element_type=jnp.float32) * factor
    masked = jnp.where(allowed[None], scores, NEGATIVE)
    probs = jnp.exp(masked - log_total)
    grad_value = jnp.einsum(
        "hqk,qhd->khd", probs.astype(jnp.bfloat16), grad_mixed, preferred_element_type=jnp.float32
    )
    grad_probs = jnp.einsum("qhd,khd->hqk", grad_mixed, value, preferred_element_type=jnp.float32)
    delta = jnp.sum(probs * grad_probs, axis=-1, keepdims=True)
    grad_scores = (probs * (grad_probs - delta)).astype(jnp.bfloat16)
    grad_query = (
        jnp.einsum("hqk,khd->qhd", grad_scores, key, preferred_element_type=jnp.float32) * factor
    )
    grad_key = (
        jnp.einsum("hqk,qhd->khd", grad_scores, query, preferred_element_type=jnp.float32) * factor
    )
    return jnp.stack([grad_query, grad_key, grad_value], axis=1)


def partner(me, step, count):
    other, bit = 0, 1
    while bit < count:
        other = other + bit * lax.rem(lax.div(me, bit) + lax.div(step, bit), 2)
        bit *= 2
    return other


def expert_kernel(
    count,
    experts,
    sent_rows,
    sent_grads,
    up_ref,
    down_ref,
    router_ref,
    back_ref,
    ret_ref,
    grad_up_ref,
    grad_down_ref,
    grad_router_ref,
    rows,
    grads,
    gated,
    act,
    grad_pre,
    logit_grads,
    out_grads,
    out_ret,
    turned,
    sems,
    local_sem,
):
    me = lax.axis_index("ep")
    block, width = rows.shape[1:]
    hidden = up_ref.shape[1]
    chunk = 512
    barrier = pltpu.get_barrier_semaphore()

    def greet(step, carry):
        pl.semaphore_signal(
            barrier, inc=1, device_id={"ep": partner(me, step, count)}, device_id_type=MESH
        )
        return carry

    lax.fori_loop(1, count, greet, 0)
    pl.semaphore_wait(barrier, count - 1)

    def remote(kind, source, target, step):
        return pltpu.make_async_remote_copy(
            src_ref=source,
            dst_ref=target,
            send_sem=sems.at[2 * kind, step],
            recv_sem=sems.at[2 * kind + 1, step],
            device_id={"ep": partner(me, step, count)},
            device_id_type=MESH,
        )

    def send_rows(step):
        return remote(0, sent_rows.at[partner(me, step, count)], rows.at[step], step)

    def send_grads(step):
        return remote(1, sent_grads.at[partner(me, step, count)], grads.at[step], step)

    def send_back(step):
        return remote(2, out_grads.at[step], back_ref.at[me], step)

    def send_ret(step):
        return remote(3, out_ret.at[step], ret_ref.at[me], step)

    own = [
        pltpu.make_async_copy(sent_rows.at[me], rows.at[0], local_sem.at[0]),
        pltpu.make_async_copy(sent_grads.at[me], grads.at[0], local_sem.at[1]),
        pltpu.make_async_copy(out_grads.at[0], back_ref.at[me], local_sem.at[2]),
        pltpu.make_async_copy(out_ret.at[0], ret_ref.at[me], local_sem.at[3]),
    ]
    own[0].start()
    own[1].start()

    def start(step, carry):
        send_rows(step).start()
        send_grads(step).start()
        return carry

    lax.fori_loop(1, count, start, 0)
    own[0].wait()
    own[1].wait()
    lanes = lax.broadcasted_iota(jnp.int32, (block, router_ref.shape[1]), 1)

    def one_block(step, carry):
        @pl.when(step > 0)
        def _():
            send_rows(step).wait_recv()
            send_grads(step).wait_recv()

        mine = rows[step]
        cotangent = grads[step].astype(jnp.float32)
        place = pl.ds(pl.multiple_of(step * block, 16), block)
        logits = jnp.dot(mine, router_ref[...], preferred_element_type=jnp.float32)
        logits = jnp.where(lanes < experts, logits, NEGATIVE)
        weights = jnp.exp(logits - jnp.max(logits, axis=1, keepdims=True))
        gate_all = weights / jnp.sum(weights, axis=1, keepdims=True)
        here = (lanes == me).astype(jnp.float32)
        gate = jnp.sum(gate_all * here, axis=1, keepdims=True)
        pair = (gate * cotangent).astype(jnp.bfloat16)
        gated[place, :] = pair
        ret = jnp.zeros((block, width), jnp.float32)
        back = jnp.zeros((block, width), jnp.float32)
        for first in range(0, hidden, chunk):
            span = slice(first, first + chunk)
            pre = jnp.dot(mine, up_ref[:, span], preferred_element_type=jnp.float32)
            cdf = 0.5 * (1.0 + lax.erf(pre * 0.7071067811865476))
            density = jnp.exp(-0.5 * pre * pre) * 0.3989422804014327
            low = (pre * cdf).astype(jnp.bfloat16)
            act[place, span] = low
            ret = ret + jnp.dot(low, down_ref[span, :], preferred_element_type=jnp.float32)
            grad_act = times_t(pair, down_ref[span, :])
            slope = (grad_act * (cdf + pre * density)).astype(jnp.bfloat16)
            grad_pre[place, span] = slope
            back = back + times_t(slope, up_ref[:, span])
        ret = ret.astype(jnp.bfloat16).astype(jnp.float32)
        out_ret[step] = (gate * ret).astype(jnp.bfloat16)
        gate_grad = jnp.sum(cotangent * ret, axis=1, keepdims=True)
        low_logits = (gate * gate_grad * (here - gate_all)).astype(jnp.bfloat16)
        logit_grads[place, :] = low_logits
        back = back + times_t(low_logits, router_ref[...])
        out_grads[step] = back.astype(jnp.bfloat16)

        @pl.when(step > 0)
        def _():
            send_back(step).start()

        @pl.when(step == 0)
        def _():
            own[2].start()

        return carry

    lax.fori_loop(0, count, one_block, 0)
    own[3].start()

    def start_ret(step, carry):
        send_ret(step).start()
        return carry

    lax.fori_loop(1, count, start_ret, 0)
    turned[...] = jnp.transpose(rows[...].reshape(count * block, width))
    grad_router_ref[...] = jnp.dot(
        turned[...], logit_grads[...], preferred_element_type=jnp.float32
    )

    def up_chunk(index, carry):
        span = pl.ds(pl.multiple_of(index * chunk, chunk), chunk)
        grad_up_ref[:, span] = jnp.dot(
            turned[...], grad_pre[:, span], preferred_element_type=jnp.float32
        ).astype(jnp.bfloat16)
        return carry

    lax.fori_loop(0, hidden // chunk, up_chunk, 0)
    turned[...] = jnp.transpose(gated[...])

    def down_chunk(index, carry):
        span = pl.ds(pl.multiple_of(index * chunk, chunk), chunk)
        part = jnp.dot(turned[...], act[:, span], preferred_element_type=jnp.float32)
        grad_down_ref[span, :] = jnp.transpose(part).astype(jnp.bfloat16)
        return carry

    lax.fori_loop(0, hidden // chunk, down_chunk, 0)

    def finish(step, carry):
        send_rows(step).wait_send()
        send_grads(step).wait_send()
        send_back(step).wait()
        send_ret(step).wait()
        return carry

    lax.fori_loop(1, count, finish, 0)
    own[2].wait()
    own[3].wait()


def column(values, lane):
    lanes = lax.broadcasted_iota(jnp.int32, values.shape, 1)
    return jnp.sum(jnp.where(lanes == lane, values, 0), axis=1, keepdims=True)


def core_peer(grp):
    return grp + 1 - 2 * lax.rem(grp, 2)


def x_peer(grp):
    return lax.rem(grp + 2, 4)


def flags(condition):
    return jnp.where(condition, 1.0, 0.0).astype(jnp.bfloat16)


def remote_copy(source, target, send_sem, recv_sem, device):
    return pltpu.make_async_remote_copy(
        src_ref=source,
        dst_ref=target,
        send_sem=send_sem,
        recv_sem=recv_sem,
        device_id=device,
        device_id_type=MESH,
    )


def expert_of(me, grp, count):
    half = count // 2
    other = lax.rem(lax.div(me, half) + lax.rem(grp, 2), 2)
    return lax.rem(me, half) + half * other


def seat(me, grp, step, count):
    half = count // 2
    core = lax.rem(lax.rem(grp, 2) + lax.div(step, half), 2)
    return {
        "grp": 2 * lax.div(grp, 2) + core,
        "ep": partner(me, lax.rem(step, half), count),
    }


def visit(index, count):
    return lax.div(index, 2) + (count // 2) * lax.rem(index, 2)


def greet_all(count, me, grp):
    barrier = pltpu.get_barrier_semaphore()
    half = count // 2

    def greet(step, carry):
        device = {"grp": grp, "ep": partner(me, step, count)}
        pl.semaphore_signal(barrier, inc=1, device_id=device, device_id_type=MESH)
        return carry

    lax.fori_loop(1, count, greet, 0)

    def greet_mate(step, carry):
        device = {"grp": core_peer(grp), "ep": partner(me, step, count)}
        pl.semaphore_signal(barrier, inc=1, device_id=device, device_id_type=MESH)
        return carry

    lax.fori_loop(0, half + 1, greet_mate, 0)
    pl.semaphore_signal(barrier, inc=1, device_id={"grp": x_peer(grp)}, device_id_type=MESH)
    pl.semaphore_wait(barrier, count + half + 1)


def pieces_of(layer_rows):
    def rows(chunk, side):
        size = layer_rows[chunk // PIECES] // (2 * PIECES)
        first = side * PIECES * size + (chunk % PIECES) * size
        return pl.ds(pl.multiple_of(first, size), size)

    return rows


def up_piece(piece, side, side_rows, columns):
    rows = pl.ds(pl.multiple_of(side * side_rows, side_rows), side_rows)
    return rows, pl.ds(piece * columns, columns)


def down_piece(piece, side, size):
    return pl.ds(pl.multiple_of(piece * 2 * size + side * size, size), size)


def seen(segment_row, live_row, segment_col):
    length = segment_row.shape[1]
    index = lax.broadcasted_iota(jnp.int32, (length, length), 0)
    other = lax.broadcasted_iota(jnp.int32, (length, length), 1)
    return (segment_col == segment_row) & ((live_row > 0) | (index == other))


def forward_kernel(
    count,
    capacity,
    tokens_in,
    segments,
    live,
    picks,
    ranks,
    out_grad_in,
    joint_shard,
    output_shard,
    gains_shard,
    router_shard,
    own_up,
    own_down,
    weights_out,
    joint_out,
    mixed_out,
    state_out,
    rows_out,
    logs_out,
    slots_out,
    router_out,
    grads,
    used_up,
    used_down,
    tokens,
    out_grad,
    weights,
    joint,
    mixed,
    state,
    sent_rows,
    logs,
    slots,
    own_grads,
    normed_two,
    int_columns,
    ep_sems,
    x_sems,
    core_sems,
    grad_sems,
    fetch_sems,
    local_sems,
    move_sems,
):
    me, grp = lax.axis_index("ep"), lax.axis_index("grp")
    expert = expert_of(me, grp, count)
    core, side_x = lax.rem(grp, 2), lax.div(grp, 2)
    half_ep = count // 2
    row_count, width = tokens.shape
    sequences, length = segments.shape
    block = sent_rows.shape[1]
    moves = {
        name: pltpu.make_async_copy(source, target, move_sems.at[place])
        for place, (name, source, target) in enumerate(
            (
                ("out_grad", out_grad_in, out_grad),
                ("tokens", tokens_in, tokens),
                ("slots", slots, slots_out),
                ("weights", weights, weights_out),
                ("joint", joint, joint_out),
                ("mixed", mixed, mixed_out),
                ("state", state, state_out),
                ("logs", logs, logs_out),
                ("rows", sent_rows, rows_out),
            )
        )
    }
    moves["out_grad"].start()
    moves["tokens"].start()
    joint_width = joint.shape[1]
    head_size = width // HEADS
    factor = head_size ** (-0.5)
    mate, across = core_peer(grp), x_peer(grp)
    greet_all(count, me, grp)

    def shard(owner_grp, owner):
        return weights.at[owner_grp * count + owner]

    def to_ep(step):
        place = shard(grp, me)
        other = partner(me, step, count)
        return remote_copy(place, place, ep_sems.at[0, step], ep_sems.at[1, step], {"ep": other})

    def relay(step):
        place = shard(grp, partner(me, half_ep, count))
        sems = ep_sems.at[0, half_ep + step], ep_sems.at[1, half_ep + step]
        return remote_copy(place, place, *sems, {"ep": partner(me, step, count)})

    def to_x(step):
        place = shard(grp, partner(me, step, count))
        return remote_copy(place, place, x_sems.at[0, step], x_sems.at[1, step], {"grp": across})

    def to_core(owner_grp, part, step):
        place = shard(owner_grp, partner(me, step, count))
        sems = core_sems.at[0, part, step], core_sems.at[1, part, step]
        return remote_copy(place, place, *sems, {"grp": mate})

    def send_grads(step):
        return remote_copy(
            own_grads.at[step],
            grads.at[step],
            grad_sems.at[0, step],
            grad_sems.at[1, step],
            seat(me, grp, step, count),
        )

    layers = ((own_up, used_up), (own_down, used_down))
    rows_at = pieces_of((own_up.shape[0], own_down.shape[0]))

    def fetch(chunk):
        source, target = layers[chunk // PIECES]
        place = rows_at(chunk, side_x)
        sems = fetch_sems.at[0, chunk], fetch_sems.at[1, chunk]
        device = {"grp": mate, "ep": partner(me, half_ep, count)}
        return remote_copy(source.at[place], target.at[place], *sems, device)

    def share_fetch(chunk):
        place = layers[chunk // PIECES][1].at[rows_at(chunk, side_x)]
        sems = fetch_sems.at[2, chunk], fetch_sems.at[3, chunk]
        return remote_copy(place, place, *sems, {"grp": across})

    far_steps = [step for step in range(count) if step % half_ep >= half_ep // 2]

    def advance_grads(index):
        send_grads(far_steps[index]).wait_send()
        if index + 1 < len(far_steps):
            send_grads(far_steps[index + 1]).start()

    def advance(chunk):
        @pl.when(core == 0)
        def _():
            fetch(chunk).wait_send()
            if chunk + 3 < CHUNKS:
                fetch(chunk + 3).start()

        @pl.when(core == 1)
        def _():
            fetch(chunk).wait_recv()
            share_fetch(chunk).start()

    mine = grp * count + me
    fill = [
        pltpu.make_async_copy(
            joint_shard, weights.at[mine, :, pl.ds(0, joint_width)], local_sems.at[0]
        ),
        pltpu.make_async_copy(
            output_shard, weights.at[mine, :, pl.ds(joint_width, width)], local_sems.at[1]
        ),
    ]
    for copy in fill:
        copy.start()
    shard_rows = weights.shape[1]
    stacked = jnp.concatenate(
        [
            router_shard[...].astype(jnp.float32),
            gains_shard[...].astype(jnp.float32),
            jnp.zeros((16 - count - 2, shard_rows), jnp.float32),
        ],
        axis=0,
    ).astype(jnp.bfloat16)
    tile = (16, 128)
    diagonal = flags(
        lax.broadcasted_iota(jnp.int32, tile, 0) == lax.broadcasted_iota(jnp.int32, tile, 1)
    )
    weights[mine, :, joint_width + width :] = outer(stacked, diagonal).astype(jnp.bfloat16)
    for copy in fill:
        copy.wait()

    def first_hop(step, carry):
        to_ep(step).start()
        return carry

    lax.fori_loop(1, half_ep + 1, first_hop, 0)
    to_x(0).start()
    to_core(grp, 0, 0).start()

    @pl.when(core == 0)
    def _():
        fetch(0).start()
        fetch(1).start()
        fetch(2).start()

    ints = jnp.concatenate([segments[...], live[...]], axis=0).astype(jnp.float32)
    turned = jnp.transpose(ints)
    int_columns[...] = turned.astype(jnp.int32)
    live_col = jnp.concatenate(
        [turned[:, sequences + i : sequences + i + 1] for i in range(sequences)], axis=0
    )
    rank_row = ranks[...].astype(jnp.float32)
    lines = jnp.concatenate(
        [rank_row, picks[...].astype(jnp.float32), jnp.zeros((5, row_count), jnp.float32)], axis=0
    )
    token_columns = jnp.transpose(lines)
    rank_col = token_columns[:, 0:1]
    earlier = flags(rank_row < rank_col)
    first = token_columns[:, 1:2].astype(jnp.int32)
    second = token_columns[:, 2:3].astype(jnp.int32)
    lanes = lax.broadcasted_iota(jnp.int32, (row_count, 128), 1)
    one = jnp.where(lanes == first, 1.0, 0.0)
    two = jnp.where(lanes == second + count, 1.0, 0.0)
    counts = jnp.dot(
        earlier, ((one + two) * live_col).astype(jnp.bfloat16), preferred_element_type=jnp.float32
    )
    ahead = jnp.sum(jnp.where(lanes == first + count, live_col, 0.0), axis=0, keepdims=True)
    place_one = jnp.sum(counts * one, axis=1, keepdims=True)
    place_two = jnp.sum((counts + ahead) * two, axis=1, keepdims=True)
    nowhere = 1.0 * count * block
    slot_one = jnp.where(
        (live_col > 0) & (place_one < capacity),
        first.astype(jnp.float32) * block + place_one,
        nowhere,
    )
    slot_two = jnp.where(
        (live_col > 0) & (place_two < capacity),
        second.astype(jnp.float32) * block + place_two,
        nowhere,
    )
    both = jnp.where(lanes == 0, slot_one, jnp.where(lanes == 1, slot_two, nowhere))
    slots[...] = both.astype(jnp.int32)
    moves["slots"].start()
    moves["out_grad"].wait()
    slot_rows = jnp.transpose(both)[0:8].astype(jnp.int32)
    row_one, row_two = slot_rows[0:1], slot_rows[1:2]

    def rows_of(number, values):
        index = lax.broadcasted_iota(jnp.int32, (block, row_count), 0) + number * block
        chosen = flags((index == row_one) | (index == row_two))
        return jnp.dot(chosen, values[...], preferred_element_type=jnp.float32).astype(jnp.bfloat16)

    def spread_grads(index, carry):
        step = visit(index, count)
        own_grads[step] = rows_of(partner(expert, step, count), out_grad)

        @pl.when((step > 0) & (lax.rem(step, half_ep) < half_ep // 2))
        def _():
            send_grads(step).start()

        return carry

    lax.fori_loop(0, count, spread_grads, 0)
    send_grads(far_steps[0]).start()
    keep = pltpu.make_async_copy(own_grads.at[0], grads.at[0], local_sems.at[3])
    keep.start()

    to_ep(half_ep).wait_recv()

    def pass_far(step, carry):
        relay(step).start()
        return carry

    lax.fori_loop(1, half_ep, pass_far, 0)
    to_x(half_ep).start()
    to_core(grp, 0, half_ep).start()

    def pass_on(step, carry):
        @pl.when(step != half_ep)
        def _():
            to_ep(step).wait_recv()
            to_x(step).start()
            to_core(grp, 0, step).start()

        return carry

    lax.fori_loop(1, count, pass_on, 0)

    def pass_further(step, carry):
        to_x(step).wait_recv()
        to_core(across, 1, step).start()
        return carry

    lax.fori_loop(0, count, pass_further, 0)

    def arrive(step, carry):
        to_core(mate, 0, step).wait_recv()
        to_core(x_peer(mate), 1, step).wait_recv()
        return carry

    lax.fori_loop(0, count, arrive, 0)
    advance(0)
    advance_grads(0)

    moves["weights"].start()
    moves["tokens"].wait()
    devices = weights.shape[0]
    total = devices * weights.shape[1]
    pack = weights[:, :, joint_width + width :].reshape(total, 128)
    router_out[...] = pack
    gains = jnp.transpose(pack.astype(jnp.float32))
    gain_one = gains[count : count + 1]
    gain_two = gains[count + 1 : count + 2]
    half = lax.broadcasted_iota(jnp.int32, (length, 128), 1) < head_size
    halves = (flags(half), flags(jnp.logical_not(half)))

    def attend(number, carry):
        rows = pl.ds(pl.multiple_of(number * length, length), length)
        values = tokens[rows, :].astype(jnp.float32)
        normed = normalize(values, gain_one)[0].astype(jnp.bfloat16)
        joint[rows, :] = jnp.dot(
            normed,
            weights[:, :, :joint_width].reshape(total, joint_width),
            preferred_element_type=jnp.float32,
        ).astype(jnp.bfloat16)
        allowed = seen(
            segments[pl.ds(number, 1), :], live[pl.ds(number, 1), :], column(int_columns[...], number)
        )
        log_all = jnp.zeros((length, 128), jnp.float32)
        log_lanes = lax.broadcasted_iota(jnp.int32, (length, 128), 1)
        for pair in range(HEADS // 2):
            at = pair * 128
            query = joint[rows, at : at + 128]
            key = joint[rows, width + at : width + at + 128]
            value = joint[rows, 2 * width + at : 2 * width + at + 128]
            results = []
            for side in range(2):
                scores = times_t(query * halves[side], key) * factor
                masked = jnp.where(allowed, scores, NEGATIVE)
                top = jnp.max(masked, axis=-1, keepdims=True)
                powers = jnp.exp(masked - top)
                added = jnp.sum(powers, axis=-1, keepdims=True)
                probs = (powers * (1.0 / added)).astype(jnp.bfloat16)
                results.append(jnp.dot(probs, value, preferred_element_type=jnp.float32))
                log_all = jnp.where(log_lanes == 2 * pair + side, top + jnp.log(added), log_all)
            mixed[rows, at : at + 128] = jnp.where(half, results[0], results[1]).astype(jnp.bfloat16)
        logs[rows, :] = log_all
        after = values + jnp.dot(
            mixed[rows, :],
            weights[:, :, joint_width : joint_width + width].reshape(total, width),
            preferred_element_type=jnp.float32,
        )
        state[rows, :] = after
        normed_two[rows, :] = normalize(after, gain_two)[0].astype(jnp.bfloat16)
        for place in range(sequences):

            @pl.when(number == place)
            def _(place=place):
                advance(place + 1)
                if place % 2 == 1:
                    advance_grads((place + 1) // 2)

        return carry

    lax.fori_loop(0, sequences, attend, 0)
    for name in ("joint", "mixed", "state", "logs"):
        moves[name].start()

    def spread_rows(number, carry):
        sent_rows[number] = rows_of(number, normed_two)
        return carry

    lax.fori_loop(0, count, spread_rows, 0)
    moves["rows"].start()

    for chunk in range(sequences + 1, CHUNKS):
        advance(chunk)
    advance_grads(3)

    @pl.when(core == 1)
    def _():
        for chunk in range(CHUNKS):
            share_fetch(chunk).wait()

    for name in ("slots", "weights", "joint", "mixed", "state", "logs", "rows"):
        moves[name].wait()
    keep.wait()
    to_x(0).wait_send()
    to_core(grp, 0, 0).wait_send()
    to_core(across, 1, 0).wait_send()

    def finish(step, carry):
        to_ep(step).wait_send()
        to_x(step).wait_send()
        to_core(grp, 0, step).wait_send()
        to_core(across, 1, step).wait_send()
        send_grads(step).wait_recv()

        @pl.when(lax.rem(step, half_ep) < half_ep // 2)
        def _():
            send_grads(step).wait_send()

        return carry

    lax.fori_loop(1, count, finish, 0)


def forward(
    count,
    capacity,
    block,
    tokens,
    segments,
    live,
    picks,
    ranks,
    out_grad,
    joint,
    output,
    gains,
    router,
    up,
    down,
):
    row_count, width = tokens.shape
    devices = width // joint.shape[0]
    all_width = joint.shape[1] + width + 128
    hbm = pl.BlockSpec(memory_space=pltpu.HBM)
    vmem = pl.BlockSpec(memory_space=pltpu.VMEM)
    low = jnp.bfloat16
    return pl.pallas_call(
        functools.partial(forward_kernel, count, capacity),
        out_shape=(
            jax.ShapeDtypeStruct((devices, joint.shape[0], all_width), low),
            jax.ShapeDtypeStruct((row_count, joint.shape[1]), low),
            jax.ShapeDtypeStruct((row_count, width), low),
            jax.ShapeDtypeStruct((row_count, width), jnp.float32),
            jax.ShapeDtypeStruct((count, block, width), low),
            jax.ShapeDtypeStruct((row_count, 128), jnp.float32),
            jax.ShapeDtypeStruct((row_count, 128), jnp.int32),
            jax.ShapeDtypeStruct((width, 128), low),
            jax.ShapeDtypeStruct((count, block, width), low),
            jax.ShapeDtypeStruct(up.shape, low),
            jax.ShapeDtypeStruct(down.shape, low),
        ),
        in_specs=[hbm] + [vmem] * 4 + [hbm] * 3 + [vmem] * 2 + [hbm] * 2,
        out_specs=(hbm,) * 7 + (vmem,) + (hbm,) * 3,
        scratch_shapes=[
            pltpu.VMEM(tokens.shape, low),
            pltpu.VMEM(out_grad.shape, low),
            pltpu.VMEM((devices, joint.shape[0], all_width), low),
            pltpu.VMEM((row_count, joint.shape[1]), low),
            pltpu.VMEM((row_count, width), low),
            pltpu.VMEM((row_count, width), jnp.float32),
            pltpu.VMEM((count, block, width), low),
            pltpu.VMEM((row_count, 128), jnp.float32),
            pltpu.VMEM((row_count, 128), jnp.int32),
            pltpu.VMEM((count, block, width), low),
            pltpu.VMEM((row_count, width), low),
            pltpu.VMEM((segments.shape[1], 2 * segments.shape[0]), jnp.int32),
            pltpu.SemaphoreType.DMA((2, count)),
            pltpu.SemaphoreType.DMA((2, count)),
            pltpu.SemaphoreType.DMA((2, 2, count)),
            pltpu.SemaphoreType.DMA((2, count)),
            pltpu.SemaphoreType.DMA((4, CHUNKS)),
            pltpu.SemaphoreType.DMA((4,)),
            pltpu.SemaphoreType.DMA((9,)),
        ],
        compiler_params=pltpu.CompilerParams(
            collective_id=2, has_side_effects=True, vmem_limit_bytes=63 * MIB
        ),
    )(
        tokens,
        segments,
        live,
        picks,
        ranks,
        out_grad,
        joint,
        output,
        gains,
        router,
        up,
        down,
    )


def middle_kernel(
    count,
    sent_rows,
    grads_in,
    own_up,
    own_down,
    used_up,
    used_down,
    router_ref,
    back_ref,
    out_ret,
    part_up,
    part_down,
    early_up,
    early_down,
    grad_router_ref,
    grads,
    rows,
    gated,
    act,
    grad_pre,
    logit_grads,
    out_grads,
    turned,
    turned_gated,
    up_ref,
    down_ref,
    ret_sums,
    back_sums,
    x_up,
    x_down,
    half_up,
    far_up,
    sems,
    x_sems,
    local_sem,
):
    me, grp = lax.axis_index("ep"), lax.axis_index("grp")
    expert = expert_of(me, grp, count)
    block, width = rows.shape[1:]
    hidden = up_ref.shape[1]
    chunk = 512

    bring = pltpu.make_async_copy(grads_in, grads, local_sem.at[4])
    bring.start()

    def load(up, down):
        return (
            pltpu.make_async_copy(up, up_ref, local_sem.at[2]),
            pltpu.make_async_copy(down, down_ref, local_sem.at[3]),
        )

    @pl.when(lax.rem(grp, 2) == 0)
    def _():
        for copy in load(own_up, own_down):
            copy.start()

    @pl.when(lax.rem(grp, 2) == 1)
    def _():
        for copy in load(used_up, used_down):
            copy.start()

    greet_all(count, me, grp)

    def send_rows(step):
        other = partner(expert, step, count)
        there = seat(me, grp, step, count)
        return remote_copy(
            sent_rows.at[other], rows.at[step], sems.at[0, step], sems.at[1, step], there
        )

    def send_back(step):
        there = seat(me, grp, step, count)
        return remote_copy(
            out_grads.at[step], back_ref.at[expert], sems.at[2, step], sems.at[3, step], there
        )

    own = [
        pltpu.make_async_copy(sent_rows.at[expert], rows.at[0], local_sem.at[0]),
        pltpu.make_async_copy(out_grads.at[0], back_ref.at[expert], local_sem.at[1]),
    ]
    own[0].start()

    def start(index, carry):
        send_rows(visit(index, count)).start()
        return carry

    lax.fori_loop(1, count, start, 0)
    own[0].wait()
    for copy in load(used_up, used_down):
        copy.wait()
    bring.wait()
    lanes = lax.broadcasted_iota(jnp.int32, (block, router_ref.shape[1]), 1)

    across, side_x = x_peer(grp), lax.div(grp, 2)
    part_hidden = hidden // 2
    early = len(EARLY)

    def over_x(index):
        layer, piece = EARLY[index]
        sems = x_sems.at[0, index], x_sems.at[1, index]
        if layer == 0:
            source = part_up.at[up_piece(piece, 1 - side_x, width // 2, chunk)]
            target = x_up.at[:, pl.ds(piece * chunk, chunk)]
        else:
            source = part_down.at[down_piece(piece, 1 - side_x, chunk // 2)]
            target = x_down.at[pl.ds(piece * chunk // 2, chunk // 2)]
        return remote_copy(source, target, *sems, {"grp": across})

    def go_home(index):
        place = pl.ds(EARLY[index][1] * chunk, chunk)
        sems = x_sems.at[2, index], x_sems.at[3, index]
        device = {"grp": core_peer(grp), "ep": partner(me, count // 2, count)}
        return remote_copy(half_up.at[:, place], far_up.at[:, place], *sems, device)

    def add_x(index):
        layer, piece = EARLY[index]
        over_x(index).wait_recv()
        if layer == 0:
            kept = part_up[up_piece(piece, side_x, width // 2, chunk)]
            span = slice(piece * chunk, (piece + 1) * chunk)
            added = kept.astype(jnp.float32) + x_up[:, span].astype(jnp.float32)
            half_up[:, span] = added.astype(jnp.bfloat16)

            @pl.when(lax.rem(grp, 2) == 1)
            def _():
                go_home(index).start()

        else:
            kept = part_down[down_piece(piece, side_x, chunk // 2), :]
            span = slice(piece * chunk // 2, (piece + 1) * chunk // 2)
            added = kept.astype(jnp.float32) + x_down[span, :].astype(jnp.float32)
            early_down[span, :] = added.astype(jnp.bfloat16)

    def gates_of(values):
        logits = jnp.dot(values, router_ref[...], preferred_element_type=jnp.float32)
        logits = jnp.where(lanes < count, logits, NEGATIVE)
        weights = jnp.exp(logits - jnp.max(logits, axis=1, keepdims=True))
        return weights / jnp.sum(weights, axis=1, keepdims=True)

    here = (lanes == expert).astype(jnp.float32)

    def through(step, mine, pair, base):
        place = pl.ds(pl.multiple_of(step * block, 16), block)
        ret = jnp.zeros((block, width), jnp.float32)
        back = jnp.zeros((block, width), jnp.float32)
        for first in range(0, part_hidden, chunk):
            span = slice(base + first, base + first + chunk)
            kept = slice(first, first + chunk)
            pre = jnp.dot(mine, up_ref[:, span], preferred_element_type=jnp.float32)
            cdf = 0.5 * (1.0 + lax.erf(pre * 0.7071067811865476))
            density = jnp.exp(-0.5 * pre * pre) * 0.3989422804014327
            low = (pre * cdf).astype(jnp.bfloat16)
            act[place, kept] = low
            ret = ret + jnp.dot(low, down_ref[span, :], preferred_element_type=jnp.float32)
            grad_act = times_t(pair, down_ref[span, :])
            slope = (grad_act * (cdf + pre * density)).astype(jnp.bfloat16)
            grad_pre[place, kept] = slope
            back = back + times_t(slope, up_ref[:, span])
        return ret, back

    def first_half(index, carry):
        step = visit(index, count)

        @pl.when(step > 0)
        def _():
            send_rows(step).wait_recv()

        mine = rows[step]
        gate = jnp.sum(gates_of(mine) * here, axis=1, keepdims=True)
        pair = (gate * grads[step].astype(jnp.float32)).astype(jnp.bfloat16)
        gated[pl.ds(pl.multiple_of(step * block, 16), block), :] = pair
        ret_sums[step], back_sums[step] = through(step, mine, pair, 0)
        return carry

    def second_half(index, carry):
        step = visit(count - 1 - index, count)
        mine = rows[step]
        cotangent = grads[step].astype(jnp.float32)
        place = pl.ds(pl.multiple_of(step * block, 16), block)
        gate_all = gates_of(mine)
        gate = jnp.sum(gate_all * here, axis=1, keepdims=True)
        ret, back = through(step, mine, gated[place, :], part_hidden)
        ret = (ret + ret_sums[step]).astype(jnp.bfloat16).astype(jnp.float32)
        out_ret[step] = (gate * ret).astype(jnp.bfloat16)
        gate_grad = jnp.sum(cotangent * ret, axis=1, keepdims=True)
        low_logits = (gate * gate_grad * (here - gate_all)).astype(jnp.bfloat16)
        logit_grads[place, :] = low_logits
        back = back + back_sums[step] + times_t(low_logits, router_ref[...])
        out_grads[step] = back.astype(jnp.bfloat16)

        @pl.when(step > 0)
        def _():
            send_back(step).start()

        @pl.when(step == 0)
        def _():
            own[1].start()

        @pl.when(index == count // 2)
        def _():
            for part in range(SETTLED):
                add_x(part)
            for part in range(SETTLED, early):
                over_x(part).start()

        return carry

    def layer_sums(base):
        def up_chunk(index, carry):
            span = pl.ds(pl.multiple_of(index * chunk, chunk), chunk)
            part_up[:, pl.ds(pl.multiple_of(base + index * chunk, chunk), chunk)] = jnp.dot(
                turned[...], grad_pre[:, span], preferred_element_type=jnp.float32
            ).astype(jnp.bfloat16)
            return carry

        def down_chunk(index, carry):
            span = pl.ds(pl.multiple_of(index * chunk, chunk), chunk)
            part = jnp.dot(turned_gated[...], act[:, span], preferred_element_type=jnp.float32)
            part_down[pl.ds(pl.multiple_of(base + index * chunk, chunk), chunk), :] = jnp.transpose(
                part
            ).astype(jnp.bfloat16)
            return carry

        lax.fori_loop(0, part_hidden // chunk, up_chunk, 0)
        lax.fori_loop(0, part_hidden // chunk, down_chunk, 0)

    lax.fori_loop(0, count, first_half, 0)
    turned[...] = jnp.transpose(rows[...].reshape(count * block, width))
    turned_gated[...] = jnp.transpose(gated[...])
    layer_sums(0)
    for index in range(SETTLED):
        over_x(index).start()
    lax.fori_loop(0, count, second_half, 0)
    layer_sums(part_hidden)
    grad_router_ref[...] = jnp.dot(
        turned[...], logit_grads[...], preferred_element_type=jnp.float32
    )
    for index in range(SETTLED, early):
        add_x(index)

    @pl.when(lax.rem(grp, 2) == 0)
    def _():
        for index in range(SETTLED):
            go_home(index).wait_recv()
        early_up[...] = (half_up[...].astype(jnp.float32) + far_up[...].astype(jnp.float32)).astype(
            jnp.bfloat16
        )

    @pl.when(lax.rem(grp, 2) == 1)
    def _():
        for index in range(SETTLED):
            go_home(index).wait_send()

    for index in range(early):
        over_x(index).wait_send()

    def finish(step, carry):
        send_rows(step).wait_send()
        send_back(step).wait()
        return carry

    lax.fori_loop(1, count, finish, 0)
    own[1].wait()


def middle(sent_rows, grads, up, down, used_up, used_down, router):
    count, block, width = sent_rows.shape
    hidden = up.shape[1]
    any_space = pl.BlockSpec(memory_space=pl.ANY)
    hbm = pl.BlockSpec(memory_space=pltpu.HBM)
    vmem = pl.BlockSpec(memory_space=pltpu.VMEM)
    low = jnp.bfloat16
    slots = count * block
    return pl.pallas_call(
        functools.partial(middle_kernel, count),
        out_shape=(
            jax.ShapeDtypeStruct((count, block, width), low),
            jax.ShapeDtypeStruct((count, block, width), low),
            jax.ShapeDtypeStruct((width, hidden), low),
            jax.ShapeDtypeStruct((hidden, width), low),
            jax.ShapeDtypeStruct((width // 2, hidden // 2), low),
            jax.ShapeDtypeStruct((hidden // 4, width), low),
            jax.ShapeDtypeStruct((width, 128), jnp.float32),
        ),
        in_specs=[hbm] * 6 + [vmem],
        out_specs=(any_space,) + (vmem,) * 6,
        scratch_shapes=[
            pltpu.VMEM((count, block, width), low),
            pltpu.VMEM((count, block, width), low),
            pltpu.VMEM((slots, width), low),
            pltpu.VMEM((slots, hidden // 2), low),
            pltpu.VMEM((slots, hidden // 2), low),
            pltpu.VMEM((slots, 128), low),
            pltpu.VMEM((count, block, width), low),
            pltpu.VMEM((width, slots), low),
            pltpu.VMEM((width, slots), low),
            pltpu.VMEM(up.shape, low),
            pltpu.VMEM(down.shape, low),
            pltpu.VMEM((count, block, width), jnp.float32),
            pltpu.VMEM((count, block, width), jnp.float32),
            pltpu.VMEM((width // 2, hidden // 2), low),
            pltpu.VMEM((hidden // 4, width), low),
            pltpu.VMEM((width // 2, hidden // 2), low),
            pltpu.VMEM((width // 2, hidden // 2), low),
            pltpu.SemaphoreType.DMA((4, count)),
            pltpu.SemaphoreType.DMA((4, len(EARLY))),
            pltpu.SemaphoreType.DMA((5,)),
        ],
        compiler_params=pltpu.CompilerParams(
            collective_id=3, has_side_effects=True, vmem_limit_bytes=63 * MIB
        ),
        cost_estimate=pl.CostEstimate(
            flops=12 * slots * width * hidden, bytes_accessed=16 * MIB, transcendentals=0
        ),
    )(sent_rows, grads, up, down, used_up, used_down, router)


def backward_kernel(
    count,
    tokens_in,
    segments,
    live,
    out_grad_in,
    weights_in,
    joint_in,
    mixed_in,
    state_in,
    logs_in,
    slots_in,
    back_in,
    out_ret,
    grad_router,
    part_up_in,
    part_down_in,
    early_up_in,
    early_down_in,
    output_out,
    tokens_grad_out,
    joint_share,
    output_share,
    pack_share,
    sum_up,
    sum_down,
    tokens,
    out_grad,
    weights,
    joint,
    mixed,
    state,
    logs,
    slots,
    back,
    part_up,
    part_down,
    early_up,
    early_down,
    output,
    tokens_grad,
    returned,
    grad_joint,
    normed_all,
    branch_all,
    mixed_grads,
    hidden_pairs,
    part,
    mate_part,
    pair_part,
    x_part,
    far_part,
    ep_part,
    turned,
    x_up,
    x_down,
    half_up,
    half_down,
    far_up,
    far_down,
    ret_sems,
    mate_sems,
    x_sems,
    ep_sems,
    sum_sems,
    local_sems,
    bring_sems,
):
    bring = [
        pltpu.make_async_copy(source, target, bring_sems.at[place])
        for place, (source, target) in enumerate(
            (
                (weights_in, weights),
                (slots_in, slots),
                (back_in, back),
                (state_in, state),
                (out_grad_in, out_grad),
                (tokens_in, tokens),
                (mixed_in, mixed),
                (joint_in, joint),
                (logs_in, logs),
                (part_up_in, part_up),
                (part_down_in, part_down),
                (early_up_in, early_up),
                (early_down_in, early_down),
            )
        )
    ]
    for copy in bring:
        copy.start()
    me, grp = lax.axis_index("ep"), lax.axis_index("grp")
    row_count, width = tokens.shape
    sequences, length = segments.shape
    block = back.shape[1]
    slot_count = count * block
    joint_width = joint.shape[1]
    head_size = width // HEADS
    factor = head_size ** (-0.5)
    mate, across = core_peer(grp), x_peer(grp)
    core, side_x = lax.rem(grp, 2), lax.div(grp, 2)
    devices = weights.shape[0]
    total = devices * weights.shape[1]
    expert = expert_of(me, grp, count)
    greet_all(count, me, grp)

    parts = EARLY + LATE
    early = len(EARLY)
    rows_up, size_up = part_up.shape[0] // 2, part_up.shape[1] // PIECES
    size_down = part_down.shape[0] // (2 * PIECES)

    def whole(index, arrays, side):
        layer, piece = parts[index]
        if layer == 0:
            return arrays[0].at[up_piece(piece, side, rows_up, size_up)]
        return arrays[1].at[down_piece(piece, side, size_down)]

    def narrow(index, arrays):
        layer, piece = parts[index]
        if layer == 0:
            return arrays[0].at[:, pl.ds((piece % 2) * size_up, size_up)]
        return arrays[1].at[pl.ds((piece % 2) * size_down, size_down)]

    def summed_x(index):
        return narrow(index, (early_up, early_down) if index < early else (half_up, half_down))

    def from_foreign(index):
        return narrow(index, (far_up.at[index // early], far_down.at[index // early]))

    def over_x(index):
        sems = sum_sems.at[0, index], sum_sems.at[1, index]
        source = whole(index, (part_up_in, part_down_in), 1 - side_x)
        return remote_copy(source, narrow(index, (x_up, x_down)), *sems, {"grp": across})

    def go_home(index):
        sems = sum_sems.at[2, index], sum_sems.at[3, index]
        device = {"grp": mate, "ep": partner(me, count // 2, count)}
        source = narrow(index, (early_up_in, early_down_in)) if index < early else summed_x(index)
        return remote_copy(source, from_foreign(index), *sems, device)

    def spread_x(index):
        place = whole(index, (sum_up, sum_down), side_x)
        sems = sum_sems.at[4, index], sum_sems.at[5, index]
        return remote_copy(place, place, *sems, {"grp": across})

    def spread_core(index, side, first):
        place = whole(index, (sum_up, sum_down), side)
        sems = sum_sems.at[first, index], sum_sems.at[first + 1, index]
        return remote_copy(place, place, *sems, {"grp": mate})

    def own_half(index):
        return spread_core(index, side_x, 6)

    def other_half(index):
        return spread_core(index, 1 - side_x, 8)

    def leave(index):
        @pl.when(core == 1)
        def _():
            go_home(index).start()

    def add_x(index):
        over_x(index).wait_recv()
        kept = whole(index, (part_up, part_down), side_x)[...].astype(jnp.float32)
        landed = narrow(index, (x_up, x_down))[...].astype(jnp.float32)
        summed_x(index)[...] = (kept + landed).astype(jnp.bfloat16)
        if index + 2 < len(parts):
            over_x(index + 2).start()
        leave(index)

    def spread(index):
        spread_x(index).start()
        own_half(index).start()

    def add_home(index):
        @pl.when(core == 0)
        def _():
            go_home(index).wait_recv()
            near = summed_x(index)[...].astype(jnp.float32)
            foreign = from_foreign(index)[...].astype(jnp.float32)
            whole(index, (sum_up, sum_down), side_x)[...] = (near + foreign).astype(jnp.bfloat16)
            spread(index)

    def pass_half(index):
        @pl.when(core == 0)
        def _():
            spread_x(index).wait_recv()
            other_half(index).start()

    for index in range(SETTLED, early):
        leave(index)
    over_x(early).start()
    over_x(early + 1).start()

    def send_ret(step):
        return remote_copy(
            out_ret.at[step],
            returned.at[expert],
            ret_sems.at[0, step],
            ret_sems.at[1, step],
            seat(me, grp, step, count),
        )

    keep = pltpu.make_async_copy(out_ret.at[0], returned.at[expert], local_sems.at[0])
    keep.start()

    def start(step, carry):
        send_ret(step).start()
        return carry

    lax.fori_loop(1, count, start, 0)
    pairs = HEADS // 2
    columns = [(pair * 384, 384) for pair in range(pairs)]
    columns += [(joint_width, width), (joint_width + width, 128)]
    for copy in bring[:6]:
        copy.wait()
    pack = weights[:, :, joint_width + width :].reshape(total, 128)
    gains = jnp.transpose(pack.astype(jnp.float32))
    gain_one = gains[count : count + 1]
    gain_two = gains[count + 1 : count + 2]
    half = lax.broadcasted_iota(jnp.int32, (length, 128), 1) < head_size
    halves = (flags(half), flags(jnp.logical_not(half)))
    ints = jnp.transpose(segments[...].astype(jnp.float32)).astype(jnp.int32)

    def chosen_of(rows):
        index = lax.broadcasted_iota(jnp.int32, (length, slot_count), 1)
        pair = slots[rows, :]
        return flags((index == pair[:, 0:1]) | (index == pair[:, 1:2]))

    def to_mate(chunk, which):
        first, size = columns[chunk]
        span = pl.ds(first, size)
        return remote_copy(
            part.at[pl.ds((2 * which + 1 - core) * count, count), :, span],
            mate_part.at[which, :, :, span],
            mate_sems.at[0, chunk, which],
            mate_sems.at[1, chunk, which],
            {"grp": mate},
        )

    def to_x(chunk):
        first, size = columns[chunk]
        span = pl.ds(first, size)
        sems = x_sems.at[0, chunk], x_sems.at[1, chunk]
        source = pair_part.at[1 - side_x, :, :, span]
        return remote_copy(source, x_part.at[:, :, span], *sems, {"grp": across})

    def to_ep(chunk, step):
        first, size = columns[chunk]
        span = pl.ds(first, size)
        other = partner(me, step, count)
        return remote_copy(
            far_part.at[other, :, span],
            ep_part.at[step, :, span],
            ep_sems.at[0, chunk, step],
            ep_sems.at[1, chunk, step],
            {"ep": other},
        )

    def sum_core(chunk):
        first, size = columns[chunk]
        span = slice(first, first + size)
        for which in range(2):
            to_mate(chunk, which).wait_recv()
            owner = 2 * which + core
            pair_part[which, :, :, span] = (
                part[pl.ds(owner * count, count), :, span].astype(jnp.float32)
                + mate_part[which, :, :, span].astype(jnp.float32)
            ).astype(jnp.bfloat16)
        to_x(chunk).start()

    def sum_x(chunk):
        first, size = columns[chunk]
        span = slice(first, first + size)
        to_x(chunk).wait_recv()
        far_part[:, :, span] = (
            pair_part[side_x, :, :, span].astype(jnp.float32) + x_part[:, :, span].astype(jnp.float32)
        ).astype(jnp.bfloat16)

        def start(step, carry):
            to_ep(chunk, step).start()
            return carry

        lax.fori_loop(1, count, start, 0)

    def sum_ep(chunk):
        first, size = columns[chunk]
        span = slice(first, first + size)

        def add(step, added):
            to_ep(chunk, step).wait_recv()
            return added + ep_part[step, :, span].astype(jnp.float32)

        share = lax.fori_loop(1, count, add, far_part[me, :, span].astype(jnp.float32))
        if chunk < pairs:
            for third in range(3):
                at = third * width + chunk * 128
                joint_share[:, at : at + 128] = share[:, third * 128 : third * 128 + 128]
        elif chunk == pairs:
            output_share[...] = share
        else:
            pack_share[...] = share

    shape = (devices, total // devices)

    def lower_part(number, carry):
        rows = pl.ds(pl.multiple_of(number * length, length), length)
        grad_normed_two = jnp.dot(
            chosen_of(rows),
            back[...].reshape(slot_count, width),
            preferred_element_type=jnp.float32,
        )
        _, unit, inverse = normalize(state[rows, :], gain_two)
        inner, share = normalize_back(grad_normed_two, gain_two, unit, inverse)
        grad_state = out_grad[rows, :].astype(jnp.float32) + inner
        tokens_grad[rows, :] = grad_state
        branch = grad_state.astype(jnp.bfloat16)
        branch_all[rows, :] = branch
        mixed_grads[rows, :] = times_t(
            branch, weights[:, :, joint_width : joint_width + width].reshape(total, width)
        ).astype(jnp.bfloat16)
        allowed = seen(segments[pl.ds(number, 1), :], live[pl.ds(number, 1), :], column(ints, number))
        hidden_pairs[rows, :] = jnp.where(allowed, 0.0, NEGATIVE)
        normed = normalize(tokens[rows, :].astype(jnp.float32), gain_one)[0]
        normed_all[rows, :] = normed.astype(jnp.bfloat16)
        return carry + share[None, :]

    nothing = jnp.zeros((1, width), jnp.float32)
    grad_two = lax.fori_loop(0, sequences, lower_part, nothing)
    for copy in bring[6:]:
        copy.wait()

    @pl.when(core == 0)
    def _():
        for index in range(SETTLED):
            whole(index, (sum_up, sum_down), side_x)[...] = summed_x(index)[...]
            spread(index)

    turned[...] = jnp.transpose(mixed[...])
    first, size = columns[pairs]
    part[:, :, first : first + size] = (
        jnp.dot(turned[...], branch_all[...], preferred_element_type=jnp.float32)
        .astype(jnp.bfloat16)
        .reshape(*shape, size)
    )
    to_mate(pairs, 0).start()
    to_mate(pairs, 1).start()
    turned[...] = jnp.transpose(normed_all[...])

    for pair in range(pairs):
        at = pair * 128

        def attend(number, carry, pair=pair, at=at):
            rows = pl.ds(pl.multiple_of(number * length, length), length)
            query = joint[rows, at : at + 128]
            key = joint[rows, width + at : width + at + 128]
            value = joint[rows, 2 * width + at : 2 * width + at + 128]
            grad_out = mixed_grads[rows, at : at + 128]
            unseen = hidden_pairs[rows, :]
            results = []
            for side in range(2):
                scores = times_t(query * halves[side], key) * factor
                log_all = logs[rows, 2 * pair + side : 2 * pair + side + 1]
                probs = jnp.exp(scores + unseen - log_all)
                grad_value = outer(probs.astype(jnp.bfloat16), grad_out)
                grad_probs = times_t(grad_out * halves[side], value)
                delta = jnp.sum(probs * grad_probs, axis=-1, keepdims=True)
                grad_scores = (probs * (grad_probs - delta)).astype(jnp.bfloat16)
                grad_query = jnp.dot(grad_scores, key, preferred_element_type=jnp.float32) * factor
                grad_key = outer(grad_scores, query) * factor
                results.append((grad_query, grad_key, grad_value))
            for third in range(3):
                grad_joint[rows, third * width + at : third * width + at + 128] = jnp.where(
                    half, results[0][third], results[1][third]
                ).astype(jnp.bfloat16)
            return carry

        lax.fori_loop(0, sequences, attend, 0, unroll=4)
        first, size = columns[pair]
        mine = jnp.concatenate(
            [grad_joint[:, third * width + at : third * width + at + 128] for third in range(3)], axis=1
        )
        part[:, :, first : first + size] = (
            jnp.dot(turned[...], mine, preferred_element_type=jnp.float32)
            .astype(jnp.bfloat16)
            .reshape(*shape, size)
        )
        to_mate(pair, 0).start()
        to_mate(pair, 1).start()
        sum_core(pairs if pair == 0 else pair - 1)
        if pair == 0:
            add_x(early)
            add_x(early + 1)
        elif pair == 1:
            sum_x(pairs)
        else:
            sum_x(pair - 2)
        if pair == 2:
            for index in range(SETTLED, early):
                add_home(index)
            add_x(early + 2)
            add_x(early + 3)
            sum_ep(pairs)

    def upper_part(number, carry):
        rows = pl.ds(pl.multiple_of(number * length, length), length)
        grad_normed = times_t(
            grad_joint[rows, :], weights[:, :, :joint_width].reshape(total, joint_width)
        )
        _, unit, inverse = normalize(tokens[rows, :].astype(jnp.float32), gain_one)
        inner, share = normalize_back(grad_normed, gain_one, unit, inverse)
        tokens_grad[rows, :] = tokens_grad[rows, :] + inner
        return carry + share[None, :]

    grad_one = lax.fori_loop(0, sequences, upper_part, nothing)
    leaving = (
        pltpu.make_async_copy(tokens_grad, tokens_grad_out, bring_sems.at[len(bring)]),
        pltpu.make_async_copy(output, output_out, bring_sems.at[len(bring) + 1]),
    )
    leaving[0].start()
    lines = lax.broadcasted_iota(jnp.int32, (128, width), 0)
    gain_lines = jnp.where(
        lines == count, grad_one, jnp.where(lines == count + 1, grad_two, 0.0)
    )
    first, size = columns[pairs + 1]
    part[:, :, first : first + size] = (
        (grad_router[...] + jnp.transpose(gain_lines)).astype(jnp.bfloat16).reshape(*shape, 128)
    )
    to_mate(pairs + 1, 0).start()
    to_mate(pairs + 1, 1).start()
    for index in range(SETTLED):
        pass_half(index)
    sum_core(pairs - 1)
    sum_core(pairs + 1)
    sum_x(pairs - 2)
    add_home(early)
    add_home(early + 1)
    sum_x(pairs - 1)
    sum_x(pairs + 1)
    for index in range(SETTLED, early):
        pass_half(index)
    keep.wait()

    def from_all(step, carry):
        send_ret(step).wait()
        return carry

    lax.fori_loop(1, count, from_all, 0)

    def combine(number, carry):
        rows = pl.ds(pl.multiple_of(number * length, length), length)
        gathered = jnp.dot(
            chosen_of(rows),
            returned[...].reshape(slot_count, width),
            preferred_element_type=jnp.float32,
        )
        output[rows, :] = (state[rows, :] + gathered).astype(jnp.bfloat16)
        return carry

    lax.fori_loop(0, sequences, combine, 0)
    leaving[1].start()
    add_home(early + 2)
    pass_half(early)
    pass_half(early + 1)
    add_home(early + 3)
    for chunk in range(pairs):
        sum_ep(chunk)
    sum_ep(pairs + 1)
    pass_half(early + 2)
    pass_half(early + 3)

    @pl.when(core == 0)
    def _():
        for chunk in range(CHUNKS):
            spread_x(chunk).wait_send()
            own_half(chunk).wait_send()
            other_half(chunk).wait_send()

    @pl.when(core == 1)
    def _():
        for index in range(SETTLED, CHUNKS):
            go_home(index).wait_send()
        for chunk in range(CHUNKS):
            own_half(chunk).wait_recv()
            other_half(chunk).wait_recv()

    for copy in leaving:
        copy.wait()
    for index in range(early, len(parts)):
        over_x(index).wait_send()
    for chunk in range(len(columns)):
        to_mate(chunk, 0).wait_send()
        to_mate(chunk, 1).wait_send()
        to_x(chunk).wait_send()

        def finish(step, carry, chunk=chunk):
            to_ep(chunk, step).wait_send()
            return carry

        lax.fori_loop(1, count, finish, 0)


def backward(
    tokens,
    segments,
    live,
    out_grad,
    weights,
    joint,
    mixed,
    state,
    logs,
    slots,
    back,
    ret,
    router,
    part_up,
    part_down,
    early_up,
    early_down,
):
    row_count, width = tokens.shape
    count = back.shape[0]
    devices, shard_rows, all_width = weights.shape
    hbm = pl.BlockSpec(memory_space=pltpu.HBM)
    vmem = pl.BlockSpec(memory_space=pltpu.VMEM)
    low = jnp.bfloat16
    quarter = (count, shard_rows, all_width)
    return pl.pallas_call(
        functools.partial(backward_kernel, count),
        out_shape=(
            jax.ShapeDtypeStruct((row_count, width), low),
            jax.ShapeDtypeStruct((row_count, width), jnp.float32),
            jax.ShapeDtypeStruct((shard_rows, joint.shape[1]), jnp.float32),
            jax.ShapeDtypeStruct((shard_rows, width), jnp.float32),
            jax.ShapeDtypeStruct((shard_rows, 128), jnp.float32),
            jax.ShapeDtypeStruct(part_up.shape, low),
            jax.ShapeDtypeStruct(part_down.shape, low),
        ),
        in_specs=[hbm, vmem, vmem] + [hbm] * 9 + [vmem] + [hbm] * 4,
        out_specs=(hbm,) * 2 + (vmem,) * 5,
        scratch_shapes=[
            pltpu.VMEM(array.shape, array.dtype)
            for array in (
                tokens,
                out_grad,
                weights,
                joint,
                mixed,
                state,
                logs,
                slots,
                back,
                part_up,
                part_down,
                early_up,
                early_down,
            )
        ]
        + [
            pltpu.VMEM((row_count, width), low),
            pltpu.VMEM((row_count, width), jnp.float32),
            pltpu.VMEM(back.shape, low),
            pltpu.VMEM(joint.shape, low),
            pltpu.VMEM((row_count, width), low),
            pltpu.VMEM((row_count, width), low),
            pltpu.VMEM((row_count, width), low),
            pltpu.VMEM((row_count, segments.shape[1]), jnp.float32),
            pltpu.VMEM(weights.shape, low),
            pltpu.VMEM((2,) + quarter, low),
            pltpu.VMEM((2,) + quarter, low),
            pltpu.VMEM(quarter, low),
            pltpu.VMEM(quarter, low),
            pltpu.VMEM(quarter, low),
            pltpu.VMEM((width, row_count), low),
            pltpu.VMEM(early_up.shape, low),
            pltpu.VMEM(early_down.shape, low),
            pltpu.VMEM(early_up.shape, low),
            pltpu.VMEM(early_down.shape, low),
            pltpu.VMEM((2,) + early_up.shape, low),
            pltpu.VMEM((2,) + early_down.shape, low),
            pltpu.SemaphoreType.DMA((2, count)),
            pltpu.SemaphoreType.DMA((2, HEADS // 2 + 2, 2)),
            pltpu.SemaphoreType.DMA((2, HEADS // 2 + 2)),
            pltpu.SemaphoreType.DMA((2, HEADS // 2 + 2, count)),
            pltpu.SemaphoreType.DMA((10, CHUNKS)),
            pltpu.SemaphoreType.DMA((1,)),
            pltpu.SemaphoreType.DMA((15,)),
        ],
        compiler_params=pltpu.CompilerParams(
            collective_id=4, has_side_effects=True, vmem_limit_bytes=63 * MIB
        ),
    )(
        tokens,
        segments,
        live,
        out_grad,
        weights,
        joint,
        mixed,
        state,
        logs,
        slots,
        back,
        ret,
        router,
        part_up,
        part_down,
        early_up,
        early_down,
    )


def finish_kernel(
    copied_in,
    pack,
    summed_in,
    copied_out,
    pack_out,
    summed_out,
    copied,
    narrow,
    wide,
    in_sems,
    out_sems,
    piece_sems,
):
    arrive = [
        pltpu.make_async_copy(source, target, in_sems.at[place])
        for place, (source, target) in enumerate(zip(copied_in, copied))
    ]
    leave = [
        pltpu.make_async_copy(source, target, out_sems.at[place])
        for place, (source, target) in enumerate(zip(copied, copied_out))
    ]

    def piece(layer, number):
        size = narrow[layer].shape[0] // PIECES
        rows = pl.ds(number * size, size)
        return (
            pltpu.make_async_copy(
                summed_in[layer].at[rows], narrow[layer].at[rows], piece_sems.at[0, layer, number]
            ),
            pltpu.make_async_copy(
                wide[layer].at[rows], summed_out[layer].at[rows], piece_sems.at[1, layer, number]
            ),
            rows,
        )

    pieces = [piece(layer, number) for number in range(PIECES) for layer in range(2)]
    for number, part in enumerate(pieces):
        part[0].start()
        if number < len(arrive):
            arrive[number].start()
    shard_rows = pack.shape[0]
    tall = jnp.concatenate([pack[...], jnp.zeros((128 - shard_rows, 128), jnp.float32)], axis=0)
    pack_out[...] = jnp.transpose(tall)[:16, :shard_rows]
    for number, (load, store, rows) in enumerate(pieces):
        load.wait()
        wide[number % 2][rows, :] = narrow[number % 2][rows, :].astype(jnp.float32)
        store.start()
        if number < len(arrive):
            arrive[number].wait()
            leave[number].start()
    for copy in leave:
        copy.wait()
    for _, store, _ in pieces:
        store.wait()


def finish(copied, pack, summed):
    hbm = pl.BlockSpec(memory_space=pltpu.HBM)
    vmem = pl.BlockSpec(memory_space=pltpu.VMEM)
    wide = [jax.ShapeDtypeStruct(array.shape, jnp.float32) for array in summed]
    return pl.pallas_call(
        finish_kernel,
        out_shape=(
            [jax.ShapeDtypeStruct(array.shape, array.dtype) for array in copied],
            jax.ShapeDtypeStruct((16, pack.shape[0]), jnp.float32),
            wide,
        ),
        in_specs=[[hbm] * len(copied), vmem, [hbm] * 2],
        out_specs=([hbm] * len(copied), vmem, [hbm] * 2),
        scratch_shapes=[
            [pltpu.VMEM(array.shape, array.dtype) for array in copied],
            [pltpu.VMEM(array.shape, array.dtype) for array in summed],
            [pltpu.VMEM(array.shape, jnp.float32) for array in summed],
            pltpu.SemaphoreType.DMA((len(copied),)),
            pltpu.SemaphoreType.DMA((len(copied),)),
            pltpu.SemaphoreType.DMA((2, 2, PIECES)),
        ],
        compiler_params=pltpu.CompilerParams(vmem_limit_bytes=63 * MIB),
    )(copied, pack, summed)


def per_device_fused(
    tokens,
    segments,
    patch_mask,
    choices,
    priority,
    first_gain,
    joint_weight,
    output_weight,
    second_gain,
    router_weight,
    expert_up,
    expert_down,
    out_grad,
):
    row_count, width = tokens.shape
    experts = router_weight.shape[1]
    capacity = (21 * choices.shape[1] * row_count + 20 * experts - 1) // (20 * experts)
    block = -(-capacity // 16) * 16
    weights, joint, mixed, state, sent_rows, logs, slots, router, grads, used_up, used_down = forward(
        experts,
        capacity,
        block,
        tokens,
        segments,
        patch_mask,
        choices.T,
        priority,
        out_grad,
        joint_weight,
        output_weight,
        jnp.stack([first_gain, second_gain]),
        router_weight.T,
        expert_up[0],
        expert_down[0],
    )
    back, ret, part_up, part_down, early_up, early_down, grad_router = middle(
        sent_rows, grads, expert_up[0], expert_down[0], used_up, used_down, router
    )
    output, tokens_grad, grad_joint, grad_output, grad_pack, grad_up, grad_down = backward(
        tokens,
        segments,
        patch_mask,
        out_grad,
        weights,
        joint,
        mixed,
        state,
        logs,
        slots,
        back,
        ret,
        grad_router,
        part_up,
        part_down,
        early_up,
        early_down,
    )
    (output, tokens_grad, grad_joint, grad_output), lines, (grad_up, grad_down) = finish(
        [output, tokens_grad, grad_joint, grad_output], grad_pack, [grad_up, grad_down]
    )
    return (
        output,
        tokens_grad,
        lines[experts],
        grad_joint,
        grad_output,
        lines[experts + 1],
        lines[:experts].T,
        grad_up[None],
        grad_down[None],
    )


def experts_both_ways(sent_rows, sent_grads, up, down, router):
    count, block, width = sent_rows.shape
    experts = router.shape[1]
    hidden = up.shape[1]
    router = jnp.pad(router, ((0, 0), (0, 128 - experts)))
    any_space = pl.BlockSpec(memory_space=pl.ANY)
    vmem = pl.BlockSpec(memory_space=pltpu.VMEM)
    low = jnp.bfloat16
    slots = count * block
    return pl.pallas_call(
        functools.partial(expert_kernel, count, experts),
        out_shape=(
            jax.ShapeDtypeStruct((count, block, width), low),
            jax.ShapeDtypeStruct((count, block, width), low),
            jax.ShapeDtypeStruct((width, hidden), low),
            jax.ShapeDtypeStruct((hidden, width), low),
            jax.ShapeDtypeStruct((width, 128), jnp.float32),
        ),
        in_specs=[any_space, any_space, vmem, vmem, vmem],
        out_specs=(any_space, any_space, vmem, vmem, vmem),
        scratch_shapes=[
            pltpu.VMEM((count, block, width), low),
            pltpu.VMEM((count, block, width), low),
            pltpu.VMEM((slots, width), low),
            pltpu.VMEM((slots, hidden), low),
            pltpu.VMEM((slots, hidden), low),
            pltpu.VMEM((slots, 128), low),
            pltpu.VMEM((count, block, width), low),
            pltpu.VMEM((count, block, width), low),
            pltpu.VMEM((width, slots), low),
            pltpu.SemaphoreType.DMA((8, count)),
            pltpu.SemaphoreType.DMA((4,)),
        ],
        compiler_params=pltpu.CompilerParams(
            collective_id=1, has_side_effects=True, vmem_limit_bytes=58 * MIB
        ),
        cost_estimate=pl.CostEstimate(
            flops=12 * slots * width * hidden, bytes_accessed=16 * MIB, transcendentals=0
        ),
    )(sent_rows, sent_grads, up, down, router)


def per_device(
    tokens,
    segments,
    patch_mask,
    choices,
    priority,
    first_gain,
    joint_weight,
    output_weight,
    second_gain,
    router_weight,
    expert_up,
    expert_down,
    out_grad,
):
    row_count, width = tokens.shape
    head_size = width // HEADS
    factor = head_size ** (-0.5)
    expert_count = router_weight.shape[1]
    length = segments.shape[1]
    capacity = (21 * choices.shape[1] * row_count + 20 * expert_count - 1) // (20 * expert_count)
    block_rows = min(row_count, 512)
    gain_one, joint_full, output_full, gain_two, router_full = (
        lax.all_gather(first_gain, ("grp", "ep"), axis=0, tiled=True),
        lax.all_gather(joint_weight, ("grp", "ep"), axis=0, tiled=True),
        lax.all_gather(output_weight, ("grp", "ep"), axis=0, tiled=True),
        lax.all_gather(second_gain, ("grp", "ep"), axis=0, tiled=True),
        lax.all_gather(router_weight, ("grp", "ep"), axis=0, tiled=True),
    )
    inputs = tokens.astype(jnp.float32)
    gain_one = gain_one.astype(jnp.float32)
    gain_two = gain_two.astype(jnp.float32)
    normed_f, unit_one, inverse_one = normalize(inputs, gain_one)
    normed = normed_f.astype(jnp.bfloat16)
    joint = jnp.dot(normed, joint_full, preferred_element_type=jnp.float32).astype(jnp.bfloat16)
    joint = joint.reshape(row_count, 3, HEADS, head_size)
    live = patch_mask.reshape(row_count)
    position = lax.broadcasted_iota(jnp.int32, (row_count,), 0)
    group = position // length * length + segments.reshape(row_count)
    masks = []
    mixed_parts = []
    log_parts = []
    for start in range(0, row_count, block_rows):
        allowed = visible(group[start : start + block_rows], live[start : start + block_rows])
        block = joint[start : start + block_rows]
        mixed_block, log_total = attend_forward(
            block[:, 0], block[:, 1], block[:, 2], allowed, factor
        )
        masks.append(allowed)
        mixed_parts.append(mixed_block)
        log_parts.append(log_total)
    mixed = jnp.concatenate(mixed_parts, axis=0).reshape(row_count, width).astype(jnp.bfloat16)
    state = inputs + jnp.dot(mixed, output_full, preferred_element_type=jnp.float32)
    normed_two_f, unit_two, inverse_two = normalize(state, gain_two)
    normed_two = normed_two_f.astype(jnp.bfloat16)
    slot_one, slot_two = route(
        choices, live, priority.reshape(row_count), expert_count, capacity
    )
    block = -(-capacity // 16) * 16
    slots = expert_count * block
    index = lax.broadcasted_iota(jnp.int32, (slots, row_count), 0)
    chosen = ((index == slot_one[None, :]) | (index == slot_two[None, :])).astype(jnp.bfloat16)
    spread = lambda values: (
        jnp.dot(chosen, values, preferred_element_type=jnp.float32)
        .astype(jnp.bfloat16)
        .reshape(expert_count, block, width)
    )
    collect = lambda values: outer(chosen, values.reshape(slots, width))
    grad = out_grad.astype(jnp.float32)
    back, returned, grad_up, grad_down, grad_router = experts_both_ways(
        spread(normed_two), spread(out_grad), expert_up[0], expert_down[0], router_full
    )
    output = (state + collect(returned)).astype(jnp.bfloat16)
    grad_router = grad_router[:, :expert_count]
    grad_normed_two = collect(back)
    grad_state_in, grad_gain_two = normalize_back(grad_normed_two, gain_two, unit_two, inverse_two)
    grad_state = grad + grad_state_in
    grad_branch = grad_state.astype(jnp.bfloat16)
    grad_output_w = outer(mixed, grad_branch)
    grad_mixed = (
        times_t(grad_branch, output_full).astype(jnp.bfloat16).reshape(row_count, HEADS, head_size)
    )
    grad_parts = []
    for number, start in enumerate(range(0, row_count, block_rows)):
        block = joint[start : start + block_rows]
        grad_parts.append(
            attend_backward(
                block[:, 0],
                block[:, 1],
                block[:, 2],
                masks[number],
                log_parts[number],
                grad_mixed[start : start + block_rows],
                factor,
            )
        )
    grad_joint = (
        jnp.concatenate(grad_parts, axis=0).reshape(row_count, 3 * width).astype(jnp.bfloat16)
    )
    grad_joint_w = outer(normed, grad_joint)
    grad_normed = times_t(grad_joint, joint_full)
    grad_inputs_in, grad_gain_one = normalize_back(grad_normed, gain_one, unit_one, inverse_one)
    tokens_grad = grad_state + grad_inputs_in
    shares = (
        lax.psum_scatter(grad_gain_one, ("grp", "ep"), scatter_dimension=0, tiled=True),
        lax.psum_scatter(grad_joint_w, ("grp", "ep"), scatter_dimension=0, tiled=True),
        lax.psum_scatter(grad_output_w, ("grp", "ep"), scatter_dimension=0, tiled=True),
        lax.psum_scatter(grad_gain_two, ("grp", "ep"), scatter_dimension=0, tiled=True),
        lax.psum_scatter(grad_router, ("grp", "ep"), scatter_dimension=0, tiled=True),
    )
    grad_up, grad_down = (
        lax.psum(grad_up, "grp").astype(jnp.float32)[None],
        lax.psum(grad_down, "grp").astype(jnp.float32)[None],
    )
    return (
        output,
        tokens_grad,
        shares[0],
        shares[1],
        shares[2],
        shares[3],
        shares[4],
        grad_up,
        grad_down,
    )


def solution(mesh):
    in_specs = (
        P(("grp", "ep"), None),
        P(("grp", "ep"), None),
        P(("grp", "ep"), None),
        P(("grp", "ep"), None),
        P(("grp", "ep"), None),
        P(("grp", "ep")),
        P(("grp", "ep"), None),
        P(("grp", "ep"), None),
        P(("grp", "ep")),
        P(("grp", "ep"), None),
        P("ep", None, None),
        P("ep", None, None),
        P(("grp", "ep"), None),
    )
    out_specs = (
        P(("grp", "ep"), None),
        P(("grp", "ep"), None),
        P(("grp", "ep")),
        P(("grp", "ep"), None),
        P(("grp", "ep"), None),
        P(("grp", "ep")),
        P(("grp", "ep"), None),
        P("ep", None, None),
        P("ep", None, None),
    )
    fused = mesh.shape["grp"] == 4 and mesh.shape["ep"] == 8
    return jax.shard_map(
        per_device_fused if fused else per_device, mesh=mesh, in_specs=in_specs, out_specs=out_specs, check_vma=False
    )
```

```python
import functools

import jax
import jax.numpy as jnp
from jax import lax
from jax.experimental import pallas as pl
from jax.experimental.pallas import tpu as pltpu
from jax.sharding import PartitionSpec as P

MESH = pl.DeviceIdType.MESH
MIB = 1 << 20
PIECES = 4
CHUNKS = 2 * PIECES
EARLY = ((0, 0), (0, 1), (1, 0), (1, 1))
SETTLED = 2
LATE = ((0, 2), (0, 3), (1, 2), (1, 3))

HEADS = 8


EPSILON = 1e-06
NEGATIVE = -1e30


def normalize(values, gain):
    mean = jnp.mean(values, axis=-1, keepdims=True)
    centred = values - mean
    inverse = lax.rsqrt(jnp.mean(centred * centred, axis=-1, keepdims=True) + EPSILON)
    unit = centred * inverse
    return (unit * gain, unit, inverse)


def normalize_back(incoming, gain, unit, inverse):
    scaled = incoming * gain
    inner = (
        scaled
        - jnp.mean(scaled, axis=-1, keepdims=True)
        - unit * jnp.mean(scaled * unit, axis=-1, keepdims=True)
    )
    return (inverse * inner, jnp.sum(incoming * unit, axis=0))


def outer(left, right):
    return lax.dot_general(
        left, right, (((0,), (0,)), ((), ())), preferred_element_type=jnp.float32
    )


def times_t(left, right):
    return lax.dot_general(
        left, right, (((1,), (1,)), ((), ())), preferred_element_type=jnp.float32
    )


def route(picks, live, ranks, expert_count, capacity):
    row_count = picks.shape[0]
    labels = lax.broadcasted_iota(jnp.int32, (row_count, expert_count), 1)
    first = (picks[:, 0:1] == labels).astype(jnp.int32)
    second = (picks[:, 1:2] == labels).astype(jnp.int32)
    live_col = live[:, None]
    earlier = (ranks[None, :] < ranks[:, None]).astype(jnp.int32)
    first_live = first * live_col
    second_live = second * live_col
    place_one = jnp.sum(
        jnp.dot(earlier, first_live, preferred_element_type=jnp.int32) * first, axis=1
    )
    ahead = (
        jnp.dot(earlier, second_live, preferred_element_type=jnp.int32)
        + jnp.sum(first_live, axis=0)[None, :]
    )
    place_two = jnp.sum(ahead * second, axis=1)
    keep_one = (live > 0) & (place_one < capacity)
    keep_two = (live > 0) & (place_two < capacity)
    stride = -(-capacity // 16) * 16
    dummy = expert_count * stride
    slot_one = jnp.where(keep_one, picks[:, 0] * stride + place_one, dummy)
    slot_two = jnp.where(keep_two, picks[:, 1] * stride + place_two, dummy)
    return (slot_one, slot_two)


def visible(group, live):
    rows = group.shape[0]
    index = lax.broadcasted_iota(jnp.int32, (rows, rows), 0)
    other = lax.broadcasted_iota(jnp.int32, (rows, rows), 1)
    return (group[:, None] == group[None, :]) & ((live[None, :] > 0) | (index == other))


def attend_forward(query, key, value, allowed, factor):
    scores = jnp.einsum("qhd,khd->hqk", query, key, preferred_element_type=jnp.float32) * factor
    masked = jnp.where(allowed[None], scores, NEGATIVE)
    top = jnp.max(masked, axis=-1, keepdims=True)
    weights = jnp.exp(masked - top)
    total = jnp.sum(weights, axis=-1, keepdims=True)
    probs = (weights / total).astype(jnp.bfloat16)
    mixed = jnp.einsum("hqk,khd->qhd", probs, value, preferred_element_type=jnp.float32)
    return (mixed, top + jnp.log(total))


def attend_backward(query, key, value, allowed, log_total, grad_mixed, factor):
    scores = jnp.einsum("qhd,khd->hqk", query, key, preferred_element_type=jnp.float32) * factor
    masked = jnp.where(allowed[None], scores, NEGATIVE)
    probs = jnp.exp(masked - log_total)
    grad_value = jnp.einsum(
        "hqk,qhd->khd", probs.astype(jnp.bfloat16), grad_mixed, preferred_element_type=jnp.float32
    )
    grad_probs = jnp.einsum("qhd,khd->hqk", grad_mixed, value, preferred_element_type=jnp.float32)
    delta = jnp.sum(probs * grad_probs, axis=-1, keepdims=True)
    grad_scores = (probs * (grad_probs - delta)).astype(jnp.bfloat16)
    grad_query = (
        jnp.einsum("hqk,khd->qhd", grad_scores, key, preferred_element_type=jnp.float32) * factor
    )
    grad_key = (
        jnp.einsum("hqk,qhd->khd", grad_scores, query, preferred_element_type=jnp.float32) * factor
    )
    return jnp.stack([grad_query, grad_key, grad_value], axis=1)


def partner(me, step, count):
    other, bit = 0, 1
    while bit < count:
        other = other + bit * lax.rem(lax.div(me, bit) + lax.div(step, bit), 2)
        bit *= 2
    return other


def expert_kernel(
    count,
    experts,
    sent_rows,
    sent_grads,
    up_ref,
    down_ref,
    router_ref,
    back_ref,
    ret_ref,
    grad_up_ref,
    grad_down_ref,
    grad_router_ref,
    rows,
    grads,
    gated,
    act,
    grad_pre,
    logit_grads,
    out_grads,
    out_ret,
    turned,
    sems,
    local_sem,
):
    me = lax.axis_index("ep")
    block, width = rows.shape[1:]
    hidden = up_ref.shape[1]
    chunk = 512
    barrier = pltpu.get_barrier_semaphore()

    def greet(step, carry):
        pl.semaphore_signal(
            barrier, inc=1, device_id={"ep": partner(me, step, count)}, device_id_type=MESH
        )
        return carry

    lax.fori_loop(1, count, greet, 0)
    pl.semaphore_wait(barrier, count - 1)

    def remote(kind, source, target, step):
        return pltpu.make_async_remote_copy(
            src_ref=source,
            dst_ref=target,
            send_sem=sems.at[2 * kind, step],
            recv_sem=sems.at[2 * kind + 1, step],
            device_id={"ep": partner(me, step, count)},
            device_id_type=MESH,
        )

    def send_rows(step):
        return remote(0, sent_rows.at[partner(me, step, count)], rows.at[step], step)

    def send_grads(step):
        return remote(1, sent_grads.at[partner(me, step, count)], grads.at[step], step)

    def send_back(step):
        return remote(2, out_grads.at[step], back_ref.at[me], step)

    def send_ret(step):
        return remote(3, out_ret.at[step], ret_ref.at[me], step)

    own = [
        pltpu.make_async_copy(sent_rows.at[me], rows.at[0], local_sem.at[0]),
        pltpu.make_async_copy(sent_grads.at[me], grads.at[0], local_sem.at[1]),
        pltpu.make_async_copy(out_grads.at[0], back_ref.at[me], local_sem.at[2]),
        pltpu.make_async_copy(out_ret.at[0], ret_ref.at[me], local_sem.at[3]),
    ]
    own[0].start()
    own[1].start()

    def start(step, carry):
        send_rows(step).start()
        send_grads(step).start()
        return carry

    lax.fori_loop(1, count, start, 0)
    own[0].wait()
    own[1].wait()
    lanes = lax.broadcasted_iota(jnp.int32, (block, router_ref.shape[1]), 1)

    def one_block(step, carry):
        @pl.when(step > 0)
        def _():
            send_rows(step).wait_recv()
            send_grads(step).wait_recv()

        mine = rows[step]
        cotangent = grads[step].astype(jnp.float32)
        place = pl.ds(pl.multiple_of(step * block, 16), block)
        logits = jnp.dot(mine, router_ref[...], preferred_element_type=jnp.float32)
        logits = jnp.where(lanes < experts, logits, NEGATIVE)
        weights = jnp.exp(logits - jnp.max(logits, axis=1, keepdims=True))
        gate_all = weights / jnp.sum(weights, axis=1, keepdims=True)
        here = (lanes == me).astype(jnp.float32)
        gate = jnp.sum(gate_all * here, axis=1, keepdims=True)
        pair = (gate * cotangent).astype(jnp.bfloat16)
        gated[place, :] = pair
        ret = jnp.zeros((block, width), jnp.float32)
        back = jnp.zeros((block, width), jnp.float32)
        for first in range(0, hidden, chunk):
            span = slice(first, first + chunk)
            pre = jnp.dot(mine, up_ref[:, span], preferred_element_type=jnp.float32)
            cdf = 0.5 * (1.0 + lax.erf(pre * 0.7071067811865476))
            density = jnp.exp(-0.5 * pre * pre) * 0.3989422804014327
            low = (pre * cdf).astype(jnp.bfloat16)
            act[place, span] = low
            ret = ret + jnp.dot(low, down_ref[span, :], preferred_element_type=jnp.float32)
            grad_act = times_t(pair, down_ref[span, :])
            slope = (grad_act * (cdf + pre * density)).astype(jnp.bfloat16)
            grad_pre[place, span] = slope
            back = back + times_t(slope, up_ref[:, span])
        ret = ret.astype(jnp.bfloat16).astype(jnp.float32)
        out_ret[step] = (gate * ret).astype(jnp.bfloat16)
        gate_grad = jnp.sum(cotangent * ret, axis=1, keepdims=True)
        low_logits = (gate * gate_grad * (here - gate_all)).astype(jnp.bfloat16)
        logit_grads[place, :] = low_logits
        back = back + times_t(low_logits, router_ref[...])
        out_grads[step] = back.astype(jnp.bfloat16)

        @pl.when(step > 0)
        def _():
            send_back(step).start()

        @pl.when(step == 0)
        def _():
            own[2].start()

        return carry

    lax.fori_loop(0, count, one_block, 0)
    own[3].start()

    def start_ret(step, carry):
        send_ret(step).start()
        return carry

    lax.fori_loop(1, count, start_ret, 0)
    turned[...] = jnp.transpose(rows[...].reshape(count * block, width))
    grad_router_ref[...] = jnp.dot(
        turned[...], logit_grads[...], preferred_element_type=jnp.float32
    )

    def up_chunk(index, carry):
        span = pl.ds(pl.multiple_of(index * chunk, chunk), chunk)
        grad_up_ref[:, span] = jnp.dot(
            turned[...], grad_pre[:, span], preferred_element_type=jnp.float32
        ).astype(jnp.bfloat16)
        return carry

    lax.fori_loop(0, hidden // chunk, up_chunk, 0)
    turned[...] = jnp.transpose(gated[...])

    def down_chunk(index, carry):
        span = pl.ds(pl.multiple_of(index * chunk, chunk), chunk)
        part = jnp.dot(turned[...], act[:, span], preferred_element_type=jnp.float32)
        grad_down_ref[span, :] = jnp.transpose(part).astype(jnp.bfloat16)
        return carry

    lax.fori_loop(0, hidden // chunk, down_chunk, 0)

    def finish(step, carry):
        send_rows(step).wait_send()
        send_grads(step).wait_send()
        send_back(step).wait()
        send_ret(step).wait()
        return carry

    lax.fori_loop(1, count, finish, 0)
    own[2].wait()
    own[3].wait()


def column(values, lane):
    lanes = lax.broadcasted_iota(jnp.int32, values.shape, 1)
    return jnp.sum(jnp.where(lanes == lane, values, 0), axis=1, keepdims=True)


def core_peer(grp):
    return grp + 1 - 2 * lax.rem(grp, 2)


def x_peer(grp):
    return lax.rem(grp + 2, 4)


def flags(condition):
    return jnp.where(condition, 1.0, 0.0).astype(jnp.bfloat16)


def remote_copy(source, target, send_sem, recv_sem, device):
    return pltpu.make_async_remote_copy(
        src_ref=source,
        dst_ref=target,
        send_sem=send_sem,
        recv_sem=recv_sem,
        device_id=device,
        device_id_type=MESH,
    )


def expert_of(me, grp, count):
    half = count // 2
    other = lax.rem(lax.div(me, half) + lax.rem(grp, 2), 2)
    return lax.rem(me, half) + half * other


def seat(me, grp, step, count):
    half = count // 2
    core = lax.rem(lax.rem(grp, 2) + lax.div(step, half), 2)
    return {
        "grp": 2 * lax.div(grp, 2) + core,
        "ep": partner(me, lax.rem(step, half), count),
    }


def visit(index, count):
    return lax.div(index, 2) + (count // 2) * lax.rem(index, 2)


def greet_all(count, me, grp):
    barrier = pltpu.get_barrier_semaphore()
    half = count // 2

    def greet(step, carry):
        device = {"grp": grp, "ep": partner(me, step, count)}
        pl.semaphore_signal(barrier, inc=1, device_id=device, device_id_type=MESH)
        return carry

    lax.fori_loop(1, count, greet, 0)

    def greet_mate(step, carry):
        device = {"grp": core_peer(grp), "ep": partner(me, step, count)}
        pl.semaphore_signal(barrier, inc=1, device_id=device, device_id_type=MESH)
        return carry

    lax.fori_loop(0, half + 1, greet_mate, 0)
    pl.semaphore_signal(barrier, inc=1, device_id={"grp": x_peer(grp)}, device_id_type=MESH)
    pl.semaphore_wait(barrier, count + half + 1)


def pieces_of(layer_rows):
    def rows(chunk, side):
        size = layer_rows[chunk // PIECES] // (2 * PIECES)
        first = side * PIECES * size + (chunk % PIECES) * size
        return pl.ds(pl.multiple_of(first, size), size)

    return rows


def up_piece(piece, side, side_rows, columns):
    rows = pl.ds(pl.multiple_of(side * side_rows, side_rows), side_rows)
    return rows, pl.ds(piece * columns, columns)


def down_piece(piece, side, size):
    return pl.ds(pl.multiple_of(piece * 2 * size + side * size, size), size)


def seen(segment_row, live_row, segment_col):
    length = segment_row.shape[1]
    index = lax.broadcasted_iota(jnp.int32, (length, length), 0)
    other = lax.broadcasted_iota(jnp.int32, (length, length), 1)
    return (segment_col == segment_row) & ((live_row > 0) | (index == other))


def forward_kernel(
    count,
    capacity,
    tokens_in,
    segments,
    live,
    picks,
    ranks,
    out_grad_in,
    joint_shard,
    output_shard,
    gains_shard,
    router_shard,
    own_up,
    own_down,
    weights_out,
    joint_out,
    mixed_out,
    state_out,
    rows_out,
    logs_out,
    slots_out,
    router_out,
    grads,
    used_up,
    used_down,
    tokens,
    out_grad,
    weights,
    joint,
    mixed,
    state,
    sent_rows,
    logs,
    slots,
    own_grads,
    normed_two,
    int_columns,
    ep_sems,
    x_sems,
    core_sems,
    grad_sems,
    fetch_sems,
    local_sems,
    move_sems,
):
    me, grp = lax.axis_index("ep"), lax.axis_index("grp")
    expert = expert_of(me, grp, count)
    core, side_x = lax.rem(grp, 2), lax.div(grp, 2)
    half_ep = count // 2
    row_count, width = tokens.shape
    sequences, length = segments.shape
    block = sent_rows.shape[1]
    moves = {
        name: pltpu.make_async_copy(source, target, move_sems.at[place])
        for place, (name, source, target) in enumerate(
            (
                ("out_grad", out_grad_in, out_grad),
                ("tokens", tokens_in, tokens),
                ("slots", slots, slots_out),
                ("weights", weights, weights_out),
                ("joint", joint, joint_out),
                ("mixed", mixed, mixed_out),
                ("state", state, state_out),
                ("logs", logs, logs_out),
                ("rows", sent_rows, rows_out),
            )
        )
    }
    moves["out_grad"].start()
    moves["tokens"].start()
    joint_width = joint.shape[1]
    head_size = width // HEADS
    factor = head_size ** (-0.5)
    mate, across = core_peer(grp), x_peer(grp)
    greet_all(count, me, grp)

    def shard(owner_grp, owner):
        return weights.at[owner_grp * count + owner]

    def to_ep(step):
        place = shard(grp, me)
        other = partner(me, step, count)
        return remote_copy(place, place, ep_sems.at[0, step], ep_sems.at[1, step], {"ep": other})

    def relay(step):
        place = shard(grp, partner(me, half_ep, count))
        sems = ep_sems.at[0, half_ep + step], ep_sems.at[1, half_ep + step]
        return remote_copy(place, place, *sems, {"ep": partner(me, step, count)})

    def to_x(step):
        place = shard(grp, partner(me, step, count))
        return remote_copy(place, place, x_sems.at[0, step], x_sems.at[1, step], {"grp": across})

    def to_core(owner_grp, part, step):
        place = shard(owner_grp, partner(me, step, count))
        sems = core_sems.at[0, part, step], core_sems.at[1, part, step]
        return remote_copy(place, place, *sems, {"grp": mate})

    def send_grads(step):
        return remote_copy(
            own_grads.at[step],
            grads.at[step],
            grad_sems.at[0, step],
            grad_sems.at[1, step],
            seat(me, grp, step, count),
        )

    layers = ((own_up, used_up), (own_down, used_down))
    rows_at = pieces_of((own_up.shape[0], own_down.shape[0]))

    def fetch(chunk):
        source, target = layers[chunk // PIECES]
        place = rows_at(chunk, side_x)
        sems = fetch_sems.at[0, chunk], fetch_sems.at[1, chunk]
        device = {"grp": mate, "ep": partner(me, half_ep, count)}
        return remote_copy(source.at[place], target.at[place], *sems, device)

    def share_fetch(chunk):
        place = layers[chunk // PIECES][1].at[rows_at(chunk, side_x)]
        sems = fetch_sems.at[2, chunk], fetch_sems.at[3, chunk]
        return remote_copy(place, place, *sems, {"grp": across})

    far_steps = [step for step in range(count) if step % half_ep >= half_ep // 2]

    def advance_grads(index):
        send_grads(far_steps[index]).wait_send()
        if index + 1 < len(far_steps):
            send_grads(far_steps[index + 1]).start()

    def advance(chunk):
        @pl.when(core == 0)
        def _():
            fetch(chunk).wait_send()
            if chunk + 3 < CHUNKS:
                fetch(chunk + 3).start()

        @pl.when(core == 1)
        def _():
            fetch(chunk).wait_recv()
            share_fetch(chunk).start()

    mine = grp * count + me
    fill = [
        pltpu.make_async_copy(
            joint_shard, weights.at[mine, :, pl.ds(0, joint_width)], local_sems.at[0]
        ),
        pltpu.make_async_copy(
            output_shard, weights.at[mine, :, pl.ds(joint_width, width)], local_sems.at[1]
        ),
    ]
    for copy in fill:
        copy.start()
    shard_rows = weights.shape[1]
    stacked = jnp.concatenate(
        [
            router_shard[...].astype(jnp.float32),
            gains_shard[...].astype(jnp.float32),
            jnp.zeros((16 - count - 2, shard_rows), jnp.float32),
        ],
        axis=0,
    ).astype(jnp.bfloat16)
    tile = (16, 128)
    diagonal = flags(
        lax.broadcasted_iota(jnp.int32, tile, 0) == lax.broadcasted_iota(jnp.int32, tile, 1)
    )
    weights[mine, :, joint_width + width :] = outer(stacked, diagonal).astype(jnp.bfloat16)
    for copy in fill:
        copy.wait()

    def first_hop(step, carry):
        to_ep(step).start()
        return carry

    lax.fori_loop(1, half_ep + 1, first_hop, 0)
    to_x(0).start()
    to_core(grp, 0, 0).start()

    @pl.when(core == 0)
    def _():
        fetch(0).start()
        fetch(1).start()
        fetch(2).start()

    ints = jnp.concatenate([segments[...], live[...]], axis=0).astype(jnp.float32)
    turned = jnp.transpose(ints)
    int_columns[...] = turned.astype(jnp.int32)
    live_col = jnp.concatenate(
        [turned[:, sequences + i : sequences + i + 1] for i in range(sequences)], axis=0
    )
    rank_row = ranks[...].astype(jnp.float32)
    lines = jnp.concatenate(
        [rank_row, picks[...].astype(jnp.float32), jnp.zeros((5, row_count), jnp.float32)], axis=0
    )
    token_columns = jnp.transpose(lines)
    rank_col = token_columns[:, 0:1]
    earlier = flags(rank_row < rank_col)
    first = token_columns[:, 1:2].astype(jnp.int32)
    second = token_columns[:, 2:3].astype(jnp.int32)
    lanes = lax.broadcasted_iota(jnp.int32, (row_count, 128), 1)
    one = jnp.where(lanes == first, 1.0, 0.0)
    two = jnp.where(lanes == second + count, 1.0, 0.0)
    counts = jnp.dot(
        earlier, ((one + two) * live_col).astype(jnp.bfloat16), preferred_element_type=jnp.float32
    )
    ahead = jnp.sum(jnp.where(lanes == first + count, live_col, 0.0), axis=0, keepdims=True)
    place_one = jnp.sum(counts * one, axis=1, keepdims=True)
    place_two = jnp.sum((counts + ahead) * two, axis=1, keepdims=True)
    nowhere = 1.0 * count * block
    slot_one = jnp.where(
        (live_col > 0) & (place_one < capacity),
        first.astype(jnp.float32) * block + place_one,
        nowhere,
    )
    slot_two = jnp.where(
        (live_col > 0) & (place_two < capacity),
        second.astype(jnp.float32) * block + place_two,
        nowhere,
    )
    both = jnp.where(lanes == 0, slot_one, jnp.where(lanes == 1, slot_two, nowhere))
    slots[...] = both.astype(jnp.int32)
    moves["slots"].start()
    moves["out_grad"].wait()
    slot_rows = jnp.transpose(both)[0:8].astype(jnp.int32)
    row_one, row_two = slot_rows[0:1], slot_rows[1:2]

    def rows_of(number, values):
        index = lax.broadcasted_iota(jnp.int32, (block, row_count), 0) + number * block
        chosen = flags((index == row_one) | (index == row_two))
        return jnp.dot(chosen, values[...], preferred_element_type=jnp.float32).astype(jnp.bfloat16)

    def spread_grads(index, carry):
        step = visit(index, count)
        own_grads[step] = rows_of(partner(expert, step, count), out_grad)

        @pl.when((step > 0) & (lax.rem(step, half_ep) < half_ep // 2))
        def _():
            send_grads(step).start()

        return carry

    lax.fori_loop(0, count, spread_grads, 0)
    send_grads(far_steps[0]).start()
    keep = pltpu.make_async_copy(own_grads.at[0], grads.at[0], local_sems.at[3])
    keep.start()

    to_ep(half_ep).wait_recv()

    def pass_far(step, carry):
        relay(step).start()
        return carry

    lax.fori_loop(1, half_ep, pass_far, 0)
    to_x(half_ep).start()
    to_core(grp, 0, half_ep).start()

    def pass_on(step, carry):
        @pl.when(step != half_ep)
        def _():
            to_ep(step).wait_recv()
            to_x(step).start()
            to_core(grp, 0, step).start()

        return carry

    lax.fori_loop(1, count, pass_on, 0)

    def pass_further(step, carry):
        to_x(step).wait_recv()
        to_core(across, 1, step).start()
        return carry

    lax.fori_loop(0, count, pass_further, 0)

    def arrive(step, carry):
        to_core(mate, 0, step).wait_recv()
        to_core(x_peer(mate), 1, step).wait_recv()
        return carry

    lax.fori_loop(0, count, arrive, 0)
    advance(0)
    advance_grads(0)

    moves["weights"].start()
    moves["tokens"].wait()
    devices = weights.shape[0]
    total = devices * weights.shape[1]
    pack = weights[:, :, joint_width + width :].reshape(total, 128)
    router_out[...] = pack
    gains = jnp.transpose(pack.astype(jnp.float32))
    gain_one = gains[count : count + 1]
    gain_two = gains[count + 1 : count + 2]
    half = lax.broadcasted_iota(jnp.int32, (length, 128), 1) < head_size
    halves = (flags(half), flags(jnp.logical_not(half)))

    def attend(number, carry):
        rows = pl.ds(pl.multiple_of(number * length, length), length)
        values = tokens[rows, :].astype(jnp.float32)
        normed = normalize(values, gain_one)[0].astype(jnp.bfloat16)
        joint[rows, :] = jnp.dot(
            normed,
            weights[:, :, :joint_width].reshape(total, joint_width),
            preferred_element_type=jnp.float32,
        ).astype(jnp.bfloat16)
        allowed = seen(
            segments[pl.ds(number, 1), :], live[pl.ds(number, 1), :], column(int_columns[...], number)
        )
        log_all = jnp.zeros((length, 128), jnp.float32)
        log_lanes = lax.broadcasted_iota(jnp.int32, (length, 128), 1)
        for pair in range(HEADS // 2):
            at = pair * 128
            query = joint[rows, at : at + 128]
            key = joint[rows, width + at : width + at + 128]
            value = joint[rows, 2 * width + at : 2 * width + at + 128]
            results = []
            for side in range(2):
                scores = times_t(query * halves[side], key) * factor
                masked = jnp.where(allowed, scores, NEGATIVE)
                top = jnp.max(masked, axis=-1, keepdims=True)
                powers = jnp.exp(masked - top)
                added = jnp.sum(powers, axis=-1, keepdims=True)
                probs = (powers * (1.0 / added)).astype(jnp.bfloat16)
                results.append(jnp.dot(probs, value, preferred_element_type=jnp.float32))
                log_all = jnp.where(log_lanes == 2 * pair + side, top + jnp.log(added), log_all)
            mixed[rows, at : at + 128] = jnp.where(half, results[0], results[1]).astype(jnp.bfloat16)
        logs[rows, :] = log_all
        after = values + jnp.dot(
            mixed[rows, :],
            weights[:, :, joint_width : joint_width + width].reshape(total, width),
            preferred_element_type=jnp.float32,
        )
        state[rows, :] = after
        normed_two[rows, :] = normalize(after, gain_two)[0].astype(jnp.bfloat16)
        for place in range(sequences):

            @pl.when(number == place)
            def _(place=place):
                advance(place + 1)
                if place % 2 == 1:
                    advance_grads((place + 1) // 2)

        return carry

    lax.fori_loop(0, sequences, attend, 0)
    for name in ("joint", "mixed", "state", "logs"):
        moves[name].start()

    def spread_rows(number, carry):
        sent_rows[number] = rows_of(number, normed_two)
        return carry

    lax.fori_loop(0, count, spread_rows, 0)
    moves["rows"].start()

    for chunk in range(sequences + 1, CHUNKS):
        advance(chunk)
    advance_grads(3)

    @pl.when(core == 1)
    def _():
        for chunk in range(CHUNKS):
            share_fetch(chunk).wait()

    for name in ("slots", "weights", "joint", "mixed", "state", "logs", "rows"):
        moves[name].wait()
    keep.wait()
    to_x(0).wait_send()
    to_core(grp, 0, 0).wait_send()
    to_core(across, 1, 0).wait_send()

    def finish(step, carry):
        to_ep(step).wait_send()
        to_x(step).wait_send()
        to_core(grp, 0, step).wait_send()
        to_core(across, 1, step).wait_send()
        send_grads(step).wait_recv()

        @pl.when(lax.rem(step, half_ep) < half_ep // 2)
        def _():
            send_grads(step).wait_send()

        return carry

    lax.fori_loop(1, count, finish, 0)


def forward(
    count,
    capacity,
    block,
    tokens,
    segments,
    live,
    picks,
    ranks,
    out_grad,
    joint,
    output,
    gains,
    router,
    up,
    down,
):
    row_count, width = tokens.shape
    devices = width // joint.shape[0]
    all_width = joint.shape[1] + width + 128
    hbm = pl.BlockSpec(memory_space=pltpu.HBM)
    vmem = pl.BlockSpec(memory_space=pltpu.VMEM)
    low = jnp.bfloat16
    return pl.pallas_call(
        functools.partial(forward_kernel, count, capacity),
        out_shape=(
            jax.ShapeDtypeStruct((devices, joint.shape[0], all_width), low),
            jax.ShapeDtypeStruct((row_count, joint.shape[1]), low),
            jax.ShapeDtypeStruct((row_count, width), low),
            jax.ShapeDtypeStruct((row_count, width), jnp.float32),
            jax.ShapeDtypeStruct((count, block, width), low),
            jax.ShapeDtypeStruct((row_count, 128), jnp.float32),
            jax.ShapeDtypeStruct((row_count, 128), jnp.int32),
            jax.ShapeDtypeStruct((width, 128), low),
            jax.ShapeDtypeStruct((count, block, width), low),
            jax.ShapeDtypeStruct(up.shape, low),
            jax.ShapeDtypeStruct(down.shape, low),
        ),
        in_specs=[hbm] + [vmem] * 4 + [hbm] * 3 + [vmem] * 2 + [hbm] * 2,
        out_specs=(hbm,) * 7 + (vmem,) + (hbm,) * 3,
        scratch_shapes=[
            pltpu.VMEM(tokens.shape, low),
            pltpu.VMEM(out_grad.shape, low),
            pltpu.VMEM((devices, joint.shape[0], all_width), low),
            pltpu.VMEM((row_count, joint.shape[1]), low),
            pltpu.VMEM((row_count, width), low),
            pltpu.VMEM((row_count, width), jnp.float32),
            pltpu.VMEM((count, block, width), low),
            pltpu.VMEM((row_count, 128), jnp.float32),
            pltpu.VMEM((row_count, 128), jnp.int32),
            pltpu.VMEM((count, block, width), low),
            pltpu.VMEM((row_count, width), low),
            pltpu.VMEM((segments.shape[1], 2 * segments.shape[0]), jnp.int32),
            pltpu.SemaphoreType.DMA((2, count)),
            pltpu.SemaphoreType.DMA((2, count)),
            pltpu.SemaphoreType.DMA((2, 2, count)),
            pltpu.SemaphoreType.DMA((2, count)),
            pltpu.SemaphoreType.DMA((4, CHUNKS)),
            pltpu.SemaphoreType.DMA((4,)),
            pltpu.SemaphoreType.DMA((9,)),
        ],
        compiler_params=pltpu.CompilerParams(
            collective_id=2, has_side_effects=True, vmem_limit_bytes=63 * MIB
        ),
    )(
        tokens,
        segments,
        live,
        picks,
        ranks,
        out_grad,
        joint,
        output,
        gains,
        router,
        up,
        down,
    )


def middle_kernel(
    count,
    sent_rows,
    grads_in,
    own_up,
    own_down,
    used_up,
    used_down,
    router_ref,
    back_ref,
    out_ret,
    part_up,
    part_down,
    early_up,
    early_down,
    grad_router_ref,
    grads,
    rows,
    gated,
    act,
    grad_pre,
    logit_grads,
    out_grads,
    turned,
    turned_gated,
    up_ref,
    down_ref,
    ret_sums,
    back_sums,
    x_up,
    x_down,
    half_up,
    far_up,
    sems,
    x_sems,
    local_sem,
):
    me, grp = lax.axis_index("ep"), lax.axis_index("grp")
    expert = expert_of(me, grp, count)
    block, width = rows.shape[1:]
    hidden = up_ref.shape[1]
    chunk = 512

    bring = pltpu.make_async_copy(grads_in, grads, local_sem.at[4])
    bring.start()

    def load(up, down):
        return (
            pltpu.make_async_copy(up, up_ref, local_sem.at[2]),
            pltpu.make_async_copy(down, down_ref, local_sem.at[3]),
        )

    @pl.when(lax.rem(grp, 2) == 0)
    def _():
        for copy in load(own_up, own_down):
            copy.start()

    @pl.when(lax.rem(grp, 2) == 1)
    def _():
        for copy in load(used_up, used_down):
            copy.start()

    greet_all(count, me, grp)

    def send_rows(step):
        other = partner(expert, step, count)
        there = seat(me, grp, step, count)
        return remote_copy(
            sent_rows.at[other], rows.at[step], sems.at[0, step], sems.at[1, step], there
        )

    def send_back(step):
        there = seat(me, grp, step, count)
        return remote_copy(
            out_grads.at[step], back_ref.at[expert], sems.at[2, step], sems.at[3, step], there
        )

    own = [
        pltpu.make_async_copy(sent_rows.at[expert], rows.at[0], local_sem.at[0]),
        pltpu.make_async_copy(out_grads.at[0], back_ref.at[expert], local_sem.at[1]),
    ]
    own[0].start()

    def start(index, carry):
        send_rows(visit(index, count)).start()
        return carry

    lax.fori_loop(1, count, start, 0)
    own[0].wait()
    for copy in load(used_up, used_down):
        copy.wait()
    bring.wait()
    lanes = lax.broadcasted_iota(jnp.int32, (block, router_ref.shape[1]), 1)

    across, side_x = x_peer(grp), lax.div(grp, 2)
    part_hidden = hidden // 2
    early = len(EARLY)

    def over_x(index):
        layer, piece = EARLY[index]
        sems = x_sems.at[0, index], x_sems.at[1, index]
        if layer == 0:
            source = part_up.at[up_piece(piece, 1 - side_x, width // 2, chunk)]
            target = x_up.at[:, pl.ds(piece * chunk, chunk)]
        else:
            source = part_down.at[down_piece(piece, 1 - side_x, chunk // 2)]
            target = x_down.at[pl.ds(piece * chunk // 2, chunk // 2)]
        return remote_copy(source, target, *sems, {"grp": across})

    def go_home(index):
        place = pl.ds(EARLY[index][1] * chunk, chunk)
        sems = x_sems.at[2, index], x_sems.at[3, index]
        device = {"grp": core_peer(grp), "ep": partner(me, count // 2, count)}
        return remote_copy(half_up.at[:, place], far_up.at[:, place], *sems, device)

    def add_x(index):
        layer, piece = EARLY[index]
        over_x(index).wait_recv()
        if layer == 0:
            kept = part_up[up_piece(piece, side_x, width // 2, chunk)]
            span = slice(piece * chunk, (piece + 1) * chunk)
            added = kept.astype(jnp.float32) + x_up[:, span].astype(jnp.float32)
            half_up[:, span] = added.astype(jnp.bfloat16)

            @pl.when(lax.rem(grp, 2) == 1)
            def _():
                go_home(index).start()

        else:
            kept = part_down[down_piece(piece, side_x, chunk // 2), :]
            span = slice(piece * chunk // 2, (piece + 1) * chunk // 2)
            added = kept.astype(jnp.float32) + x_down[span, :].astype(jnp.float32)
            early_down[span, :] = added.astype(jnp.bfloat16)

    def gates_of(values):
        logits = jnp.dot(values, router_ref[...], preferred_element_type=jnp.float32)
        logits = jnp.where(lanes < count, logits, NEGATIVE)
        weights = jnp.exp(logits - jnp.max(logits, axis=1, keepdims=True))
        return weights / jnp.sum(weights, axis=1, keepdims=True)

    here = (lanes == expert).astype(jnp.float32)

    def through(step, mine, pair, base):
        place = pl.ds(pl.multiple_of(step * block, 16), block)
        ret = jnp.zeros((block, width), jnp.float32)
        back = jnp.zeros((block, width), jnp.float32)
        for first in range(0, part_hidden, chunk):
            span = slice(base + first, base + first + chunk)
            kept = slice(first, first + chunk)
            pre = jnp.dot(mine, up_ref[:, span], preferred_element_type=jnp.float32)
            cdf = 0.5 * (1.0 + lax.erf(pre * 0.7071067811865476))
            density = jnp.exp(-0.5 * pre * pre) * 0.3989422804014327
            low = (pre * cdf).astype(jnp.bfloat16)
            act[place, kept] = low
            ret = ret + jnp.dot(low, down_ref[span, :], preferred_element_type=jnp.float32)
            grad_act = times_t(pair, down_ref[span, :])
            slope = (grad_act * (cdf + pre * density)).astype(jnp.bfloat16)
            grad_pre[place, kept] = slope
            back = back + times_t(slope, up_ref[:, span])
        return ret, back

    def first_half(index, carry):
        step = visit(index, count)

        @pl.when(step > 0)
        def _():
            send_rows(step).wait_recv()

        mine = rows[step]
        gate = jnp.sum(gates_of(mine) * here, axis=1, keepdims=True)
        pair = (gate * grads[step].astype(jnp.float32)).astype(jnp.bfloat16)
        gated[pl.ds(pl.multiple_of(step * block, 16), block), :] = pair
        ret_sums[step], back_sums[step] = through(step, mine, pair, 0)
        return carry

    def second_half(index, carry):
        step = visit(count - 1 - index, count)
        mine = rows[step]
        cotangent = grads[step].astype(jnp.float32)
        place = pl.ds(pl.multiple_of(step * block, 16), block)
        gate_all = gates_of(mine)
        gate = jnp.sum(gate_all * here, axis=1, keepdims=True)
        ret, back = through(step, mine, gated[place, :], part_hidden)
        ret = (ret + ret_sums[step]).astype(jnp.bfloat16).astype(jnp.float32)
        out_ret[step] = (gate * ret).astype(jnp.bfloat16)
        gate_grad = jnp.sum(cotangent * ret, axis=1, keepdims=True)
        low_logits = (gate * gate_grad * (here - gate_all)).astype(jnp.bfloat16)
        logit_grads[place, :] = low_logits
        back = back + back_sums[step] + times_t(low_logits, router_ref[...])
        out_grads[step] = back.astype(jnp.bfloat16)

        @pl.when(step > 0)
        def _():
            send_back(step).start()

        @pl.when(step == 0)
        def _():
            own[1].start()

        @pl.when(index == count // 2)
        def _():
            for part in range(SETTLED):
                add_x(part)
            for part in range(SETTLED, early):
                over_x(part).start()

        return carry

    def layer_sums(base):
        def up_chunk(index, carry):
            span = pl.ds(pl.multiple_of(index * chunk, chunk), chunk)
            part_up[:, pl.ds(pl.multiple_of(base + index * chunk, chunk), chunk)] = jnp.dot(
                turned[...], grad_pre[:, span], preferred_element_type=jnp.float32
            ).astype(jnp.bfloat16)
            return carry

        def down_chunk(index, carry):
            span = pl.ds(pl.multiple_of(index * chunk, chunk), chunk)
            part = jnp.dot(turned_gated[...], act[:, span], preferred_element_type=jnp.float32)
            part_down[pl.ds(pl.multiple_of(base + index * chunk, chunk), chunk), :] = jnp.transpose(
                part
            ).astype(jnp.bfloat16)
            return carry

        lax.fori_loop(0, part_hidden // chunk, up_chunk, 0)
        lax.fori_loop(0, part_hidden // chunk, down_chunk, 0)

    lax.fori_loop(0, count, first_half, 0)
    turned[...] = jnp.transpose(rows[...].reshape(count * block, width))
    turned_gated[...] = jnp.transpose(gated[...])
    layer_sums(0)
    for index in range(SETTLED):
        over_x(index).start()
    lax.fori_loop(0, count, second_half, 0)
    layer_sums(part_hidden)
    grad_router_ref[...] = jnp.dot(
        turned[...], logit_grads[...], preferred_element_type=jnp.float32
    )
    for index in range(SETTLED, early):
        add_x(index)

    @pl.when(lax.rem(grp, 2) == 0)
    def _():
        for index in range(SETTLED):
            go_home(index).wait_recv()
        early_up[...] = (half_up[...].astype(jnp.float32) + far_up[...].astype(jnp.float32)).astype(
            jnp.bfloat16
        )

    @pl.when(lax.rem(grp, 2) == 1)
    def _():
        for index in range(SETTLED):
            go_home(index).wait_send()

    for index in range(early):
        over_x(index).wait_send()

    def finish(step, carry):
        send_rows(step).wait_send()
        send_back(step).wait()
        return carry

    lax.fori_loop(1, count, finish, 0)
    own[1].wait()


def middle(sent_rows, grads, up, down, used_up, used_down, router):
    count, block, width = sent_rows.shape
    hidden = up.shape[1]
    any_space = pl.BlockSpec(memory_space=pl.ANY)
    hbm = pl.BlockSpec(memory_space=pltpu.HBM)
    vmem = pl.BlockSpec(memory_space=pltpu.VMEM)
    low = jnp.bfloat16
    slots = count * block
    return pl.pallas_call(
        functools.partial(middle_kernel, count),
        out_shape=(
            jax.ShapeDtypeStruct((count, block, width), low),
            jax.ShapeDtypeStruct((count, block, width), low),
            jax.ShapeDtypeStruct((width, hidden), low),
            jax.ShapeDtypeStruct((hidden, width), low),
            jax.ShapeDtypeStruct((width // 2, hidden // 2), low),
            jax.ShapeDtypeStruct((hidden // 4, width), low),
            jax.ShapeDtypeStruct((width, 128), jnp.float32),
        ),
        in_specs=[hbm] * 6 + [vmem],
        out_specs=(any_space,) + (vmem,) * 6,
        scratch_shapes=[
            pltpu.VMEM((count, block, width), low),
            pltpu.VMEM((count, block, width), low),
            pltpu.VMEM((slots, width), low),
            pltpu.VMEM((slots, hidden // 2), low),
            pltpu.VMEM((slots, hidden // 2), low),
            pltpu.VMEM((slots, 128), low),
            pltpu.VMEM((count, block, width), low),
            pltpu.VMEM((width, slots), low),
            pltpu.VMEM((width, slots), low),
            pltpu.VMEM(up.shape, low),
            pltpu.VMEM(down.shape, low),
            pltpu.VMEM((count, block, width), jnp.float32),
            pltpu.VMEM((count, block, width), jnp.float32),
            pltpu.VMEM((width // 2, hidden // 2), low),
            pltpu.VMEM((hidden // 4, width), low),
            pltpu.VMEM((width // 2, hidden // 2), low),
            pltpu.VMEM((width // 2, hidden // 2), low),
            pltpu.SemaphoreType.DMA((4, count)),
            pltpu.SemaphoreType.DMA((4, len(EARLY))),
            pltpu.SemaphoreType.DMA((5,)),
        ],
        compiler_params=pltpu.CompilerParams(
            collective_id=3, has_side_effects=True, vmem_limit_bytes=63 * MIB
        ),
        cost_estimate=pl.CostEstimate(
            flops=12 * slots * width * hidden, bytes_accessed=16 * MIB, transcendentals=0
        ),
    )(sent_rows, grads, up, down, used_up, used_down, router)


def backward_kernel(
    count,
    tokens_in,
    segments,
    live,
    out_grad_in,
    weights_in,
    joint_in,
    mixed_in,
    state_in,
    logs_in,
    slots_in,
    back_in,
    out_ret,
    grad_router,
    part_up_in,
    part_down_in,
    early_up_in,
    early_down_in,
    output_out,
    tokens_grad_out,
    joint_share,
    output_share,
    pack_share,
    sum_up,
    sum_down,
    tokens,
    out_grad,
    weights,
    joint,
    mixed,
    state,
    logs,
    slots,
    back,
    part_up,
    part_down,
    early_up,
    early_down,
    output,
    tokens_grad,
    returned,
    grad_joint,
    normed_all,
    branch_all,
    mixed_grads,
    hidden_pairs,
    part,
    mate_part,
    pair_part,
    x_part,
    far_part,
    ep_part,
    turned,
    x_up,
    x_down,
    half_up,
    half_down,
    far_up,
    far_down,
    ret_sems,
    mate_sems,
    x_sems,
    ep_sems,
    sum_sems,
    local_sems,
    bring_sems,
):
    bring = [
        pltpu.make_async_copy(source, target, bring_sems.at[place])
        for place, (source, target) in enumerate(
            (
                (weights_in, weights),
                (slots_in, slots),
                (back_in, back),
                (state_in, state),
                (out_grad_in, out_grad),
                (tokens_in, tokens),
                (mixed_in, mixed),
                (joint_in, joint),
                (logs_in, logs),
                (part_up_in, part_up),
                (part_down_in, part_down),
                (early_up_in, early_up),
                (early_down_in, early_down),
            )
        )
    ]
    for copy in bring:
        copy.start()
    me, grp = lax.axis_index("ep"), lax.axis_index("grp")
    row_count, width = tokens.shape
    sequences, length = segments.shape
    block = back.shape[1]
    slot_count = count * block
    joint_width = joint.shape[1]
    head_size = width // HEADS
    factor = head_size ** (-0.5)
    mate, across = core_peer(grp), x_peer(grp)
    core, side_x = lax.rem(grp, 2), lax.div(grp, 2)
    devices = weights.shape[0]
    total = devices * weights.shape[1]
    expert = expert_of(me, grp, count)
    greet_all(count, me, grp)

    parts = EARLY + LATE
    early = len(EARLY)
    rows_up, size_up = part_up.shape[0] // 2, part_up.shape[1] // PIECES
    size_down = part_down.shape[0] // (2 * PIECES)

    def whole(index, arrays, side):
        layer, piece = parts[index]
        if layer == 0:
            return arrays[0].at[up_piece(piece, side, rows_up, size_up)]
        return arrays[1].at[down_piece(piece, side, size_down)]

    def narrow(index, arrays):
        layer, piece = parts[index]
        if layer == 0:
            return arrays[0].at[:, pl.ds((piece % 2) * size_up, size_up)]
        return arrays[1].at[pl.ds((piece % 2) * size_down, size_down)]

    def summed_x(index):
        return narrow(index, (early_up, early_down) if index < early else (half_up, half_down))

    def from_foreign(index):
        return narrow(index, (far_up.at[index // early], far_down.at[index // early]))

    def over_x(index):
        sems = sum_sems.at[0, index], sum_sems.at[1, index]
        source = whole(index, (part_up_in, part_down_in), 1 - side_x)
        return remote_copy(source, narrow(index, (x_up, x_down)), *sems, {"grp": across})

    def go_home(index):
        sems = sum_sems.at[2, index], sum_sems.at[3, index]
        device = {"grp": mate, "ep": partner(me, count // 2, count)}
        source = narrow(index, (early_up_in, early_down_in)) if index < early else summed_x(index)
        return remote_copy(source, from_foreign(index), *sems, device)

    def spread_x(index):
        place = whole(index, (sum_up, sum_down), side_x)
        sems = sum_sems.at[4, index], sum_sems.at[5, index]
        return remote_copy(place, place, *sems, {"grp": across})

    def spread_core(index, side, first):
        place = whole(index, (sum_up, sum_down), side)
        sems = sum_sems.at[first, index], sum_sems.at[first + 1, index]
        return remote_copy(place, place, *sems, {"grp": mate})

    def own_half(index):
        return spread_core(index, side_x, 6)

    def other_half(index):
        return spread_core(index, 1 - side_x, 8)

    def leave(index):
        @pl.when(core == 1)
        def _():
            go_home(index).start()

    def add_x(index):
        over_x(index).wait_recv()
        kept = whole(index, (part_up, part_down), side_x)[...].astype(jnp.float32)
        landed = narrow(index, (x_up, x_down))[...].astype(jnp.float32)
        summed_x(index)[...] = (kept + landed).astype(jnp.bfloat16)
        if index + 2 < len(parts):
            over_x(index + 2).start()
        leave(index)

    def spread(index):
        spread_x(index).start()
        own_half(index).start()

    def add_home(index):
        @pl.when(core == 0)
        def _():
            go_home(index).wait_recv()
            near = summed_x(index)[...].astype(jnp.float32)
            foreign = from_foreign(index)[...].astype(jnp.float32)
            whole(index, (sum_up, sum_down), side_x)[...] = (near + foreign).astype(jnp.bfloat16)
            spread(index)

    def pass_half(index):
        @pl.when(core == 0)
        def _():
            spread_x(index).wait_recv()
            other_half(index).start()

    for index in range(SETTLED, early):
        leave(index)
    over_x(early).start()
    over_x(early + 1).start()

    def send_ret(step):
        return remote_copy(
            out_ret.at[step],
            returned.at[expert],
            ret_sems.at[0, step],
            ret_sems.at[1, step],
            seat(me, grp, step, count),
        )

    keep = pltpu.make_async_copy(out_ret.at[0], returned.at[expert], local_sems.at[0])
    keep.start()

    half_ep = count // 2
    far_steps = [step for step in range(count) if step % half_ep >= half_ep // 2]
    for step in range(1, count):
        if step not in far_steps:
            send_ret(step).start()
    send_ret(far_steps[0]).start()
    send_ret(far_steps[1]).start()
    pairs = HEADS // 2
    columns = [(pair * 384, 384) for pair in range(pairs)]
    columns += [(joint_width, width), (joint_width + width, 128)]
    for copy in bring[:6]:
        copy.wait()
    pack = weights[:, :, joint_width + width :].reshape(total, 128)
    gains = jnp.transpose(pack.astype(jnp.float32))
    gain_one = gains[count : count + 1]
    gain_two = gains[count + 1 : count + 2]
    half = lax.broadcasted_iota(jnp.int32, (length, 128), 1) < head_size
    halves = (flags(half), flags(jnp.logical_not(half)))
    ints = jnp.transpose(segments[...].astype(jnp.float32)).astype(jnp.int32)

    def chosen_of(rows):
        index = lax.broadcasted_iota(jnp.int32, (length, slot_count), 1)
        pair = slots[rows, :]
        return flags((index == pair[:, 0:1]) | (index == pair[:, 1:2]))

    def to_mate(chunk, which):
        first, size = columns[chunk]
        span = pl.ds(first, size)
        return remote_copy(
            part.at[pl.ds((2 * which + 1 - core) * count, count), :, span],
            mate_part.at[which, :, :, span],
            mate_sems.at[0, chunk, which],
            mate_sems.at[1, chunk, which],
            {"grp": mate},
        )

    def to_x(chunk):
        first, size = columns[chunk]
        span = pl.ds(first, size)
        sems = x_sems.at[0, chunk], x_sems.at[1, chunk]
        source = pair_part.at[1 - side_x, :, :, span]
        return remote_copy(source, x_part.at[:, :, span], *sems, {"grp": across})

    def to_ep(chunk, step):
        first, size = columns[chunk]
        span = pl.ds(first, size)
        other = partner(me, step, count)
        return remote_copy(
            far_part.at[other, :, span],
            ep_part.at[step, :, span],
            ep_sems.at[0, chunk, step],
            ep_sems.at[1, chunk, step],
            {"ep": other},
        )

    def sum_core(chunk):
        first, size = columns[chunk]
        span = slice(first, first + size)
        for which in range(2):
            to_mate(chunk, which).wait_recv()
            owner = 2 * which + core
            pair_part[which, :, :, span] = (
                part[pl.ds(owner * count, count), :, span].astype(jnp.float32)
                + mate_part[which, :, :, span].astype(jnp.float32)
            ).astype(jnp.bfloat16)
        to_x(chunk).start()

    def sum_x(chunk):
        first, size = columns[chunk]
        span = slice(first, first + size)
        to_x(chunk).wait_recv()
        far_part[:, :, span] = (
            pair_part[side_x, :, :, span].astype(jnp.float32) + x_part[:, :, span].astype(jnp.float32)
        ).astype(jnp.bfloat16)

        def start(step, carry):
            to_ep(chunk, step).start()
            return carry

        lax.fori_loop(1, count, start, 0)

    def sum_ep(chunk):
        first, size = columns[chunk]
        span = slice(first, first + size)

        def add(step, added):
            to_ep(chunk, step).wait_recv()
            return added + ep_part[step, :, span].astype(jnp.float32)

        share = lax.fori_loop(1, count, add, far_part[me, :, span].astype(jnp.float32))
        if chunk < pairs:
            for third in range(3):
                at = third * width + chunk * 128
                joint_share[:, at : at + 128] = share[:, third * 128 : third * 128 + 128]
        elif chunk == pairs:
            output_share[...] = share
        else:
            pack_share[...] = share

    shape = (devices, total // devices)

    def lower_part(number, carry):
        rows = pl.ds(pl.multiple_of(number * length, length), length)
        grad_normed_two = jnp.dot(
            chosen_of(rows),
            back[...].reshape(slot_count, width),
            preferred_element_type=jnp.float32,
        )
        _, unit, inverse = normalize(state[rows, :], gain_two)
        inner, share = normalize_back(grad_normed_two, gain_two, unit, inverse)
        grad_state = out_grad[rows, :].astype(jnp.float32) + inner
        tokens_grad[rows, :] = grad_state
        branch = grad_state.astype(jnp.bfloat16)
        branch_all[rows, :] = branch
        mixed_grads[rows, :] = times_t(
            branch, weights[:, :, joint_width : joint_width + width].reshape(total, width)
        ).astype(jnp.bfloat16)
        allowed = seen(segments[pl.ds(number, 1), :], live[pl.ds(number, 1), :], column(ints, number))
        hidden_pairs[rows, :] = jnp.where(allowed, 0.0, NEGATIVE)
        normed = normalize(tokens[rows, :].astype(jnp.float32), gain_one)[0]
        normed_all[rows, :] = normed.astype(jnp.bfloat16)
        return carry + share[None, :]

    nothing = jnp.zeros((1, width), jnp.float32)
    grad_two = lax.fori_loop(0, sequences, lower_part, nothing)
    for copy in bring[6:]:
        copy.wait()

    @pl.when(core == 0)
    def _():
        for index in range(SETTLED):
            whole(index, (sum_up, sum_down), side_x)[...] = summed_x(index)[...]
            spread(index)

    turned[...] = jnp.transpose(mixed[...])
    first, size = columns[pairs]
    part[:, :, first : first + size] = (
        jnp.dot(turned[...], branch_all[...], preferred_element_type=jnp.float32)
        .astype(jnp.bfloat16)
        .reshape(*shape, size)
    )
    to_mate(pairs, 0).start()
    to_mate(pairs, 1).start()
    turned[...] = jnp.transpose(normed_all[...])

    for pair in range(pairs):
        at = pair * 128

        def attend(number, carry, pair=pair, at=at):
            rows = pl.ds(pl.multiple_of(number * length, length), length)
            query = joint[rows, at : at + 128]
            key = joint[rows, width + at : width + at + 128]
            value = joint[rows, 2 * width + at : 2 * width + at + 128]
            grad_out = mixed_grads[rows, at : at + 128]
            unseen = hidden_pairs[rows, :]
            results = []
            for side in range(2):
                scores = times_t(query * halves[side], key) * factor
                log_all = logs[rows, 2 * pair + side : 2 * pair + side + 1]
                probs = jnp.exp(scores + unseen - log_all)
                grad_value = outer(probs.astype(jnp.bfloat16), grad_out)
                grad_probs = times_t(grad_out * halves[side], value)
                delta = jnp.sum(probs * grad_probs, axis=-1, keepdims=True)
                grad_scores = (probs * (grad_probs - delta)).astype(jnp.bfloat16)
                grad_query = jnp.dot(grad_scores, key, preferred_element_type=jnp.float32) * factor
                grad_key = outer(grad_scores, query) * factor
                results.append((grad_query, grad_key, grad_value))
            for third in range(3):
                grad_joint[rows, third * width + at : third * width + at + 128] = jnp.where(
                    half, results[0][third], results[1][third]
                ).astype(jnp.bfloat16)
            return carry

        lax.fori_loop(0, sequences, attend, 0, unroll=4)
        first, size = columns[pair]
        mine = jnp.concatenate(
            [grad_joint[:, third * width + at : third * width + at + 128] for third in range(3)], axis=1
        )
        part[:, :, first : first + size] = (
            jnp.dot(turned[...], mine, preferred_element_type=jnp.float32)
            .astype(jnp.bfloat16)
            .reshape(*shape, size)
        )
        to_mate(pair, 0).start()
        to_mate(pair, 1).start()
        sum_core(pairs if pair == 0 else pair - 1)
        if pair == 0:
            add_x(early)
            add_x(early + 1)
        elif pair == 1:
            sum_x(pairs)
        else:
            sum_x(pair - 2)
        if pair == 2:
            for index in range(SETTLED, early):
                add_home(index)
            add_x(early + 2)
            add_x(early + 3)
            sum_ep(pairs)
        if pair == 1:
            send_ret(far_steps[2]).start()
            send_ret(far_steps[3]).start()

    def upper_part(number, carry):
        rows = pl.ds(pl.multiple_of(number * length, length), length)
        grad_normed = times_t(
            grad_joint[rows, :], weights[:, :, :joint_width].reshape(total, joint_width)
        )
        _, unit, inverse = normalize(tokens[rows, :].astype(jnp.float32), gain_one)
        inner, share = normalize_back(grad_normed, gain_one, unit, inverse)
        tokens_grad[rows, :] = tokens_grad[rows, :] + inner
        return carry + share[None, :]

    grad_one = lax.fori_loop(0, sequences, upper_part, nothing)
    leaving = (
        pltpu.make_async_copy(tokens_grad, tokens_grad_out, bring_sems.at[len(bring)]),
        pltpu.make_async_copy(output, output_out, bring_sems.at[len(bring) + 1]),
    )
    leaving[0].start()
    lines = lax.broadcasted_iota(jnp.int32, (128, width), 0)
    gain_lines = jnp.where(
        lines == count, grad_one, jnp.where(lines == count + 1, grad_two, 0.0)
    )
    first, size = columns[pairs + 1]
    part[:, :, first : first + size] = (
        (grad_router[...] + jnp.transpose(gain_lines)).astype(jnp.bfloat16).reshape(*shape, 128)
    )
    to_mate(pairs + 1, 0).start()
    to_mate(pairs + 1, 1).start()
    for index in range(SETTLED):
        pass_half(index)
    sum_core(pairs - 1)
    sum_core(pairs + 1)
    sum_x(pairs - 2)
    add_home(early)
    add_home(early + 1)
    sum_x(pairs - 1)
    sum_x(pairs + 1)
    for index in range(SETTLED, early):
        pass_half(index)
    keep.wait()

    def from_all(step, carry):
        send_ret(step).wait()
        return carry

    lax.fori_loop(1, count, from_all, 0)

    def combine(number, carry):
        rows = pl.ds(pl.multiple_of(number * length, length), length)
        gathered = jnp.dot(
            chosen_of(rows),
            returned[...].reshape(slot_count, width),
            preferred_element_type=jnp.float32,
        )
        output[rows, :] = (state[rows, :] + gathered).astype(jnp.bfloat16)
        return carry

    lax.fori_loop(0, sequences, combine, 0)
    leaving[1].start()
    add_home(early + 2)
    pass_half(early)
    pass_half(early + 1)
    add_home(early + 3)
    for chunk in range(pairs):
        sum_ep(chunk)
    sum_ep(pairs + 1)
    pass_half(early + 2)
    pass_half(early + 3)

    @pl.when(core == 0)
    def _():
        for chunk in range(CHUNKS):
            spread_x(chunk).wait_send()
            own_half(chunk).wait_send()
            other_half(chunk).wait_send()

    @pl.when(core == 1)
    def _():
        for index in range(SETTLED, CHUNKS):
            go_home(index).wait_send()
        for chunk in range(CHUNKS):
            own_half(chunk).wait_recv()
            other_half(chunk).wait_recv()

    for copy in leaving:
        copy.wait()
    for index in range(early, len(parts)):
        over_x(index).wait_send()
    for chunk in range(len(columns)):
        to_mate(chunk, 0).wait_send()
        to_mate(chunk, 1).wait_send()
        to_x(chunk).wait_send()

        def finish(step, carry, chunk=chunk):
            to_ep(chunk, step).wait_send()
            return carry

        lax.fori_loop(1, count, finish, 0)


def backward(
    tokens,
    segments,
    live,
    out_grad,
    weights,
    joint,
    mixed,
    state,
    logs,
    slots,
    back,
    ret,
    router,
    part_up,
    part_down,
    early_up,
    early_down,
):
    row_count, width = tokens.shape
    count = back.shape[0]
    devices, shard_rows, all_width = weights.shape
    hbm = pl.BlockSpec(memory_space=pltpu.HBM)
    vmem = pl.BlockSpec(memory_space=pltpu.VMEM)
    low = jnp.bfloat16
    quarter = (count, shard_rows, all_width)
    return pl.pallas_call(
        functools.partial(backward_kernel, count),
        out_shape=(
            jax.ShapeDtypeStruct((row_count, width), low),
            jax.ShapeDtypeStruct((row_count, width), jnp.float32),
            jax.ShapeDtypeStruct((shard_rows, joint.shape[1]), jnp.float32),
            jax.ShapeDtypeStruct((shard_rows, width), jnp.float32),
            jax.ShapeDtypeStruct((shard_rows, 128), jnp.float32),
            jax.ShapeDtypeStruct(part_up.shape, low),
            jax.ShapeDtypeStruct(part_down.shape, low),
        ),
        in_specs=[hbm, vmem, vmem] + [hbm] * 9 + [vmem] + [hbm] * 4,
        out_specs=(hbm,) * 2 + (vmem,) * 5,
        scratch_shapes=[
            pltpu.VMEM(array.shape, array.dtype)
            for array in (
                tokens,
                out_grad,
                weights,
                joint,
                mixed,
                state,
                logs,
                slots,
                back,
                part_up,
                part_down,
                early_up,
                early_down,
            )
        ]
        + [
            pltpu.VMEM((row_count, width), low),
            pltpu.VMEM((row_count, width), jnp.float32),
            pltpu.VMEM(back.shape, low),
            pltpu.VMEM(joint.shape, low),
            pltpu.VMEM((row_count, width), low),
            pltpu.VMEM((row_count, width), low),
            pltpu.VMEM((row_count, width), low),
            pltpu.VMEM((row_count, segments.shape[1]), jnp.float32),
            pltpu.VMEM(weights.shape, low),
            pltpu.VMEM((2,) + quarter, low),
            pltpu.VMEM((2,) + quarter, low),
            pltpu.VMEM(quarter, low),
            pltpu.VMEM(quarter, low),
            pltpu.VMEM(quarter, low),
            pltpu.VMEM((width, row_count), low),
            pltpu.VMEM(early_up.shape, low),
            pltpu.VMEM(early_down.shape, low),
            pltpu.VMEM(early_up.shape, low),
            pltpu.VMEM(early_down.shape, low),
            pltpu.VMEM((2,) + early_up.shape, low),
            pltpu.VMEM((2,) + early_down.shape, low),
            pltpu.SemaphoreType.DMA((2, count)),
            pltpu.SemaphoreType.DMA((2, HEADS // 2 + 2, 2)),
            pltpu.SemaphoreType.DMA((2, HEADS // 2 + 2)),
            pltpu.SemaphoreType.DMA((2, HEADS // 2 + 2, count)),
            pltpu.SemaphoreType.DMA((10, CHUNKS)),
            pltpu.SemaphoreType.DMA((1,)),
            pltpu.SemaphoreType.DMA((15,)),
        ],
        compiler_params=pltpu.CompilerParams(
            collective_id=4, has_side_effects=True, vmem_limit_bytes=63 * MIB
        ),
    )(
        tokens,
        segments,
        live,
        out_grad,
        weights,
        joint,
        mixed,
        state,
        logs,
        slots,
        back,
        ret,
        router,
        part_up,
        part_down,
        early_up,
        early_down,
    )


def finish_kernel(
    copied_in,
    pack,
    summed_in,
    copied_out,
    pack_out,
    summed_out,
    copied,
    narrow,
    wide,
    in_sems,
    out_sems,
    piece_sems,
):
    arrive = [
        pltpu.make_async_copy(source, target, in_sems.at[place])
        for place, (source, target) in enumerate(zip(copied_in, copied))
    ]
    leave = [
        pltpu.make_async_copy(source, target, out_sems.at[place])
        for place, (source, target) in enumerate(zip(copied, copied_out))
    ]

    def piece(layer, number):
        size = narrow[layer].shape[0] // PIECES
        rows = pl.ds(number * size, size)
        return (
            pltpu.make_async_copy(
                summed_in[layer].at[rows], narrow[layer].at[rows], piece_sems.at[0, layer, number]
            ),
            pltpu.make_async_copy(
                wide[layer].at[rows], summed_out[layer].at[rows], piece_sems.at[1, layer, number]
            ),
            rows,
        )

    pieces = [piece(layer, number) for number in range(PIECES) for layer in range(2)]
    for number, part in enumerate(pieces):
        part[0].start()
        if number < len(arrive):
            arrive[number].start()
    shard_rows = pack.shape[0]
    tall = jnp.concatenate([pack[...], jnp.zeros((128 - shard_rows, 128), jnp.float32)], axis=0)
    pack_out[...] = jnp.transpose(tall)[:16, :shard_rows]
    for number, (load, store, rows) in enumerate(pieces):
        load.wait()
        wide[number % 2][rows, :] = narrow[number % 2][rows, :].astype(jnp.float32)
        store.start()
        if number < len(arrive):
            arrive[number].wait()
            leave[number].start()
    for copy in leave:
        copy.wait()
    for _, store, _ in pieces:
        store.wait()


def finish(copied, pack, summed):
    hbm = pl.BlockSpec(memory_space=pltpu.HBM)
    vmem = pl.BlockSpec(memory_space=pltpu.VMEM)
    wide = [jax.ShapeDtypeStruct(array.shape, jnp.float32) for array in summed]
    return pl.pallas_call(
        finish_kernel,
        out_shape=(
            [jax.ShapeDtypeStruct(array.shape, array.dtype) for array in copied],
            jax.ShapeDtypeStruct((16, pack.shape[0]), jnp.float32),
            wide,
        ),
        in_specs=[[hbm] * len(copied), vmem, [hbm] * 2],
        out_specs=([hbm] * len(copied), vmem, [hbm] * 2),
        scratch_shapes=[
            [pltpu.VMEM(array.shape, array.dtype) for array in copied],
            [pltpu.VMEM(array.shape, array.dtype) for array in summed],
            [pltpu.VMEM(array.shape, jnp.float32) for array in summed],
            pltpu.SemaphoreType.DMA((len(copied),)),
            pltpu.SemaphoreType.DMA((len(copied),)),
            pltpu.SemaphoreType.DMA((2, 2, PIECES)),
        ],
        compiler_params=pltpu.CompilerParams(vmem_limit_bytes=63 * MIB),
    )(copied, pack, summed)


def per_device_fused(
    tokens,
    segments,
    patch_mask,
    choices,
    priority,
    first_gain,
    joint_weight,
    output_weight,
    second_gain,
    router_weight,
    expert_up,
    expert_down,
    out_grad,
):
    row_count, width = tokens.shape
    experts = router_weight.shape[1]
    capacity = (21 * choices.shape[1] * row_count + 20 * experts - 1) // (20 * experts)
    block = -(-capacity // 16) * 16
    weights, joint, mixed, state, sent_rows, logs, slots, router, grads, used_up, used_down = forward(
        experts,
        capacity,
        block,
        tokens,
        segments,
        patch_mask,
        choices.T,
        priority,
        out_grad,
        joint_weight,
        output_weight,
        jnp.stack([first_gain, second_gain]),
        router_weight.T,
        expert_up[0],
        expert_down[0],
    )
    back, ret, part_up, part_down, early_up, early_down, grad_router = middle(
        sent_rows, grads, expert_up[0], expert_down[0], used_up, used_down, router
    )
    output, tokens_grad, grad_joint, grad_output, grad_pack, grad_up, grad_down = backward(
        tokens,
        segments,
        patch_mask,
        out_grad,
        weights,
        joint,
        mixed,
        state,
        logs,
        slots,
        back,
        ret,
        grad_router,
        part_up,
        part_down,
        early_up,
        early_down,
    )
    (output, tokens_grad, grad_joint, grad_output), lines, (grad_up, grad_down) = finish(
        [output, tokens_grad, grad_joint, grad_output], grad_pack, [grad_up, grad_down]
    )
    return (
        output,
        tokens_grad,
        lines[experts],
        grad_joint,
        grad_output,
        lines[experts + 1],
        lines[:experts].T,
        grad_up[None],
        grad_down[None],
    )


def experts_both_ways(sent_rows, sent_grads, up, down, router):
    count, block, width = sent_rows.shape
    experts = router.shape[1]
    hidden = up.shape[1]
    router = jnp.pad(router, ((0, 0), (0, 128 - experts)))
    any_space = pl.BlockSpec(memory_space=pl.ANY)
    vmem = pl.BlockSpec(memory_space=pltpu.VMEM)
    low = jnp.bfloat16
    slots = count * block
    return pl.pallas_call(
        functools.partial(expert_kernel, count, experts),
        out_shape=(
            jax.ShapeDtypeStruct((count, block, width), low),
            jax.ShapeDtypeStruct((count, block, width), low),
            jax.ShapeDtypeStruct((width, hidden), low),
            jax.ShapeDtypeStruct((hidden, width), low),
            jax.ShapeDtypeStruct((width, 128), jnp.float32),
        ),
        in_specs=[any_space, any_space, vmem, vmem, vmem],
        out_specs=(any_space, any_space, vmem, vmem, vmem),
        scratch_shapes=[
            pltpu.VMEM((count, block, width), low),
            pltpu.VMEM((count, block, width), low),
            pltpu.VMEM((slots, width), low),
            pltpu.VMEM((slots, hidden), low),
            pltpu.VMEM((slots, hidden), low),
            pltpu.VMEM((slots, 128), low),
            pltpu.VMEM((count, block, width), low),
            pltpu.VMEM((count, block, width), low),
            pltpu.VMEM((width, slots), low),
            pltpu.SemaphoreType.DMA((8, count)),
            pltpu.SemaphoreType.DMA((4,)),
        ],
        compiler_params=pltpu.CompilerParams(
            collective_id=1, has_side_effects=True, vmem_limit_bytes=58 * MIB
        ),
        cost_estimate=pl.CostEstimate(
            flops=12 * slots * width * hidden, bytes_accessed=16 * MIB, transcendentals=0
        ),
    )(sent_rows, sent_grads, up, down, router)


def per_device(
    tokens,
    segments,
    patch_mask,
    choices,
    priority,
    first_gain,
    joint_weight,
    output_weight,
    second_gain,
    router_weight,
    expert_up,
    expert_down,
    out_grad,
):
    row_count, width = tokens.shape
    head_size = width // HEADS
    factor = head_size ** (-0.5)
    expert_count = router_weight.shape[1]
    length = segments.shape[1]
    capacity = (21 * choices.shape[1] * row_count + 20 * expert_count - 1) // (20 * expert_count)
    block_rows = min(row_count, 512)
    gain_one, joint_full, output_full, gain_two, router_full = (
        lax.all_gather(first_gain, ("grp", "ep"), axis=0, tiled=True),
        lax.all_gather(joint_weight, ("grp", "ep"), axis=0, tiled=True),
        lax.all_gather(output_weight, ("grp", "ep"), axis=0, tiled=True),
        lax.all_gather(second_gain, ("grp", "ep"), axis=0, tiled=True),
        lax.all_gather(router_weight, ("grp", "ep"), axis=0, tiled=True),
    )
    inputs = tokens.astype(jnp.float32)
    gain_one = gain_one.astype(jnp.float32)
    gain_two = gain_two.astype(jnp.float32)
    normed_f, unit_one, inverse_one = normalize(inputs, gain_one)
    normed = normed_f.astype(jnp.bfloat16)
    joint = jnp.dot(normed, joint_full, preferred_element_type=jnp.float32).astype(jnp.bfloat16)
    joint = joint.reshape(row_count, 3, HEADS, head_size)
    live = patch_mask.reshape(row_count)
    position = lax.broadcasted_iota(jnp.int32, (row_count,), 0)
    group = position // length * length + segments.reshape(row_count)
    masks = []
    mixed_parts = []
    log_parts = []
    for start in range(0, row_count, block_rows):
        allowed = visible(group[start : start + block_rows], live[start : start + block_rows])
        block = joint[start : start + block_rows]
        mixed_block, log_total = attend_forward(
            block[:, 0], block[:, 1], block[:, 2], allowed, factor
        )
        masks.append(allowed)
        mixed_parts.append(mixed_block)
        log_parts.append(log_total)
    mixed = jnp.concatenate(mixed_parts, axis=0).reshape(row_count, width).astype(jnp.bfloat16)
    state = inputs + jnp.dot(mixed, output_full, preferred_element_type=jnp.float32)
    normed_two_f, unit_two, inverse_two = normalize(state, gain_two)
    normed_two = normed_two_f.astype(jnp.bfloat16)
    slot_one, slot_two = route(
        choices, live, priority.reshape(row_count), expert_count, capacity
    )
    block = -(-capacity // 16) * 16
    slots = expert_count * block
    index = lax.broadcasted_iota(jnp.int32, (slots, row_count), 0)
    chosen = ((index == slot_one[None, :]) | (index == slot_two[None, :])).astype(jnp.bfloat16)
    spread = lambda values: (
        jnp.dot(chosen, values, preferred_element_type=jnp.float32)
        .astype(jnp.bfloat16)
        .reshape(expert_count, block, width)
    )
    collect = lambda values: outer(chosen, values.reshape(slots, width))
    grad = out_grad.astype(jnp.float32)
    back, returned, grad_up, grad_down, grad_router = experts_both_ways(
        spread(normed_two), spread(out_grad), expert_up[0], expert_down[0], router_full
    )
    output = (state + collect(returned)).astype(jnp.bfloat16)
    grad_router = grad_router[:, :expert_count]
    grad_normed_two = collect(back)
    grad_state_in, grad_gain_two = normalize_back(grad_normed_two, gain_two, unit_two, inverse_two)
    grad_state = grad + grad_state_in
    grad_branch = grad_state.astype(jnp.bfloat16)
    grad_output_w = outer(mixed, grad_branch)
    grad_mixed = (
        times_t(grad_branch, output_full).astype(jnp.bfloat16).reshape(row_count, HEADS, head_size)
    )
    grad_parts = []
    for number, start in enumerate(range(0, row_count, block_rows)):
        block = joint[start : start + block_rows]
        grad_parts.append(
            attend_backward(
                block[:, 0],
                block[:, 1],
                block[:, 2],
                masks[number],
                log_parts[number],
                grad_mixed[start : start + block_rows],
                factor,
            )
        )
    grad_joint = (
        jnp.concatenate(grad_parts, axis=0).reshape(row_count, 3 * width).astype(jnp.bfloat16)
    )
    grad_joint_w = outer(normed, grad_joint)
    grad_normed = times_t(grad_joint, joint_full)
    grad_inputs_in, grad_gain_one = normalize_back(grad_normed, gain_one, unit_one, inverse_one)
    tokens_grad = grad_state + grad_inputs_in
    shares = (
        lax.psum_scatter(grad_gain_one, ("grp", "ep"), scatter_dimension=0, tiled=True),
        lax.psum_scatter(grad_joint_w, ("grp", "ep"), scatter_dimension=0, tiled=True),
        lax.psum_scatter(grad_output_w, ("grp", "ep"), scatter_dimension=0, tiled=True),
        lax.psum_scatter(grad_gain_two, ("grp", "ep"), scatter_dimension=0, tiled=True),
        lax.psum_scatter(grad_router, ("grp", "ep"), scatter_dimension=0, tiled=True),
    )
    grad_up, grad_down = (
        lax.psum(grad_up, "grp").astype(jnp.float32)[None],
        lax.psum(grad_down, "grp").astype(jnp.float32)[None],
    )
    return (
        output,
        tokens_grad,
        shares[0],
        shares[1],
        shares[2],
        shares[3],
        shares[4],
        grad_up,
        grad_down,
    )


def solution(mesh):
    in_specs = (
        P(("grp", "ep"), None),
        P(("grp", "ep"), None),
        P(("grp", "ep"), None),
        P(("grp", "ep"), None),
        P(("grp", "ep"), None),
        P(("grp", "ep")),
        P(("grp", "ep"), None),
        P(("grp", "ep"), None),
        P(("grp", "ep")),
        P(("grp", "ep"), None),
        P("ep", None, None),
        P("ep", None, None),
        P(("grp", "ep"), None),
    )
    out_specs = (
        P(("grp", "ep"), None),
        P(("grp", "ep"), None),
        P(("grp", "ep")),
        P(("grp", "ep"), None),
        P(("grp", "ep"), None),
        P(("grp", "ep")),
        P(("grp", "ep"), None),
        P("ep", None, None),
        P("ep", None, None),
    )
    fused = mesh.shape["grp"] == 4 and mesh.shape["ep"] == 8
    return jax.shard_map(
        per_device_fused if fused else per_device, mesh=mesh, in_specs=in_specs, out_specs=out_specs, check_vma=False
    )
```
